32 devices in a mesh: dp: 4 (over z), ctx: 8 (over y, x, core).
Axes of the slice: x: 2, y: 2, z: 4, core: 2. Of those that a mesh axis runs over, the one named last changes fastest.
Arguments:
- tokens: float32 [16, 2048, 768], P('dp', 'ctx'), may hold values from -6 to 6
- cotangent: float32 [16, 2048, 768], P('dp', 'ctx'), may hold values from -6 to 6
- lengths: int32 [16], replicated, may hold values from 1024 to 2048, as said below
- w_query: bfloat16 [768, 768], P(('dp', 'ctx')), may hold values from -0.21875 to 0.21875
- w_key: bfloat16 [768, 768], P(('dp', 'ctx')), may hold values from -0.21875 to 0.21875
- w_value: bfloat16 [768, 768], P(('dp', 'ctx')), may hold values from -0.21875 to 0.21875
- w_attn_out: bfloat16 [768, 768], P(('dp', 'ctx')), may hold values from -6 to 6
- w_up: bfloat16 [768, 3072], P(('dp', 'ctx')), may hold values from -0.21875 to 0.21875
- b_up: bfloat16 [3072], P(('dp', 'ctx')), may hold values from -4 to 4
- w_down: bfloat16 [3072, 768], P(('dp', 'ctx')), may hold values from -0.109375 to 0.109375
- vectors: bfloat16 [8, 768], P(None, ('dp', 'ctx')), may hold values from -0.6 to 1.4
Outputs:
- output: float32 [16, 2048, 768], P('dp', 'ctx')
- d_tokens: float32 [16, 2048, 768], P('dp', 'ctx')
- d_w_query: float32 [768, 768], P(('dp', 'ctx'))
- d_w_key: float32 [768, 768], P(('dp', 'ctx'))
- d_w_value: float32 [768, 768], P(('dp', 'ctx'))
- d_w_attn_out: float32 [768, 768], P(('dp', 'ctx'))
- d_w_up: float32 [768, 3072], P(('dp', 'ctx'))
- d_b_up: float32 [3072], P(('dp', 'ctx'))
- d_w_down: float32 [3072, 768], P(('dp', 'ctx'))
- d_vectors: float32 [8, 768], P(None, ('dp', 'ctx'))
The draws below stay inside these ranges and needn't reach their ends.
Inputs may be any that keep to these rules, and one draw needn't show every extreme that they name: `lengths`: each sequence fills 2048 / 2 to 2048 of its 2048 slots; among the 4 sequences of every index of dp one has length 2048.
All inputs are finite; a program needn't handle non-finite values.
Results may differ from the reference program's by a relative error of at most 0.018.
The reference program's roundings to bfloat16 on the way count: a program that leaves them out, or rounds other values in their place, can miss the bound.
Values may be sent and summed in bfloat16 or wider, within the bound.
A program may use at most 320 MiB of HBM per device.

```python
import math
import jax
import jax.numpy as jnp
from jax import lax

D = 768
HEADS = 12
HEAD_DIM = 64
FF = 3072
CAP = 2048
SEQ_GRP = 4
SEQS = 16
N_CTX = 8


def draw_lengths(key, part):
    length_key = jax.random.fold_in(key, 11)
    pick_key = jax.random.fold_in(key, 12)
    uniform_len = jax.random.randint(length_key, (SEQS,), CAP // 2, CAP + 1, dtype=jnp.int32)
    chosen = jax.random.randint(pick_key, (SEQS // SEQ_GRP,), 0, SEQ_GRP, dtype=jnp.int32)
    seq_slots = jnp.arange(SEQS, dtype=jnp.int32)
    longest = seq_slots % SEQ_GRP == jnp.repeat(chosen, SEQ_GRP, total_repeat_length=SEQS)
    return jnp.where(longest, CAP, uniform_len).astype(jnp.int32)


def draw_vectors(key, part):
    row_index = jnp.arange(8, dtype=jnp.int32)[:, None]
    bias_key = jax.random.fold_in(key, 21)
    gain_key = jax.random.fold_in(key, 22)
    biases = jax.random.uniform(bias_key, (8, D), jnp.float32, -0.58, 0.58)
    gains = jax.random.uniform(gain_key, (8, D), jnp.float32, 0.7, 1.3)
    return jnp.where(row_index >= 6, gains, biases).astype(jnp.bfloat16)


def raised(entries, key, source, target, blocks, factor):
    owner, partner = [(jnp.arange(entries.shape[axis_at]) // (entries.shape[axis_at] // blocks)).reshape([-1 if axis == axis_at else 1 for axis in range(entries.ndim)]) for axis_at in (source, target)]
    chosen = jax.random.permutation(key, blocks)[partner]
    strong = (owner == chosen) | (owner == (partner + blocks // 2) % blocks)
    return jnp.where(strong, factor * entries, entries)


def shard_levels(key, dims, cuts, low, top_value):
    def one(axis_at, parts):
        steps = jax.random.uniform(jax.random.fold_in(jax.random.fold_in(key, 6), axis_at), (parts,), jnp.float32, low / len(cuts), top_value / len(cuts))
        return jnp.repeat(jnp.exp(steps), dims[axis_at] // parts).reshape((-1,) + (1,) * (len(dims) - axis_at - 1))

    gain = one(*cuts[0])
    for cut in cuts[1:]:
        gain = gain * one(*cut)
    return gain


def bell_draw(stream_key, dims, width, most, pieces=(), kind=jnp.bfloat16):
    loudness = shard_levels(stream_key, dims, pieces, -0.22, 0.18) if pieces else 1.0
    array = jax.random.normal(stream_key, dims, jnp.float32) * width * loudness
    return jnp.minimum(jnp.maximum(array, -most), most).astype(kind)


def heavy_noise(rng, shape, scale, limit, pieces, heavy, held_as=jnp.bfloat16):
    array = scale * jax.random.normal(rng, shape, jnp.float32)
    if pieces:
        array = array * shard_levels(rng, shape, pieces, -0.22, 0.18)
    return jnp.clip(raised(array, jax.random.fold_in(rng, 3), *heavy), -limit, limit).astype(held_as)


def setup_inputs(seed: int = 0) -> dict:
    streams_of = jax.random.split(jax.random.key(seed), 12)
    return {
        "tokens": heavy_noise(streams_of[0], (SEQS, CAP, D), 1.0, 6.0, ((0, 4), (1, 8)), (1, 2, 8, 2.0), jnp.float32),
        "cotangent": heavy_noise(streams_of[1], (SEQS, CAP, D), 1.0, 6.0, ((0, 4), (1, 8)), (0, 2, 4, 2.0), jnp.float32),
        "lengths": draw_lengths(jax.random.fold_in(streams_of[11], 71), 0),
        "w_query": bell_draw(streams_of[3], (D, D), D ** -0.5, 0.21875, ((0, 32),)),
        "w_key": bell_draw(streams_of[4], (D, D), D ** -0.5, 0.21875, ((0, 32),)),
        "w_value": bell_draw(streams_of[5], (D, D), D ** -0.5, 0.21875, ((0, 32),)),
        "w_attn_out": bell_draw(streams_of[6], (D, D), (max(4 * D // CAP, 1)) ** -0.5, 6.0, ((0, 32),)),
        "w_up": bell_draw(streams_of[7], (D, FF), D ** -0.5, 0.21875, ((0, 32),)),
        "b_up": bell_draw(streams_of[8], (FF,), 0.3, 4.0, ((0, 32),)),
        "w_down": bell_draw(streams_of[9], (FF, D), FF ** -0.5, 0.109375, ((0, 32),)),
        "vectors": draw_vectors(jax.random.fold_in(streams_of[11], 71), 0),
    }


@jax.custom_vjp
def low(v):
    return lax.optimization_barrier(v.astype(jnp.bfloat16)).astype(jnp.float32)

@jax.custom_vjp
def low_back(v):
    return v

def low_keep(v):
    return (low(v), None)

def low_pass(kept, grad):
    return (grad,)

def back_keep(v):
    return (v, None)

def back_low(kept, grad):
    return (low(grad),)
low.defvjp(low_keep, low_pass)
low_back.defvjp(back_keep, back_low)
epsilon = 1e-12
floor_score = -1e+30
highest = lax.Precision.HIGHEST

def stored_position(row_ids, rows_dev, ctx_count):
    device = row_ids // rows_dev
    offset = row_ids % rows_dev
    half_rows = rows_dev // 2
    return jnp.where(offset < half_rows, device * half_rows + offset, (2 * ctx_count - 1 - device) * half_rows + offset - half_rows)

def normalize(hidden, scale_row, shift_row):
    centred = hidden - lax.optimization_barrier(jnp.mean(hidden, axis=-1, keepdims=True))
    variance = lax.optimization_barrier(jnp.mean(centred * centred, axis=-1, keepdims=True))
    return centred * lax.rsqrt(variance + epsilon) * scale_row + shift_row

def project(operand, matrix):
    return jnp.einsum('bld,de->ble', operand, matrix, precision=highest)

def sequences(tokens, seq_len, params):
    w_query, w_key, w_value, w_attn_out, w_up, b_up, w_down, vectors = params
    batch_size = tokens.shape[0]

    def heads_of(operand):
        return operand.reshape(batch_size, CAP, HEADS, HEAD_DIM)
    low_tokens = low(tokens)
    queries = low(low_back(project(low_tokens, w_query) + vectors[0]))
    keys = low(low_back(project(low_tokens, w_key)))
    values = low(low_back(project(low_tokens, w_value) + vectors[1]))
    scores = jnp.einsum('bqhd,bkhd->bhqk', heads_of(queries), heads_of(keys), precision=highest) * HEAD_DIM ** (-0.5)
    scores = low_back(scores)
    position = stored_position(jnp.arange(CAP, dtype=jnp.int32), CAP // N_CTX, N_CTX)
    counted = (position[None, :] < seq_len[:, None])[:, None, None, :]
    scores = jnp.where(counted, scores, floor_score)
    row_max = lax.optimization_barrier(jnp.max(scores, axis=-1, keepdims=True))
    weights = jnp.where(counted, jnp.exp(scores - row_max), 0.0)
    probabilities = low(weights / lax.optimization_barrier(jnp.sum(weights, axis=-1, keepdims=True)))
    mixed_rows = jnp.einsum('bhqk,bkhd->bqhd', probabilities, heads_of(values), precision=highest).reshape(batch_size, CAP, D)
    mixed_rows = low(low_back(mixed_rows))
    attention = low_back(project(mixed_rows, w_attn_out) + vectors[2])
    normed_one = normalize(tokens + attention, vectors[6], vectors[4])
    inner = low_back(project(low(normed_one), w_up) + b_up)
    activated = low(jax.nn.gelu(inner, approximate=False))
    branch = low_back(project(activated, w_down) + vectors[3])
    return normalize(normed_one + branch, vectors[7], vectors[5])

def reference(tokens, cotangent, lengths, w_query, w_key, w_value, w_attn_out, w_up, b_up, w_down, vectors):
    params = tuple((operand.astype(jnp.float32) for operand in (w_query, w_key, w_value, w_attn_out, w_up, b_up, w_down, vectors)))
    batch_size = math.gcd(SEQS, max(1, 4096 // CAP))
    blocked = jax.checkpoint(sequences)

    def forward(inputs, weights):
        blocks = inputs.reshape(SEQS // batch_size, batch_size, CAP, D)
        block_lengths = lengths.reshape(SEQS // batch_size, batch_size)
        results = lax.map(lambda pair_item: blocked(pair_item[0], pair_item[1], weights), (blocks, block_lengths))
        return results.reshape(SEQS, CAP, D)
    output, pullback = jax.vjp(forward, tokens.astype(jnp.float32), params)
    d_tokens, grads = pullback(cotangent.astype(jnp.float32))
    return (output, d_tokens, grads[0], grads[1], grads[2], grads[3], grads[4], grads[5], grads[6], grads[7])
```

```python
import functools
import jax
import jax.numpy as jnp
from jax import lax
from jax.experimental import pallas as pl
from jax.experimental.pallas import tpu as pltpu
from jax.sharding import PartitionSpec as P

HEAD_DIM = 64
F32 = jnp.float32
BF = jnp.bfloat16
NN = (((1,), (0,)), ((), ()))
NT = (((1,), (1,)), ((), ()))
TN = (((0,), (0,)), ((), ()))
epsilon = 1e-12
masked_score = -1e30


def dg(left, right, dims):
    return lax.dot_general(left, right, dims, preferred_element_type=F32)


def head_lanes(shape, h):
    lane=lax.broadcasted_iota(jnp.int32, shape, len(shape)-1)
    return (lane>=64)==(h==1), lane==(64 if h==0 else 0)

def fwd_kernel(q_ref, ko_ref, ks_ref, vo_ref, vs_ref, bias_ref, mb_ref, mix_ref, lse_ref, kh):
    half=ko_ref.shape[0]
    @pl.when(pl.program_id(1)==0)
    def _():
        for h in range(2):
            for i,kr in enumerate((ko_ref,ks_ref)):
                inside,spare=head_lanes((half,128),h)
                kh[h,i*half:(i+1)*half,:]=jnp.where(inside,kr[...],jnp.where(spare,bias_ref[i],jnp.zeros((),BF)))
    bq=q_ref.shape[0]
    q=q_ref[...]*jnp.asarray(0.125,BF)
    outs=[];lses=[]
    for h in range(2):
        inside,spare=head_lanes((bq,128),h)
        qm=jnp.where(inside,q,jnp.where(spare,jnp.ones((),BF),jnp.zeros((),BF)))
        s=dg(qm,kh[h],NT)
        m=jnp.max(s,axis=1,keepdims=True)
        e=jnp.exp(s-m)
        l=jnp.sum(e,axis=1,keepdims=True)
        eb=e.astype(BF)
        acc=dg(eb[:,:half],vo_ref[...],NN)+dg(eb[:,half:],vs_ref[...],NN)
        outs.append(acc/l); lses.append(m+jnp.log(l))
    lane=lax.broadcasted_iota(jnp.int32,(bq,128),1)
    mix=jnp.where(lane<64,outs[0],outs[1])
    mix_ref[...]=mix; mb_ref[...]=mix.astype(BF)
    packed=jnp.where(lane==0,lses[0],lses[1])
    lse_ref[0]=packed.T[:8]

def attention_forward(q, kv, kv_sib, bias, bq=256, vmem=48<<20):
    rows=q.shape[0]; pairs=q.shape[1]//128
    return pl.pallas_call(fwd_kernel, grid=(pairs, rows//bq),
        in_specs=[pl.BlockSpec((bq,128),lambda p,j:(j,p)),
                  pl.BlockSpec((rows,128),lambda p,j:(0,p)), pl.BlockSpec((rows,128),lambda p,j:(0,p)),
                  pl.BlockSpec((rows,128),lambda p,j:(0,pairs+p)), pl.BlockSpec((rows,128),lambda p,j:(0,pairs+p)),
                  pl.BlockSpec((2,rows,128),lambda p,j:(0,0,0))],
        out_specs=[pl.BlockSpec((bq,128),lambda p,j:(j,p)),pl.BlockSpec((bq,128),lambda p,j:(j,p)),pl.BlockSpec((1,8,bq),lambda p,j:(p,0,j))],
        out_shape=[jax.ShapeDtypeStruct(q.shape,BF),jax.ShapeDtypeStruct(q.shape,F32),jax.ShapeDtypeStruct((pairs,8,rows),F32)],
        scratch_shapes=[pltpu.VMEM((2,2*rows,128),BF)],
        compiler_params=pltpu.CompilerParams(vmem_limit_bytes=vmem),
        cost_estimate=pl.CostEstimate(flops=4*rows*2*rows*128*pairs*2,bytes_accessed=14*rows*768,transcendentals=rows*rows*4*pairs),
        name="attend")(q,kv,kv_sib,kv,kv_sib,bias)

def bwd_kernel(q_ref, do_ref, mix_ref, ko_ref, ks_ref, vo_ref, vs_ref, bias_ref, lse_ref, dq_ref, dko_ref, dvo_ref, dks_ref, dvs_ref, kh, dk, dv, *, ck):
    half=ko_ref.shape[0]; j=pl.program_id(1)
    @pl.when(j==0)
    def _():
        for h in range(2):
            for i,kr in enumerate((ko_ref,ks_ref)):
                inside,spare=head_lanes((half,128),h)
                kh[h,i*half:(i+1)*half,:]=jnp.where(inside,kr[...],jnp.where(spare,bias_ref[i],jnp.zeros((),BF)))
        dk[...]=jnp.zeros_like(dk); dv[...]=jnp.zeros_like(dv)
    bq=q_ref.shape[0]
    q=q_ref[...]*jnp.asarray(0.125,BF); do=do_ref[...]
    prod=(do.astype(F32)*mix_ref[...]).T
    zero=jnp.zeros((),BF); one=jnp.ones((),BF)
    hs=[]
    for h in range(2):
        inside,spare=head_lanes((bq,128),h)
        hs.append((jnp.where(inside,q,jnp.where(spare,one,zero)),jnp.where(inside,q,zero),jnp.where(inside,do,zero),
                   lse_ref[0,h:h+1,:],jnp.sum(prod[h*64:(h+1)*64],axis=0,keepdims=True)))
    dq=jnp.zeros((bq,128),F32)
    for c in range(2*half//ck):
        vr=vo_ref if c*ck<half else vs_ref
        off=c*ck if c*ck<half else c*ck-half
        v=vr[off:off+ck,:]
        sl=slice(c*ck,(c+1)*ck)
        for h in range(2):
            qm,qz,dom,lse,delta=hs[h]
            k=kh[h,sl,:]
            p=jnp.exp(dg(k,qm,NT)-lse)
            dp=dg(v,dom,NT)
            ds=(p*(dp-delta)).astype(BF)
            dv[sl,:]+=dg(p.astype(BF),dom,NN)
            dk[sl,:]+=dg(ds,qz,NN)
            dq=dq+dg(ds,k,TN)
    dq_ref[...]=(dq*0.125).astype(BF)
    @pl.when(j==pl.num_programs(1)-1)
    def _():
        dko_ref[...]=dk[:half,:]; dvo_ref[...]=dv[:half,:]
        dks_ref[...]=dk[half:,:].astype(BF); dvs_ref[...]=dv[half:,:].astype(BF)

def attention_backward(q, do, mix, kv, kv_sib, bias, lse, bq=256, ck=512, vmem=48<<20):
    rows=q.shape[0]; pairs=q.shape[1]//128
    blk=pl.BlockSpec((bq,128),lambda p,j:(j,p)); full=pl.BlockSpec((rows,128),lambda p,j:(0,p)); fullv=pl.BlockSpec((rows,128),lambda p,j:(0,pairs+p))
    S=jax.ShapeDtypeStruct
    return pl.pallas_call(functools.partial(bwd_kernel,ck=ck), grid=(pairs, rows//bq),
        in_specs=[blk,blk,blk,full,full,fullv,fullv,pl.BlockSpec((2,rows,128),lambda p,j:(0,0,0)),pl.BlockSpec((1,8,bq),lambda p,j:(p,0,j))],
        out_specs=[blk,full,full,full,full],
        out_shape=[S(q.shape,BF),S(q.shape,F32),S(q.shape,F32),S(q.shape,BF),S(q.shape,BF)],
        scratch_shapes=[pltpu.VMEM((2,2*rows,128),BF),pltpu.VMEM((2*rows,128),F32),pltpu.VMEM((2*rows,128),F32)],
        compiler_params=pltpu.CompilerParams(vmem_limit_bytes=vmem),
        cost_estimate=pl.CostEstimate(flops=10*rows*2*rows*128*pairs*2,bytes_accessed=26*rows*768,transcendentals=rows*rows*4*pairs),
        name="attend_back")(q,do,mix,kv,kv_sib,kv,kv_sib,bias,lse)


def normalize(hidden, scale_row, shift_row):
    centred = hidden - jnp.mean(hidden, axis=-1, keepdims=True)
    inverse = lax.rsqrt(jnp.mean(centred * centred, axis=-1, keepdims=True) + epsilon)
    standard = centred * inverse
    return (standard * scale_row + shift_row, standard, inverse)


def normalize_back(gradient, standard, inverse, scale_row):
    scaled = gradient * scale_row
    centred = scaled - jnp.mean(scaled, axis=-1, keepdims=True)
    return (centred - standard * jnp.mean(scaled * standard, axis=-1, keepdims=True)) * inverse


def reduce_blocks(grad, pair_perm, groups, dp, ctx):
    width = grad.shape[1]
    rows = grad.shape[0] // (dp * ctx)
    parity = lax.axis_index("ctx") % 2
    parts = grad.astype(BF).reshape(dp, ctx // 2, 2, rows, width)
    keep = lax.dynamic_index_in_dim(parts, parity, 2, keepdims=False)
    send = lax.dynamic_index_in_dim(parts, 1 - parity, 2, keepdims=False)
    got = lax.ppermute(send, "ctx", pair_perm)
    part = (keep.astype(F32) + got.astype(F32)).astype(BF)
    got = lax.all_to_all(part, "ctx", 1, 1, axis_index_groups=groups, tiled=True)
    part = jnp.sum(got.astype(F32), axis=1).astype(BF)
    got = lax.all_to_all(part, "dp", 0, 0, tiled=True)
    return jnp.sum(got.astype(F32), axis=0)


def on_device(
    tokens, cotangent, lengths, w_query, w_key, w_value, w_attn_out, w_up, b_up, w_down, vectors
):
    seqs, rows_dev, width = tokens.shape
    dp = lax.axis_size("dp")
    ctx = lax.axis_size("ctx")
    half = rows_dev // 2
    rows = half * ctx
    member = lax.axis_index("ctx") % 2
    own_seq = lax.axis_index("dp") * seqs + lax.axis_index("ctx") // 2
    length = lax.dynamic_index_in_dim(lengths, own_seq, 0, keepdims=False)
    pair_perm = [(i, i ^ 1) for i in range(ctx)]
    groups = [list(range(k, ctx, 2)) for k in range(2)]

    def exchange(array):
        return lax.all_to_all(array, "ctx", 0, 0, tiled=True)

    def collect(array, axis=0):
        return lax.all_gather(array, ("dp", "ctx"), axis=axis, tiled=True)

    split = tokens.reshape(ctx, half, width)
    low_in = exchange(split.astype(BF)).reshape(rows, width)
    full_qkv = collect(jnp.concatenate([w_query, w_key, w_value], axis=1))
    small = collect(jnp.concatenate([b_up.reshape(1, -1), vectors.reshape(1, -1)], axis=1))
    up_slots = b_up.shape[0]
    full_bias_up = small[:, :up_slots].reshape(-1).astype(F32)
    vector_rows = (
        small[:, up_slots:].reshape(dp * ctx, 8, -1).transpose(1, 0, 2).reshape(8, width).astype(F32)
    )
    full_attn = collect(w_attn_out)
    full_up = collect(w_up)
    full_down = collect(w_down)
    residual = exchange(split).reshape(rows, width)
    upstream = exchange(cotangent.reshape(ctx, half, width)).reshape(rows, width)

    slot = jnp.arange(rows, dtype=jnp.int32)
    source = slot // half
    high = (2 * ctx - 1 - source) * half + slot % half

    def key_bias(kind):
        position = jnp.where(kind == 0, slot, high)
        return jnp.where(position < length, 0.0, masked_score).astype(BF)

    bias = jnp.stack([key_bias(member), key_bias(1 - member)])
    bias = jnp.broadcast_to(bias[:, :, None], (2, rows, 128))

    row_of = jnp.concatenate([jnp.zeros_like(vector_rows[1]), vector_rows[1]])
    kv = (dg(low_in, full_qkv[:, width:], NN) + row_of).astype(BF)
    kv_sib = lax.ppermute(kv, "ctx", pair_perm)
    queries = (dg(low_in, full_qkv[:, :width], NN) + vector_rows[0]).astype(BF)
    low_mixed, mixed, lse = attention_forward(queries, kv, kv_sib, bias)

    attention = dg(low_mixed, full_attn, NN) + vector_rows[2]
    normed_one, standard_one, inverse_one = normalize(
        residual + attention, vector_rows[6], vector_rows[4]
    )
    low_first = normed_one.astype(BF)
    inner = dg(low_first, full_up, NN) + full_bias_up
    active = jax.nn.gelu(inner, approximate=False).astype(BF)
    branch = dg(active, full_down, NN) + vector_rows[3]
    result, standard_two, inverse_two = normalize(
        normed_one + branch, vector_rows[7], vector_rows[5]
    )
    output = exchange(result.reshape(ctx, half, width)).reshape(seqs, rows_dev, width)

    d_gain_two = jnp.sum(upstream * standard_two, axis=0)
    d_shift_two = jnp.sum(upstream, axis=0)
    grad_second = normalize_back(upstream, standard_two, inverse_two, vector_rows[7])
    low_branch = grad_second.astype(BF)
    d_bias_down = jnp.sum(low_branch.astype(F32), axis=0)
    d_down = dg(active, low_branch, TN)
    d_active = dg(low_branch, full_down, NT)
    gelu_back = jax.vjp(lambda v: jax.nn.gelu(v, approximate=False), inner)[1]
    low_inner = gelu_back(d_active)[0].astype(BF)
    d_bias_up = jnp.sum(low_inner.astype(F32), axis=0)
    d_up = dg(low_first, low_inner, TN)
    own_down = reduce_blocks(d_down, pair_perm, groups, dp, ctx)
    own_up = reduce_blocks(d_up, pair_perm, groups, dp, ctx)
    grad_first = grad_second + dg(low_inner, full_up, NT)
    d_gain_one = jnp.sum(grad_first * standard_one, axis=0)
    d_shift_one = jnp.sum(grad_first, axis=0)
    grad_sum = normalize_back(grad_first, standard_one, inverse_one, vector_rows[6])
    low_attn = grad_sum.astype(BF)
    d_bias_attn = jnp.sum(low_attn.astype(F32), axis=0)
    d_attn = dg(low_mixed, low_attn, TN)
    d_mixed = dg(low_attn, full_attn, NT).astype(BF)

    dq, dk_own, dv_own, dk_sib, dv_sib = attention_backward(
        queries, d_mixed, mixed, kv, kv_sib, bias, lse
    )
    dk_got = lax.ppermute(dk_sib, "ctx", pair_perm)
    dv_got = lax.ppermute(dv_sib, "ctx", pair_perm)
    dk = (dk_own + dk_got.astype(F32)).astype(BF)
    dv = (dv_own + dv_got.astype(F32)).astype(BF)
    grad_in = grad_sum + (
        dg(dq, full_qkv[:, :width], NT)
        + dg(dk, full_qkv[:, width : 2 * width], NT)
        + dg(dv, full_qkv[:, 2 * width :], NT)
    )
    grad_tokens = exchange(grad_in.reshape(ctx, half, width)).reshape(seqs, rows_dev, width)
    d_vector_rows = jnp.stack(
        [
            jnp.sum(dq.astype(F32), axis=0),
            jnp.sum(dv.astype(F32), axis=0),
            d_bias_attn,
            d_bias_down,
            d_shift_one,
            d_shift_two,
            d_gain_one,
            d_gain_two,
        ]
    )
    extra = jnp.concatenate([d_vector_rows.T, d_bias_up.reshape(width, -1)], axis=1)
    extra = jnp.pad(extra, ((0, 0), (0, 128 - extra.shape[1])))
    joined = jnp.concatenate(
        [d_attn, dg(low_in, dq, TN), dg(low_in, dk, TN), dg(low_in, dv, TN), extra], axis=1
    )
    own = reduce_blocks(joined, pair_perm, groups, dp, ctx)
    own_attn, own_query, own_key, own_value = (
        own[:, i * width : (i + 1) * width] for i in range(4)
    )
    own_extra = own[:, 4 * width :]
    own_vectors = own_extra[:, :8].T
    own_bias_up = own_extra[:, 8 : 8 + d_bias_up.shape[0] // width].reshape(-1)
    return (
        output,
        grad_tokens,
        own_query,
        own_key,
        own_value,
        own_attn,
        own_up,
        own_bias_up,
        own_down,
        own_vectors,
    )


def solution(mesh):
    in_specs = (
        P("dp", "ctx", None),
        P("dp", "ctx", None),
        P(),
        P(("dp", "ctx"), None),
        P(("dp", "ctx"), None),
        P(("dp", "ctx"), None),
        P(("dp", "ctx"), None),
        P(("dp", "ctx"), None),
        P(("dp", "ctx")),
        P(("dp", "ctx"), None),
        P(None, ("dp", "ctx")),
    )
    out_specs = (
        P("dp", "ctx", None),
        P("dp", "ctx", None),
        P(("dp", "ctx"), None),
        P(("dp", "ctx"), None),
        P(("dp", "ctx"), None),
        P(("dp", "ctx"), None),
        P(("dp", "ctx"), None),
        P(("dp", "ctx")),
        P(("dp", "ctx"), None),
        P(None, ("dp", "ctx")),
    )
    return jax.shard_map(
        on_device, mesh=mesh, in_specs=in_specs, out_specs=out_specs, check_vma=False
    )
```

```python
import functools
import jax
import jax.numpy as jnp
from jax import lax
from jax.experimental import pallas as pl
from jax.experimental.pallas import tpu as pltpu
from jax.sharding import PartitionSpec as P

HEAD_DIM = 64
F32 = jnp.float32
BF = jnp.bfloat16
NN = (((1,), (0,)), ((), ()))
NT = (((1,), (1,)), ((), ()))
TN = (((0,), (0,)), ((), ()))
epsilon = 1e-12
masked_score = -1e30


def dg(left, right, dims):
    return lax.dot_general(left, right, dims, preferred_element_type=F32)


MESH = pl.DeviceIdType.MESH


class Mover:
    def __init__(self, local_sem, send_sem, recv_sem):
        self.local_sem, self.send_sem, self.recv_sem = local_sem, send_sem, recv_sem
        self.locals = self.remotes = 0

    def local(self, source, target):
        copy = pltpu.make_async_copy(source, target, self.local_sem.at[self.locals])
        self.locals += 1
        return copy

    def remote(self, source, target, device):
        number = self.remotes
        self.remotes += 1
        return pltpu.make_async_remote_copy(
            src_ref=source,
            dst_ref=target,
            send_sem=self.send_sem.at[number],
            recv_sem=self.recv_sem.at[number],
            device_id=device,
            device_id_type=MESH,
        )


def greet(devices):
    barrier = pltpu.get_barrier_semaphore()
    for device in devices:
        pl.semaphore_signal(barrier, inc=1, device_id=device, device_id_type=MESH)
    pl.semaphore_wait(barrier, len(devices))


def place(dp, ctx):
    d, c = lax.axis_index("dp"), lax.axis_index("ctx")
    groups = ctx // 2
    g, m = c // 2, c % 2
    over_dp = [((d + k) % dp, c) for k in range(1, dp)]
    over_groups = [(d, (g + k) % groups * 2 + m) for k in range(1, groups)]
    return d, c, g, m, over_dp, over_groups, (d, g * 2 + 1 - m)


def gather_kernel(dp, ctx, x, w, wo, wu, wd, x_in, w_full, zo, zu, zd, local_sem, send_sem, recv_sem):
    d, c, g, m, over_dp, over_groups, sibling = place(dp, ctx)
    groups = ctx // 2
    greet(over_dp + [(d, (c + k) % ctx) for k in range(1, ctx)])
    mover = Mover(local_sem, send_sem, recv_sem)
    own = [
        mover.local(source, target)
        for source, target in (
            (w, w_full.at[d, c]),
            (x.at[c], x_in.at[c]),
            (wo, zo.at[d]),
            (wu, zu.at[d]),
            (wd, zd.at[d]),
        )
    ]
    along = [mover.remote(w, w_full.at[d, c], device) for device in over_dp]
    across = [[mover.remote(w, w_full.at[d, c], device) for device in over_groups]]
    rows = [
        mover.remote(x.at[(c + k) % ctx], x_in.at[c], (d, (c + k) % ctx)) for k in range(1, ctx)
    ]
    rest = [
        mover.remote(source, target.at[d], device)
        for source, target in ((wo, zo), (wu, zu), (wd, zd))
        for device in over_dp
    ]
    for copy in own + along + across[0] + rows + rest:
        copy.start()
    for k in range(1, dp):
        along[k - 1].wait_recv()
        piece = w_full.at[(d - k + dp) % dp, c]
        across.append([mover.remote(piece, piece, device) for device in over_groups])
        for copy in across[-1]:
            copy.start()
    own[0].wait()
    mine = w_full.at[:, c]
    over = [mover.remote(mine, mine, sibling)]
    over[0].start()
    for k in range(1, groups):
        for batch in across:
            batch[k - 1].wait_recv()
        block = w_full.at[:, (g - k + groups) % groups * 2 + m]
        over.append(mover.remote(block, block, sibling))
        over[-1].start()
    for copy in over + rows + rest:
        copy.wait()
    for copy in along + [copy for batch in across for copy in batch]:
        copy.wait_send()
    for copy in own[1:]:
        copy.wait()


def gather_first(x, w, wo, wu, wd, dp, ctx):
    groups = ctx // 2
    remotes = (dp - 1) + dp * (groups - 1) + (ctx - 1) + 3 * (dp - 1) + groups
    any_space = pl.BlockSpec(memory_space=pl.ANY)
    return pl.pallas_call(
        functools.partial(gather_kernel, dp, ctx),
        in_specs=[any_space] * 5,
        out_specs=[any_space] * 5,
        out_shape=[
            jax.ShapeDtypeStruct(x.shape, BF),
            jax.ShapeDtypeStruct((dp, ctx) + w.shape, BF),
        ]
        + [jax.ShapeDtypeStruct((dp,) + array.shape, BF) for array in (wo, wu, wd)],
        scratch_shapes=[
            pltpu.SemaphoreType.DMA((5,)),
            pltpu.SemaphoreType.DMA((remotes,)),
            pltpu.SemaphoreType.DMA((remotes,)),
        ],
        compiler_params=pltpu.CompilerParams(collective_id=0, has_side_effects=True),
        name="gather_first",
    )(x, w, wo, wu, wd)


class Spread:
    def __init__(self, dp, ctx, sources, targets, mover):
        d, c, g, m, over_dp, over_groups, sibling = place(dp, ctx)
        groups = ctx // 2
        self.devices = over_groups + [sibling]
        self.own = [mover.local(s, t.at[:, c]) for s, t in zip(sources, targets)]
        self.direct = [mover.remote(s, t.at[:, c], sibling) for s, t in zip(sources, targets)]
        self.across = [
            [mover.remote(s, t.at[:, c], device) for device in over_groups]
            for s, t in zip(sources, targets)
        ]
        self.onward = []
        for t in targets:
            blocks = [t.at[:, (g - k + groups) % groups * 2 + m] for k in range(1, groups)]
            self.onward.append([mover.remote(block, block, sibling) for block in blocks])

    @staticmethod
    def count(groups, arrays):
        return arrays * (1 + 2 * (groups - 1))

    def begin(self):
        greet(self.devices)
        for copy in self.own + [copy for batch in self.across for copy in batch] + self.direct:
            copy.start()

    def forward(self, index):
        for came, copy in zip(self.across[index], self.onward[index]):
            came.wait_recv()
            copy.start()

    def finish(self):
        for copy in self.own + self.direct + [copy for batch in self.onward for copy in batch]:
            copy.wait()
        for batch in self.across:
            for copy in batch:
                copy.wait_send()


class Scatter:
    def __init__(self, dp, ctx, sources, outs, buffers, mover):
        d, c, g, m, over_dp, over_groups, sibling = place(dp, ctx)
        groups = ctx // 2
        self.dp, self.groups, self.d = dp, groups, d
        self.devices = over_groups + over_dp
        self.outs = outs
        self.mine = [b[0] for b in buffers]
        self.came = [b[1] for b in buffers]
        self.sums = [b[2] for b in buffers]
        self.last = [b[3] for b in buffers]
        self.own = [mover.local(s.at[:, g], b) for s, b in zip(sources, self.mine)]
        self.across = [
            [
                mover.remote(s.at[:, (g + k) % groups], b.at[k - 1], over_groups[k - 1])
                for k in range(1, groups)
            ]
            for s, b in zip(sources, self.came)
        ]
        self.along = [
            [
                mover.remote(s.at[(d + k) % dp], b.at[k - 1], over_dp[k - 1])
                for k in range(1, dp)
            ]
            for s, b in zip(self.sums, self.last)
        ]

    @staticmethod
    def count(dp, groups, arrays):
        return arrays * (groups - 1 + dp - 1)

    @staticmethod
    def scratch(dp, groups, sources):
        shapes = []
        for s in sources:
            block = s.shape[2:]
            shapes += [
                pltpu.VMEM((dp,) + block, BF),
                pltpu.VMEM((groups - 1, dp) + block, BF),
                pltpu.VMEM((dp,) + block, BF),
                pltpu.VMEM((dp - 1,) + block, BF),
            ]
        return shapes

    def begin(self):
        for copy in self.own + [copy for batch in self.across for copy in batch]:
            copy.start()

    def middle(self, index):
        self.own[index].wait()
        for copy in self.across[index]:
            copy.wait_recv()
        for k in range(self.dp):
            total = self.mine[index][k].astype(F32)
            for j in range(self.groups - 1):
                total = total + self.came[index][j, k].astype(F32)
            self.sums[index][k] = total.astype(BF)
        for copy in self.along[index]:
            copy.start()

    def finish(self):
        for index, out in enumerate(self.outs):
            for copy in self.along[index]:
                copy.wait_recv()
            total = self.sums[index][self.d].astype(F32)
            for j in range(self.dp - 1):
                total = total + self.last[index][j].astype(F32)
            out[...] = total
        for batch in self.across + self.along:
            for copy in batch:
                copy.wait_send()


def finish_kernel(dp, ctx, s, x, out, x_out, *scratch):
    buffers, (local_sem, send_sem, recv_sem) = scratch[:-3], scratch[-3:]
    d, c, g, m, over_dp, over_groups, sibling = place(dp, ctx)
    mover = Mover(local_sem, send_sem, recv_sem)
    scatter = Scatter(dp, ctx, [s], [out], [buffers], mover)
    own = mover.local(x.at[c], x_out.at[c])
    rows = [
        mover.remote(x.at[(c + k) % ctx], x_out.at[c], (d, (c + k) % ctx)) for k in range(1, ctx)
    ]
    greet(over_dp + [(d, (c + k) % ctx) for k in range(1, ctx)])
    scatter.begin()
    own.start()
    for copy in rows:
        copy.start()
    scatter.middle(0)
    scatter.finish()
    for copy in rows:
        copy.wait()
    own.wait()


def finish_gradients(s, x, dp, ctx):
    groups = ctx // 2
    remotes = Scatter.count(dp, groups, 1) + ctx - 1
    any_space = pl.BlockSpec(memory_space=pl.ANY)
    return pl.pallas_call(
        functools.partial(finish_kernel, dp, ctx),
        in_specs=[any_space] * 2,
        out_specs=[pl.BlockSpec(memory_space=pltpu.VMEM), any_space],
        out_shape=[jax.ShapeDtypeStruct(s.shape[2:], F32), jax.ShapeDtypeStruct(x.shape, x.dtype)],
        scratch_shapes=Scatter.scratch(dp, groups, [s])
        + [
            pltpu.SemaphoreType.DMA((2,)),
            pltpu.SemaphoreType.DMA((remotes,)),
            pltpu.SemaphoreType.DMA((remotes,)),
        ],
        compiler_params=pltpu.CompilerParams(
            collective_id=3, has_side_effects=True, vmem_limit_bytes=32 << 20
        ),
        name="finish_gradients",
    )(s, x)


def head_lanes(shape, h):
    lane = lax.broadcasted_iota(jnp.int32, shape, len(shape) - 1)
    return (lane >= 64) == (h == 1), lane == (64 if h == 0 else 0)


def load_keys(keys, own_ref, sib_ref, bias_ref):
    half = own_ref.shape[0]
    for h in range(2):
        for i, ref in enumerate((own_ref, sib_ref)):
            inside, spare = head_lanes((half, 128), h)
            rest = jnp.where(spare, bias_ref[i], jnp.zeros((), BF))
            keys[h, i * half : (i + 1) * half, :] = jnp.where(inside, ref[...], rest)


def forward_kernel(dp, ctx, *refs):
    (q_ref, ko_ref, ks_ref, vo_ref, vs_ref, bias_ref), refs = refs[:6], refs[6:]
    gathered, (mb_ref, mix_ref, lse_ref), spread_to, refs = refs[:3], refs[3:6], refs[6:9], refs[9:]
    keys, local_sem, send_sem, recv_sem = refs
    spread = Spread(dp, ctx, gathered, spread_to, Mover(local_sem, send_sem, recv_sem))
    steps = pl.num_programs(1)
    step = pl.program_id(0) * steps + pl.program_id(1)
    last = forward_steps(pl.num_programs(0), steps)

    @pl.when(step == 0)
    def _():
        spread.begin()

    @pl.when(pl.program_id(1) == 0)
    def _():
        load_keys(keys, ko_ref, ks_ref, bias_ref)

    half, bq = ko_ref.shape[0], q_ref.shape[0]
    q = q_ref[...] * jnp.asarray(0.125, BF)
    outs, lses = [], []
    for h in range(2):
        inside, spare = head_lanes((bq, 128), h)
        rest = jnp.where(spare, jnp.ones((), BF), jnp.zeros((), BF))
        scores = dg(jnp.where(inside, q, rest), keys[h], NT)
        top = jnp.max(scores, axis=1, keepdims=True)
        weights = jnp.exp(scores - top)
        total = jnp.sum(weights, axis=1, keepdims=True)
        low = weights.astype(BF)
        mixed = dg(low[:, :half], vo_ref[...], NN) + dg(low[:, half:], vs_ref[...], NN)
        outs.append(mixed / total)
        lses.append(top + jnp.log(total))
    lane = lax.broadcasted_iota(jnp.int32, (bq, 128), 1)
    mixed = jnp.where(lane < 64, outs[0], outs[1])
    mix_ref[...] = mixed
    mb_ref[...] = mixed.astype(BF)
    lse_ref[0] = jnp.where(lane == 0, lses[0], lses[1]).T[:8]

    for index, at in enumerate(last):

        @pl.when(step == at)
        def _(index=index):
            spread.forward(index)

    @pl.when(step == last[-1])
    def _():
        spread.finish()


def attention_forward(q, kv, kv_sib, bias, gathered, dp, ctx, bq=256):
    rows = q.shape[0]
    pairs = q.shape[1] // 128
    S = jax.ShapeDtypeStruct
    blk = pl.BlockSpec((bq, 128), lambda p, j: (j, p))
    k_spec = pl.BlockSpec((rows, 128), lambda p, j: (0, p))
    v_spec = pl.BlockSpec((rows, 128), lambda p, j: (0, pairs + p))
    any_space = pl.BlockSpec(memory_space=pl.ANY)
    remotes = Spread.count(ctx // 2, 3)
    return pl.pallas_call(
        functools.partial(forward_kernel, dp, ctx),
        grid=(pairs, rows // bq),
        in_specs=[blk, k_spec, k_spec, v_spec, v_spec]
        + [pl.BlockSpec((2, rows, 128), lambda p, j: (0, 0, 0))]
        + [any_space] * 3,
        out_specs=[blk, blk, pl.BlockSpec((1, 8, bq), lambda p, j: (p, 0, j))] + [any_space] * 3,
        out_shape=[S(q.shape, BF), S(q.shape, F32), S((pairs, 8, rows), F32)]
        + [S((dp, ctx) + array.shape[1:], BF) for array in gathered],
        scratch_shapes=[
            pltpu.VMEM((2, 2 * rows, 128), BF),
            pltpu.SemaphoreType.DMA((3,)),
            pltpu.SemaphoreType.DMA((remotes,)),
            pltpu.SemaphoreType.DMA((remotes,)),
        ],
        compiler_params=pltpu.CompilerParams(
            vmem_limit_bytes=48 << 20, collective_id=1, has_side_effects=True
        ),
        cost_estimate=pl.CostEstimate(
            flops=16 * rows * rows * 128 * pairs,
            bytes_accessed=14 * rows * 768,
            transcendentals=4 * rows * rows * pairs,
        ),
        name="attend",
    )(q, kv, kv_sib, kv, kv_sib, bias, *gathered)


def forward_steps(pairs, steps):
    count = pairs * steps
    return (count * 5 // 24, count * 15 // 24, count - 1)


def backward_steps(pairs, steps):
    count = pairs * steps
    return (count * 8 // 16, count * 3 // 16, count * 13 // 16)


def backward_kernel(dp, ctx, ck, *refs):
    (q_ref, do_ref, mix_ref, ko_ref, ks_ref, vo_ref, vs_ref, bias_ref, lse_ref), refs = (
        refs[:9],
        refs[9:],
    )
    sources, refs = refs[:3], refs[3:]
    (dq_ref, dko_ref, dvo_ref, dks_ref, dvs_ref), refs = refs[:5], refs[5:]
    summed, refs = refs[:3], refs[3:]
    (keys, dk, dv), refs = refs[:3], refs[3:]
    buffers, (local_sem, send_sem, recv_sem) = refs[:12], refs[12:]
    scatter = Scatter(
        dp,
        ctx,
        sources,
        summed,
        [buffers[i * 4 : i * 4 + 4] for i in range(3)],
        Mover(local_sem, send_sem, recv_sem),
    )
    steps = pl.num_programs(1)
    j = pl.program_id(1)
    step = pl.program_id(0) * steps + j

    @pl.when(step == 0)
    def _():
        greet(scatter.devices)
        scatter.begin()

    @pl.when(j == 0)
    def _():
        load_keys(keys, ko_ref, ks_ref, bias_ref)
        dk[...] = jnp.zeros_like(dk)
        dv[...] = jnp.zeros_like(dv)

    half, bq = ko_ref.shape[0], q_ref.shape[0]
    q = q_ref[...] * jnp.asarray(0.125, BF)
    do = do_ref[...]
    prod = (do.astype(F32) * mix_ref[...]).T
    zero, one = jnp.zeros((), BF), jnp.ones((), BF)
    heads = []
    for h in range(2):
        inside, spare = head_lanes((bq, 128), h)
        heads.append(
            (
                jnp.where(inside, q, jnp.where(spare, one, zero)),
                jnp.where(inside, q, zero),
                jnp.where(inside, do, zero),
                lse_ref[0, h : h + 1, :],
                jnp.sum(prod[h * 64 : (h + 1) * 64], axis=0, keepdims=True),
            )
        )
    dq = jnp.zeros((bq, 128), F32)
    for first in range(0, 2 * half, ck):
        rows = slice(first, first + ck)
        v = vo_ref[rows, :] if first < half else vs_ref[first - half : first - half + ck, :]
        for h in range(2):
            qm, qz, dom, lse, delta = heads[h]
            k = keys[h, rows, :]
            p = jnp.exp(dg(k, qm, NT) - lse)
            ds = (p * (dg(v, dom, NT) - delta)).astype(BF)
            dv[rows, :] += dg(p.astype(BF), dom, NN)
            dk[rows, :] += dg(ds, qz, NN)
            dq = dq + dg(ds, k, TN)
    dq_ref[...] = (dq * 0.125).astype(BF)

    @pl.when(j == steps - 1)
    def _():
        dko_ref[...] = dk[:half, :]
        dvo_ref[...] = dv[:half, :]
        dks_ref[...] = dk[half:, :].astype(BF)
        dvs_ref[...] = dv[half:, :].astype(BF)

    for index, at in enumerate(backward_steps(pl.num_programs(0), steps)):

        @pl.when(step == at)
        def _(index=index):
            scatter.middle(index)

    @pl.when(step == pl.num_programs(0) * steps - 1)
    def _():
        scatter.finish()


def attention_backward(q, do, mix, kv, kv_sib, bias, lse, sources, dp, ctx, bq=512, ck=512):
    rows = q.shape[0]
    pairs = q.shape[1] // 128
    S = jax.ShapeDtypeStruct
    blk = pl.BlockSpec((bq, 128), lambda p, j: (j, p))
    full = pl.BlockSpec((rows, 128), lambda p, j: (0, p))
    v_spec = pl.BlockSpec((rows, 128), lambda p, j: (0, pairs + p))
    any_space = pl.BlockSpec(memory_space=pl.ANY)
    remotes = Scatter.count(dp, ctx // 2, 3)
    sums = [s.shape[2:] for s in sources]
    return pl.pallas_call(
        functools.partial(backward_kernel, dp, ctx, ck),
        grid=(pairs, rows // bq),
        in_specs=[blk, blk, blk, full, full, v_spec, v_spec]
        + [pl.BlockSpec((2, rows, 128), lambda p, j: (0, 0, 0))]
        + [pl.BlockSpec((1, 8, bq), lambda p, j: (p, 0, j))]
        + [any_space] * 3,
        out_specs=[blk, full, full, full, full]
        + [pl.BlockSpec(shape, lambda p, j: (0, 0)) for shape in sums],
        out_shape=[
            S(q.shape, BF),
            S(q.shape, F32),
            S(q.shape, F32),
            S(q.shape, BF),
            S(q.shape, BF),
        ]
        + [S(shape, F32) for shape in sums],
        scratch_shapes=[
            pltpu.VMEM((2, 2 * rows, 128), BF),
            pltpu.VMEM((2 * rows, 128), F32),
            pltpu.VMEM((2 * rows, 128), F32),
        ]
        + Scatter.scratch(dp, ctx // 2, sources)
        + [
            pltpu.SemaphoreType.DMA((3,)),
            pltpu.SemaphoreType.DMA((remotes,)),
            pltpu.SemaphoreType.DMA((remotes,)),
        ],
        compiler_params=pltpu.CompilerParams(
            vmem_limit_bytes=56 << 20, collective_id=2, has_side_effects=True
        ),
        cost_estimate=pl.CostEstimate(
            flops=40 * rows * rows * 128 * pairs,
            bytes_accessed=26 * rows * 768,
            transcendentals=4 * rows * rows * pairs,
        ),
        name="attend_back",
    )(q, do, mix, kv, kv_sib, kv, kv_sib, bias, lse, *sources)


def normalize(hidden, scale_row, shift_row):
    centred = hidden - jnp.mean(hidden, axis=-1, keepdims=True)
    inverse = lax.rsqrt(jnp.mean(centred * centred, axis=-1, keepdims=True) + epsilon)
    standard = centred * inverse
    return (standard * scale_row + shift_row, standard, inverse)


def normalize_back(gradient, standard, inverse, scale_row):
    scaled = gradient * scale_row
    centred = scaled - jnp.mean(scaled, axis=-1, keepdims=True)
    return (centred - standard * jnp.mean(scaled * standard, axis=-1, keepdims=True)) * inverse


def on_device(
    tokens, cotangent, lengths, w_query, w_key, w_value, w_attn_out, w_up, b_up, w_down, vectors
):
    seqs, rows_dev, width = tokens.shape
    dp = lax.axis_size("dp")
    ctx = lax.axis_size("ctx")
    half = rows_dev // 2
    rows = half * ctx
    member = lax.axis_index("ctx") % 2
    own_seq = lax.axis_index("dp") * seqs + lax.axis_index("ctx") // 2
    length = lax.dynamic_index_in_dim(lengths, own_seq, 0, keepdims=False)
    pair_perm = [(i, i ^ 1) for i in range(ctx)]

    def exchange(array):
        return lax.all_to_all(array, "ctx", 0, 0, tiled=True)

    def over_pair(grad):
        parts = grad.astype(BF).reshape(dp, ctx // 2, 2, -1, grad.shape[1])
        keep = lax.dynamic_index_in_dim(parts, member, 2, keepdims=False)
        send = lax.dynamic_index_in_dim(parts, 1 - member, 2, keepdims=False)
        got = lax.ppermute(send, "ctx", pair_perm)
        return (keep.astype(F32) + got.astype(F32)).astype(BF)

    split = tokens.reshape(ctx, half, width)
    held = w_query.shape[0]
    extra = jnp.concatenate([vectors.T, b_up.reshape(held, -1)], axis=1)
    extra = jnp.pad(extra, ((0, 0), (0, 128 - extra.shape[1])))
    low_in, full_first, *over_dp = gather_first(
        split.astype(BF),
        jnp.concatenate([w_query, w_key, w_value, extra], axis=1),
        w_attn_out,
        w_up,
        w_down,
        dp,
        ctx,
    )
    low_in = low_in.reshape(rows, width)
    full_first = full_first.reshape(width, -1)
    full_qkv = full_first[:, : 3 * width]
    vector_rows = full_first[:, 3 * width : 3 * width + 8].T.astype(F32)
    bias_columns = b_up.shape[0] // held
    full_bias_up = full_first[:, 3 * width + 8 : 3 * width + 8 + bias_columns].reshape(-1).astype(F32)
    residual = exchange(split).reshape(rows, width)
    upstream = exchange(cotangent.reshape(ctx, half, width)).reshape(rows, width)

    slot = jnp.arange(rows, dtype=jnp.int32)
    source = slot // half
    high = (2 * ctx - 1 - source) * half + slot % half

    def key_bias(kind):
        position = jnp.where(kind == 0, slot, high)
        return jnp.where(position < length, 0.0, masked_score).astype(BF)

    bias = jnp.stack([key_bias(member), key_bias(1 - member)])
    bias = jnp.broadcast_to(bias[:, :, None], (2, rows, 128))

    row_of = jnp.concatenate([jnp.zeros_like(vector_rows[1]), vector_rows[1]])
    kv = (dg(low_in, full_qkv[:, width:], NN) + row_of).astype(BF)
    kv_sib = lax.ppermute(kv, "ctx", pair_perm)
    queries = (dg(low_in, full_qkv[:, :width], NN) + vector_rows[0]).astype(BF)
    low_mixed, mixed, lse, full_attn, full_up, full_down = attention_forward(
        queries, kv, kv_sib, bias, over_dp, dp, ctx
    )
    full_attn = full_attn.reshape(width, width)
    full_up = full_up.reshape(width, -1)
    full_down = full_down.reshape(-1, width)

    attention = dg(low_mixed, full_attn, NN) + vector_rows[2]
    normed_one, standard_one, inverse_one = normalize(
        residual + attention, vector_rows[6], vector_rows[4]
    )
    low_first = normed_one.astype(BF)
    inner = dg(low_first, full_up, NN) + full_bias_up
    active = jax.nn.gelu(inner, approximate=False).astype(BF)
    branch = dg(active, full_down, NN) + vector_rows[3]
    result, standard_two, inverse_two = normalize(
        normed_one + branch, vector_rows[7], vector_rows[5]
    )
    output = exchange(result.reshape(ctx, half, width)).reshape(seqs, rows_dev, width)

    d_gain_two = jnp.sum(upstream * standard_two, axis=0)
    d_shift_two = jnp.sum(upstream, axis=0)
    grad_second = normalize_back(upstream, standard_two, inverse_two, vector_rows[7])
    low_branch = grad_second.astype(BF)
    d_bias_down = jnp.sum(low_branch.astype(F32), axis=0)
    d_down = dg(active, low_branch, TN)
    d_active = dg(low_branch, full_down, NT)
    gelu_back = jax.vjp(lambda v: jax.nn.gelu(v, approximate=False), inner)[1]
    low_inner = gelu_back(d_active)[0].astype(BF)
    d_bias_up = jnp.sum(low_inner.astype(F32), axis=0)
    d_up = dg(low_first, low_inner, TN)
    part_down = over_pair(d_down)
    part_up = over_pair(d_up)
    grad_first = grad_second + dg(low_inner, full_up, NT)
    d_gain_one = jnp.sum(grad_first * standard_one, axis=0)
    d_shift_one = jnp.sum(grad_first, axis=0)
    grad_sum = normalize_back(grad_first, standard_one, inverse_one, vector_rows[6])
    low_attn = grad_sum.astype(BF)
    d_bias_attn = jnp.sum(low_attn.astype(F32), axis=0)
    d_attn = dg(low_mixed, low_attn, TN)
    d_mixed = dg(low_attn, full_attn, NT).astype(BF)

    d_vector_rows = jnp.stack(
        [d_bias_attn, d_bias_down, d_shift_one, d_shift_two, d_gain_one, d_gain_two]
    )
    extra = jnp.concatenate([d_vector_rows.T, d_bias_up.reshape(width, -1)], axis=1)
    extra = jnp.pad(extra, ((0, 0), (0, 128 - extra.shape[1])))
    part_attn = over_pair(jnp.concatenate([d_attn, extra], axis=1))
    dq, dk_own, dv_own, dk_sib, dv_sib, own_up, own_down, own_attn = attention_backward(
        queries, d_mixed, mixed, kv, kv_sib, bias, lse, [part_up, part_down, part_attn], dp, ctx
    )
    dk_got = lax.ppermute(dk_sib, "ctx", pair_perm)
    dv_got = lax.ppermute(dv_sib, "ctx", pair_perm)
    dk = (dk_own + dk_got.astype(F32)).astype(BF)
    dv = (dv_own + dv_got.astype(F32)).astype(BF)
    grad_in = grad_sum + (
        dg(dq, full_qkv[:, :width], NT)
        + dg(dk, full_qkv[:, width : 2 * width], NT)
        + dg(dv, full_qkv[:, 2 * width :], NT)
    )
    sums = jnp.stack([jnp.sum(dq.astype(F32), axis=0), jnp.sum(dv.astype(F32), axis=0)])
    sums = jnp.pad(sums.T, ((0, 0), (0, 126)))
    part = over_pair(
        jnp.concatenate([dg(low_in, dq, TN), dg(low_in, dk, TN), dg(low_in, dv, TN), sums], axis=1)
    )
    own, grad_tokens = finish_gradients(
        part, grad_in.astype(BF).reshape(ctx, half, width), dp, ctx
    )
    grad_tokens = grad_tokens.astype(F32).reshape(seqs, rows_dev, width)
    own_query, own_key, own_value = (own[:, i * width : (i + 1) * width] for i in range(3))
    own_vectors = jnp.concatenate(
        [own[:, 3 * width : 3 * width + 2], own_attn[:, width : width + 6]], axis=1
    ).T
    own_bias_up = own_attn[:, width + 6 : width + 6 + bias_columns].reshape(-1)
    own_attn = own_attn[:, :width]
    return (
        output,
        grad_tokens,
        own_query,
        own_key,
        own_value,
        own_attn,
        own_up,
        own_bias_up,
        own_down,
        own_vectors,
    )


def solution(mesh):
    in_specs = (
        P("dp", "ctx", None),
        P("dp", "ctx", None),
        P(),
        P(("dp", "ctx"), None),
        P(("dp", "ctx"), None),
        P(("dp", "ctx"), None),
        P(("dp", "ctx"), None),
        P(("dp", "ctx"), None),
        P(("dp", "ctx")),
        P(("dp", "ctx"), None),
        P(None, ("dp", "ctx")),
    )
    out_specs = (
        P("dp", "ctx", None),
        P("dp", "ctx", None),
        P(("dp", "ctx"), None),
        P(("dp", "ctx"), None),
        P(("dp", "ctx"), None),
        P(("dp", "ctx"), None),
        P(("dp", "ctx"), None),
        P(("dp", "ctx")),
        P(("dp", "ctx"), None),
        P(None, ("dp", "ctx")),
    )
    return jax.shard_map(
        on_device, mesh=mesh, in_specs=in_specs, out_specs=out_specs, check_vma=False
    )
```

```python
import functools
import jax
import jax.numpy as jnp
from jax import lax
from jax.experimental import pallas as pl
from jax.experimental.pallas import tpu as pltpu
from jax.sharding import PartitionSpec as P

HEAD_DIM = 64
F32 = jnp.float32
BF = jnp.bfloat16
NN = (((1,), (0,)), ((), ()))
NT = (((1,), (1,)), ((), ()))
TN = (((0,), (0,)), ((), ()))
epsilon = 1e-12
masked_score = -1e30


def dg(left, right, dims):
    return lax.dot_general(left, right, dims, preferred_element_type=F32)


MESH = pl.DeviceIdType.MESH


class Mover:
    def __init__(self, local_sem, send_sem, recv_sem):
        self.local_sem, self.send_sem, self.recv_sem = local_sem, send_sem, recv_sem
        self.locals = self.remotes = 0

    def local(self, source, target):
        copy = pltpu.make_async_copy(source, target, self.local_sem.at[self.locals])
        self.locals += 1
        return copy

    def remote(self, source, target, device):
        number = self.remotes
        self.remotes += 1
        return pltpu.make_async_remote_copy(
            src_ref=source,
            dst_ref=target,
            send_sem=self.send_sem.at[number],
            recv_sem=self.recv_sem.at[number],
            device_id=device,
            device_id_type=MESH,
        )


def greet(devices):
    barrier = pltpu.get_barrier_semaphore()
    for device in devices:
        pl.semaphore_signal(barrier, inc=1, device_id=device, device_id_type=MESH)
    pl.semaphore_wait(barrier, len(devices))


def place(dp, ctx):
    d, c = lax.axis_index("dp"), lax.axis_index("ctx")
    groups = ctx // 2
    g, m = c // 2, c % 2
    over_dp = [((d + k) % dp, c) for k in range(1, dp)]
    over_groups = [(d, (g + k) % groups * 2 + m) for k in range(1, groups)]
    return d, c, g, m, over_dp, over_groups, (d, g * 2 + 1 - m)


def gather_kernel(dp, ctx, x, w, wo, wu, wd, x_in, w_full, zo, zu, zd, local_sem, send_sem, recv_sem):
    d, c, g, m, over_dp, over_groups, sibling = place(dp, ctx)
    groups = ctx // 2
    greet(over_dp + [(d, (c + k) % ctx) for k in range(1, ctx)])
    mover = Mover(local_sem, send_sem, recv_sem)
    own = [
        mover.local(source, target)
        for source, target in (
            (w, w_full.at[d, c]),
            (x.at[c], x_in.at[c]),
            (wo, zo.at[d]),
            (wu, zu.at[d]),
            (wd, zd.at[d]),
        )
    ]
    along = [mover.remote(w, w_full.at[d, c], device) for device in over_dp]
    across = [[mover.remote(w, w_full.at[d, c], device) for device in over_groups]]
    rows = [
        mover.remote(x.at[(c + k) % ctx], x_in.at[c], (d, (c + k) % ctx)) for k in range(1, ctx)
    ]
    rest = [
        mover.remote(source, target.at[d], device)
        for source, target in ((wo, zo), (wu, zu), (wd, zd))
        for device in over_dp
    ]
    for copy in own + along + across[0] + rows + rest:
        copy.start()
    for k in range(1, dp):
        along[k - 1].wait_recv()
        piece = w_full.at[(d - k + dp) % dp, c]
        across.append([mover.remote(piece, piece, device) for device in over_groups])
        for copy in across[-1]:
            copy.start()
    own[0].wait()
    mine = w_full.at[:, c]
    over = [mover.remote(mine, mine, sibling)]
    over[0].start()
    for k in range(1, groups):
        for batch in across:
            batch[k - 1].wait_recv()
        block = w_full.at[:, (g - k + groups) % groups * 2 + m]
        over.append(mover.remote(block, block, sibling))
        over[-1].start()
    for copy in over + rows + rest:
        copy.wait()
    for copy in along + [copy for batch in across for copy in batch]:
        copy.wait_send()
    for copy in own[1:]:
        copy.wait()


def gather_first(x, w, wo, wu, wd, dp, ctx):
    groups = ctx // 2
    remotes = (dp - 1) + dp * (groups - 1) + (ctx - 1) + 3 * (dp - 1) + groups
    any_space = pl.BlockSpec(memory_space=pl.ANY)
    return pl.pallas_call(
        functools.partial(gather_kernel, dp, ctx),
        in_specs=[any_space] * 5,
        out_specs=[any_space] * 5,
        out_shape=[
            jax.ShapeDtypeStruct(x.shape, BF),
            jax.ShapeDtypeStruct((dp, ctx) + w.shape, BF),
        ]
        + [jax.ShapeDtypeStruct((dp,) + array.shape, BF) for array in (wo, wu, wd)],
        scratch_shapes=[
            pltpu.SemaphoreType.DMA((5,)),
            pltpu.SemaphoreType.DMA((remotes,)),
            pltpu.SemaphoreType.DMA((remotes,)),
        ],
        compiler_params=pltpu.CompilerParams(collective_id=0, has_side_effects=True),
        name="gather_first",
    )(x, w, wo, wu, wd)


class Spread:
    def __init__(self, dp, ctx, sources, targets, mover):
        d, c, g, m, over_dp, over_groups, sibling = place(dp, ctx)
        groups = ctx // 2
        self.devices = over_groups + [sibling]
        self.own = [mover.local(s, t.at[:, c]) for s, t in zip(sources, targets)]
        self.direct = [mover.remote(s, t.at[:, c], sibling) for s, t in zip(sources, targets)]
        self.across = [
            [mover.remote(s, t.at[:, c], device) for device in over_groups]
            for s, t in zip(sources, targets)
        ]
        self.onward = []
        for t in targets:
            blocks = [t.at[:, (g - k + groups) % groups * 2 + m] for k in range(1, groups)]
            self.onward.append([mover.remote(block, block, sibling) for block in blocks])

    @staticmethod
    def count(groups, arrays):
        return arrays * (1 + 2 * (groups - 1))

    def begin(self):
        greet(self.devices)
        for copy in self.own + [copy for batch in self.across for copy in batch] + self.direct:
            copy.start()

    def forward(self, index):
        for came, copy in zip(self.across[index], self.onward[index]):
            came.wait_recv()
            copy.start()

    def finish(self):
        for copy in self.own + self.direct + [copy for batch in self.onward for copy in batch]:
            copy.wait()
        for batch in self.across:
            for copy in batch:
                copy.wait_send()


class Scatter:
    def __init__(self, dp, ctx, sources, outs, buffers, mover):
        d, c, g, m, over_dp, over_groups, sibling = place(dp, ctx)
        groups = ctx // 2
        self.dp, self.groups, self.d = dp, groups, d
        self.devices = over_groups + over_dp
        self.outs = outs
        self.mine = [b[0] for b in buffers]
        self.came = [b[1] for b in buffers]
        self.sums = [b[2] for b in buffers]
        self.last = [b[3] for b in buffers]
        self.own = [mover.local(s.at[:, g], b) for s, b in zip(sources, self.mine)]
        self.across = [
            [
                mover.remote(s.at[:, (g + k) % groups], b.at[k - 1], over_groups[k - 1])
                for k in range(1, groups)
            ]
            for s, b in zip(sources, self.came)
        ]
        self.along = [
            [
                mover.remote(s.at[(d + k) % dp], b.at[k - 1], over_dp[k - 1])
                for k in range(1, dp)
            ]
            for s, b in zip(self.sums, self.last)
        ]

    @staticmethod
    def count(dp, groups, arrays):
        return arrays * (groups - 1 + dp - 1)

    @staticmethod
    def scratch(dp, groups, sources):
        shapes = []
        for s in sources:
            block = s.shape[2:]
            shapes += [
                pltpu.VMEM((dp,) + block, BF),
                pltpu.VMEM((groups - 1, dp) + block, BF),
                pltpu.VMEM((dp,) + block, BF),
                pltpu.VMEM((dp - 1,) + block, BF),
            ]
        return shapes

    def begin(self):
        for copy in self.own + [copy for batch in self.across for copy in batch]:
            copy.start()

    def middle(self, index):
        self.own[index].wait()
        for copy in self.across[index]:
            copy.wait_recv()
        for k in range(self.dp):
            total = self.mine[index][k].astype(F32)
            for j in range(self.groups - 1):
                total = total + self.came[index][j, k].astype(F32)
            self.sums[index][k] = total.astype(BF)
        for copy in self.along[index]:
            copy.start()

    def finish(self):
        for index, out in enumerate(self.outs):
            for copy in self.along[index]:
                copy.wait_recv()
            total = self.sums[index][self.d].astype(F32)
            for j in range(self.dp - 1):
                total = total + self.last[index][j].astype(F32)
            out[...] = total
        for batch in self.across + self.along:
            for copy in batch:
                copy.wait_send()


def finish_kernel(dp, ctx, s, x, out, x_out, *scratch):
    buffers, (local_sem, send_sem, recv_sem) = scratch[:-3], scratch[-3:]
    d, c, g, m, over_dp, over_groups, sibling = place(dp, ctx)
    mover = Mover(local_sem, send_sem, recv_sem)
    scatter = Scatter(dp, ctx, [s], [out], [buffers], mover)
    own = mover.local(x.at[c], x_out.at[c])
    rows = [
        mover.remote(x.at[(c + k) % ctx], x_out.at[c], (d, (c + k) % ctx)) for k in range(1, ctx)
    ]
    greet(over_dp + [(d, (c + k) % ctx) for k in range(1, ctx)])
    scatter.begin()
    own.start()
    for copy in rows:
        copy.start()
    scatter.middle(0)
    scatter.finish()
    for copy in rows:
        copy.wait()
    own.wait()


def finish_gradients(s, x, dp, ctx):
    groups = ctx // 2
    remotes = Scatter.count(dp, groups, 1) + ctx - 1
    any_space = pl.BlockSpec(memory_space=pl.ANY)
    return pl.pallas_call(
        functools.partial(finish_kernel, dp, ctx),
        in_specs=[any_space] * 2,
        out_specs=[pl.BlockSpec(memory_space=pltpu.VMEM), any_space],
        out_shape=[jax.ShapeDtypeStruct(s.shape[2:], F32), jax.ShapeDtypeStruct(x.shape, x.dtype)],
        scratch_shapes=Scatter.scratch(dp, groups, [s])
        + [
            pltpu.SemaphoreType.DMA((2,)),
            pltpu.SemaphoreType.DMA((remotes,)),
            pltpu.SemaphoreType.DMA((remotes,)),
        ],
        compiler_params=pltpu.CompilerParams(
            collective_id=3, has_side_effects=True, vmem_limit_bytes=32 << 20
        ),
        name="finish_gradients",
    )(s, x)


def head_lanes(shape, h):
    lane = lax.broadcasted_iota(jnp.int32, shape, len(shape) - 1)
    return (lane >= 64) == (h == 1), lane == (64 if h == 0 else 0)


def load_keys(keys, own_ref, sib_ref, bias_ref):
    half = own_ref.shape[0]
    for h in range(2):
        for i, ref in enumerate((own_ref, sib_ref)):
            inside, spare = head_lanes((half, 128), h)
            rest = jnp.where(spare, bias_ref[i], jnp.zeros((), BF))
            keys[h, i * half : (i + 1) * half, :] = jnp.where(inside, ref[...], rest)


def forward_kernel(dp, ctx, *refs):
    (q_ref, ko_ref, ks_ref, vo_ref, vs_ref, bias_ref), refs = refs[:6], refs[6:]
    gathered, (mb_ref, mix_ref, lse_ref), spread_to, refs = refs[:3], refs[3:6], refs[6:9], refs[9:]
    keys, local_sem, send_sem, recv_sem = refs
    spread = Spread(dp, ctx, gathered, spread_to, Mover(local_sem, send_sem, recv_sem))
    steps = pl.num_programs(1)
    step = pl.program_id(0) * steps + pl.program_id(1)
    last = forward_steps(pl.num_programs(0), steps)

    @pl.when(step == 0)
    def _():
        spread.begin()

    @pl.when(pl.program_id(1) == 0)
    def _():
        load_keys(keys, ko_ref, ks_ref, bias_ref)

    half, bq = ko_ref.shape[0], q_ref.shape[0]
    q = q_ref[...] * jnp.asarray(0.125, BF)
    outs, lses = [], []
    for h in range(2):
        inside, spare = head_lanes((bq, 128), h)
        rest = jnp.where(spare, jnp.ones((), BF), jnp.zeros((), BF))
        scores = dg(jnp.where(inside, q, rest), keys[h], NT)
        top = jnp.max(scores, axis=1, keepdims=True)
        weights = jnp.exp(scores - top)
        total = jnp.sum(weights, axis=1, keepdims=True)
        low = weights.astype(BF)
        mixed = dg(low[:, :half], vo_ref[...], NN) + dg(low[:, half:], vs_ref[...], NN)
        outs.append(mixed / total)
        lses.append(top + jnp.log(total))
    lane = lax.broadcasted_iota(jnp.int32, (bq, 128), 1)
    mixed = jnp.where(lane < 64, outs[0], outs[1])
    mix_ref[...] = mixed
    mb_ref[...] = mixed.astype(BF)
    lse_ref[0] = jnp.where(lane == 0, lses[0], lses[1]).T[:8]

    for index, at in enumerate(last):

        @pl.when(step == at)
        def _(index=index):
            spread.forward(index)

    @pl.when(step == last[-1])
    def _():
        spread.finish()


def attention_forward(q, kv, kv_sib, bias, gathered, dp, ctx, bq=256):
    rows = q.shape[0]
    pairs = q.shape[1] // 128
    S = jax.ShapeDtypeStruct
    blk = pl.BlockSpec((bq, 128), lambda p, j: (j, p))
    k_spec = pl.BlockSpec((rows, 128), lambda p, j: (0, p))
    v_spec = pl.BlockSpec((rows, 128), lambda p, j: (0, pairs + p))
    any_space = pl.BlockSpec(memory_space=pl.ANY)
    remotes = Spread.count(ctx // 2, 3)
    return pl.pallas_call(
        functools.partial(forward_kernel, dp, ctx),
        grid=(pairs, rows // bq),
        in_specs=[blk, k_spec, k_spec, v_spec, v_spec]
        + [pl.BlockSpec((2, rows, 128), lambda p, j: (0, 0, 0))]
        + [any_space] * 3,
        out_specs=[blk, blk, pl.BlockSpec((1, 8, bq), lambda p, j: (p, 0, j))] + [any_space] * 3,
        out_shape=[S(q.shape, BF), S(q.shape, F32), S((pairs, 8, rows), F32)]
        + [S((dp, ctx) + array.shape[1:], BF) for array in gathered],
        scratch_shapes=[
            pltpu.VMEM((2, 2 * rows, 128), BF),
            pltpu.SemaphoreType.DMA((3,)),
            pltpu.SemaphoreType.DMA((remotes,)),
            pltpu.SemaphoreType.DMA((remotes,)),
        ],
        compiler_params=pltpu.CompilerParams(
            vmem_limit_bytes=48 << 20, collective_id=1, has_side_effects=True
        ),
        cost_estimate=pl.CostEstimate(
            flops=16 * rows * rows * 128 * pairs,
            bytes_accessed=14 * rows * 768,
            transcendentals=4 * rows * rows * pairs,
        ),
        name="attend",
    )(q, kv, kv_sib, kv, kv_sib, bias, *gathered)


def forward_steps(pairs, steps):
    count = pairs * steps
    return (count * 5 // 24, count * 15 // 24, count - 1)


def backward_steps(pairs, steps):
    count = pairs * steps
    return (count * 7 // 12, count * 8 // 12, count * 9 // 12)


def backward_kernel(dp, ctx, ck, *refs):
    (q_ref, do_ref, mix_ref, ko_ref, ks_ref, vo_ref, vs_ref, bias_ref, lse_ref), refs = (
        refs[:9],
        refs[9:],
    )
    sources, refs = refs[:3], refs[3:]
    (dq_ref, dko_ref, dvo_ref, dks_ref, dvs_ref), refs = refs[:5], refs[5:]
    summed, refs = refs[:3], refs[3:]
    (keys, dk, dv), refs = refs[:3], refs[3:]
    buffers, (local_sem, send_sem, recv_sem) = refs[:12], refs[12:]
    scatter = Scatter(
        dp,
        ctx,
        sources,
        summed,
        [buffers[i * 4 : i * 4 + 4] for i in range(3)],
        Mover(local_sem, send_sem, recv_sem),
    )
    steps = pl.num_programs(1)
    j = pl.program_id(1)
    step = pl.program_id(0) * steps + j

    @pl.when(step == 0)
    def _():
        greet(scatter.devices)
        scatter.begin()

    @pl.when(j == 0)
    def _():
        load_keys(keys, ko_ref, ks_ref, bias_ref)
        dk[...] = jnp.zeros_like(dk)
        dv[...] = jnp.zeros_like(dv)

    half, bq = ko_ref.shape[0], q_ref.shape[0]
    q = q_ref[...] * jnp.asarray(0.125, BF)
    do = do_ref[...]
    prod = (do.astype(F32) * mix_ref[...]).T
    zero, one = jnp.zeros((), BF), jnp.ones((), BF)
    heads = []
    for h in range(2):
        inside, spare = head_lanes((bq, 128), h)
        heads.append(
            (
                jnp.where(inside, q, jnp.where(spare, one, zero)),
                jnp.where(inside, q, zero),
                jnp.where(inside, do, zero),
                lse_ref[0, h : h + 1, :],
                jnp.sum(prod[h * 64 : (h + 1) * 64], axis=0, keepdims=True),
            )
        )
    dq = jnp.zeros((bq, 128), F32)
    for first in range(0, 2 * half, ck):
        rows = slice(first, first + ck)
        v = vo_ref[rows, :] if first < half else vs_ref[first - half : first - half + ck, :]
        for h in range(2):
            qm, qz, dom, lse, delta = heads[h]
            k = keys[h, rows, :]
            p = jnp.exp(dg(k, qm, NT) - lse)
            ds = (p * (dg(v, dom, NT) - delta)).astype(BF)
            dv[rows, :] += dg(p.astype(BF), dom, NN)
            dk[rows, :] += dg(ds, qz, NN)
            dq = dq + dg(ds, k, TN)
    dq_ref[...] = (dq * 0.125).astype(BF)

    @pl.when(j == steps - 1)
    def _():
        dko_ref[...] = dk[:half, :]
        dvo_ref[...] = dv[:half, :]
        dks_ref[...] = dk[half:, :].astype(BF)
        dvs_ref[...] = dv[half:, :].astype(BF)

    for index, at in enumerate(backward_steps(pl.num_programs(0), steps)):

        @pl.when(step == at)
        def _(index=index):
            scatter.middle(index)

    @pl.when(step == pl.num_programs(0) * steps - 1)
    def _():
        scatter.finish()


def attention_backward(q, do, mix, kv, kv_sib, bias, lse, sources, dp, ctx, bq=512, ck=512):
    rows = q.shape[0]
    pairs = q.shape[1] // 128
    S = jax.ShapeDtypeStruct
    blk = pl.BlockSpec((bq, 128), lambda p, j: (j, p))
    full = pl.BlockSpec((rows, 128), lambda p, j: (0, p))
    v_spec = pl.BlockSpec((rows, 128), lambda p, j: (0, pairs + p))
    any_space = pl.BlockSpec(memory_space=pl.ANY)
    remotes = Scatter.count(dp, ctx // 2, 3)
    sums = [s.shape[2:] for s in sources]
    return pl.pallas_call(
        functools.partial(backward_kernel, dp, ctx, ck),
        grid=(pairs, rows // bq),
        in_specs=[blk, blk, blk, full, full, v_spec, v_spec]
        + [pl.BlockSpec((2, rows, 128), lambda p, j: (0, 0, 0))]
        + [pl.BlockSpec((1, 8, bq), lambda p, j: (p, 0, j))]
        + [any_space] * 3,
        out_specs=[blk, full, full, full, full]
        + [pl.BlockSpec(shape, lambda p, j: (0, 0)) for shape in sums],
        out_shape=[
            S(q.shape, BF),
            S(q.shape, F32),
            S(q.shape, F32),
            S(q.shape, BF),
            S(q.shape, BF),
        ]
        + [S(shape, F32) for shape in sums],
        scratch_shapes=[
            pltpu.VMEM((2, 2 * rows, 128), BF),
            pltpu.VMEM((2 * rows, 128), F32),
            pltpu.VMEM((2 * rows, 128), F32),
        ]
        + Scatter.scratch(dp, ctx // 2, sources)
        + [
            pltpu.SemaphoreType.DMA((3,)),
            pltpu.SemaphoreType.DMA((remotes,)),
            pltpu.SemaphoreType.DMA((remotes,)),
        ],
        compiler_params=pltpu.CompilerParams(
            vmem_limit_bytes=56 << 20, collective_id=2, has_side_effects=True
        ),
        cost_estimate=pl.CostEstimate(
            flops=40 * rows * rows * 128 * pairs,
            bytes_accessed=26 * rows * 768,
            transcendentals=4 * rows * rows * pairs,
        ),
        name="attend_back",
    )(q, do, mix, kv, kv_sib, kv, kv_sib, bias, lse, *sources)


def normalize(hidden, scale_row, shift_row):
    centred = hidden - jnp.mean(hidden, axis=-1, keepdims=True)
    inverse = lax.rsqrt(jnp.mean(centred * centred, axis=-1, keepdims=True) + epsilon)
    standard = centred * inverse
    return (standard * scale_row + shift_row, standard, inverse)


def normalize_back(gradient, standard, inverse, scale_row):
    scaled = gradient * scale_row
    centred = scaled - jnp.mean(scaled, axis=-1, keepdims=True)
    return (centred - standard * jnp.mean(scaled * standard, axis=-1, keepdims=True)) * inverse


def on_device(
    tokens, cotangent, lengths, w_query, w_key, w_value, w_attn_out, w_up, b_up, w_down, vectors
):
    seqs, rows_dev, width = tokens.shape
    dp = lax.axis_size("dp")
    ctx = lax.axis_size("ctx")
    half = rows_dev // 2
    rows = half * ctx
    member = lax.axis_index("ctx") % 2
    own_seq = lax.axis_index("dp") * seqs + lax.axis_index("ctx") // 2
    length = lax.dynamic_index_in_dim(lengths, own_seq, 0, keepdims=False)
    pair_perm = [(i, i ^ 1) for i in range(ctx)]

    def exchange(array):
        return lax.all_to_all(array, "ctx", 0, 0, tiled=True)

    def over_pair(grad):
        parts = grad.astype(BF).reshape(dp, ctx // 2, 2, -1, grad.shape[1])
        keep = lax.dynamic_index_in_dim(parts, member, 2, keepdims=False)
        send = lax.dynamic_index_in_dim(parts, 1 - member, 2, keepdims=False)
        got = lax.ppermute(send, "ctx", pair_perm)
        return (keep.astype(F32) + got.astype(F32)).astype(BF)

    split = tokens.reshape(ctx, half, width)
    held = w_query.shape[0]
    extra = jnp.concatenate([vectors.T, b_up.reshape(held, -1)], axis=1)
    extra = jnp.pad(extra, ((0, 0), (0, 128 - extra.shape[1])))
    low_in, full_first, *over_dp = gather_first(
        split.astype(BF),
        jnp.concatenate([w_query, w_key, w_value, extra], axis=1),
        w_attn_out,
        w_up,
        w_down,
        dp,
        ctx,
    )
    low_in = low_in.reshape(rows, width)
    full_first = full_first.reshape(width, -1)
    full_qkv = full_first[:, : 3 * width]
    vector_rows = full_first[:, 3 * width : 3 * width + 8].T.astype(F32)
    bias_columns = b_up.shape[0] // held
    full_bias_up = full_first[:, 3 * width + 8 : 3 * width + 8 + bias_columns].reshape(-1).astype(F32)
    left_out, low_in = lax.optimization_barrier(
        ((split - split.astype(BF).astype(F32)).astype(BF), low_in)
    )
    residual = low_in.astype(F32) + exchange(left_out).reshape(rows, width).astype(F32)

    slot = jnp.arange(rows, dtype=jnp.int32)
    source = slot // half
    high = (2 * ctx - 1 - source) * half + slot % half

    def key_bias(kind):
        position = jnp.where(kind == 0, slot, high)
        return jnp.where(position < length, 0.0, masked_score).astype(BF)

    bias = jnp.stack([key_bias(member), key_bias(1 - member)])
    bias = jnp.broadcast_to(bias[:, :, None], (2, rows, 128))

    row_of = jnp.concatenate([jnp.zeros_like(vector_rows[1]), vector_rows[1]])
    kv = (dg(low_in, full_qkv[:, width:], NN) + row_of).astype(BF)
    kv_sib = lax.ppermute(kv, "ctx", pair_perm)
    queries = (dg(low_in, full_qkv[:, :width], NN) + vector_rows[0]).astype(BF)
    low_mixed, mixed, lse, full_attn, full_up, full_down = attention_forward(
        queries, kv, kv_sib, bias, over_dp, dp, ctx
    )
    late, low_mixed = lax.optimization_barrier((cotangent, low_mixed))
    upstream = exchange(late.reshape(ctx, half, width)).reshape(rows, width)
    full_attn = full_attn.reshape(width, width)
    full_up = full_up.reshape(width, -1)
    full_down = full_down.reshape(-1, width)

    attention = dg(low_mixed, full_attn, NN) + vector_rows[2]
    normed_one, standard_one, inverse_one = normalize(
        residual + attention, vector_rows[6], vector_rows[4]
    )
    low_first = normed_one.astype(BF)
    inner = dg(low_first, full_up, NN) + full_bias_up
    active = jax.nn.gelu(inner, approximate=False).astype(BF)
    branch = dg(active, full_down, NN) + vector_rows[3]
    result, standard_two, inverse_two = normalize(
        normed_one + branch, vector_rows[7], vector_rows[5]
    )
    output = exchange(result.reshape(ctx, half, width)).reshape(seqs, rows_dev, width)

    d_gain_two = jnp.sum(upstream * standard_two, axis=0)
    d_shift_two = jnp.sum(upstream, axis=0)
    grad_second = normalize_back(upstream, standard_two, inverse_two, vector_rows[7])
    low_branch = grad_second.astype(BF)
    d_bias_down = jnp.sum(low_branch.astype(F32), axis=0)
    d_down = dg(active, low_branch, TN)
    d_active = dg(low_branch, full_down, NT)
    gelu_back = jax.vjp(lambda v: jax.nn.gelu(v, approximate=False), inner)[1]
    low_inner = gelu_back(d_active)[0].astype(BF)
    d_bias_up = jnp.sum(low_inner.astype(F32), axis=0)
    d_up = dg(low_first, low_inner, TN)
    part_down = over_pair(d_down)
    part_up = over_pair(d_up)
    grad_first = grad_second + dg(low_inner, full_up, NT)
    d_gain_one = jnp.sum(grad_first * standard_one, axis=0)
    d_shift_one = jnp.sum(grad_first, axis=0)
    grad_sum = normalize_back(grad_first, standard_one, inverse_one, vector_rows[6])
    low_attn = grad_sum.astype(BF)
    d_bias_attn = jnp.sum(low_attn.astype(F32), axis=0)
    d_attn = dg(low_mixed, low_attn, TN)
    d_mixed = dg(low_attn, full_attn, NT).astype(BF)

    output, d_mixed = lax.optimization_barrier((output, d_mixed))
    d_vector_rows = jnp.stack(
        [d_bias_attn, d_bias_down, d_shift_one, d_shift_two, d_gain_one, d_gain_two]
    )
    extra = jnp.concatenate([d_vector_rows.T, d_bias_up.reshape(width, -1)], axis=1)
    extra = jnp.pad(extra, ((0, 0), (0, 128 - extra.shape[1])))
    part_attn = over_pair(jnp.concatenate([d_attn, extra], axis=1))
    dq, dk_own, dv_own, dk_sib, dv_sib, own_up, own_down, own_attn = attention_backward(
        queries, d_mixed, mixed, kv, kv_sib, bias, lse, [part_up, part_down, part_attn], dp, ctx
    )
    dk_got = lax.ppermute(dk_sib, "ctx", pair_perm)
    dv_got = lax.ppermute(dv_sib, "ctx", pair_perm)
    dk = (dk_own + dk_got.astype(F32)).astype(BF)
    dv = (dv_own + dv_got.astype(F32)).astype(BF)
    grad_in = grad_sum + (
        dg(dq, full_qkv[:, :width], NT)
        + dg(dk, full_qkv[:, width : 2 * width], NT)
        + dg(dv, full_qkv[:, 2 * width :], NT)
    )
    sums = jnp.stack([jnp.sum(dq.astype(F32), axis=0), jnp.sum(dv.astype(F32), axis=0)])
    sums = jnp.pad(sums.T, ((0, 0), (0, 126)))
    part = over_pair(
        jnp.concatenate([dg(low_in, dq, TN), dg(low_in, dk, TN), dg(low_in, dv, TN), sums], axis=1)
    )
    own, grad_tokens = finish_gradients(
        part, grad_in.astype(BF).reshape(ctx, half, width), dp, ctx
    )
    grad_tokens = grad_tokens.astype(F32).reshape(seqs, rows_dev, width)
    own_query, own_key, own_value = (own[:, i * width : (i + 1) * width] for i in range(3))
    own_vectors = jnp.concatenate(
        [own[:, 3 * width : 3 * width + 2], own_attn[:, width : width + 6]], axis=1
    ).T
    own_bias_up = own_attn[:, width + 6 : width + 6 + bias_columns].reshape(-1)
    own_attn = own_attn[:, :width]
    return (
        output,
        grad_tokens,
        own_query,
        own_key,
        own_value,
        own_attn,
        own_up,
        own_bias_up,
        own_down,
        own_vectors,
    )


def solution(mesh):
    in_specs = (
        P("dp", "ctx", None),
        P("dp", "ctx", None),
        P(),
        P(("dp", "ctx"), None),
        P(("dp", "ctx"), None),
        P(("dp", "ctx"), None),
        P(("dp", "ctx"), None),
        P(("dp", "ctx"), None),
        P(("dp", "ctx")),
        P(("dp", "ctx"), None),
        P(None, ("dp", "ctx")),
    )
    out_specs = (
        P("dp", "ctx", None),
        P("dp", "ctx", None),
        P(("dp", "ctx"), None),
        P(("dp", "ctx"), None),
        P(("dp", "ctx"), None),
        P(("dp", "ctx"), None),
        P(("dp", "ctx"), None),
        P(("dp", "ctx")),
        P(("dp", "ctx"), None),
        P(None, ("dp", "ctx")),
    )
    return jax.shard_map(
        on_device, mesh=mesh, in_specs=in_specs, out_specs=out_specs, check_vma=False
    )
```

```python
import functools
import jax
import jax.numpy as jnp
from jax import lax
from jax.experimental import pallas as pl
from jax.experimental.pallas import tpu as pltpu
from jax.sharding import PartitionSpec as P

HEAD_DIM = 64
F32 = jnp.float32
BF = jnp.bfloat16
NN = (((1,), (0,)), ((), ()))
NT = (((1,), (1,)), ((), ()))
TN = (((0,), (0,)), ((), ()))
epsilon = 1e-12
masked_score = -1e30


def dg(left, right, dims):
    return lax.dot_general(left, right, dims, preferred_element_type=F32)


MESH = pl.DeviceIdType.MESH


class Mover:
    def __init__(self, local_sem, send_sem, recv_sem):
        self.local_sem, self.send_sem, self.recv_sem = local_sem, send_sem, recv_sem
        self.locals = self.remotes = 0

    def local(self, source, target):
        copy = pltpu.make_async_copy(source, target, self.local_sem.at[self.locals])
        self.locals += 1
        return copy

    def remote(self, source, target, device):
        number = self.remotes
        self.remotes += 1
        return pltpu.make_async_remote_copy(
            src_ref=source,
            dst_ref=target,
            send_sem=self.send_sem.at[number],
            recv_sem=self.recv_sem.at[number],
            device_id=device,
            device_id_type=MESH,
        )


def greet(devices):
    barrier = pltpu.get_barrier_semaphore()
    for device in devices:
        pl.semaphore_signal(barrier, inc=1, device_id=device, device_id_type=MESH)
    pl.semaphore_wait(barrier, len(devices))


def place(dp, ctx):
    d, c = lax.axis_index("dp"), lax.axis_index("ctx")
    groups = ctx // 2
    g, m = c // 2, c % 2
    over_dp = [((d + k) % dp, c) for k in range(1, dp)]
    over_groups = [(d, (g + k) % groups * 2 + m) for k in range(1, groups)]
    return d, c, g, m, over_dp, over_groups, (d, g * 2 + 1 - m)


def gather_kernel(dp, ctx, x, w, wo, wu, wd, x_in, w_full, zo, zu, zd, local_sem, send_sem, recv_sem):
    d, c, g, m, over_dp, over_groups, sibling = place(dp, ctx)
    groups = ctx // 2
    greet(over_dp + [(d, (c + k) % ctx) for k in range(1, ctx)])
    mover = Mover(local_sem, send_sem, recv_sem)
    own = [
        mover.local(source, target)
        for source, target in (
            (w, w_full.at[d, c]),
            (x.at[c], x_in.at[c]),
            (wo, zo.at[d]),
            (wu, zu.at[d]),
            (wd, zd.at[d]),
        )
    ]
    along = [mover.remote(w, w_full.at[d, c], device) for device in over_dp]
    across = [[mover.remote(w, w_full.at[d, c], device) for device in over_groups]]
    rows = [
        mover.remote(x.at[(c + k) % ctx], x_in.at[c], (d, (c + k) % ctx)) for k in range(1, ctx)
    ]
    rest = [
        mover.remote(source, target.at[d], device)
        for source, target in ((wo, zo), (wu, zu), (wd, zd))
        for device in over_dp
    ]
    for copy in own + along + across[0] + rows + rest:
        copy.start()
    for k in range(1, dp):
        along[k - 1].wait_recv()
        piece = w_full.at[(d - k + dp) % dp, c]
        across.append([mover.remote(piece, piece, device) for device in over_groups])
        for copy in across[-1]:
            copy.start()
    own[0].wait()
    mine = w_full.at[:, c]
    over = [mover.remote(mine, mine, sibling)]
    over[0].start()
    for k in range(1, groups):
        for batch in across:
            batch[k - 1].wait_recv()
        block = w_full.at[:, (g - k + groups) % groups * 2 + m]
        over.append(mover.remote(block, block, sibling))
        over[-1].start()
    for copy in over + rows + rest:
        copy.wait()
    for copy in along + [copy for batch in across for copy in batch]:
        copy.wait_send()
    for copy in own[1:]:
        copy.wait()


def gather_first(x, w, wo, wu, wd, dp, ctx):
    groups = ctx // 2
    remotes = (dp - 1) + dp * (groups - 1) + (ctx - 1) + 3 * (dp - 1) + groups
    any_space = pl.BlockSpec(memory_space=pl.ANY)
    return pl.pallas_call(
        functools.partial(gather_kernel, dp, ctx),
        in_specs=[any_space] * 5,
        out_specs=[any_space] * 5,
        out_shape=[
            jax.ShapeDtypeStruct(x.shape, BF),
            jax.ShapeDtypeStruct((dp, ctx) + w.shape, BF),
        ]
        + [jax.ShapeDtypeStruct((dp,) + array.shape, BF) for array in (wo, wu, wd)],
        scratch_shapes=[
            pltpu.SemaphoreType.DMA((5,)),
            pltpu.SemaphoreType.DMA((remotes,)),
            pltpu.SemaphoreType.DMA((remotes,)),
        ],
        compiler_params=pltpu.CompilerParams(collective_id=0, has_side_effects=True),
        name="gather_first",
    )(x, w, wo, wu, wd)


class Spread:
    def __init__(self, dp, ctx, sources, targets, mover):
        d, c, g, m, over_dp, over_groups, sibling = place(dp, ctx)
        groups = ctx // 2
        self.devices = over_groups + [sibling]
        self.own = [mover.local(s, t.at[:, c]) for s, t in zip(sources, targets)]
        self.direct = [mover.remote(s, t.at[:, c], sibling) for s, t in zip(sources, targets)]
        self.across = [
            [mover.remote(s, t.at[:, c], device) for device in over_groups]
            for s, t in zip(sources, targets)
        ]
        self.onward = []
        for t in targets:
            blocks = [t.at[:, (g - k + groups) % groups * 2 + m] for k in range(1, groups)]
            self.onward.append([mover.remote(block, block, sibling) for block in blocks])

    @staticmethod
    def count(groups, arrays):
        return arrays * (1 + 2 * (groups - 1))

    def begin(self):
        greet(self.devices)
        for copy in self.own + [copy for batch in self.across for copy in batch] + self.direct:
            copy.start()

    def forward(self, index):
        for came, copy in zip(self.across[index], self.onward[index]):
            came.wait_recv()
            copy.start()

    def finish(self):
        for copy in self.own + self.direct + [copy for batch in self.onward for copy in batch]:
            copy.wait()
        for batch in self.across:
            for copy in batch:
                copy.wait_send()


class Scatter:
    def __init__(self, dp, ctx, sources, outs, buffers, small, small_out, small_buffers, mover):
        d, c, g, m, over_dp, over_groups, sibling = place(dp, ctx)
        groups = ctx // 2
        self.dp, self.groups, self.d, self.g = dp, groups, d, g
        self.devices = over_groups + over_dp + [sibling]
        self.outs = list(outs)
        self.buffers = buffers
        self.own, self.pair, self.across, self.along = [], [], [], []
        for source, (mine, other, came, sums, last) in zip(sources, buffers):
            self.own.append(mover.local(source.at[:, :, m], mine))
            self.pair.append([mover.remote(source.at[:, :, 1 - m], other, sibling)])
            self.across.append(
                [
                    mover.remote(mine.at[:, (g + k) % groups], came.at[k - 1], over_groups[k - 1])
                    for k in range(1, groups)
                ]
            )
            self.along.append(
                [
                    mover.remote(sums.at[(d + k) % dp], last.at[k - 1], over_dp[k - 1])
                    for k in range(1, dp)
                ]
            )
        self.small, self.small_out = small, small_out
        one, came, two, groups_in, three, dp_in = small_buffers
        self.small_buffers = small_buffers
        self.pair.append([mover.remote(one, came, sibling)])
        self.across.append(
            [mover.remote(two, groups_in.at[k - 1], over_groups[k - 1]) for k in range(1, groups)]
        )
        self.along.append(
            [mover.remote(three, dp_in.at[k - 1], over_dp[k - 1]) for k in range(1, dp)]
        )

    @staticmethod
    def count(dp, ctx, arrays):
        return (arrays + 1) * (1 + ctx // 2 - 1 + dp - 1)

    @staticmethod
    def scratch(dp, ctx, sources, small):
        groups = ctx // 2
        shapes = []
        for s in sources:
            block = s.shape[3:]
            shapes += [
                pltpu.VMEM((dp, groups) + block, BF),
                pltpu.VMEM((dp, groups) + block, BF),
                pltpu.VMEM((groups - 1, dp) + block, BF),
                pltpu.VMEM((dp,) + block, BF),
                pltpu.VMEM((dp - 1,) + block, BF),
            ]
        shape = small.shape
        shapes += [pltpu.VMEM(shape, F32)] * 3
        shapes += [
            pltpu.VMEM((groups - 1,) + shape, F32),
            pltpu.VMEM(shape, F32),
            pltpu.VMEM((dp - 1,) + shape, F32),
        ]
        return shapes

    def begin(self):
        self.small_buffers[0][...] = self.small[...]
        for batch in self.pair[-1:] + self.pair[:-1]:
            batch[0].start()
        for copy in self.own:
            copy.start()

    def first(self, index):
        mine, other = self.buffers[index][:2]
        groups = self.groups
        self.own[index].wait()
        self.pair[index][0].wait_recv()

        def add(i, carry):
            at = (i // groups, i % groups)
            mine[at] = (mine[at].astype(F32) + other[at].astype(F32)).astype(BF)
            return carry

        lax.fori_loop(0, self.dp * groups, add, 0)
        for copy in self.across[index]:
            copy.start()

    def first_small(self):
        one, came, two = self.small_buffers[:3]
        self.pair[-1][0].wait_recv()
        two[...] = one[...] + came[...]
        for copy in self.across[-1]:
            copy.start()

    def middle(self, index):
        mine, _, came, sums, _ = self.buffers[index]
        for copy in self.across[index]:
            copy.wait_recv()

        def add(k, carry):
            total = mine[k, self.g].astype(F32)
            for j in range(self.groups - 1):
                total = total + came[j, k].astype(F32)
            sums[k] = total.astype(BF)
            return carry

        lax.fori_loop(0, self.dp, add, 0)
        for copy in self.along[index]:
            copy.start()

    def middle_small(self):
        _, _, two, groups_in, three, _ = self.small_buffers
        for copy in self.across[-1]:
            copy.wait_recv()
        total = two[...]
        for j in range(self.groups - 1):
            total = total + groups_in[j]
        three[...] = total
        for copy in self.along[-1]:
            copy.start()

    def finish(self):
        for index, out in enumerate(self.outs):
            sums, last = self.buffers[index][3:]
            for copy in self.along[index]:
                copy.wait_recv()
            total = sums[self.d].astype(F32)
            for j in range(self.dp - 1):
                total = total + last[j].astype(F32)
            out[...] = total
        three, dp_in = self.small_buffers[4:]
        for copy in self.along[-1]:
            copy.wait_recv()
        total = three[...]
        for j in range(self.dp - 1):
            total = total + dp_in[j]
        self.small_out[...] = total
        for batch in self.pair + self.across + self.along:
            for copy in batch:
                copy.wait_send()


def finish_kernel(dp, ctx, s, small, x, out, small_out, x_out, *scratch):
    buffers, (local_sem, send_sem, recv_sem) = scratch[:-3], scratch[-3:]
    d, c = lax.axis_index("dp"), lax.axis_index("ctx")
    mover = Mover(local_sem, send_sem, recv_sem)
    scatter = Scatter(
        dp, ctx, [s], [out], [buffers[:5]], small, small_out, buffers[5:], mover
    )
    own = mover.local(x.at[c], x_out.at[c])
    rows = [
        mover.remote(x.at[(c + k) % ctx], x_out.at[c], (d, (c + k) % ctx)) for k in range(1, ctx)
    ]
    greet([((d + k) % dp, c) for k in range(1, dp)] + [(d, (c + k) % ctx) for k in range(1, ctx)])
    scatter.begin()
    own.start()
    scatter.first_small()
    scatter.first(0)
    for copy in rows:
        copy.start()
    scatter.middle_small()
    scatter.middle(0)
    scatter.finish()
    for copy in rows:
        copy.wait()
    own.wait()


def finish_gradients(s, small, x, dp, ctx):
    remotes = Scatter.count(dp, ctx, 1) + ctx - 1
    any_space = pl.BlockSpec(memory_space=pl.ANY)
    vmem = pl.BlockSpec(memory_space=pltpu.VMEM)
    return pl.pallas_call(
        functools.partial(finish_kernel, dp, ctx),
        in_specs=[any_space, vmem, any_space],
        out_specs=[vmem, vmem, any_space],
        out_shape=[
            jax.ShapeDtypeStruct(s.shape[3:], F32),
            jax.ShapeDtypeStruct(small.shape, F32),
            jax.ShapeDtypeStruct(x.shape, x.dtype),
        ],
        scratch_shapes=Scatter.scratch(dp, ctx, [s], small)
        + [
            pltpu.SemaphoreType.DMA((2,)),
            pltpu.SemaphoreType.DMA((remotes,)),
            pltpu.SemaphoreType.DMA((remotes,)),
        ],
        compiler_params=pltpu.CompilerParams(
            collective_id=3, has_side_effects=True, vmem_limit_bytes=32 << 20
        ),
        name="finish_gradients",
    )(s, small, x)


def head_lanes(shape, h):
    lane = lax.broadcasted_iota(jnp.int32, shape, len(shape) - 1)
    return (lane >= 64) == (h == 1), lane == (64 if h == 0 else 0)


def load_keys(keys, own_ref, sib_ref, bias_ref):
    half = own_ref.shape[0]
    for h in range(2):
        for i, ref in enumerate((own_ref, sib_ref)):
            inside, spare = head_lanes((half, 128), h)
            rest = jnp.where(spare, bias_ref[i], jnp.zeros((), BF))
            keys[h, i * half : (i + 1) * half, :] = jnp.where(inside, ref[...], rest)


def forward_kernel(dp, ctx, *refs):
    (q_ref, ko_ref, ks_ref, vo_ref, vs_ref, bias_ref), refs = refs[:6], refs[6:]
    gathered, (mb_ref, mix_ref, lse_ref), spread_to, refs = refs[:3], refs[3:6], refs[6:9], refs[9:]
    keys, local_sem, send_sem, recv_sem = refs
    spread = Spread(dp, ctx, gathered, spread_to, Mover(local_sem, send_sem, recv_sem))
    steps = pl.num_programs(1)
    step = pl.program_id(0) * steps + pl.program_id(1)
    last = forward_steps(pl.num_programs(0), steps)

    @pl.when(step == 0)
    def _():
        spread.begin()

    @pl.when(pl.program_id(1) == 0)
    def _():
        load_keys(keys, ko_ref, ks_ref, bias_ref)

    half, bq = ko_ref.shape[0], q_ref.shape[0]
    q = q_ref[...] * jnp.asarray(0.125, BF)
    outs, lses = [], []
    for h in range(2):
        inside, spare = head_lanes((bq, 128), h)
        rest = jnp.where(spare, jnp.ones((), BF), jnp.zeros((), BF))
        scores = dg(jnp.where(inside, q, rest), keys[h], NT)
        top = jnp.max(scores, axis=1, keepdims=True)
        weights = jnp.exp(scores - top)
        total = jnp.sum(weights, axis=1, keepdims=True)
        low = weights.astype(BF)
        mixed = dg(low[:, :half], vo_ref[...], NN) + dg(low[:, half:], vs_ref[...], NN)
        outs.append(mixed / total)
        lses.append(top + jnp.log(total))
    lane = lax.broadcasted_iota(jnp.int32, (bq, 128), 1)
    mixed = jnp.where(lane < 64, outs[0], outs[1])
    mix_ref[...] = mixed
    mb_ref[...] = mixed.astype(BF)
    lse_ref[0] = jnp.where(lane == 0, lses[0], lses[1]).T[:8]

    for index, at in enumerate(last):

        @pl.when(step == at)
        def _(index=index):
            spread.forward(index)

    @pl.when(step == last[-1])
    def _():
        spread.finish()


def attention_forward(q, kv, kv_sib, bias, gathered, dp, ctx, bq=256):
    rows = q.shape[0]
    pairs = q.shape[1] // 128
    S = jax.ShapeDtypeStruct
    blk = pl.BlockSpec((bq, 128), lambda p, j: (j, p))
    k_spec = pl.BlockSpec((rows, 128), lambda p, j: (0, p))
    v_spec = pl.BlockSpec((rows, 128), lambda p, j: (0, pairs + p))
    any_space = pl.BlockSpec(memory_space=pl.ANY)
    remotes = Spread.count(ctx // 2, 3)
    return pl.pallas_call(
        functools.partial(forward_kernel, dp, ctx),
        grid=(pairs, rows // bq),
        in_specs=[blk, k_spec, k_spec, v_spec, v_spec]
        + [pl.BlockSpec((2, rows, 128), lambda p, j: (0, 0, 0))]
        + [any_space] * 3,
        out_specs=[blk, blk, pl.BlockSpec((1, 8, bq), lambda p, j: (p, 0, j))] + [any_space] * 3,
        out_shape=[S(q.shape, BF), S(q.shape, F32), S((pairs, 8, rows), F32)]
        + [S((dp, ctx) + array.shape[1:], BF) for array in gathered],
        scratch_shapes=[
            pltpu.VMEM((2, 2 * rows, 128), BF),
            pltpu.SemaphoreType.DMA((3,)),
            pltpu.SemaphoreType.DMA((remotes,)),
            pltpu.SemaphoreType.DMA((remotes,)),
        ],
        compiler_params=pltpu.CompilerParams(
            vmem_limit_bytes=48 << 20, collective_id=1, has_side_effects=True
        ),
        cost_estimate=pl.CostEstimate(
            flops=16 * rows * rows * 128 * pairs,
            bytes_accessed=14 * rows * 768,
            transcendentals=4 * rows * rows * pairs,
        ),
        name="attend",
    )(q, kv, kv_sib, kv, kv_sib, bias, *gathered)


def forward_steps(pairs, steps):
    count = pairs * steps
    return (count * 5 // 24, count * 15 // 24, count - 1)


def backward_steps(pairs, steps):
    count = pairs * steps
    first = [count * at // 12 for at in (1, 1, 2)]
    middle = [count * at // 12 for at in (6, 7, 9)]
    return first, middle


def backward_kernel(dp, ctx, ck, *refs):
    (q_ref, do_ref, mix_ref, ko_ref, ks_ref, vo_ref, vs_ref, bias_ref, lse_ref), refs = (
        refs[:9],
        refs[9:],
    )
    sources, small, refs = refs[:3], refs[3], refs[4:]
    (dq_ref, dko_ref, dvo_ref, dks_ref, dvs_ref), refs = refs[:5], refs[5:]
    summed, small_out, refs = refs[:3], refs[3], refs[4:]
    (keys, dk, dv), refs = refs[:3], refs[3:]
    buffers, small_buffers, (local_sem, send_sem, recv_sem) = refs[:15], refs[15:21], refs[21:]
    scatter = Scatter(
        dp,
        ctx,
        sources,
        summed,
        [buffers[i * 5 : i * 5 + 5] for i in range(3)],
        small,
        small_out,
        small_buffers,
        Mover(local_sem, send_sem, recv_sem),
    )
    steps = pl.num_programs(1)
    j = pl.program_id(1)
    step = pl.program_id(0) * steps + j

    @pl.when(step == 0)
    def _():
        greet(scatter.devices)
        scatter.begin()

    @pl.when(j == 0)
    def _():
        load_keys(keys, ko_ref, ks_ref, bias_ref)
        dk[...] = jnp.zeros_like(dk)
        dv[...] = jnp.zeros_like(dv)

    half, bq = ko_ref.shape[0], q_ref.shape[0]
    q = q_ref[...] * jnp.asarray(0.125, BF)
    do = do_ref[...]
    prod = (do.astype(F32) * mix_ref[...]).T
    zero, one = jnp.zeros((), BF), jnp.ones((), BF)
    heads = []
    for h in range(2):
        inside, spare = head_lanes((bq, 128), h)
        heads.append(
            (
                jnp.where(inside, q, jnp.where(spare, one, zero)),
                jnp.where(inside, q, zero),
                jnp.where(inside, do, zero),
                lse_ref[0, h : h + 1, :],
                jnp.sum(prod[h * 64 : (h + 1) * 64], axis=0, keepdims=True),
            )
        )
    dq = jnp.zeros((bq, 128), F32)
    for first in range(0, 2 * half, ck):
        rows = slice(first, first + ck)
        v = vo_ref[rows, :] if first < half else vs_ref[first - half : first - half + ck, :]
        for h in range(2):
            qm, qz, dom, lse, delta = heads[h]
            k = keys[h, rows, :]
            p = jnp.exp(dg(k, qm, NT) - lse)
            ds = (p * (dg(v, dom, NT) - delta)).astype(BF)
            dv[rows, :] += dg(p.astype(BF), dom, NN)
            dk[rows, :] += dg(ds, qz, NN)
            dq = dq + dg(ds, k, TN)
    dq_ref[...] = (dq * 0.125).astype(BF)

    @pl.when(j == steps - 1)
    def _():
        dko_ref[...] = dk[:half, :]
        dvo_ref[...] = dv[:half, :]
        dks_ref[...] = dk[half:, :].astype(BF)
        dvs_ref[...] = dv[half:, :].astype(BF)

    first, middle_at = backward_steps(pl.num_programs(0), steps)

    @pl.when(step == first[0])
    def _():
        scatter.first_small()

    @pl.when(step == middle_at[0])
    def _():
        scatter.middle_small()

    for index in range(3):

        @pl.when(step == first[index])
        def _(index=index):
            scatter.first(index)

        @pl.when(step == middle_at[index])
        def _(index=index):
            scatter.middle(index)

    @pl.when(step == pl.num_programs(0) * steps - 1)
    def _():
        scatter.finish()


def attention_backward(
    q, do, mix, kv, kv_sib, bias, lse, sources, small, dp, ctx, bq=512, ck=512
):
    rows = q.shape[0]
    pairs = q.shape[1] // 128
    S = jax.ShapeDtypeStruct
    blk = pl.BlockSpec((bq, 128), lambda p, j: (j, p))
    full = pl.BlockSpec((rows, 128), lambda p, j: (0, p))
    v_spec = pl.BlockSpec((rows, 128), lambda p, j: (0, pairs + p))
    any_space = pl.BlockSpec(memory_space=pl.ANY)
    remotes = Scatter.count(dp, ctx, 3)
    whole = pl.BlockSpec(small.shape, lambda p, j: (0, 0))
    sums = [s.shape[3:] for s in sources]
    return pl.pallas_call(
        functools.partial(backward_kernel, dp, ctx, ck),
        grid=(pairs, rows // bq),
        in_specs=[blk, blk, blk, full, full, v_spec, v_spec]
        + [pl.BlockSpec((2, rows, 128), lambda p, j: (0, 0, 0))]
        + [pl.BlockSpec((1, 8, bq), lambda p, j: (p, 0, j))]
        + [any_space] * 3
        + [whole],
        out_specs=[blk, full, full, full, full]
        + [pl.BlockSpec(shape, lambda p, j: (0, 0)) for shape in sums]
        + [whole],
        out_shape=[
            S(q.shape, BF),
            S(q.shape, F32),
            S(q.shape, F32),
            S(q.shape, BF),
            S(q.shape, BF),
        ]
        + [S(shape, F32) for shape in sums]
        + [S(small.shape, F32)],
        scratch_shapes=[
            pltpu.VMEM((2, 2 * rows, 128), BF),
            pltpu.VMEM((2 * rows, 128), F32),
            pltpu.VMEM((2 * rows, 128), F32),
        ]
        + Scatter.scratch(dp, ctx, sources, small)
        + [
            pltpu.SemaphoreType.DMA((3,)),
            pltpu.SemaphoreType.DMA((remotes,)),
            pltpu.SemaphoreType.DMA((remotes,)),
        ],
        compiler_params=pltpu.CompilerParams(
            vmem_limit_bytes=56 << 20, collective_id=2, has_side_effects=True
        ),
        cost_estimate=pl.CostEstimate(
            flops=40 * rows * rows * 128 * pairs,
            bytes_accessed=26 * rows * 768,
            transcendentals=4 * rows * rows * pairs,
        ),
        name="attend_back",
    )(q, do, mix, kv, kv_sib, kv, kv_sib, bias, lse, *sources, small)


class Exchange:
    def __init__(self, ctx, mover, source, target, bringing):
        d, c = lax.axis_index("dp"), lax.axis_index("ctx")
        groups = ctx // 2
        self.steps = []
        for t in range(groups):
            group = (c // 2 + (groups - t if bringing else t)) % groups
            same, other = group * 2 + c % 2, group * 2 + 1 - c % 2
            if t == 0:
                self.own = mover.local(source.at[c], target.at[c])
                batch = []
            else:
                batch = [mover.remote(source.at[same], target.at[c], (d, same))]
            batch.append(mover.remote(source.at[other], target.at[c], (d, other)))
            self.steps.append(batch)

    @staticmethod
    def count(ctx):
        return ctx - 1

    def start(self, t):
        if t == 0:
            self.own.start()
        for copy in self.steps[t]:
            copy.start()

    def arrive(self, t):
        if t == 0:
            self.own.wait()
        for copy in self.steps[t]:
            copy.wait_recv()

    def sent(self):
        for batch in self.steps:
            for copy in batch:
                copy.wait_send()


def gelu_and_slope(x):
    t = 1.0 / (1.0 + 0.2316419 * jnp.abs(x))
    bell = 0.3989422804 * jnp.exp(-0.5 * x * x)
    poly = 1.330274429 * t - 1.821255978
    poly = poly * t + 1.781477937
    poly = poly * t - 0.356563782
    poly = poly * t + 0.319381530
    tail = bell * (poly * t)
    below = jnp.where(x < 0.0, tail, 1.0 - tail)
    return x * below, below + x * bell


def columns(values):
    return jnp.sum(values, axis=0, keepdims=True)


def middle_kernel(dp, ctx, *refs):
    (mb, xb, rest_src, up_src, vec, bias_up, wo_src, wu_src, wd_src), refs = refs[:9], refs[9:]
    (dm, grad_sum, out_to, go_to, gu_to, gd_to, small), refs = refs[:7], refs[7:]
    (wo, wu, wd, rest, upstream, result, active, dinner, slope, fb, db, da), refs = (
        refs[:12],
        refs[12:],
    )
    load_sem, local_sem, send_sem, recv_sem = refs
    groups = ctx // 2
    g = lax.axis_index("ctx") // 2
    half, width = result.shape[1:]
    tile = 2 * half
    chunks = range(wu.shape[1] // width)
    step = pl.program_id(0)
    mover = Mover(local_sem, send_sem, recv_sem)
    rest_in = Exchange(ctx, mover, rest_src, rest, True)
    up_in = Exchange(ctx, mover, up_src, upstream, True)
    give = Exchange(ctx, mover, result, out_to, False)
    loads = [
        pltpu.make_async_copy(source, target, load_sem.at[i])
        for i, (source, target) in enumerate(((wo_src, wo), (wu_src, wu), (wd_src, wd)))
    ]
    stores = [
        pltpu.make_async_copy(source, target, load_sem.at[i])
        for i, (source, target) in enumerate(((wo, go_to), (wu, gu_to), (wd, gd_to)))
    ]

    def load(index):
        @pl.when(step == 0)
        def _():
            loads[index].wait()

    @pl.when(step == 0)
    def _():
        for copy in loads:
            copy.start()
        d, c = lax.axis_index("dp"), lax.axis_index("ctx")
        greet([(d, (c + k) % ctx) for k in range(1, ctx)])
        for t in range(groups):
            rest_in.start(t)
            up_in.start(t)
        small[...] = jnp.zeros_like(small)

    @pl.when(step < groups)
    def _():
        block = (g + step) % groups
        rows = pl.ds(pl.multiple_of(block * tile, tile), tile)
        pair = pl.ds(block * 2, 2)
        load(0)
        hidden = dg(mb[rows, :], wo[...], NN) + vec[2:3, :] + xb[rows, :].astype(F32)
        for t in range(groups):

            @pl.when(step == t)
            def _(t=t):
                rest_in.arrive(t)

        hidden = hidden + rest[pair].reshape(tile, width).astype(F32)
        normed, standard_one, inverse_one = normalize(hidden, vec[6:7, :], vec[4:5, :])
        low = normed.astype(BF)
        fb[rows, :] = low
        load(1)
        for i in chunks:
            part = slice(i * width, (i + 1) * width)
            inner = dg(low, wu[:, part], NN) + bias_up[:, part]
            value, slope[:, part] = gelu_and_slope(inner)
            active[rows, part] = value.astype(BF)
        load(2)
        hidden = normed + dg(active[rows, :], wd[...], NN) + vec[3:4, :]
        out, standard, inverse = normalize(hidden, vec[7:8, :], vec[5:6, :])
        result[pair] = out.astype(BF).reshape(2, half, width)
        for t in range(groups):

            @pl.when(step == t)
            def _(t=t):
                give.start(t)
                up_in.arrive(t)

        error = upstream[pair].reshape(tile, width).astype(F32)
        grad = normalize_back(error, standard, inverse, vec[7:8, :])
        low_grad = grad.astype(BF)
        db[rows, :] = low_grad
        small[1:2, :] += columns(low_grad.astype(F32))
        small[3:4, :] += columns(error)
        small[5:6, :] += columns(error * standard)
        for i in chunks:
            part = slice(i * width, (i + 1) * width)
            change = dg(low_grad, wd[part, :], NT) * slope[:, part]
            change = change.astype(BF)
            dinner[rows, part] = change
            small[6 + i : 7 + i, :] += columns(change.astype(F32))
        grad = grad + dg(dinner[rows, :], wu[...], NT)
        small[2:3, :] += columns(grad)
        small[4:5, :] += columns(grad * standard_one)
        grad = normalize_back(grad, standard_one, inverse_one, vec[6:7, :])
        grad_sum[rows, :] = grad
        low_grad = grad.astype(BF)
        da[rows, :] = low_grad
        small[0:1, :] += columns(low_grad.astype(F32))
        dm[rows, :] = dg(low_grad, wo[...], NT).astype(BF)

    @pl.when(step == groups)
    def _():
        for i in chunks:
            part = slice(i * width, (i + 1) * width)
            wd[part, :] = dg(active[:, part], db[...], TN).astype(BF)
        stores[2].start()
        for i in chunks:
            part = slice(i * width, (i + 1) * width)
            wu[:, part] = dg(fb[...], dinner[:, part], TN).astype(BF)
        stores[1].start()
        wo[...] = dg(mb[...], da[...], TN).astype(BF)
        stores[0].start()
        for t in range(groups):
            give.arrive(t)
        for move in (rest_in, up_in, give):
            move.sent()
        for copy in stores:
            copy.wait()


def middle(mb, xb, rest, upstream, vec, bias_up, wo, wu, wd, dp, ctx):
    rows, width = mb.shape
    hidden = wu.shape[1]
    half = rows // ctx
    S = jax.ShapeDtypeStruct
    any_space = pl.BlockSpec(memory_space=pl.ANY)
    vmem = pl.BlockSpec(memory_space=pltpu.VMEM)
    remotes = 3 * Exchange.count(ctx)
    return pl.pallas_call(
        functools.partial(middle_kernel, dp, ctx),
        grid=(ctx // 2 + 1,),
        in_specs=[vmem, vmem, any_space, any_space, vmem, vmem] + [any_space] * 3,
        out_specs=[vmem, vmem] + [any_space] * 4 + [vmem],
        out_shape=[S(mb.shape, BF), S(mb.shape, F32), S(rest.shape, BF)]
        + [S(array.shape, BF) for array in (wo, wu, wd)]
        + [S((16, width), F32)],
        scratch_shapes=[pltpu.VMEM(array.shape, BF) for array in (wo, wu, wd)]
        + [pltpu.VMEM(rest.shape, BF)] * 3
        + [pltpu.VMEM((rows, hidden), BF)] * 2
        + [pltpu.VMEM((2 * half, hidden), F32)]
        + [pltpu.VMEM((rows, width), BF)] * 3
        + [
            pltpu.SemaphoreType.DMA((3,)),
            pltpu.SemaphoreType.DMA((3,)),
            pltpu.SemaphoreType.DMA((remotes,)),
            pltpu.SemaphoreType.DMA((remotes,)),
        ],
        compiler_params=pltpu.CompilerParams(
            vmem_limit_bytes=58 << 20, collective_id=4, has_side_effects=True
        ),
        cost_estimate=pl.CostEstimate(
            flops=2 * 3 * rows * width * (2 * hidden + width),
            bytes_accessed=50 << 20,
            transcendentals=rows * hidden,
        ),
        name="middle",
    )(mb, xb, rest, upstream, vec, bias_up, wo, wu, wd)


def normalize(hidden, scale_row, shift_row):
    centred = hidden - jnp.mean(hidden, axis=-1, keepdims=True)
    inverse = lax.rsqrt(jnp.mean(centred * centred, axis=-1, keepdims=True) + epsilon)
    standard = centred * inverse
    return (standard * scale_row + shift_row, standard, inverse)


def normalize_back(gradient, standard, inverse, scale_row):
    scaled = gradient * scale_row
    centred = scaled - jnp.mean(scaled, axis=-1, keepdims=True)
    return (centred - standard * jnp.mean(scaled * standard, axis=-1, keepdims=True)) * inverse


def on_device(
    tokens, cotangent, lengths, w_query, w_key, w_value, w_attn_out, w_up, b_up, w_down, vectors
):
    seqs, rows_dev, width = tokens.shape
    dp = lax.axis_size("dp")
    ctx = lax.axis_size("ctx")
    half = rows_dev // 2
    rows = half * ctx
    member = lax.axis_index("ctx") % 2
    own_seq = lax.axis_index("dp") * seqs + lax.axis_index("ctx") // 2
    length = lax.dynamic_index_in_dim(lengths, own_seq, 0, keepdims=False)
    pair_perm = [(i, i ^ 1) for i in range(ctx)]

    def by_owner(grad):
        return grad.reshape(dp, ctx // 2, 2, -1, grad.shape[1])

    split = tokens.reshape(ctx, half, width)
    held = w_query.shape[0]
    extra = jnp.concatenate([vectors.T, b_up.reshape(held, -1)], axis=1)
    extra = jnp.pad(extra, ((0, 0), (0, 128 - extra.shape[1])))
    low_in, full_first, *over_dp = gather_first(
        split.astype(BF),
        jnp.concatenate([w_query, w_key, w_value, extra], axis=1),
        w_attn_out,
        w_up,
        w_down,
        dp,
        ctx,
    )
    low_in = low_in.reshape(rows, width)
    full_first = full_first.reshape(width, -1)
    full_qkv = full_first[:, : 3 * width]
    vector_rows = full_first[:, 3 * width : 3 * width + 8].T.astype(F32)
    bias_columns = b_up.shape[0] // held
    full_bias_up = full_first[:, 3 * width + 8 : 3 * width + 8 + bias_columns].reshape(-1).astype(F32)
    left_out = (split - split.astype(BF).astype(F32)).astype(BF)

    slot = jnp.arange(rows, dtype=jnp.int32)
    source = slot // half
    high = (2 * ctx - 1 - source) * half + slot % half

    def key_bias(kind):
        position = jnp.where(kind == 0, slot, high)
        return jnp.where(position < length, 0.0, masked_score).astype(BF)

    bias = jnp.stack([key_bias(member), key_bias(1 - member)])
    bias = jnp.broadcast_to(bias[:, :, None], (2, rows, 128))

    row_of = jnp.concatenate([jnp.zeros_like(vector_rows[1]), vector_rows[1]])
    kv = (dg(low_in, full_qkv[:, width:], NN) + row_of).astype(BF)
    kv_sib = lax.ppermute(kv, "ctx", pair_perm)
    queries = (dg(low_in, full_qkv[:, :width], NN) + vector_rows[0]).astype(BF)
    low_mixed, mixed, lse, full_attn, full_up, full_down = attention_forward(
        queries, kv, kv_sib, bias, over_dp, dp, ctx
    )
    full_attn = full_attn.reshape(width, width)
    full_up = full_up.reshape(width, -1)
    full_down = full_down.reshape(-1, width)

    d_mixed, grad_sum, result, d_attn, d_up, d_down, small = middle(
        low_mixed,
        low_in,
        left_out,
        cotangent.reshape(ctx, half, width).astype(BF),
        vector_rows,
        full_bias_up.reshape(1, -1),
        full_attn,
        full_up,
        full_down,
        dp,
        ctx,
    )
    output = result.astype(F32).reshape(seqs, rows_dev, width)
    dq, dk_own, dv_own, dk_sib, dv_sib, own_attn, own_down, own_up, small = attention_backward(
        queries,
        d_mixed,
        mixed,
        kv,
        kv_sib,
        bias,
        lse,
        [by_owner(d_attn), by_owner(d_down), by_owner(d_up)],
        small,
        dp,
        ctx,
    )
    dk_got = lax.ppermute(dk_sib, "ctx", pair_perm)
    dv_got = lax.ppermute(dv_sib, "ctx", pair_perm)
    dk = (dk_own + dk_got.astype(F32)).astype(BF)
    dv = (dv_own + dv_got.astype(F32)).astype(BF)
    grad_in = grad_sum + (
        dg(dq, full_qkv[:, :width], NT)
        + dg(dk, full_qkv[:, width : 2 * width], NT)
        + dg(dv, full_qkv[:, 2 * width :], NT)
    )
    sums = jnp.stack([jnp.sum(dq.astype(F32), axis=0), jnp.sum(dv.astype(F32), axis=0)])
    joined = [dg(low_in, part, TN).astype(BF) for part in (dq, dk, dv)]
    own, sums, grad_tokens = finish_gradients(
        by_owner(jnp.concatenate(joined, axis=1)),
        jnp.pad(sums, ((0, 6), (0, 0))),
        grad_in.astype(BF).reshape(ctx, half, width),
        dp,
        ctx,
    )
    grad_tokens = grad_tokens.astype(F32).reshape(seqs, rows_dev, width)
    own_query, own_key, own_value = (own[:, i * width : (i + 1) * width] for i in range(3))
    index = lax.axis_index("dp") * ctx + lax.axis_index("ctx")
    own_vectors = lax.dynamic_slice_in_dim(
        jnp.concatenate([sums[:2], small[:6]]), index * held, held, 1
    )
    own_bias_up = lax.dynamic_slice_in_dim(
        small[6 : 6 + bias_columns].reshape(-1), index * b_up.shape[0], b_up.shape[0], 0
    )
    return (
        output,
        grad_tokens,
        own_query,
        own_key,
        own_value,
        own_attn,
        own_up,
        own_bias_up,
        own_down,
        own_vectors,
    )


def solution(mesh):
    in_specs = (
        P("dp", "ctx", None),
        P("dp", "ctx", None),
        P(),
        P(("dp", "ctx"), None),
        P(("dp", "ctx"), None),
        P(("dp", "ctx"), None),
        P(("dp", "ctx"), None),
        P(("dp", "ctx"), None),
        P(("dp", "ctx")),
        P(("dp", "ctx"), None),
        P(None, ("dp", "ctx")),
    )
    out_specs = (
        P("dp", "ctx", None),
        P("dp", "ctx", None),
        P(("dp", "ctx"), None),
        P(("dp", "ctx"), None),
        P(("dp", "ctx"), None),
        P(("dp", "ctx"), None),
        P(("dp", "ctx"), None),
        P(("dp", "ctx")),
        P(("dp", "ctx"), None),
        P(None, ("dp", "ctx")),
    )
    return jax.shard_map(
        on_device, mesh=mesh, in_specs=in_specs, out_specs=out_specs, check_vma=False
    )
```

```python
import functools
import jax
import jax.numpy as jnp
from jax import lax
from jax.experimental import pallas as pl
from jax.experimental.pallas import tpu as pltpu
from jax.sharding import PartitionSpec as P

HEAD_DIM = 64
F32 = jnp.float32
BF = jnp.bfloat16
NN = (((1,), (0,)), ((), ()))
NT = (((1,), (1,)), ((), ()))
TN = (((0,), (0,)), ((), ()))
epsilon = 1e-12
masked_score = -1e30


def dg(left, right, dims):
    return lax.dot_general(left, right, dims, preferred_element_type=F32)


MESH = pl.DeviceIdType.MESH


class Mover:
    def __init__(self, local_sem, send_sem, recv_sem):
        self.local_sem, self.send_sem, self.recv_sem = local_sem, send_sem, recv_sem
        self.locals = self.remotes = 0

    def local(self, source, target):
        copy = pltpu.make_async_copy(source, target, self.local_sem.at[self.locals])
        self.locals += 1
        return copy

    def remote(self, source, target, device):
        number = self.remotes
        self.remotes += 1
        return pltpu.make_async_remote_copy(
            src_ref=source,
            dst_ref=target,
            send_sem=self.send_sem.at[number],
            recv_sem=self.recv_sem.at[number],
            device_id=device,
            device_id_type=MESH,
        )


def greet(devices):
    barrier = pltpu.get_barrier_semaphore()
    for device in devices:
        pl.semaphore_signal(barrier, inc=1, device_id=device, device_id_type=MESH)
    pl.semaphore_wait(barrier, len(devices))


def place(dp, ctx):
    d, c = lax.axis_index("dp"), lax.axis_index("ctx")
    groups = ctx // 2
    g, m = c // 2, c % 2
    over_dp = [((d + k) % dp, c) for k in range(1, dp)]
    over_groups = [(d, (g + k) % groups * 2 + m) for k in range(1, groups)]
    return d, c, g, m, over_dp, over_groups, (d, g * 2 + 1 - m)


def gather_kernel(dp, ctx, x, w, wo, wu, wd, x_in, w_full, zo, zu, zd, local_sem, send_sem, recv_sem):
    d, c, g, m, over_dp, over_groups, sibling = place(dp, ctx)
    groups = ctx // 2
    greet(over_dp + [(d, (c + k) % ctx) for k in range(1, ctx)])
    mover = Mover(local_sem, send_sem, recv_sem)
    own = [
        mover.local(source, target)
        for source, target in (
            (w, w_full.at[d, c]),
            (x.at[c], x_in.at[c]),
            (wo, zo.at[d]),
            (wu, zu.at[d]),
            (wd, zd.at[d]),
        )
    ]
    along = [mover.remote(w, w_full.at[d, c], device) for device in over_dp]
    across = [[mover.remote(w, w_full.at[d, c], device) for device in over_groups]]
    rows = [
        mover.remote(x.at[(c + k) % ctx], x_in.at[c], (d, (c + k) % ctx)) for k in range(1, ctx)
    ]
    rest = [
        mover.remote(source, target.at[d], device)
        for source, target in ((wo, zo), (wu, zu), (wd, zd))
        for device in over_dp
    ]
    for copy in own + along + across[0] + rows + rest:
        copy.start()
    for k in range(1, dp):
        along[k - 1].wait_recv()
        piece = w_full.at[(d - k + dp) % dp, c]
        across.append([mover.remote(piece, piece, device) for device in over_groups])
        for copy in across[-1]:
            copy.start()
    own[0].wait()
    mine = w_full.at[:, c]
    over = [mover.remote(mine, mine, sibling)]
    over[0].start()
    for k in range(1, groups):
        for batch in across:
            batch[k - 1].wait_recv()
        block = w_full.at[:, (g - k + groups) % groups * 2 + m]
        over.append(mover.remote(block, block, sibling))
        over[-1].start()
    for copy in over + rows + rest:
        copy.wait()
    for copy in along + [copy for batch in across for copy in batch]:
        copy.wait_send()
    for copy in own[1:]:
        copy.wait()


def gather_first(x, w, wo, wu, wd, dp, ctx):
    groups = ctx // 2
    remotes = (dp - 1) + dp * (groups - 1) + (ctx - 1) + 3 * (dp - 1) + groups
    any_space = pl.BlockSpec(memory_space=pl.ANY)
    return pl.pallas_call(
        functools.partial(gather_kernel, dp, ctx),
        in_specs=[any_space] * 5,
        out_specs=[any_space] * 5,
        out_shape=[
            jax.ShapeDtypeStruct(x.shape, BF),
            jax.ShapeDtypeStruct((dp, ctx) + w.shape, BF),
        ]
        + [jax.ShapeDtypeStruct((dp,) + array.shape, BF) for array in (wo, wu, wd)],
        scratch_shapes=[
            pltpu.SemaphoreType.DMA((5,)),
            pltpu.SemaphoreType.DMA((remotes,)),
            pltpu.SemaphoreType.DMA((remotes,)),
        ],
        compiler_params=pltpu.CompilerParams(collective_id=0, has_side_effects=True),
        name="gather_first",
    )(x, w, wo, wu, wd)


class Spread:
    def __init__(self, dp, ctx, sources, targets, mover):
        d, c, g, m, over_dp, over_groups, sibling = place(dp, ctx)
        groups = ctx // 2
        self.devices = over_groups + [sibling]
        self.own = [mover.local(s, t.at[:, c]) for s, t in zip(sources, targets)]
        self.direct = [mover.remote(s, t.at[:, c], sibling) for s, t in zip(sources, targets)]
        self.across = [
            [mover.remote(s, t.at[:, c], device) for device in over_groups]
            for s, t in zip(sources, targets)
        ]
        self.onward = []
        for t in targets:
            blocks = [t.at[:, (g - k + groups) % groups * 2 + m] for k in range(1, groups)]
            self.onward.append([mover.remote(block, block, sibling) for block in blocks])

    @staticmethod
    def count(groups, arrays):
        return arrays * (1 + 2 * (groups - 1))

    def begin(self):
        greet(self.devices)
        for copy in self.own + [copy for batch in self.across for copy in batch] + self.direct:
            copy.start()

    def forward(self, index):
        for came, copy in zip(self.across[index], self.onward[index]):
            came.wait_recv()
            copy.start()

    def finish(self):
        for copy in self.own + self.direct + [copy for batch in self.onward for copy in batch]:
            copy.wait()
        for batch in self.across:
            for copy in batch:
                copy.wait_send()


class Scatter:
    def __init__(self, dp, ctx, sources, outs, buffers, small, small_out, small_buffers, mover):
        d, c, g, m, over_dp, over_groups, sibling = place(dp, ctx)
        groups = ctx // 2
        self.dp, self.groups, self.d, self.g = dp, groups, d, g
        self.devices = over_groups + over_dp + [sibling]
        self.outs = list(outs)
        self.buffers = buffers
        self.own, self.pair, self.across, self.along = [], [], [], []
        for source, (mine, other, came, sums, last) in zip(sources, buffers):
            summed = len(source.shape) == 4
            if summed:
                self.own.append(mover.local(source, mine))
                self.pair.append([])
            else:
                self.own.append(mover.local(source.at[:, :, m], mine))
                self.pair.append([mover.remote(source.at[:, :, 1 - m], other, sibling)])
            onward = source if summed else mine
            self.across.append(
                [
                    mover.remote(onward.at[:, (g + k) % groups], came.at[k - 1], over_groups[k - 1])
                    for k in range(1, groups)
                ]
            )
            self.along.append(
                [
                    mover.remote(sums.at[(d + k) % dp], last.at[k - 1], over_dp[k - 1])
                    for k in range(1, dp)
                ]
            )
        self.small, self.small_out = small, small_out
        one, came, two, groups_in, three, dp_in = small_buffers
        self.small_buffers = small_buffers
        self.pair.append([mover.remote(one, came, sibling)])
        self.across.append(
            [mover.remote(two, groups_in.at[k - 1], over_groups[k - 1]) for k in range(1, groups)]
        )
        self.along.append(
            [mover.remote(three, dp_in.at[k - 1], over_dp[k - 1]) for k in range(1, dp)]
        )

    @staticmethod
    def count(dp, ctx, arrays):
        return (arrays + 1) * (1 + ctx // 2 - 1 + dp - 1)

    @staticmethod
    def scratch(dp, ctx, sources, small):
        groups = ctx // 2
        shapes = []
        for s in sources:
            block = s.shape[-2:]
            shapes += [
                pltpu.VMEM((dp, groups) + block, BF),
                pltpu.VMEM((dp, groups) + block if len(s.shape) == 5 else (8, 128), BF),
                pltpu.VMEM((groups - 1, dp) + block, BF),
                pltpu.VMEM((dp,) + block, BF),
                pltpu.VMEM((dp - 1,) + block, BF),
            ]
        shape = small.shape
        shapes += [pltpu.VMEM(shape, F32)] * 3
        shapes += [
            pltpu.VMEM((groups - 1,) + shape, F32),
            pltpu.VMEM(shape, F32),
            pltpu.VMEM((dp - 1,) + shape, F32),
        ]
        return shapes

    def begin_small(self):
        self.small_buffers[0][...] = self.small[...]
        self.pair[-1][0].start()

    def begin(self, index):
        for copy in self.pair[index] or self.across[index]:
            copy.start()
        self.own[index].start()

    def first(self, index):
        mine, other = self.buffers[index][:2]
        groups = self.groups
        self.own[index].wait()
        if not self.pair[index]:
            return
        self.pair[index][0].wait_recv()

        def add(i, carry):
            at = (i // groups, i % groups)
            mine[at] = mine[at] + other[at]
            return carry

        lax.fori_loop(0, self.dp * groups, add, 0)
        for copy in self.across[index]:
            copy.start()

    def first_small(self):
        one, came, two = self.small_buffers[:3]
        self.pair[-1][0].wait_recv()
        two[...] = one[...] + came[...]
        for copy in self.across[-1]:
            copy.start()

    def middle(self, index):
        mine, _, came, sums, _ = self.buffers[index]
        for copy in self.across[index]:
            copy.wait_recv()

        def add(k, carry):
            total = mine[k, self.g].astype(F32)
            for j in range(self.groups - 1):
                total = total + came[j, k].astype(F32)
            sums[k] = total.astype(BF)
            return carry

        lax.fori_loop(0, self.dp, add, 0)
        for copy in self.along[index]:
            copy.start()

    def middle_small(self):
        _, _, two, groups_in, three, _ = self.small_buffers
        for copy in self.across[-1]:
            copy.wait_recv()
        total = two[...]
        for j in range(self.groups - 1):
            total = total + groups_in[j]
        three[...] = total
        for copy in self.along[-1]:
            copy.start()

    def finish(self):
        for index, out in enumerate(self.outs):
            sums, last = self.buffers[index][3:]
            for copy in self.along[index]:
                copy.wait_recv()
            total = sums[self.d].astype(F32)
            for j in range(self.dp - 1):
                total = total + last[j].astype(F32)
            out[...] = total
        three, dp_in = self.small_buffers[4:]
        for copy in self.along[-1]:
            copy.wait_recv()
        total = three[...]
        for j in range(self.dp - 1):
            total = total + dp_in[j]
        self.small_out[...] = total
        for batch in self.pair + self.across + self.along:
            for copy in batch:
                copy.wait_send()


class Exchange:
    def __init__(self, ctx, mover, source, target, bringing):
        d, c = lax.axis_index("dp"), lax.axis_index("ctx")
        groups = ctx // 2
        self.steps = []
        for t in range(groups):
            group = (c // 2 + (groups - t if bringing else t)) % groups
            same, other = group * 2 + c % 2, group * 2 + 1 - c % 2
            if t == 0:
                self.own = mover.local(source.at[c], target.at[c])
                batch = []
            else:
                batch = [mover.remote(source.at[same], target.at[c], (d, same))]
            batch.append(mover.remote(source.at[other], target.at[c], (d, other)))
            self.steps.append(batch)

    @staticmethod
    def count(ctx):
        return ctx - 1

    def start(self, t):
        if t == 0:
            self.own.start()
        for copy in self.steps[t]:
            copy.start()

    def arrive(self, t):
        if t == 0:
            self.own.wait()
        for copy in self.steps[t]:
            copy.wait_recv()

    def sent(self):
        for batch in self.steps:
            for copy in batch:
                copy.wait_send()


def columns(values):
    return jnp.sum(values, axis=0, keepdims=True)


def finish_kernel(dp, ctx, *refs):
    (xb, dq, dk, dv, w, grad_sum), refs = refs[:6], refs[6:]
    outs, small_out, x_out, refs = refs[:3], refs[3], refs[4], refs[5:]
    grads, result, small, refs = refs[:3], refs[3], refs[4], refs[5:]
    buffers, small_buffers, (local_sem, send_sem, recv_sem) = refs[:15], refs[15:21], refs[21:]
    d, c = lax.axis_index("dp"), lax.axis_index("ctx")
    groups = ctx // 2
    g = c // 2
    half, width = result.shape[1:]
    held = grads[0].shape[3]
    mover = Mover(local_sem, send_sem, recv_sem)
    scatter = Scatter(
        dp,
        ctx,
        grads,
        outs,
        [buffers[i * 5 : i * 5 + 5] for i in range(3)],
        small,
        small_out,
        small_buffers,
        mover,
    )
    give = Exchange(ctx, mover, result, x_out, False)
    greet([((d + k) % dp, c) for k in range(1, dp)] + [(d, (c + k) % ctx) for k in range(1, ctx)])
    small[...] = jnp.zeros_like(small)
    small[0:1, :] = columns(dq[...].astype(F32))
    small[1:2, :] = columns(dv[...].astype(F32))
    scatter.begin_small()

    across = xb[...].T

    def weight_gradient(index, rows_grad):
        total = dg(across, rows_grad[...], NN)
        for block in range(dp * ctx):
            at = (block // ctx, block % ctx // 2, block % 2)
            grads[index][at] = total[block * held : (block + 1) * held].astype(BF)
        scatter.begin(index)

    def row_tile(t):
        block = (g + t) % groups
        rows = pl.ds(pl.multiple_of(block * 2 * half, 2 * half), 2 * half)
        total = grad_sum[rows, :]
        for i, rows_grad in enumerate((dq, dk, dv)):
            total = total + dg(rows_grad[rows, :], w[:, i * width : (i + 1) * width], NT)
        result[pl.ds(block * 2, 2)] = total.astype(BF).reshape(2, half, width)
        give.start(t)

    for index, rows_grad in enumerate((dq, dk, dv)):
        weight_gradient(index, rows_grad)
    scatter.first_small()
    for t in range(groups):
        row_tile(t)
        if t < 3:
            scatter.first(t)
    scatter.middle_small()
    for index in range(3):
        scatter.middle(index)
    scatter.finish()
    for t in range(groups):
        give.arrive(t)
    give.sent()


def finish_gradients(xb, dq, dk, dv, w, grad_sum, dp, ctx):
    rows, width = xb.shape
    remotes = Scatter.count(dp, ctx, 3) + Exchange.count(ctx)
    S = jax.ShapeDtypeStruct
    vmem = pl.BlockSpec(memory_space=pltpu.VMEM)
    source = S((dp, ctx // 2, 2, width // (dp * ctx), width), BF)
    small = S((8, width), F32)
    moved = (ctx, rows // ctx, width)
    return pl.pallas_call(
        functools.partial(finish_kernel, dp, ctx),
        in_specs=[vmem] * 6,
        out_specs=[vmem] * 4 + [pl.BlockSpec(memory_space=pl.ANY)],
        out_shape=[S(source.shape[3:], F32)] * 3 + [small, S(moved, BF)],
        scratch_shapes=[pltpu.VMEM(source.shape, BF)] * 3
        + [pltpu.VMEM(moved, BF), pltpu.VMEM(small.shape, F32)]
        + Scatter.scratch(dp, ctx, [source] * 3, small)
        + [
            pltpu.SemaphoreType.DMA((4,)),
            pltpu.SemaphoreType.DMA((remotes,)),
            pltpu.SemaphoreType.DMA((remotes,)),
        ],
        compiler_params=pltpu.CompilerParams(
            collective_id=3, has_side_effects=True, vmem_limit_bytes=56 << 20
        ),
        name="finish_gradients",
    )(xb, dq, dk, dv, w, grad_sum)


def head_lanes(shape, h):
    lane = lax.broadcasted_iota(jnp.int32, shape, len(shape) - 1)
    return (lane >= 64) == (h == 1), lane == (64 if h == 0 else 0)


def load_keys(keys, own_ref, sib_ref, bias_ref):
    half = own_ref.shape[0]
    for h in range(2):
        for i, ref in enumerate((own_ref, sib_ref)):
            inside, spare = head_lanes((half, 128), h)
            rest = jnp.where(spare, bias_ref[i], jnp.zeros((), BF))
            keys[h, i * half : (i + 1) * half, :] = jnp.where(inside, ref[...], rest)


def forward_kernel(dp, ctx, *refs):
    (q_ref, ko_ref, ks_ref, vo_ref, vs_ref, bias_ref), refs = refs[:6], refs[6:]
    gathered, (mb_ref, mix_ref, lse_ref), spread_to, refs = refs[:3], refs[3:6], refs[6:9], refs[9:]
    keys, local_sem, send_sem, recv_sem = refs
    spread = Spread(dp, ctx, gathered, spread_to, Mover(local_sem, send_sem, recv_sem))
    steps = pl.num_programs(1)
    step = pl.program_id(0) * steps + pl.program_id(1)
    last = forward_steps(pl.num_programs(0), steps)

    @pl.when(step == 0)
    def _():
        spread.begin()

    @pl.when(pl.program_id(1) == 0)
    def _():
        load_keys(keys, ko_ref, ks_ref, bias_ref)

    half, bq = ko_ref.shape[0], q_ref.shape[0]
    q = q_ref[...] * jnp.asarray(0.125, BF)
    outs, lses = [], []
    for h in range(2):
        inside, spare = head_lanes((bq, 128), h)
        rest = jnp.where(spare, jnp.ones((), BF), jnp.zeros((), BF))
        scores = dg(jnp.where(inside, q, rest), keys[h], NT)
        top = jnp.max(scores, axis=1, keepdims=True)
        weights = jnp.exp(scores - top)
        total = jnp.sum(weights, axis=1, keepdims=True)
        low = weights.astype(BF)
        mixed = dg(low[:, :half], vo_ref[...], NN) + dg(low[:, half:], vs_ref[...], NN)
        outs.append(mixed / total)
        lses.append(top + jnp.log(total))
    lane = lax.broadcasted_iota(jnp.int32, (bq, 128), 1)
    mixed = jnp.where(lane < 64, outs[0], outs[1])
    mix_ref[...] = mixed
    mb_ref[...] = mixed.astype(BF)
    lse_ref[0] = jnp.where(lane == 0, lses[0], lses[1]).T[:8]

    for index, at in enumerate(last):

        @pl.when(step == at)
        def _(index=index):
            spread.forward(index)

    @pl.when(step == last[-1])
    def _():
        spread.finish()


def attention_forward(q, kv, kv_sib, bias, gathered, dp, ctx, bq=256):
    rows = q.shape[0]
    pairs = q.shape[1] // 128
    S = jax.ShapeDtypeStruct
    blk = pl.BlockSpec((bq, 128), lambda p, j: (j, p))
    k_spec = pl.BlockSpec((rows, 128), lambda p, j: (0, p))
    v_spec = pl.BlockSpec((rows, 128), lambda p, j: (0, pairs + p))
    any_space = pl.BlockSpec(memory_space=pl.ANY)
    remotes = Spread.count(ctx // 2, 3)
    return pl.pallas_call(
        functools.partial(forward_kernel, dp, ctx),
        grid=(pairs, rows // bq),
        in_specs=[blk, k_spec, k_spec, v_spec, v_spec]
        + [pl.BlockSpec((2, rows, 128), lambda p, j: (0, 0, 0))]
        + [any_space] * 3,
        out_specs=[blk, blk, pl.BlockSpec((1, 8, bq), lambda p, j: (p, 0, j))] + [any_space] * 3,
        out_shape=[S(q.shape, BF), S(q.shape, F32), S((pairs, 8, rows), F32)]
        + [S((dp, ctx) + array.shape[1:], BF) for array in gathered],
        scratch_shapes=[
            pltpu.VMEM((2, 2 * rows, 128), BF),
            pltpu.SemaphoreType.DMA((3,)),
            pltpu.SemaphoreType.DMA((remotes,)),
            pltpu.SemaphoreType.DMA((remotes,)),
        ],
        compiler_params=pltpu.CompilerParams(
            vmem_limit_bytes=48 << 20, collective_id=1, has_side_effects=True
        ),
        cost_estimate=pl.CostEstimate(
            flops=16 * rows * rows * 128 * pairs,
            bytes_accessed=14 * rows * 768,
            transcendentals=4 * rows * rows * pairs,
        ),
        name="attend",
    )(q, kv, kv_sib, kv, kv_sib, bias, *gathered)


def forward_steps(pairs, steps):
    count = pairs * steps
    return (count * 5 // 24, count * 15 // 24, count - 1)


def backward_steps(pairs, steps):
    count = pairs * steps
    first = [count * at // 12 for at in (0, 0, 1)]
    middle = [count * at // 12 for at in (5, 4, 8)]
    return first, middle


def backward_kernel(dp, ctx, ck, *refs):
    (q_ref, do_ref, mix_ref, ko_ref, ks_ref, vo_ref, vs_ref, bias_ref, lse_ref), refs = (
        refs[:9],
        refs[9:],
    )
    sources, small, refs = refs[:3], refs[3], refs[4:]
    (dq_ref, dk_ref, dv_ref), refs = refs[:3], refs[3:]
    summed, small_out, refs = refs[:3], refs[3], refs[4:]
    (keys, dk, dv, held, going, coming), refs = refs[:6], refs[6:]
    buffers, small_buffers, refs = refs[:15], refs[15:21], refs[21:]
    local_sem, send_sem, recv_sem, pair_send, pair_recv = refs
    scatter = Scatter(
        dp,
        ctx,
        sources,
        summed,
        [buffers[i * 5 : i * 5 + 5] for i in range(3)],
        small,
        small_out,
        small_buffers,
        Mover(local_sem, send_sem, recv_sem),
    )
    steps = pl.num_programs(1)
    j = pl.program_id(1)
    step = pl.program_id(0) * steps + j

    pair = pl.program_id(0)
    sibling = scatter.devices[-1]

    def to_sibling(number):
        return [
            pltpu.make_async_remote_copy(
                src_ref=going.at[number, i],
                dst_ref=coming.at[number, i],
                send_sem=pair_send.at[number * 2 + i],
                recv_sem=pair_recv.at[number * 2 + i],
                device_id=sibling,
                device_id_type=MESH,
            )
            for i in range(2)
        ]

    def settle(number):
        lanes = pl.ds(pl.multiple_of(number * 128, 128), 128)
        for i, (copy, out) in enumerate(zip(to_sibling(number), (dk_ref, dv_ref))):
            copy.wait_recv()
            total = held[number % 2, i] + coming[number, i].astype(F32)
            out[:, lanes] = total.astype(BF)

    @pl.when(step == 0)
    def _():
        greet(scatter.devices)
        scatter.begin(1)
        scatter.begin_small()
        scatter.begin(0)
        scatter.begin(2)

    @pl.when((j == 0) & (pair > 0))
    def _():
        settle(pair - 1)

    @pl.when(j == 0)
    def _():
        load_keys(keys, ko_ref, ks_ref, bias_ref)
        dk[...] = jnp.zeros_like(dk)
        dv[...] = jnp.zeros_like(dv)

    half, bq = ko_ref.shape[0], q_ref.shape[0]
    q = q_ref[...] * jnp.asarray(0.125, BF)
    do = do_ref[...]
    prod = (do.astype(F32) * mix_ref[...]).T
    zero, one = jnp.zeros((), BF), jnp.ones((), BF)
    heads = []
    for h in range(2):
        inside, spare = head_lanes((bq, 128), h)
        heads.append(
            (
                jnp.where(inside, q, jnp.where(spare, one, zero)),
                jnp.where(inside, q, zero),
                jnp.where(inside, do, zero),
                lse_ref[0, h : h + 1, :],
                jnp.sum(prod[h * 64 : (h + 1) * 64], axis=0, keepdims=True),
            )
        )
    dq = jnp.zeros((bq, 128), F32)
    for first in range(0, 2 * half, ck):
        rows = slice(first, first + ck)
        v = vo_ref[rows, :] if first < half else vs_ref[first - half : first - half + ck, :]
        for h in range(2):
            qm, qz, dom, lse, delta = heads[h]
            k = keys[h, rows, :]
            p = jnp.exp(dg(k, qm, NT) - lse)
            ds = (p * (dg(v, dom, NT) - delta)).astype(BF)
            dv[rows, :] += dg(p.astype(BF), dom, NN)
            dk[rows, :] += dg(ds, qz, NN)
            dq = dq + dg(ds, k, TN)
    dq_ref[...] = (dq * 0.125).astype(BF)

    @pl.when(j == steps - 1)
    def _():
        for i, total in enumerate((dk, dv)):
            held[pair % 2, i] = total[:half, :]
            going[pair, i] = total[half:, :].astype(BF)
        for copy in to_sibling(pair):
            copy.start()

    first, middle_at = backward_steps(pl.num_programs(0), steps)

    @pl.when(step == first[0])
    def _():
        scatter.first_small()

    @pl.when(step == middle_at[0])
    def _():
        scatter.middle_small()

    for index in range(3):

        @pl.when(step == first[index])
        def _(index=index):
            scatter.first(index)

        @pl.when(step == middle_at[index])
        def _(index=index):
            scatter.middle(index)

    @pl.when(step == pl.num_programs(0) * steps - 1)
    def _():
        scatter.finish()
        settle(pair)
        for number in range(pl.num_programs(0)):
            for copy in to_sibling(number):
                copy.wait_send()


def attention_backward(
    q, do, mix, kv, kv_sib, bias, lse, sources, small, dp, ctx, bq=512, ck=512
):
    rows = q.shape[0]
    pairs = q.shape[1] // 128
    S = jax.ShapeDtypeStruct
    blk = pl.BlockSpec((bq, 128), lambda p, j: (j, p))
    full = pl.BlockSpec((rows, 128), lambda p, j: (0, p))
    v_spec = pl.BlockSpec((rows, 128), lambda p, j: (0, pairs + p))
    any_space = pl.BlockSpec(memory_space=pl.ANY)
    remotes = Scatter.count(dp, ctx, 3)
    whole = pl.BlockSpec(small.shape, lambda p, j: (0, 0))
    sums = [s.shape[-2:] for s in sources]
    all_rows = pl.BlockSpec((rows, q.shape[1]), lambda p, j: (0, 0))
    return pl.pallas_call(
        functools.partial(backward_kernel, dp, ctx, ck),
        grid=(pairs, rows // bq),
        in_specs=[blk, blk, blk, full, full, v_spec, v_spec]
        + [pl.BlockSpec((2, rows, 128), lambda p, j: (0, 0, 0))]
        + [pl.BlockSpec((1, 8, bq), lambda p, j: (p, 0, j))]
        + [any_space] * 3
        + [whole],
        out_specs=[blk, all_rows, all_rows]
        + [pl.BlockSpec(shape, lambda p, j: (0, 0)) for shape in sums]
        + [whole],
        out_shape=[S(q.shape, BF)] * 3
        + [S(shape, F32) for shape in sums]
        + [S(small.shape, F32)],
        scratch_shapes=[
            pltpu.VMEM((2, 2 * rows, 128), BF),
            pltpu.VMEM((2 * rows, 128), F32),
            pltpu.VMEM((2 * rows, 128), F32),
            pltpu.VMEM((2, 2, rows, 128), F32),
            pltpu.VMEM((pairs, 2, rows, 128), BF),
            pltpu.VMEM((pairs, 2, rows, 128), BF),
        ]
        + Scatter.scratch(dp, ctx, sources, small)
        + [
            pltpu.SemaphoreType.DMA((3,)),
            pltpu.SemaphoreType.DMA((remotes,)),
            pltpu.SemaphoreType.DMA((remotes,)),
            pltpu.SemaphoreType.DMA((2 * pairs,)),
            pltpu.SemaphoreType.DMA((2 * pairs,)),
        ],
        compiler_params=pltpu.CompilerParams(
            vmem_limit_bytes=56 << 20, collective_id=2, has_side_effects=True
        ),
        cost_estimate=pl.CostEstimate(
            flops=40 * rows * rows * 128 * pairs,
            bytes_accessed=26 * rows * 768,
            transcendentals=4 * rows * rows * pairs,
        ),
        name="attend_back",
    )(q, do, mix, kv, kv_sib, kv, kv_sib, bias, lse, *sources, small)


def gelu_and_slope(x):
    t = 1.0 / (1.0 + 0.2316419 * jnp.abs(x))
    bell = 0.3989422804 * jnp.exp(-0.5 * x * x)
    poly = 1.330274429 * t - 1.821255978
    poly = poly * t + 1.781477937
    poly = poly * t - 0.356563782
    poly = poly * t + 0.319381530
    tail = bell * (poly * t)
    below = jnp.where(x < 0.0, tail, 1.0 - tail)
    return x * below, below + x * bell


def middle_kernel(dp, ctx, *refs):
    (mb, xb, rest_src, up_src, vec, bias_up, wo_src, wu_src, wd_src), refs = refs[:9], refs[9:]
    (dm, grad_sum, out_to, go_to, gu_to, gd_to, small), refs = refs[:7], refs[7:]
    (wo, wu, wd, rest, upstream, result, active, dinner, slope, fb, db, da), refs = (
        refs[:12],
        refs[12:],
    )
    (other, summed), refs = refs[:2], refs[2:]
    load_sem, local_sem, send_sem, recv_sem = refs
    groups = ctx // 2
    g = lax.axis_index("ctx") // 2
    half, width = result.shape[1:]
    tile = 2 * half
    chunks = range(wu.shape[1] // width)
    step = pl.program_id(0)
    mover = Mover(local_sem, send_sem, recv_sem)
    rest_in = Exchange(ctx, mover, rest_src, rest, True)
    up_in = Exchange(ctx, mover, up_src, upstream, True)
    give = Exchange(ctx, mover, result, out_to, False)
    loads = [
        pltpu.make_async_copy(source, target, load_sem.at[i])
        for i, (source, target) in enumerate(((wo_src, wo), (wu_src, wu), (wd_src, wd)))
    ]
    stores = [
        pltpu.make_async_copy(source, target, load_sem.at[i])
        for i, (source, target) in enumerate(((wo, go_to), (wu, gu_to), (summed, gd_to)))
    ]
    d, c = lax.axis_index("dp"), lax.axis_index("ctx")
    held = other.shape[2]

    def block_rows(i, k, member):
        return pl.ds(pl.multiple_of(((i * groups + k) * 2 + member) * held, 8), held)

    blocks = [(i, k) for i in range(dp) for k in range(groups)]
    to_sibling = [
        mover.remote(wd.at[block_rows(i, k, 1 - c % 2)], other.at[i, k], (d, g * 2 + 1 - c % 2))
        for i, k in blocks
    ]

    def load(index):
        @pl.when(step == 0)
        def _():
            loads[index].wait()

    @pl.when(step == 0)
    def _():
        for copy in loads:
            copy.start()
        greet([(d, (c + k) % ctx) for k in range(1, ctx)])
        for t in range(groups):
            rest_in.start(t)
            up_in.start(t)
        small[...] = jnp.zeros_like(small)

    @pl.when(step < groups)
    def _():
        block = (g + step) % groups
        rows = pl.ds(pl.multiple_of(block * tile, tile), tile)
        pair = pl.ds(block * 2, 2)
        load(0)
        hidden = dg(mb[rows, :], wo[...], NN) + vec[2:3, :] + xb[rows, :].astype(F32)
        for t in range(groups):

            @pl.when(step == t)
            def _(t=t):
                rest_in.arrive(t)

        hidden = hidden + rest[pair].reshape(tile, width).astype(F32)
        normed, standard_one, inverse_one = normalize(hidden, vec[6:7, :], vec[4:5, :])
        low = normed.astype(BF)
        fb[rows, :] = low
        load(1)
        for i in chunks:
            part = slice(i * width, (i + 1) * width)
            inner = dg(low, wu[:, part], NN) + bias_up[:, part]
            value, slope[:, part] = gelu_and_slope(inner)
            active[rows, part] = value.astype(BF)
        load(2)
        hidden = normed + dg(active[rows, :], wd[...], NN) + vec[3:4, :]
        out, standard, inverse = normalize(hidden, vec[7:8, :], vec[5:6, :])
        result[pair] = out.astype(BF).reshape(2, half, width)
        for t in range(groups):

            @pl.when(step == t)
            def _(t=t):
                give.start(t)
                up_in.arrive(t)

        error = upstream[pair].reshape(tile, width).astype(F32)
        grad = normalize_back(error, standard, inverse, vec[7:8, :])
        low_grad = grad.astype(BF)
        db[rows, :] = low_grad
        small[1:2, :] += columns(low_grad.astype(F32))
        small[3:4, :] += columns(error)
        small[5:6, :] += columns(error * standard)
        for i in chunks:
            part = slice(i * width, (i + 1) * width)
            change = dg(low_grad, wd[part, :], NT) * slope[:, part]
            change = change.astype(BF)
            dinner[rows, part] = change
            small[6 + i : 7 + i, :] += columns(change.astype(F32))
        grad = grad + dg(dinner[rows, :], wu[...], NT)
        small[2:3, :] += columns(grad)
        small[4:5, :] += columns(grad * standard_one)
        grad = normalize_back(grad, standard_one, inverse_one, vec[6:7, :])
        grad_sum[rows, :] = grad
        low_grad = grad.astype(BF)
        da[rows, :] = low_grad
        small[0:1, :] += columns(low_grad.astype(F32))
        dm[rows, :] = dg(low_grad, wo[...], NT).astype(BF)

    @pl.when(step == groups)
    def _():
        for i in chunks:
            part = slice(i * width, (i + 1) * width)
            wd[part, :] = dg(active[:, part], db[...], TN).astype(BF)
        for copy in to_sibling:
            copy.start()
        across = fb[...].T
        for i in chunks:
            part = slice(i * width, (i + 1) * width)
            wu[:, part] = dg(across, dinner[:, part], NN).astype(BF)
        stores[1].start()
        for copy in to_sibling:
            copy.wait()
        for i, k in blocks:
            summed[i, k] = wd[block_rows(i, k, c % 2), :] + other[i, k]
        stores[2].start()
        wo[...] = dg(mb[...], da[...], TN).astype(BF)
        stores[0].start()
        for t in range(groups):
            give.arrive(t)
        for move in (rest_in, up_in, give):
            move.sent()
        for copy in stores:
            copy.wait()


def middle(mb, xb, rest, upstream, vec, bias_up, wo, wu, wd, dp, ctx):
    rows, width = mb.shape
    hidden = wu.shape[1]
    half = rows // ctx
    S = jax.ShapeDtypeStruct
    any_space = pl.BlockSpec(memory_space=pl.ANY)
    vmem = pl.BlockSpec(memory_space=pltpu.VMEM)
    held = (dp, ctx // 2, hidden // (dp * ctx), width)
    remotes = 3 * Exchange.count(ctx) + dp * (ctx // 2)
    return pl.pallas_call(
        functools.partial(middle_kernel, dp, ctx),
        grid=(ctx // 2 + 1,),
        in_specs=[vmem, vmem, any_space, any_space, vmem, vmem] + [any_space] * 3,
        out_specs=[vmem, vmem] + [any_space] * 4 + [vmem],
        out_shape=[S(mb.shape, BF), S(mb.shape, F32), S(rest.shape, BF)]
        + [S(wo.shape, BF), S(wu.shape, BF), S(held, BF)]
        + [S((16, width), F32)],
        scratch_shapes=[pltpu.VMEM(array.shape, BF) for array in (wo, wu, wd)]
        + [pltpu.VMEM(rest.shape, BF)] * 3
        + [pltpu.VMEM((rows, hidden), BF)] * 2
        + [pltpu.VMEM((2 * half, hidden), F32)]
        + [pltpu.VMEM((rows, width), BF)] * 3
        + [pltpu.VMEM(held, BF)] * 2
        + [
            pltpu.SemaphoreType.DMA((3,)),
            pltpu.SemaphoreType.DMA((3,)),
            pltpu.SemaphoreType.DMA((remotes,)),
            pltpu.SemaphoreType.DMA((remotes,)),
        ],
        compiler_params=pltpu.CompilerParams(
            vmem_limit_bytes=58 << 20, collective_id=4, has_side_effects=True
        ),
        cost_estimate=pl.CostEstimate(
            flops=2 * 3 * rows * width * (2 * hidden + width),
            bytes_accessed=50 << 20,
            transcendentals=rows * hidden,
        ),
        name="middle",
    )(mb, xb, rest, upstream, vec, bias_up, wo, wu, wd)


def normalize(hidden, scale_row, shift_row):
    centred = hidden - jnp.mean(hidden, axis=-1, keepdims=True)
    inverse = lax.rsqrt(jnp.mean(centred * centred, axis=-1, keepdims=True) + epsilon)
    standard = centred * inverse
    return (standard * scale_row + shift_row, standard, inverse)


def normalize_back(gradient, standard, inverse, scale_row):
    scaled = gradient * scale_row
    centred = scaled - jnp.mean(scaled, axis=-1, keepdims=True)
    return (centred - standard * jnp.mean(scaled * standard, axis=-1, keepdims=True)) * inverse


def on_device(
    tokens, cotangent, lengths, w_query, w_key, w_value, w_attn_out, w_up, b_up, w_down, vectors
):
    seqs, rows_dev, width = tokens.shape
    dp = lax.axis_size("dp")
    ctx = lax.axis_size("ctx")
    half = rows_dev // 2
    rows = half * ctx
    member = lax.axis_index("ctx") % 2
    own_seq = lax.axis_index("dp") * seqs + lax.axis_index("ctx") // 2
    length = lax.dynamic_index_in_dim(lengths, own_seq, 0, keepdims=False)
    pair_perm = [(i, i ^ 1) for i in range(ctx)]

    def by_owner(grad):
        return grad.reshape(dp, ctx // 2, 2, -1, grad.shape[1])

    split = tokens.reshape(ctx, half, width)
    held = w_query.shape[0]
    extra = jnp.concatenate([vectors.T, b_up.reshape(held, -1)], axis=1)
    extra = jnp.pad(extra, ((0, 0), (0, 128 - extra.shape[1])))
    low_in, full_first, *over_dp = gather_first(
        split.astype(BF),
        jnp.concatenate([w_query, w_key, w_value, extra], axis=1),
        w_attn_out,
        w_up,
        w_down,
        dp,
        ctx,
    )
    low_in = low_in.reshape(rows, width)
    full_first = full_first.reshape(width, -1)
    full_qkv = full_first[:, : 3 * width]
    vector_rows = full_first[:, 3 * width : 3 * width + 8].T.astype(F32)
    bias_columns = b_up.shape[0] // held
    full_bias_up = full_first[:, 3 * width + 8 : 3 * width + 8 + bias_columns].reshape(-1).astype(F32)
    left_out = (split - split.astype(BF).astype(F32)).astype(BF)

    slot = jnp.arange(rows, dtype=jnp.int32)
    source = slot // half
    high = (2 * ctx - 1 - source) * half + slot % half

    def key_bias(kind):
        position = jnp.where(kind == 0, slot, high)
        return jnp.where(position < length, 0.0, masked_score).astype(BF)

    bias = jnp.stack([key_bias(member), key_bias(1 - member)])
    bias = jnp.broadcast_to(bias[:, :, None], (2, rows, 128))

    row_of = jnp.concatenate([jnp.zeros_like(vector_rows[1]), vector_rows[1]])
    kv = (dg(low_in, full_qkv[:, width:], NN) + row_of).astype(BF)
    kv_sib = lax.ppermute(kv, "ctx", pair_perm)
    queries = (dg(low_in, full_qkv[:, :width], NN) + vector_rows[0]).astype(BF)
    low_mixed, mixed, lse, full_attn, full_up, full_down = attention_forward(
        queries, kv, kv_sib, bias, over_dp, dp, ctx
    )
    full_attn = full_attn.reshape(width, width)
    full_up = full_up.reshape(width, -1)
    full_down = full_down.reshape(-1, width)

    d_mixed, grad_sum, result, d_attn, d_up, part_down, small = middle(
        low_mixed,
        low_in,
        left_out,
        cotangent.reshape(ctx, half, width).astype(BF),
        vector_rows,
        full_bias_up.reshape(1, -1),
        full_attn,
        full_up,
        full_down,
        dp,
        ctx,
    )
    output = result.astype(F32).reshape(seqs, rows_dev, width)
    dq, dk, dv, own_attn, own_down, own_up, small = attention_backward(
        queries,
        d_mixed,
        mixed,
        kv,
        kv_sib,
        bias,
        lse,
        [by_owner(d_attn), part_down, by_owner(d_up)],
        small,
        dp,
        ctx,
    )
    own_query, own_key, own_value, sums, grad_tokens = finish_gradients(
        low_in, dq, dk, dv, full_first, grad_sum, dp, ctx
    )
    grad_tokens = grad_tokens.astype(F32).reshape(seqs, rows_dev, width)
    index = lax.axis_index("dp") * ctx + lax.axis_index("ctx")
    own_vectors = lax.dynamic_slice_in_dim(
        jnp.concatenate([sums[:2], small[:6]]), index * held, held, 1
    )
    own_bias_up = lax.dynamic_slice_in_dim(
        small[6 : 6 + bias_columns].reshape(-1), index * b_up.shape[0], b_up.shape[0], 0
    )
    return (
        output,
        grad_tokens,
        own_query,
        own_key,
        own_value,
        own_attn,
        own_up,
        own_bias_up,
        own_down,
        own_vectors,
    )


def solution(mesh):
    in_specs = (
        P("dp", "ctx", None),
        P("dp", "ctx", None),
        P(),
        P(("dp", "ctx"), None),
        P(("dp", "ctx"), None),
        P(("dp", "ctx"), None),
        P(("dp", "ctx"), None),
        P(("dp", "ctx"), None),
        P(("dp", "ctx")),
        P(("dp", "ctx"), None),
        P(None, ("dp", "ctx")),
    )
    out_specs = (
        P("dp", "ctx", None),
        P("dp", "ctx", None),
        P(("dp", "ctx"), None),
        P(("dp", "ctx"), None),
        P(("dp", "ctx"), None),
        P(("dp", "ctx"), None),
        P(("dp", "ctx"), None),
        P(("dp", "ctx")),
        P(("dp", "ctx"), None),
        P(None, ("dp", "ctx")),
    )
    return jax.shard_map(
        on_device, mesh=mesh, in_specs=in_specs, out_specs=out_specs, check_vma=False
    )
```

```python
import functools
import jax
import jax.numpy as jnp
from jax import lax
from jax.experimental import pallas as pl
from jax.experimental.pallas import tpu as pltpu
from jax.sharding import PartitionSpec as P

HEAD_DIM = 64
F32 = jnp.float32
BF = jnp.bfloat16
NN = (((1,), (0,)), ((), ()))
NT = (((1,), (1,)), ((), ()))
TN = (((0,), (0,)), ((), ()))
epsilon = 1e-12
masked_score = -1e30


def dg(left, right, dims):
    return lax.dot_general(left, right, dims, preferred_element_type=F32)


MESH = pl.DeviceIdType.MESH


class Mover:
    def __init__(self, local_sem, send_sem, recv_sem):
        self.local_sem, self.send_sem, self.recv_sem = local_sem, send_sem, recv_sem
        self.locals = self.remotes = 0

    def local(self, source, target):
        copy = pltpu.make_async_copy(source, target, self.local_sem.at[self.locals])
        self.locals += 1
        return copy

    def remote(self, source, target, device):
        number = self.remotes
        self.remotes += 1
        return pltpu.make_async_remote_copy(
            src_ref=source,
            dst_ref=target,
            send_sem=self.send_sem.at[number],
            recv_sem=self.recv_sem.at[number],
            device_id=device,
            device_id_type=MESH,
        )


def greet(devices):
    barrier = pltpu.get_barrier_semaphore()
    for device in devices:
        pl.semaphore_signal(barrier, inc=1, device_id=device, device_id_type=MESH)
    pl.semaphore_wait(barrier, len(devices))


def place(dp, ctx):
    d, c = lax.axis_index("dp"), lax.axis_index("ctx")
    groups = ctx // 2
    g, m = c // 2, c % 2
    over_dp = [((d + k) % dp, c) for k in range(1, dp)]
    over_groups = [(d, (g + k) % groups * 2 + m) for k in range(1, groups)]
    return d, c, g, m, over_dp, over_groups, (d, g * 2 + 1 - m)


def flip(group, step, groups):
    total, bit = 0, 1
    while bit < groups:
        total = total + (group // bit + step // bit) % 2 * bit
        bit *= 2
    return total


def gather_kernel(dp, ctx, *refs):
    (tokens, cotangent, w, wo, wu, wd), refs = refs[:6], refs[6:]
    (x_in, rest_to, up_to, w_full, zo, zu, zd), refs = refs[:7], refs[7:]
    wide, wide_up, x, rest, up, local_sem, send_sem, recv_sem, move_sem = refs
    d, c, g, m, over_dp, over_groups, sibling = place(dp, ctx)
    groups = ctx // 2
    moves = [
        pltpu.make_async_copy(source, target, move_sem.at[i])
        for i, (source, target) in enumerate(
            ((tokens, wide), (cotangent, wide_up), (rest, rest_to), (up, up_to))
        )
    ]
    moves[0].start()
    greet(over_dp + [(d, (c + k) % ctx) for k in range(1, ctx)])
    mover = Mover(local_sem, send_sem, recv_sem)
    own = [
        mover.local(source, target)
        for source, target in (
            (w, w_full.at[d, c]),
            (x.at[c], x_in.at[c]),
            (wo, zo.at[d]),
            (wu, zu.at[d]),
            (wd, zd.at[d]),
        )
    ]
    along = [mover.remote(w, w_full.at[d, c], device) for device in over_dp]
    across = [[mover.remote(w, w_full.at[d, c], device) for device in over_groups]]
    rows = [
        mover.remote(x.at[(c + k) % ctx], x_in.at[c], (d, (c + k) % ctx)) for k in range(1, ctx)
    ]
    others = [
        mover.remote(source, target.at[d], device)
        for source, target in ((wo, zo), (wu, zu), (wd, zd))
        for device in over_dp
    ]
    for copy in along + across[0]:
        copy.start()
    moves[0].wait()
    moves[1].start()
    x[...] = wide[...].astype(BF)
    for copy in rows + own + others:
        copy.start()
    rest[...] = (wide[...] - x[...].astype(F32)).astype(BF)
    moves[2].start()
    moves[1].wait()
    up[...] = wide_up[...].astype(BF)
    moves[3].start()
    for k in range(1, dp):
        along[k - 1].wait_recv()
        piece = w_full.at[(d - k + dp) % dp, c]
        across.append([mover.remote(piece, piece, device) for device in over_groups])
        for copy in across[-1]:
            copy.start()
    own[0].wait()
    mine = w_full.at[:, c]
    over = [mover.remote(mine, mine, sibling)]
    over[0].start()
    for k in range(1, groups):
        for batch in across:
            batch[k - 1].wait_recv()
        block = w_full.at[:, (g - k + groups) % groups * 2 + m]
        over.append(mover.remote(block, block, sibling))
        over[-1].start()
    for copy in over + rows + others + moves[2:]:
        copy.wait()
    for copy in along + [copy for batch in across for copy in batch]:
        copy.wait_send()
    for copy in own[1:]:
        copy.wait()


def gather_first(tokens, cotangent, w, wo, wu, wd, dp, ctx):
    groups = ctx // 2
    remotes = (dp - 1) + dp * (groups - 1) + (ctx - 1) + 3 * (dp - 1) + groups
    any_space = pl.BlockSpec(memory_space=pl.ANY)
    return pl.pallas_call(
        functools.partial(gather_kernel, dp, ctx),
        in_specs=[any_space] * 6,
        out_specs=[any_space] * 7,
        out_shape=[jax.ShapeDtypeStruct(tokens.shape, BF)] * 3
        + [jax.ShapeDtypeStruct((dp, ctx) + w.shape, BF)]
        + [jax.ShapeDtypeStruct((dp,) + array.shape, BF) for array in (wo, wu, wd)],
        scratch_shapes=[pltpu.VMEM(tokens.shape, F32)] * 2
        + [pltpu.VMEM(tokens.shape, BF)] * 3
        + [
            pltpu.SemaphoreType.DMA((5,)),
            pltpu.SemaphoreType.DMA((remotes,)),
            pltpu.SemaphoreType.DMA((remotes,)),
            pltpu.SemaphoreType.DMA((4,)),
        ],
        compiler_params=pltpu.CompilerParams(
            collective_id=0, has_side_effects=True, vmem_limit_bytes=58 << 20
        ),
        name="gather_first",
    )(tokens, cotangent, w, wo, wu, wd)


class Spread:
    def __init__(self, dp, ctx, sources, targets, mover):
        d, c, g, m, over_dp, over_groups, sibling = place(dp, ctx)
        groups = ctx // 2
        self.devices = over_groups + [sibling]
        self.own = [mover.local(s, t.at[:, c]) for s, t in zip(sources, targets)]
        self.direct = [mover.remote(s, t.at[:, c], sibling) for s, t in zip(sources, targets)]
        self.across = [
            [mover.remote(s, t.at[:, c], device) for device in over_groups]
            for s, t in zip(sources, targets)
        ]
        self.onward = []
        for t in targets:
            blocks = [t.at[:, (g - k + groups) % groups * 2 + m] for k in range(1, groups)]
            self.onward.append([mover.remote(block, block, sibling) for block in blocks])

    @staticmethod
    def count(groups, arrays):
        return arrays * (1 + 2 * (groups - 1))

    def begin(self):
        greet(self.devices)
        for copy in self.own + [copy for batch in self.across for copy in batch] + self.direct:
            copy.start()

    def forward(self, index):
        for came, copy in zip(self.across[index], self.onward[index]):
            came.wait_recv()
            copy.start()

    def finish(self):
        for copy in self.own + self.direct + [copy for batch in self.onward for copy in batch]:
            copy.wait()
        for batch in self.across:
            for copy in batch:
                copy.wait_send()


class Scatter:
    def __init__(self, dp, ctx, sources, outs, buffers, small, small_out, small_buffers, mover):
        d, c, g, m, over_dp, over_groups, sibling = place(dp, ctx)
        groups = ctx // 2
        self.dp, self.groups, self.d, self.g = dp, groups, d, g
        self.devices = over_groups + over_dp + [sibling]
        self.outs = list(outs)
        self.buffers = buffers
        self.own, self.pair, self.across, self.along = [], [], [], []
        for source, (mine, other, came, sums, last) in zip(sources, buffers):
            summed = len(source.shape) == 4
            if summed:
                self.own.append(mover.local(source, mine))
                self.pair.append([])
            else:
                self.own.append(mover.local(source.at[:, :, m], mine))
                self.pair.append([mover.remote(source.at[:, :, 1 - m], other, sibling)])
            onward = source if summed else mine
            self.across.append(
                [
                    mover.remote(onward.at[:, (g + k) % groups], came.at[k - 1], over_groups[k - 1])
                    for k in range(1, groups)
                ]
            )
            self.along.append(
                [
                    mover.remote(sums.at[(d + k) % dp], last.at[k - 1], over_dp[k - 1])
                    for k in range(1, dp)
                ]
            )
        self.small, self.small_out = small, small_out
        one, came, two, groups_in, three, dp_in = small_buffers
        self.small_buffers = small_buffers
        self.pair.append([mover.remote(one, came, sibling)])
        self.across.append(
            [mover.remote(two, groups_in.at[k - 1], over_groups[k - 1]) for k in range(1, groups)]
        )
        self.along.append(
            [mover.remote(three, dp_in.at[k - 1], over_dp[k - 1]) for k in range(1, dp)]
        )

    @staticmethod
    def count(dp, ctx, arrays):
        return (arrays + 1) * (1 + ctx // 2 - 1 + dp - 1)

    @staticmethod
    def scratch(dp, ctx, sources, small):
        groups = ctx // 2
        shapes = []
        for s in sources:
            block = s.shape[-2:]
            shapes += [
                pltpu.VMEM((dp, groups) + block, BF),
                pltpu.VMEM((dp, groups) + block if len(s.shape) == 5 else (8, 128), BF),
                pltpu.VMEM((groups - 1, dp) + block, BF),
                pltpu.VMEM((dp,) + block, BF),
                pltpu.VMEM((dp - 1,) + block, BF),
            ]
        shape = small.shape
        shapes += [pltpu.VMEM(shape, F32)] * 3
        shapes += [
            pltpu.VMEM((groups - 1,) + shape, F32),
            pltpu.VMEM(shape, F32),
            pltpu.VMEM((dp - 1,) + shape, F32),
        ]
        return shapes

    def begin_small(self):
        self.small_buffers[0][...] = self.small[...]
        self.pair[-1][0].start()

    def begin(self, index):
        for copy in self.pair[index] or self.across[index]:
            copy.start()
        self.own[index].start()

    def first(self, index):
        mine, other = self.buffers[index][:2]
        groups = self.groups
        self.own[index].wait()
        if not self.pair[index]:
            return
        self.pair[index][0].wait_recv()

        def add(i, carry):
            at = (i // groups, i % groups)
            mine[at] = mine[at] + other[at]
            return carry

        lax.fori_loop(0, self.dp * groups, add, 0)
        for copy in self.across[index]:
            copy.start()

    def first_small(self):
        one, came, two = self.small_buffers[:3]
        self.pair[-1][0].wait_recv()
        two[...] = one[...] + came[...]
        for copy in self.across[-1]:
            copy.start()

    def middle(self, index):
        mine, _, came, sums, _ = self.buffers[index]
        for copy in self.across[index]:
            copy.wait_recv()

        def add(k, carry):
            total = mine[k, self.g].astype(F32)
            for j in range(self.groups - 1):
                total = total + came[j, k].astype(F32)
            sums[k] = total.astype(BF)
            return carry

        lax.fori_loop(0, self.dp, add, 0)
        for copy in self.along[index]:
            copy.start()

    def middle_small(self):
        _, _, two, groups_in, three, _ = self.small_buffers
        for copy in self.across[-1]:
            copy.wait_recv()
        total = two[...]
        for j in range(self.groups - 1):
            total = total + groups_in[j]
        three[...] = total
        for copy in self.along[-1]:
            copy.start()

    def finish(self):
        for index, out in enumerate(self.outs):
            sums, last = self.buffers[index][3:]
            for copy in self.along[index]:
                copy.wait_recv()
            total = sums[self.d].astype(F32)
            for j in range(self.dp - 1):
                total = total + last[j].astype(F32)
            out[...] = total
        three, dp_in = self.small_buffers[4:]
        for copy in self.along[-1]:
            copy.wait_recv()
        total = three[...]
        for j in range(self.dp - 1):
            total = total + dp_in[j]
        self.small_out[...] = total
        for batch in self.pair + self.across + self.along:
            for copy in batch:
                copy.wait_send()


class Exchange:
    def __init__(self, ctx, mover, source, target):
        d, c = lax.axis_index("dp"), lax.axis_index("ctx")
        groups = ctx // 2
        self.steps = []
        for t in range(groups):
            group = flip(c // 2, t, groups)
            same, other = group * 2 + c % 2, group * 2 + 1 - c % 2
            if t == 0:
                self.own = mover.local(source.at[c], target.at[c])
                batch = []
            else:
                batch = [mover.remote(source.at[same], target.at[c], (d, same))]
            batch.append(mover.remote(source.at[other], target.at[c], (d, other)))
            self.steps.append(batch)

    @staticmethod
    def count(ctx):
        return ctx - 1

    def start(self, t):
        if t == 0:
            self.own.start()
        for copy in self.steps[t]:
            copy.start()

    def arrive(self, t):
        if t == 0:
            self.own.wait()
        for copy in self.steps[t]:
            copy.wait_recv()

    def sent(self):
        for batch in self.steps:
            for copy in batch:
                copy.wait_send()


def columns(values):
    return jnp.sum(values, axis=0, keepdims=True)


def finish_kernel(dp, ctx, *refs):
    (xb, dq, dk, dv, w, grad_sum), refs = refs[:6], refs[6:]
    outs, small_out, x_out, refs = refs[:3], refs[3], refs[4], refs[5:]
    grads, result, small, refs = refs[:3], refs[3], refs[4], refs[5:]
    buffers, small_buffers, (local_sem, send_sem, recv_sem) = refs[:15], refs[15:21], refs[21:]
    d, c = lax.axis_index("dp"), lax.axis_index("ctx")
    groups = ctx // 2
    g = c // 2
    half, width = result.shape[1:]
    held = grads[0].shape[3]
    mover = Mover(local_sem, send_sem, recv_sem)
    scatter = Scatter(
        dp,
        ctx,
        grads,
        outs,
        [buffers[i * 5 : i * 5 + 5] for i in range(3)],
        small,
        small_out,
        small_buffers,
        mover,
    )
    give = Exchange(ctx, mover, result, x_out)
    greet([((d + k) % dp, c) for k in range(1, dp)] + [(d, (c + k) % ctx) for k in range(1, ctx)])
    small[...] = jnp.zeros_like(small)
    small[0:1, :] = columns(dq[...].astype(F32))
    small[1:2, :] = columns(dv[...].astype(F32))
    scatter.begin_small()

    across = xb[...].T

    def weight_gradient(index, rows_grad):
        total = dg(across, rows_grad[...], NN)
        for block in range(dp * ctx):
            at = (block // ctx, block % ctx // 2, block % 2)
            grads[index][at] = total[block * held : (block + 1) * held].astype(BF)
        scatter.begin(index)

    def row_tile(t):
        block = flip(g, t, groups)
        rows = pl.ds(pl.multiple_of(block * 2 * half, 2 * half), 2 * half)
        total = grad_sum[rows, :]
        for i, rows_grad in enumerate((dq, dk, dv)):
            total = total + dg(rows_grad[rows, :], w[:, i * width : (i + 1) * width], NT)
        result[pl.ds(block * 2, 2)] = total.astype(BF).reshape(2, half, width)
        give.start(t)

    tiles = list(range(groups - 1, -1, -1))
    for index, rows_grad in enumerate((dq, dk, dv)):
        weight_gradient(index, rows_grad)
        row_tile(tiles.pop(0))
        if index == 0:
            scatter.first_small()
        scatter.first(index)
    for t in tiles:
        row_tile(t)
    scatter.middle_small()
    for index in range(3):
        scatter.middle(index)
    scatter.finish()
    for t in range(groups):
        give.arrive(t)
    give.sent()


def finish_gradients(xb, dq, dk, dv, w, grad_sum, dp, ctx):
    rows, width = xb.shape
    remotes = Scatter.count(dp, ctx, 3) + Exchange.count(ctx)
    S = jax.ShapeDtypeStruct
    vmem = pl.BlockSpec(memory_space=pltpu.VMEM)
    source = S((dp, ctx // 2, 2, width // (dp * ctx), width), BF)
    small = S((8, width), F32)
    moved = (ctx, rows // ctx, width)
    return pl.pallas_call(
        functools.partial(finish_kernel, dp, ctx),
        in_specs=[vmem] * 6,
        out_specs=[vmem] * 4 + [pl.BlockSpec(memory_space=pl.ANY)],
        out_shape=[S(source.shape[3:], F32)] * 3 + [small, S(moved, BF)],
        scratch_shapes=[pltpu.VMEM(source.shape, BF)] * 3
        + [pltpu.VMEM(moved, BF), pltpu.VMEM(small.shape, F32)]
        + Scatter.scratch(dp, ctx, [source] * 3, small)
        + [
            pltpu.SemaphoreType.DMA((4,)),
            pltpu.SemaphoreType.DMA((remotes,)),
            pltpu.SemaphoreType.DMA((remotes,)),
        ],
        compiler_params=pltpu.CompilerParams(
            collective_id=3, has_side_effects=True, vmem_limit_bytes=56 << 20
        ),
        name="finish_gradients",
    )(xb, dq, dk, dv, w, grad_sum)


def head_lanes(shape, h):
    lane = lax.broadcasted_iota(jnp.int32, shape, len(shape) - 1)
    return (lane >= 64) == (h == 1), lane == (64 if h == 0 else 0)


def load_keys(keys, own_ref, sib_ref, bias_ref):
    half = own_ref.shape[0]
    for h in range(2):
        for i, ref in enumerate((own_ref, sib_ref)):
            inside, spare = head_lanes((half, 128), h)
            rest = jnp.where(spare, bias_ref[i], jnp.zeros((), BF))
            keys[h, i * half : (i + 1) * half, :] = jnp.where(inside, ref[...], rest)


def forward_kernel(dp, ctx, bq, *refs):
    (x_ref, w_ref, vec_ref, bias_ref), gathered, refs = refs[:4], refs[4:7], refs[7:]
    (mb_ref, mix_ref, lse_ref, own_to, sib_to), spread_to, refs = refs[:5], refs[5:8], refs[8:]
    keys, own, sib, local_sem, send_sem, recv_sem, pair_send, pair_recv, store_sem = refs
    spread = Spread(dp, ctx, gathered, spread_to, Mover(local_sem, send_sem, recv_sem))
    pairs, steps = pl.num_programs(0), pl.num_programs(1)
    pair, j = pl.program_id(0), pl.program_id(1)
    step = pair * steps + j
    last = forward_steps(pairs, steps)
    half, width = x_ref.shape

    def to_sibling(number):
        return pltpu.make_async_remote_copy(
            src_ref=own.at[number, pl.ds(1, 2)],
            dst_ref=sib.at[number],
            send_sem=pair_send.at[number],
            recv_sem=pair_recv.at[number],
            device_id=spread.devices[-1],
            device_id_type=MESH,
        )

    def stores(number):
        return [
            pltpu.make_async_copy(own.at[number], own_to.at[number], store_sem.at[number, 0]),
            pltpu.make_async_copy(sib.at[number], sib_to.at[number], store_sem.at[number, 1]),
        ]

    def project(number):
        lanes = [pl.ds(pl.multiple_of(number * 128 + i * width, 128), 128) for i in range(3)]
        weights = jnp.concatenate([w_ref[:, part] for part in lanes], axis=1)
        rows = dg(x_ref[...], weights, NN)
        own[number, 0] = (rows[:, :128] + vec_ref[0:1, lanes[0]]).astype(BF)
        own[number, 1] = rows[:, 128:256].astype(BF)
        own[number, 2] = (rows[:, 256:] + vec_ref[1:2, lanes[0]]).astype(BF)
        to_sibling(number).start()

    @pl.when(step == 0)
    def _():
        spread.begin()
        project(pair)

    @pl.when(j == 0)
    def _():
        to_sibling(pair).wait_recv()
        for copy in stores(pair):
            copy.start()
        load_keys(keys, own.at[pair, 1], sib.at[pair, 0], bias_ref)

    @pl.when((j == 1) & (pair < pairs - 1))
    def _():
        project(pair + 1)

    rows = pl.ds(pl.multiple_of(j * bq, bq), bq)
    q = own[pair, 0, rows, :] * jnp.asarray(0.125, BF)
    scores = []
    for h in range(2):
        inside, spare = head_lanes((bq, 128), h)
        rest = jnp.where(spare, jnp.ones((), BF), jnp.zeros((), BF))
        scores.append(dg(jnp.where(inside, q, rest), keys[h], NT))
    outs, lses = [], []
    for h in range(2):
        top = jnp.max(scores[h], axis=1, keepdims=True)
        weights = jnp.exp(scores[h] - top)
        total = jnp.sum(weights, axis=1, keepdims=True)
        low = weights.astype(BF)
        mixed = dg(low[:, :half], own[pair, 2], NN) + dg(low[:, half:], sib[pair, 1], NN)
        outs.append(mixed / total)
        lses.append(top + jnp.log(total))
    lane = lax.broadcasted_iota(jnp.int32, (bq, 128), 1)
    mixed = jnp.where(lane < 64, outs[0], outs[1])
    mix_ref[...] = mixed
    mb_ref[...] = mixed.astype(BF)
    lse_ref[0] = jnp.where(lane == 0, lses[0], lses[1]).T[:8]

    for index, at in enumerate(last):

        @pl.when(step == at)
        def _(index=index):
            spread.forward(index)

    @pl.when(step == last[-1])
    def _():
        spread.finish()
        for number in range(pairs):
            to_sibling(number).wait_send()
            for copy in stores(number):
                copy.wait()


def attention_forward(x, w, vec, bias, gathered, dp, ctx, bq=256):
    rows, width = x.shape
    pairs = width // 128
    S = jax.ShapeDtypeStruct
    blk = pl.BlockSpec((bq, 128), lambda p, j: (j, p))
    any_space = pl.BlockSpec(memory_space=pl.ANY)
    vmem = pl.BlockSpec(memory_space=pltpu.VMEM)
    remotes = Spread.count(ctx // 2, 3)
    return pl.pallas_call(
        functools.partial(forward_kernel, dp, ctx, bq),
        grid=(pairs, rows // bq),
        in_specs=[vmem] * 4 + [any_space] * 3,
        out_specs=[blk, blk, pl.BlockSpec((1, 8, bq), lambda p, j: (p, 0, j))] + [any_space] * 5,
        out_shape=[S(x.shape, BF), S(x.shape, F32), S((pairs, 8, rows), F32)]
        + [S((pairs, count, rows, 128), BF) for count in (3, 2)]
        + [S((dp, ctx) + array.shape[1:], BF) for array in gathered],
        scratch_shapes=[
            pltpu.VMEM((2, 2 * rows, 128), BF),
            pltpu.VMEM((pairs, 3, rows, 128), BF),
            pltpu.VMEM((pairs, 2, rows, 128), BF),
            pltpu.SemaphoreType.DMA((3,)),
            pltpu.SemaphoreType.DMA((remotes,)),
            pltpu.SemaphoreType.DMA((remotes,)),
            pltpu.SemaphoreType.DMA((pairs,)),
            pltpu.SemaphoreType.DMA((pairs,)),
            pltpu.SemaphoreType.DMA((pairs, 2)),
        ],
        compiler_params=pltpu.CompilerParams(
            vmem_limit_bytes=48 << 20, collective_id=1, has_side_effects=True
        ),
        cost_estimate=pl.CostEstimate(
            flops=16 * rows * rows * 128 * pairs,
            bytes_accessed=14 * rows * 768,
            transcendentals=4 * rows * rows * pairs,
        ),
        name="attend",
    )(x, w, vec, bias, *gathered)


def forward_steps(pairs, steps):
    count = pairs * steps
    return (count * 5 // 24, count * 15 // 24, count - 1)


def backward_steps(pairs, steps):
    count = pairs * steps
    first = [count * at // 12 for at in (0, 0, 1)]
    middle = [count * at // 12 for at in (5, 4, 8)]
    return first, middle


def backward_kernel(dp, ctx, ck, *refs):
    (q_ref, ko_ref, vo_ref, ks_ref, vs_ref, do_ref, mix_ref, bias_ref, lse_ref), refs = (
        refs[:9],
        refs[9:],
    )
    q_ref, ko_ref, vo_ref, ks_ref, vs_ref = (
        ref.at[0, 0] for ref in (q_ref, ko_ref, vo_ref, ks_ref, vs_ref)
    )
    sources, small, refs = refs[:3], refs[3], refs[4:]
    (dq_ref, dk_ref, dv_ref), refs = refs[:3], refs[3:]
    summed, small_out, refs = refs[:3], refs[3], refs[4:]
    (keys, dk, dv, held, going, coming), refs = refs[:6], refs[6:]
    buffers, small_buffers, refs = refs[:15], refs[15:21], refs[21:]
    local_sem, send_sem, recv_sem, pair_send, pair_recv = refs
    scatter = Scatter(
        dp,
        ctx,
        sources,
        summed,
        [buffers[i * 5 : i * 5 + 5] for i in range(3)],
        small,
        small_out,
        small_buffers,
        Mover(local_sem, send_sem, recv_sem),
    )
    steps = pl.num_programs(1)
    j = pl.program_id(1)
    step = pl.program_id(0) * steps + j

    pair = pl.program_id(0)
    sibling = scatter.devices[-1]

    def to_sibling(number):
        return [
            pltpu.make_async_remote_copy(
                src_ref=going.at[number, i],
                dst_ref=coming.at[number, i],
                send_sem=pair_send.at[number * 2 + i],
                recv_sem=pair_recv.at[number * 2 + i],
                device_id=sibling,
                device_id_type=MESH,
            )
            for i in range(2)
        ]

    def settle(number):
        lanes = pl.ds(pl.multiple_of(number * 128, 128), 128)
        for i, (copy, out) in enumerate(zip(to_sibling(number), (dk_ref, dv_ref))):
            copy.wait_recv()
            total = held[number % 2, i] + coming[number, i].astype(F32)
            out[:, lanes] = total.astype(BF)

    @pl.when(step == 0)
    def _():
        greet(scatter.devices)
        scatter.begin(1)
        scatter.begin_small()
        scatter.begin(0)
        scatter.begin(2)

    @pl.when((j == 0) & (pair > 0))
    def _():
        settle(pair - 1)

    @pl.when(j == 0)
    def _():
        load_keys(keys, ko_ref, ks_ref, bias_ref)
        dk[...] = jnp.zeros_like(dk)
        dv[...] = jnp.zeros_like(dv)

    half, bq = ko_ref.shape[0], q_ref.shape[0]
    q = q_ref[...] * jnp.asarray(0.125, BF)
    do = do_ref[...]
    prod = (do.astype(F32) * mix_ref[...]).T
    zero, one = jnp.zeros((), BF), jnp.ones((), BF)
    heads = []
    for h in range(2):
        inside, spare = head_lanes((bq, 128), h)
        heads.append(
            (
                jnp.where(inside, q, jnp.where(spare, one, zero)),
                jnp.where(inside, q, zero),
                jnp.where(inside, do, zero),
                lse_ref[0, h : h + 1, :],
                jnp.sum(prod[h * 64 : (h + 1) * 64], axis=0, keepdims=True),
            )
        )
    dq = jnp.zeros((bq, 128), F32)
    for first in range(0, 2 * half, ck):
        rows = slice(first, first + ck)
        v = vo_ref[rows, :] if first < half else vs_ref[first - half : first - half + ck, :]
        for h in range(2):
            qm, qz, dom, lse, delta = heads[h]
            k = keys[h, rows, :]
            p = jnp.exp(dg(k, qm, NT) - lse)
            ds = (p * (dg(v, dom, NT) - delta)).astype(BF)
            dv[rows, :] += dg(p.astype(BF), dom, NN)
            dk[rows, :] += dg(ds, qz, NN)
            dq = dq + dg(ds, k, TN)
    dq_ref[...] = (dq * 0.125).astype(BF)

    @pl.when(j == steps - 1)
    def _():
        for i, total in enumerate((dk, dv)):
            held[pair % 2, i] = total[:half, :]
            going[pair, i] = total[half:, :].astype(BF)
        for copy in to_sibling(pair):
            copy.start()

    first, middle_at = backward_steps(pl.num_programs(0), steps)

    @pl.when(step == first[0])
    def _():
        scatter.first_small()

    @pl.when(step == middle_at[0])
    def _():
        scatter.middle_small()

    for index in range(3):

        @pl.when(step == first[index])
        def _(index=index):
            scatter.first(index)

        @pl.when(step == middle_at[index])
        def _(index=index):
            scatter.middle(index)

    @pl.when(step == pl.num_programs(0) * steps - 1)
    def _():
        scatter.finish()
        settle(pair)
        for number in range(pl.num_programs(0)):
            for copy in to_sibling(number):
                copy.wait_send()


def attention_backward(own, sib, do, mix, bias, lse, sources, small, dp, ctx, bq=512, ck=512):
    rows, width = do.shape
    pairs = width // 128
    S = jax.ShapeDtypeStruct
    blk = pl.BlockSpec((bq, 128), lambda p, j: (j, p))
    whole_of = [
        pl.BlockSpec((1, 1, rows, 128), lambda p, j, i=i: (p, i, 0, 0)) for i in (1, 2, 0, 1)
    ]
    any_space = pl.BlockSpec(memory_space=pl.ANY)
    remotes = Scatter.count(dp, ctx, 3)
    whole = pl.BlockSpec(small.shape, lambda p, j: (0, 0))
    sums = [s.shape[-2:] for s in sources]
    all_rows = pl.BlockSpec((rows, width), lambda p, j: (0, 0))
    return pl.pallas_call(
        functools.partial(backward_kernel, dp, ctx, ck),
        grid=(pairs, rows // bq),
        in_specs=[pl.BlockSpec((1, 1, bq, 128), lambda p, j: (p, 0, j, 0))]
        + whole_of
        + [blk, blk]
        + [pl.BlockSpec((2, rows, 128), lambda p, j: (0, 0, 0))]
        + [pl.BlockSpec((1, 8, bq), lambda p, j: (p, 0, j))]
        + [any_space] * 3
        + [whole],
        out_specs=[blk, all_rows, all_rows]
        + [pl.BlockSpec(shape, lambda p, j: (0, 0)) for shape in sums]
        + [whole],
        out_shape=[S(do.shape, BF)] * 3
        + [S(shape, F32) for shape in sums]
        + [S(small.shape, F32)],
        scratch_shapes=[
            pltpu.VMEM((2, 2 * rows, 128), BF),
            pltpu.VMEM((2 * rows, 128), F32),
            pltpu.VMEM((2 * rows, 128), F32),
            pltpu.VMEM((2, 2, rows, 128), F32),
            pltpu.VMEM((pairs, 2, rows, 128), BF),
            pltpu.VMEM((pairs, 2, rows, 128), BF),
        ]
        + Scatter.scratch(dp, ctx, sources, small)
        + [
            pltpu.SemaphoreType.DMA((3,)),
            pltpu.SemaphoreType.DMA((remotes,)),
            pltpu.SemaphoreType.DMA((remotes,)),
            pltpu.SemaphoreType.DMA((2 * pairs,)),
            pltpu.SemaphoreType.DMA((2 * pairs,)),
        ],
        compiler_params=pltpu.CompilerParams(
            vmem_limit_bytes=56 << 20, collective_id=2, has_side_effects=True
        ),
        cost_estimate=pl.CostEstimate(
            flops=40 * rows * rows * 128 * pairs,
            bytes_accessed=26 * rows * 768,
            transcendentals=4 * rows * rows * pairs,
        ),
        name="attend_back",
    )(own, own, own, sib, sib, do, mix, bias, lse, *sources, small)


def gelu_and_slope(x):
    t = 1.0 / (1.0 + 0.2316419 * jnp.abs(x))
    bell = 0.3989422804 * jnp.exp(-0.5 * x * x)
    poly = 1.330274429 * t - 1.821255978
    poly = poly * t + 1.781477937
    poly = poly * t - 0.356563782
    poly = poly * t + 0.319381530
    tail = bell * (poly * t)
    below = jnp.where(x < 0.0, tail, 1.0 - tail)
    return x * below, below + x * bell


def middle_kernel(dp, ctx, *refs):
    (mb, xb, rest_src, up_src, vec, bias_up, wo_src, wu_src, wd_src), refs = refs[:9], refs[9:]
    (dm, grad_sum, out_to, go_to, gu_to, gd_to, small), refs = refs[:7], refs[7:]
    (wo, wu, wd, rest, upstream, result, active, dinner, slope, fb, db, da), refs = (
        refs[:12],
        refs[12:],
    )
    (other, summed), refs = refs[:2], refs[2:]
    load_sem, local_sem, send_sem, recv_sem = refs
    groups = ctx // 2
    g = lax.axis_index("ctx") // 2
    half, width = result.shape[1:]
    tile = 2 * half
    chunks = range(wu.shape[1] // width)
    step = pl.program_id(0)
    mover = Mover(local_sem, send_sem, recv_sem)
    rest_in = Exchange(ctx, mover, rest_src, rest)
    up_in = Exchange(ctx, mover, up_src, upstream)
    give = Exchange(ctx, mover, result, out_to)
    loads = [
        pltpu.make_async_copy(source, target, load_sem.at[i])
        for i, (source, target) in enumerate(((wo_src, wo), (wu_src, wu), (wd_src, wd)))
    ]
    stores = [
        pltpu.make_async_copy(source, target, load_sem.at[i])
        for i, (source, target) in enumerate(((wo, go_to), (wu, gu_to), (summed, gd_to)))
    ]
    d, c = lax.axis_index("dp"), lax.axis_index("ctx")
    held = other.shape[2]

    def block_rows(i, k, member):
        return pl.ds(pl.multiple_of(((i * groups + k) * 2 + member) * held, 8), held)

    blocks = [(i, k) for i in range(dp) for k in range(groups)]
    to_sibling = [
        mover.remote(wd.at[block_rows(i, k, 1 - c % 2)], other.at[i, k], (d, g * 2 + 1 - c % 2))
        for i, k in blocks
    ]

    def load(index):
        @pl.when(step == 0)
        def _():
            loads[index].wait()

    @pl.when(step == 0)
    def _():
        for copy in loads:
            copy.start()
        greet([(d, (c + k) % ctx) for k in range(1, ctx)])
        for t in range(groups):
            rest_in.start(t)
            up_in.start(t)
        small[...] = jnp.zeros_like(small)

    @pl.when(step < groups)
    def _():
        block = flip(g, step, groups)
        rows = pl.ds(pl.multiple_of(block * tile, tile), tile)
        pair = pl.ds(block * 2, 2)
        load(0)
        hidden = dg(mb[rows, :], wo[...], NN) + vec[2:3, :] + xb[rows, :].astype(F32)
        for t in range(groups):

            @pl.when(step == t)
            def _(t=t):
                rest_in.arrive(t)

        hidden = hidden + rest[pair].reshape(tile, width).astype(F32)
        normed, standard_one, inverse_one = normalize(hidden, vec[6:7, :], vec[4:5, :])
        low = normed.astype(BF)
        fb[rows, :] = low
        load(1)
        parts = [slice(i * width, (i + 1) * width) for i in chunks]
        inner = dg(low, wu[:, parts[0]], NN)
        for i, part in enumerate(parts):
            ahead = dg(low, wu[:, parts[i + 1]], NN) if i + 1 < len(parts) else None
            value, slope[:, part] = gelu_and_slope(inner + bias_up[:, part])
            active[rows, part] = value.astype(BF)
            inner = ahead
        load(2)
        hidden = normed + dg(active[rows, :], wd[...], NN) + vec[3:4, :]
        out, standard, inverse = normalize(hidden, vec[7:8, :], vec[5:6, :])
        result[pair] = out.astype(BF).reshape(2, half, width)
        for t in range(groups):

            @pl.when(step == t)
            def _(t=t):
                give.start(t)
                up_in.arrive(t)

        error = upstream[pair].reshape(tile, width).astype(F32)
        grad = normalize_back(error, standard, inverse, vec[7:8, :])
        low_grad = grad.astype(BF)
        db[rows, :] = low_grad
        small[1:2, :] += columns(low_grad.astype(F32))
        small[3:4, :] += columns(error)
        small[5:6, :] += columns(error * standard)
        for i in chunks:
            part = slice(i * width, (i + 1) * width)
            change = dg(low_grad, wd[part, :], NT) * slope[:, part]
            change = change.astype(BF)
            dinner[rows, part] = change
            small[6 + i : 7 + i, :] += columns(change.astype(F32))
        grad = grad + dg(dinner[rows, :], wu[...], NT)
        small[2:3, :] += columns(grad)
        small[4:5, :] += columns(grad * standard_one)
        grad = normalize_back(grad, standard_one, inverse_one, vec[6:7, :])
        grad_sum[rows, :] = grad
        low_grad = grad.astype(BF)
        da[rows, :] = low_grad
        small[0:1, :] += columns(low_grad.astype(F32))
        dm[rows, :] = dg(low_grad, wo[...], NT).astype(BF)

    @pl.when(step == groups)
    def _():
        for i in chunks:
            part = slice(i * width, (i + 1) * width)
            wd[part, :] = dg(active[:, part], db[...], TN).astype(BF)
        for copy in to_sibling:
            copy.start()
        across = fb[...].T
        for i in chunks:
            part = slice(i * width, (i + 1) * width)
            wu[:, part] = dg(across, dinner[:, part], NN).astype(BF)
        stores[1].start()
        for copy in to_sibling:
            copy.wait()
        for i, k in blocks:
            summed[i, k] = wd[block_rows(i, k, c % 2), :] + other[i, k]
        stores[2].start()
        wo[...] = dg(mb[...], da[...], TN).astype(BF)
        stores[0].start()
        for t in range(groups):
            give.arrive(t)
        for move in (rest_in, up_in, give):
            move.sent()
        for copy in stores:
            copy.wait()


def middle(mb, xb, rest, upstream, vec, bias_up, wo, wu, wd, dp, ctx):
    rows, width = mb.shape
    hidden = wu.shape[1]
    half = rows // ctx
    S = jax.ShapeDtypeStruct
    any_space = pl.BlockSpec(memory_space=pl.ANY)
    vmem = pl.BlockSpec(memory_space=pltpu.VMEM)
    held = (dp, ctx // 2, hidden // (dp * ctx), width)
    remotes = 3 * Exchange.count(ctx) + dp * (ctx // 2)
    return pl.pallas_call(
        functools.partial(middle_kernel, dp, ctx),
        grid=(ctx // 2 + 1,),
        in_specs=[vmem, vmem, any_space, any_space, vmem, vmem] + [any_space] * 3,
        out_specs=[vmem, vmem] + [any_space] * 4 + [vmem],
        out_shape=[S(mb.shape, BF), S(mb.shape, F32), S(rest.shape, BF)]
        + [S(wo.shape, BF), S(wu.shape, BF), S(held, BF)]
        + [S((16, width), F32)],
        scratch_shapes=[pltpu.VMEM(array.shape, BF) for array in (wo, wu, wd)]
        + [pltpu.VMEM(rest.shape, BF)] * 3
        + [pltpu.VMEM((rows, hidden), BF)] * 2
        + [pltpu.VMEM((2 * half, hidden), F32)]
        + [pltpu.VMEM((rows, width), BF)] * 3
        + [pltpu.VMEM(held, BF)] * 2
        + [
            pltpu.SemaphoreType.DMA((3,)),
            pltpu.SemaphoreType.DMA((3,)),
            pltpu.SemaphoreType.DMA((remotes,)),
            pltpu.SemaphoreType.DMA((remotes,)),
        ],
        compiler_params=pltpu.CompilerParams(
            vmem_limit_bytes=58 << 20, collective_id=4, has_side_effects=True
        ),
        cost_estimate=pl.CostEstimate(
            flops=2 * 3 * rows * width * (2 * hidden + width),
            bytes_accessed=50 << 20,
            transcendentals=rows * hidden,
        ),
        name="middle",
    )(mb, xb, rest, upstream, vec, bias_up, wo, wu, wd)


def normalize(hidden, scale_row, shift_row):
    centred = hidden - jnp.mean(hidden, axis=-1, keepdims=True)
    inverse = lax.rsqrt(jnp.mean(centred * centred, axis=-1, keepdims=True) + epsilon)
    standard = centred * inverse
    return (standard * scale_row + shift_row, standard, inverse)


def normalize_back(gradient, standard, inverse, scale_row):
    scaled = gradient * scale_row
    centred = scaled - jnp.mean(scaled, axis=-1, keepdims=True)
    return (centred - standard * jnp.mean(scaled * standard, axis=-1, keepdims=True)) * inverse


def on_device(
    tokens, cotangent, lengths, w_query, w_key, w_value, w_attn_out, w_up, b_up, w_down, vectors
):
    seqs, rows_dev, width = tokens.shape
    dp = lax.axis_size("dp")
    ctx = lax.axis_size("ctx")
    half = rows_dev // 2
    rows = half * ctx
    member = lax.axis_index("ctx") % 2
    own_seq = lax.axis_index("dp") * seqs + lax.axis_index("ctx") // 2
    length = lax.dynamic_index_in_dim(lengths, own_seq, 0, keepdims=False)
    def by_owner(grad):
        return grad.reshape(dp, ctx // 2, 2, -1, grad.shape[1])

    split = tokens.reshape(ctx, half, width)
    held = w_query.shape[0]
    extra = jnp.concatenate([vectors.T, b_up.reshape(held, -1)], axis=1)
    extra = jnp.pad(extra, ((0, 0), (0, 128 - extra.shape[1])))
    low_in, left_out, upstream, full_first, *over_dp = gather_first(
        split,
        cotangent.reshape(ctx, half, width),
        jnp.concatenate([w_query, w_key, w_value, extra], axis=1),
        w_attn_out,
        w_up,
        w_down,
        dp,
        ctx,
    )
    low_in = low_in.reshape(rows, width)
    full_first = full_first.reshape(width, -1)
    vector_rows = full_first[:, 3 * width : 3 * width + 8].T.astype(F32)
    bias_columns = b_up.shape[0] // held
    full_bias_up = full_first[:, 3 * width + 8 : 3 * width + 8 + bias_columns].reshape(-1).astype(F32)
    slot = jnp.arange(rows, dtype=jnp.int32)
    source = slot // half
    high = (2 * ctx - 1 - source) * half + slot % half

    def key_bias(kind):
        position = jnp.where(kind == 0, slot, high)
        return jnp.where(position < length, 0.0, masked_score).astype(BF)

    bias = jnp.stack([key_bias(member), key_bias(1 - member)])
    bias = jnp.broadcast_to(bias[:, :, None], (2, rows, 128))

    low_mixed, mixed, lse, own, sib, full_attn, full_up, full_down = attention_forward(
        low_in, full_first, vector_rows, bias, over_dp, dp, ctx
    )
    full_attn = full_attn.reshape(width, width)
    full_up = full_up.reshape(width, -1)
    full_down = full_down.reshape(-1, width)

    d_mixed, grad_sum, result, d_attn, d_up, part_down, small = middle(
        low_mixed,
        low_in,
        left_out,
        upstream,
        vector_rows,
        full_bias_up.reshape(1, -1),
        full_attn,
        full_up,
        full_down,
        dp,
        ctx,
    )
    output = result.astype(F32).reshape(seqs, rows_dev, width)
    dq, dk, dv, own_attn, own_down, own_up, small = attention_backward(
        own,
        sib,
        d_mixed,
        mixed,
        bias,
        lse,
        [by_owner(d_attn), part_down, by_owner(d_up)],
        small,
        dp,
        ctx,
    )
    own_query, own_key, own_value, sums, grad_tokens = finish_gradients(
        low_in, dq, dk, dv, full_first, grad_sum, dp, ctx
    )
    grad_tokens = grad_tokens.astype(F32).reshape(seqs, rows_dev, width)
    index = lax.axis_index("dp") * ctx + lax.axis_index("ctx")
    own_vectors = lax.dynamic_slice_in_dim(
        jnp.concatenate([sums[:2], small[:6]]), index * held, held, 1
    )
    own_bias_up = lax.dynamic_slice_in_dim(
        small[6 : 6 + bias_columns].reshape(-1), index * b_up.shape[0], b_up.shape[0], 0
    )
    return (
        output,
        grad_tokens,
        own_query,
        own_key,
        own_value,
        own_attn,
        own_up,
        own_bias_up,
        own_down,
        own_vectors,
    )


def solution(mesh):
    in_specs = (
        P("dp", "ctx", None),
        P("dp", "ctx", None),
        P(),
        P(("dp", "ctx"), None),
        P(("dp", "ctx"), None),
        P(("dp", "ctx"), None),
        P(("dp", "ctx"), None),
        P(("dp", "ctx"), None),
        P(("dp", "ctx")),
        P(("dp", "ctx"), None),
        P(None, ("dp", "ctx")),
    )
    out_specs = (
        P("dp", "ctx", None),
        P("dp", "ctx", None),
        P(("dp", "ctx"), None),
        P(("dp", "ctx"), None),
        P(("dp", "ctx"), None),
        P(("dp", "ctx"), None),
        P(("dp", "ctx"), None),
        P(("dp", "ctx")),
        P(("dp", "ctx"), None),
        P(None, ("dp", "ctx")),
    )
    return jax.shard_map(
        on_device, mesh=mesh, in_specs=in_specs, out_specs=out_specs, check_vma=False
    )
```

```python
import functools
import jax
import jax.numpy as jnp
from jax import lax
from jax.experimental import pallas as pl
from jax.experimental.pallas import tpu as pltpu
from jax.sharding import PartitionSpec as P

HEAD_DIM = 64
F32 = jnp.float32
BF = jnp.bfloat16
NN = (((1,), (0,)), ((), ()))
NT = (((1,), (1,)), ((), ()))
TN = (((0,), (0,)), ((), ()))
epsilon = 1e-12
masked_score = -1e30
VMEM_BYTES = 58 << 20


def dg(left, right, dims):
    return lax.dot_general(left, right, dims, preferred_element_type=F32)


MESH = pl.DeviceIdType.MESH


class Mover:
    def __init__(self, local_sem, send_sem, recv_sem):
        self.local_sem, self.send_sem, self.recv_sem = local_sem, send_sem, recv_sem
        self.locals = self.remotes = 0

    def local(self, source, target):
        copy = pltpu.make_async_copy(source, target, self.local_sem.at[self.locals])
        self.locals += 1
        return copy

    def remote(self, source, target, device):
        number = self.remotes
        self.remotes += 1
        return pltpu.make_async_remote_copy(
            src_ref=source,
            dst_ref=target,
            send_sem=self.send_sem.at[number],
            recv_sem=self.recv_sem.at[number],
            device_id=device,
            device_id_type=MESH,
        )


def greet(devices):
    barrier = pltpu.get_barrier_semaphore()
    for device in devices:
        pl.semaphore_signal(barrier, inc=1, device_id=device, device_id_type=MESH)
    pl.semaphore_wait(barrier, len(devices))


def place(dp, ctx):
    d, c = lax.axis_index("dp"), lax.axis_index("ctx")
    groups = ctx // 2
    g, m = c // 2, c % 2
    over_dp = [((d + k) % dp, c) for k in range(1, dp)]
    over_groups = [(d, (g + k) % groups * 2 + m) for k in range(1, groups)]
    return d, c, g, m, over_dp, over_groups, (d, g * 2 + 1 - m)


def flip(group, step, groups):
    total, bit = 0, 1
    while bit < groups:
        total = total + (group // bit + step // bit) % 2 * bit
        bit *= 2
    return total


def gather_kernel(dp, ctx, *refs):
    (tokens, cotangent, w, wo, wu, wd), refs = refs[:6], refs[6:]
    (x_in, rest_to, up_to, w_full, zo, zu, zd), refs = refs[:7], refs[7:]
    wide, wide_up, x, rest, up, local_sem, send_sem, recv_sem, move_sem = refs
    d, c, g, m, over_dp, over_groups, sibling = place(dp, ctx)
    groups = ctx // 2
    moves = [
        pltpu.make_async_copy(source, target, move_sem.at[i])
        for i, (source, target) in enumerate(
            ((tokens, wide), (cotangent, wide_up), (rest, rest_to), (up, up_to))
        )
    ]
    moves[0].start()
    greet(over_dp + [(d, (c + k) % ctx) for k in range(1, ctx)])
    mover = Mover(local_sem, send_sem, recv_sem)
    own = [
        mover.local(source, target)
        for source, target in (
            (w, w_full.at[d, c]),
            (x.at[c], x_in.at[c]),
            (wo, zo.at[d]),
            (wu, zu.at[d]),
            (wd, zd.at[d]),
        )
    ]
    along = [mover.remote(w, w_full.at[d, c], device) for device in over_dp]
    across = [[mover.remote(w, w_full.at[d, c], device) for device in over_groups]]
    rows = [
        mover.remote(x.at[(c + k) % ctx], x_in.at[c], (d, (c + k) % ctx)) for k in range(1, ctx)
    ]
    others = [
        mover.remote(source, target.at[d], device)
        for source, target in ((wo, zo), (wu, zu), (wd, zd))
        for device in over_dp
    ]
    for copy in along + across[0]:
        copy.start()
    moves[0].wait()
    moves[1].start()
    x[...] = wide[...].astype(BF)
    for copy in rows + own + others:
        copy.start()
    rest[...] = (wide[...] - x[...].astype(F32)).astype(BF)
    moves[2].start()
    moves[1].wait()
    up[...] = wide_up[...].astype(BF)
    moves[3].start()
    for k in range(1, dp):
        along[k - 1].wait_recv()
        piece = w_full.at[(d - k + dp) % dp, c]
        across.append([mover.remote(piece, piece, device) for device in over_groups])
        for copy in across[-1]:
            copy.start()
    own[0].wait()
    mine = w_full.at[:, c]
    over = [mover.remote(mine, mine, sibling)]
    over[0].start()
    for k in range(1, groups):
        for batch in across:
            batch[k - 1].wait_recv()
        block = w_full.at[:, (g - k + groups) % groups * 2 + m]
        over.append(mover.remote(block, block, sibling))
        over[-1].start()
    for copy in over + rows + others + moves[2:]:
        copy.wait()
    for copy in along + [copy for batch in across for copy in batch]:
        copy.wait_send()
    for copy in own[1:]:
        copy.wait()


def gather_first(tokens, cotangent, w, wo, wu, wd, dp, ctx):
    groups = ctx // 2
    remotes = (dp - 1) + dp * (groups - 1) + (ctx - 1) + 3 * (dp - 1) + groups
    any_space = pl.BlockSpec(memory_space=pl.ANY)
    return pl.pallas_call(
        functools.partial(gather_kernel, dp, ctx),
        in_specs=[any_space] * 6,
        out_specs=[any_space] * 7,
        out_shape=[jax.ShapeDtypeStruct(tokens.shape, BF)] * 3
        + [jax.ShapeDtypeStruct((dp, ctx) + w.shape, BF)]
        + [jax.ShapeDtypeStruct((dp,) + array.shape, BF) for array in (wo, wu, wd)],
        scratch_shapes=[pltpu.VMEM(tokens.shape, F32)] * 2
        + [pltpu.VMEM(tokens.shape, BF)] * 3
        + [
            pltpu.SemaphoreType.DMA((5,)),
            pltpu.SemaphoreType.DMA((remotes,)),
            pltpu.SemaphoreType.DMA((remotes,)),
            pltpu.SemaphoreType.DMA((4,)),
        ],
        compiler_params=pltpu.CompilerParams(
            collective_id=0, has_side_effects=True, vmem_limit_bytes=VMEM_BYTES
        ),
        name="gather_first",
    )(tokens, cotangent, w, wo, wu, wd)


class Spread:
    def __init__(self, dp, ctx, sources, targets, mover):
        d, c, g, m, over_dp, over_groups, sibling = place(dp, ctx)
        groups = ctx // 2
        self.devices = over_groups + [sibling]
        self.own = [mover.local(s, t.at[:, c]) for s, t in zip(sources, targets)]
        self.direct = [mover.remote(s, t.at[:, c], sibling) for s, t in zip(sources, targets)]
        self.across = [
            [mover.remote(s, t.at[:, c], device) for device in over_groups]
            for s, t in zip(sources, targets)
        ]
        self.onward = []
        for t in targets:
            blocks = [t.at[:, (g - k + groups) % groups * 2 + m] for k in range(1, groups)]
            self.onward.append([mover.remote(block, block, sibling) for block in blocks])

    @staticmethod
    def count(groups, arrays):
        return arrays * (1 + 2 * (groups - 1))

    def begin(self):
        greet(self.devices)
        for copy in self.own + [copy for batch in self.across for copy in batch] + self.direct:
            copy.start()

    def forward(self, index):
        for came, copy in zip(self.across[index], self.onward[index]):
            came.wait_recv()
            copy.start()

    def finish(self):
        for copy in self.own + self.direct + [copy for batch in self.onward for copy in batch]:
            copy.wait()
        for batch in self.across:
            for copy in batch:
                copy.wait_send()


class Scatter:
    def __init__(self, dp, ctx, sources, outs, buffers, small, small_out, small_buffers, mover):
        d, c, g, m, over_dp, over_groups, sibling = place(dp, ctx)
        groups = ctx // 2
        self.dp, self.groups, self.d, self.g = dp, groups, d, g
        self.devices = over_groups + over_dp + [sibling]
        self.outs = list(outs)
        self.buffers = buffers
        self.own, self.pair, self.across, self.along = [], [], [], []
        for source, (mine, other, came, sums, last) in zip(sources, buffers):
            summed = len(source.shape) == 4
            if summed:
                self.own.append(mover.local(source, mine))
                self.pair.append([])
            else:
                self.own.append(mover.local(source.at[:, :, m], mine))
                self.pair.append([mover.remote(source.at[:, :, 1 - m], other, sibling)])
            onward = source if summed else mine
            self.across.append(
                [
                    mover.remote(onward.at[:, (g + k) % groups], came.at[k - 1], over_groups[k - 1])
                    for k in range(1, groups)
                ]
            )
            self.along.append(
                [
                    mover.remote(sums.at[(d + k) % dp], last.at[k - 1], over_dp[k - 1])
                    for k in range(1, dp)
                ]
            )
        self.small, self.small_out = small, small_out
        one, came, two, groups_in, three, dp_in = small_buffers
        self.small_buffers = small_buffers
        self.pair.append([mover.remote(one, came, sibling)])
        self.across.append(
            [mover.remote(two, groups_in.at[k - 1], over_groups[k - 1]) for k in range(1, groups)]
        )
        self.along.append(
            [mover.remote(three, dp_in.at[k - 1], over_dp[k - 1]) for k in range(1, dp)]
        )

    @staticmethod
    def count(dp, ctx, arrays):
        return (arrays + 1) * (1 + ctx // 2 - 1 + dp - 1)

    @staticmethod
    def scratch(dp, ctx, sources, small):
        groups = ctx // 2
        shapes = []
        for s in sources:
            block = s.shape[-2:]
            shapes += [
                pltpu.VMEM((dp, groups) + block, BF),
                pltpu.VMEM((dp, groups) + block if len(s.shape) == 5 else (8, 128), BF),
                pltpu.VMEM((groups - 1, dp) + block, BF),
                pltpu.VMEM((dp,) + block, BF),
                pltpu.VMEM((dp - 1,) + block, BF),
            ]
        shape = small.shape
        shapes += [pltpu.VMEM(shape, F32)] * 3
        shapes += [
            pltpu.VMEM((groups - 1,) + shape, F32),
            pltpu.VMEM(shape, F32),
            pltpu.VMEM((dp - 1,) + shape, F32),
        ]
        return shapes

    def begin_small(self):
        self.small_buffers[0][...] = self.small[...]
        self.pair[-1][0].start()

    def begin(self, index):
        for copy in self.pair[index] or self.across[index]:
            copy.start()
        self.own[index].start()

    def first(self, index):
        mine, other = self.buffers[index][:2]
        groups = self.groups
        self.own[index].wait()
        if not self.pair[index]:
            return
        self.pair[index][0].wait_recv()

        def add(i, carry):
            at = (i // groups, i % groups)
            mine[at] = mine[at] + other[at]
            return carry

        lax.fori_loop(0, self.dp * groups, add, 0)
        for copy in self.across[index]:
            copy.start()

    def first_small(self):
        one, came, two = self.small_buffers[:3]
        self.pair[-1][0].wait_recv()
        two[...] = one[...] + came[...]
        for copy in self.across[-1]:
            copy.start()

    def middle(self, index):
        mine, _, came, sums, _ = self.buffers[index]
        for copy in self.across[index]:
            copy.wait_recv()

        def add(k, carry):
            total = mine[k, self.g].astype(F32)
            for j in range(self.groups - 1):
                total = total + came[j, k].astype(F32)
            sums[k] = total.astype(BF)
            return carry

        lax.fori_loop(0, self.dp, add, 0)
        for copy in self.along[index]:
            copy.start()

    def middle_small(self):
        _, _, two, groups_in, three, _ = self.small_buffers
        for copy in self.across[-1]:
            copy.wait_recv()
        total = two[...]
        for j in range(self.groups - 1):
            total = total + groups_in[j]
        three[...] = total
        for copy in self.along[-1]:
            copy.start()

    def finish(self):
        for index, out in enumerate(self.outs):
            sums, last = self.buffers[index][3:]
            for copy in self.along[index]:
                copy.wait_recv()
            total = sums[self.d].astype(F32)
            for j in range(self.dp - 1):
                total = total + last[j].astype(F32)
            out[...] = total
        three, dp_in = self.small_buffers[4:]
        for copy in self.along[-1]:
            copy.wait_recv()
        total = three[...]
        for j in range(self.dp - 1):
            total = total + dp_in[j]
        self.small_out[...] = total
        for batch in self.pair + self.across + self.along:
            for copy in batch:
                copy.wait_send()


class Exchange:
    def __init__(self, ctx, mover, source, target):
        d, c = lax.axis_index("dp"), lax.axis_index("ctx")
        groups = ctx // 2
        self.steps = []
        for t in range(groups):
            group = flip(c // 2, t, groups)
            same, other = group * 2 + c % 2, group * 2 + 1 - c % 2
            if t == 0:
                self.own = mover.local(source.at[c], target.at[c])
                batch = []
            else:
                batch = [mover.remote(source.at[same], target.at[c], (d, same))]
            batch.append(mover.remote(source.at[other], target.at[c], (d, other)))
            self.steps.append(batch)

    @staticmethod
    def count(ctx):
        return ctx - 1

    def start(self, t):
        if t == 0:
            self.own.start()
        for copy in self.steps[t]:
            copy.start()

    def arrive(self, t):
        if t == 0:
            self.own.wait()
        for copy in self.steps[t]:
            copy.wait_recv()

    def sent(self):
        for batch in self.steps:
            for copy in batch:
                copy.wait_send()


def columns(values):
    return jnp.sum(values, axis=0, keepdims=True)


def finish_kernel(dp, ctx, *refs):
    (xb, dq, dk, dv, w, grad_sum), refs = refs[:6], refs[6:]
    outs, small_out, x_out, refs = refs[:3], refs[3], refs[4], refs[5:]
    grads, result, small, refs = refs[:3], refs[3], refs[4], refs[5:]
    buffers, small_buffers, (local_sem, send_sem, recv_sem) = refs[:15], refs[15:21], refs[21:]
    d, c = lax.axis_index("dp"), lax.axis_index("ctx")
    groups = ctx // 2
    g = c // 2
    half, width = result.shape[1:]
    held = grads[0].shape[3]
    mover = Mover(local_sem, send_sem, recv_sem)
    scatter = Scatter(
        dp,
        ctx,
        grads,
        outs,
        [buffers[i * 5 : i * 5 + 5] for i in range(3)],
        small,
        small_out,
        small_buffers,
        mover,
    )
    give = Exchange(ctx, mover, result, x_out)
    greet([((d + k) % dp, c) for k in range(1, dp)] + [(d, (c + k) % ctx) for k in range(1, ctx)])
    small[...] = jnp.zeros_like(small)
    small[0:1, :] = columns(dq[...].astype(F32))
    small[1:2, :] = columns(dv[...].astype(F32))
    scatter.begin_small()

    across = xb[...].T

    def weight_gradient(index, rows_grad):
        total = dg(across, rows_grad[...], NN)
        for block in range(dp * ctx):
            at = (block // ctx, block % ctx // 2, block % 2)
            grads[index][at] = total[block * held : (block + 1) * held].astype(BF)
        scatter.begin(index)

    def row_tile(t):
        block = flip(g, t, groups)
        rows = pl.ds(pl.multiple_of(block * 2 * half, 2 * half), 2 * half)
        total = grad_sum[rows, :]
        for i, rows_grad in enumerate((dq, dk, dv)):
            total = total + dg(rows_grad[rows, :], w[:, i * width : (i + 1) * width], NT)
        result[pl.ds(block * 2, 2)] = total.astype(BF).reshape(2, half, width)
        give.start(t)

    tiles = list(range(groups - 1, -1, -1))
    for index, rows_grad in enumerate((dq, dk, dv)):
        weight_gradient(index, rows_grad)
        row_tile(tiles.pop(0))
        if index == 0:
            scatter.first_small()
        scatter.first(index)
    for t in tiles:
        row_tile(t)
    scatter.middle_small()
    for index in range(3):
        scatter.middle(index)
    scatter.finish()
    for t in range(groups):
        give.arrive(t)
    give.sent()


def finish_gradients(xb, dq, dk, dv, w, grad_sum, dp, ctx):
    rows, width = xb.shape
    remotes = Scatter.count(dp, ctx, 3) + Exchange.count(ctx)
    S = jax.ShapeDtypeStruct
    vmem = pl.BlockSpec(memory_space=pltpu.VMEM)
    source = S((dp, ctx // 2, 2, width // (dp * ctx), width), BF)
    small = S((8, width), F32)
    moved = (ctx, rows // ctx, width)
    return pl.pallas_call(
        functools.partial(finish_kernel, dp, ctx),
        in_specs=[vmem] * 6,
        out_specs=[vmem] * 4 + [pl.BlockSpec(memory_space=pl.ANY)],
        out_shape=[S(source.shape[3:], F32)] * 3 + [small, S(moved, BF)],
        scratch_shapes=[pltpu.VMEM(source.shape, BF)] * 3
        + [pltpu.VMEM(moved, BF), pltpu.VMEM(small.shape, F32)]
        + Scatter.scratch(dp, ctx, [source] * 3, small)
        + [
            pltpu.SemaphoreType.DMA((4,)),
            pltpu.SemaphoreType.DMA((remotes,)),
            pltpu.SemaphoreType.DMA((remotes,)),
        ],
        compiler_params=pltpu.CompilerParams(
            collective_id=3, has_side_effects=True, vmem_limit_bytes=VMEM_BYTES
        ),
        name="finish_gradients",
    )(xb, dq, dk, dv, w, grad_sum)


def head_lanes(shape, h):
    lane = lax.broadcasted_iota(jnp.int32, shape, len(shape) - 1)
    return (lane >= 64) == (h == 1), lane == (64 if h == 0 else 0)


def load_keys(keys, own_ref, sib_ref, lengths_ref, ctx):
    c = lax.axis_index("ctx")
    rows = own_ref.shape[0]
    half = rows // ctx
    length = lengths_ref[lax.axis_index("dp") * (ctx // 2) + c // 2]
    slot = lax.broadcasted_iota(jnp.int32, (rows, 128), 0)
    source = lax.broadcasted_iota(jnp.int32, (ctx, half, 128), 0).reshape(rows, 128)
    high = (2 * ctx - 1 - 2 * source) * half + slot
    for i, ref in enumerate((own_ref, sib_ref)):
        member = c % 2 if i == 0 else 1 - c % 2
        counted = jnp.where(member == 0, slot, high) < length
        for h in range(2):
            inside, spare = head_lanes((rows, 128), h)
            rest = jnp.where(spare & ~counted, masked_score, 0.0).astype(BF)
            keys[h, i * rows : (i + 1) * rows, :] = jnp.where(inside, ref[...], rest)


def forward_kernel(dp, ctx, bq, *refs):
    (x_ref, w_ref, vec_ref, lengths_ref), gathered, refs = refs[:4], refs[4:7], refs[7:]
    (mb_ref, mix_ref, lse_ref, own_to, sib_to), spread_to, refs = refs[:5], refs[5:8], refs[8:]
    keys, own, sib, local_sem, send_sem, recv_sem, pair_send, pair_recv, store_sem = refs
    spread = Spread(dp, ctx, gathered, spread_to, Mover(local_sem, send_sem, recv_sem))
    pairs, steps = pl.num_programs(0), pl.num_programs(1)
    pair, j = pl.program_id(0), pl.program_id(1)
    step = pair * steps + j
    last = forward_steps(pairs, steps)
    half, width = x_ref.shape

    def to_sibling(number):
        return pltpu.make_async_remote_copy(
            src_ref=own.at[number, pl.ds(1, 2)],
            dst_ref=sib.at[number],
            send_sem=pair_send.at[number],
            recv_sem=pair_recv.at[number],
            device_id=spread.devices[-1],
            device_id_type=MESH,
        )

    def stores(number):
        return [
            pltpu.make_async_copy(own.at[number], own_to.at[number], store_sem.at[number, 0]),
            pltpu.make_async_copy(sib.at[number], sib_to.at[number], store_sem.at[number, 1]),
        ]

    def project(number):
        lanes = [pl.ds(pl.multiple_of(number * 128 + i * width, 128), 128) for i in range(3)]
        weights = jnp.concatenate([w_ref[:, part] for part in lanes], axis=1)
        rows = dg(x_ref[...], weights, NN)
        own[number, 0] = (rows[:, :128] + vec_ref[0:1, lanes[0]]).astype(BF)
        own[number, 1] = rows[:, 128:256].astype(BF)
        own[number, 2] = (rows[:, 256:] + vec_ref[1:2, lanes[0]]).astype(BF)
        to_sibling(number).start()

    @pl.when(step == 0)
    def _():
        spread.begin()
        project(pair)

    @pl.when(j == 0)
    def _():
        to_sibling(pair).wait_recv()
        for copy in stores(pair):
            copy.start()
        load_keys(keys, own.at[pair, 1], sib.at[pair, 0], lengths_ref, ctx)

    @pl.when((j == 1) & (pair < pairs - 1))
    def _():
        project(pair + 1)

    rows = pl.ds(pl.multiple_of(j * bq, bq), bq)
    q = own[pair, 0, rows, :] * jnp.asarray(0.125, BF)
    scores = []
    for h in range(2):
        inside, spare = head_lanes((bq, 128), h)
        rest = jnp.where(spare, jnp.ones((), BF), jnp.zeros((), BF))
        scores.append(dg(jnp.where(inside, q, rest), keys[h], NT))
    outs, lses = [], []
    for h in range(2):
        top = jnp.max(scores[h], axis=1, keepdims=True)
        weights = jnp.exp(scores[h] - top)
        total = jnp.sum(weights, axis=1, keepdims=True)
        low = weights.astype(BF)
        mixed = dg(low[:, :half], own[pair, 2], NN) + dg(low[:, half:], sib[pair, 1], NN)
        outs.append(mixed / total)
        lses.append(top + jnp.log(total))
    lane = lax.broadcasted_iota(jnp.int32, (bq, 128), 1)
    mixed = jnp.where(lane < 64, outs[0], outs[1])
    mix_ref[...] = mixed
    mb_ref[...] = mixed.astype(BF)
    lse_ref[0] = jnp.where(lane == 0, lses[0], lses[1]).T[:8]

    for index, at in enumerate(last):

        @pl.when(step == at)
        def _(index=index):
            spread.forward(index)

    @pl.when(step == last[-1])
    def _():
        spread.finish()
        for number in range(pairs):
            to_sibling(number).wait_send()
            for copy in stores(number):
                copy.wait()


def attention_forward(x, w, vec, lengths, gathered, dp, ctx, bq=256):
    rows, width = x.shape
    pairs = width // 128
    S = jax.ShapeDtypeStruct
    blk = pl.BlockSpec((bq, 128), lambda p, j: (j, p))
    any_space = pl.BlockSpec(memory_space=pl.ANY)
    vmem = pl.BlockSpec(memory_space=pltpu.VMEM)
    remotes = Spread.count(ctx // 2, 3)
    return pl.pallas_call(
        functools.partial(forward_kernel, dp, ctx, bq),
        grid=(pairs, rows // bq),
        in_specs=[vmem] * 3 + [pl.BlockSpec(memory_space=pltpu.SMEM)] + [any_space] * 3,
        out_specs=[blk, blk, pl.BlockSpec((1, 8, bq), lambda p, j: (p, 0, j))] + [any_space] * 5,
        out_shape=[S(x.shape, BF), S(x.shape, F32), S((pairs, 8, rows), F32)]
        + [S((pairs, count, rows, 128), BF) for count in (3, 2)]
        + [S((dp, ctx) + array.shape[1:], BF) for array in gathered],
        scratch_shapes=[
            pltpu.VMEM((2, 2 * rows, 128), BF),
            pltpu.VMEM((pairs, 3, rows, 128), BF),
            pltpu.VMEM((pairs, 2, rows, 128), BF),
            pltpu.SemaphoreType.DMA((3,)),
            pltpu.SemaphoreType.DMA((remotes,)),
            pltpu.SemaphoreType.DMA((remotes,)),
            pltpu.SemaphoreType.DMA((pairs,)),
            pltpu.SemaphoreType.DMA((pairs,)),
            pltpu.SemaphoreType.DMA((pairs, 2)),
        ],
        compiler_params=pltpu.CompilerParams(
            vmem_limit_bytes=VMEM_BYTES, collective_id=1, has_side_effects=True
        ),
        cost_estimate=pl.CostEstimate(
            flops=16 * rows * rows * 128 * pairs,
            bytes_accessed=14 * rows * 768,
            transcendentals=4 * rows * rows * pairs,
        ),
        name="attend",
    )(x, w, vec, lengths, *gathered)


def forward_steps(pairs, steps):
    count = pairs * steps
    return (count * 5 // 24, count * 15 // 24, count - 1)


def backward_steps(pairs, steps):
    count = pairs * steps
    first = [count * at // 12 for at in (0, 0, 1)]
    middle = [count * at // 12 for at in (5, 4, 8)]
    return first, middle


def backward_kernel(dp, ctx, ck, *refs):
    (q_ref, ko_ref, vo_ref, ks_ref, vs_ref, do_ref, mix_ref, lengths_ref, lse_ref), refs = (
        refs[:9],
        refs[9:],
    )
    q_ref, ko_ref, vo_ref, ks_ref, vs_ref = (
        ref.at[0, 0] for ref in (q_ref, ko_ref, vo_ref, ks_ref, vs_ref)
    )
    sources, small, refs = refs[:3], refs[3], refs[4:]
    (dq_ref, dk_ref, dv_ref), refs = refs[:3], refs[3:]
    summed, small_out, refs = refs[:3], refs[3], refs[4:]
    (keys, dk, dv, held, going, coming), refs = refs[:6], refs[6:]
    buffers, small_buffers, refs = refs[:15], refs[15:21], refs[21:]
    local_sem, send_sem, recv_sem, pair_send, pair_recv = refs
    scatter = Scatter(
        dp,
        ctx,
        sources,
        summed,
        [buffers[i * 5 : i * 5 + 5] for i in range(3)],
        small,
        small_out,
        small_buffers,
        Mover(local_sem, send_sem, recv_sem),
    )
    steps = pl.num_programs(1)
    j = pl.program_id(1)
    step = pl.program_id(0) * steps + j

    pair = pl.program_id(0)
    sibling = scatter.devices[-1]

    def to_sibling(number):
        return [
            pltpu.make_async_remote_copy(
                src_ref=going.at[number, i],
                dst_ref=coming.at[number, i],
                send_sem=pair_send.at[number * 2 + i],
                recv_sem=pair_recv.at[number * 2 + i],
                device_id=sibling,
                device_id_type=MESH,
            )
            for i in range(2)
        ]

    def settle(number):
        lanes = pl.ds(pl.multiple_of(number * 128, 128), 128)
        for i, (copy, out) in enumerate(zip(to_sibling(number), (dk_ref, dv_ref))):
            copy.wait_recv()
            total = held[number % 2, i] + coming[number, i].astype(F32)
            out[:, lanes] = total.astype(BF)

    @pl.when(step == 0)
    def _():
        greet(scatter.devices)
        scatter.begin(1)
        scatter.begin_small()
        scatter.begin(0)
        scatter.begin(2)

    @pl.when((j == 0) & (pair > 0))
    def _():
        settle(pair - 1)

    @pl.when(j == 0)
    def _():
        load_keys(keys, ko_ref, ks_ref, lengths_ref, ctx)
        dk[...] = jnp.zeros_like(dk)
        dv[...] = jnp.zeros_like(dv)

    half, bq = ko_ref.shape[0], q_ref.shape[0]
    q = q_ref[...] * jnp.asarray(0.125, BF)
    do = do_ref[...]
    prod = (do.astype(F32) * mix_ref[...]).T
    zero, one = jnp.zeros((), BF), jnp.ones((), BF)
    heads = []
    for h in range(2):
        inside, spare = head_lanes((bq, 128), h)
        heads.append(
            (
                jnp.where(inside, q, jnp.where(spare, one, zero)),
                jnp.where(inside, q, zero),
                jnp.where(inside, do, zero),
                lse_ref[0, h : h + 1, :],
                jnp.sum(prod[h * 64 : (h + 1) * 64], axis=0, keepdims=True),
            )
        )
    dq = jnp.zeros((bq, 128), F32)
    for first in range(0, 2 * half, ck):
        rows = slice(first, first + ck)
        v = vo_ref[rows, :] if first < half else vs_ref[first - half : first - half + ck, :]
        for h in range(2):
            qm, qz, dom, lse, delta = heads[h]
            k = keys[h, rows, :]
            p = jnp.exp(dg(k, qm, NT) - lse)
            ds = (p * (dg(v, dom, NT) - delta)).astype(BF)
            dv[rows, :] += dg(p.astype(BF), dom, NN)
            dk[rows, :] += dg(ds, qz, NN)
            dq = dq + dg(ds, k, TN)
    dq_ref[...] = (dq * 0.125).astype(BF)

    @pl.when(j == steps - 1)
    def _():
        for i, total in enumerate((dk, dv)):
            held[pair % 2, i] = total[:half, :]
            going[pair, i] = total[half:, :].astype(BF)
        for copy in to_sibling(pair):
            copy.start()

    first, middle_at = backward_steps(pl.num_programs(0), steps)

    @pl.when(step == first[0])
    def _():
        scatter.first_small()

    @pl.when(step == middle_at[0])
    def _():
        scatter.middle_small()

    for index in range(3):

        @pl.when(step == first[index])
        def _(index=index):
            scatter.first(index)

        @pl.when(step == middle_at[index])
        def _(index=index):
            scatter.middle(index)

    @pl.when(step == pl.num_programs(0) * steps - 1)
    def _():
        scatter.finish()
        settle(pair)
        for number in range(pl.num_programs(0)):
            for copy in to_sibling(number):
                copy.wait_send()


def attention_backward(own, sib, do, mix, lengths, lse, sources, small, dp, ctx, bq=512, ck=512):
    rows, width = do.shape
    pairs = width // 128
    S = jax.ShapeDtypeStruct
    blk = pl.BlockSpec((bq, 128), lambda p, j: (j, p))
    whole_of = [
        pl.BlockSpec((1, 1, rows, 128), lambda p, j, i=i: (p, i, 0, 0)) for i in (1, 2, 0, 1)
    ]
    any_space = pl.BlockSpec(memory_space=pl.ANY)
    remotes = Scatter.count(dp, ctx, 3)
    whole = pl.BlockSpec(small.shape, lambda p, j: (0, 0))
    sums = [s.shape[-2:] for s in sources]
    all_rows = pl.BlockSpec((rows, width), lambda p, j: (0, 0))
    return pl.pallas_call(
        functools.partial(backward_kernel, dp, ctx, ck),
        grid=(pairs, rows // bq),
        in_specs=[pl.BlockSpec((1, 1, bq, 128), lambda p, j: (p, 0, j, 0))]
        + whole_of
        + [blk, blk]
        + [pl.BlockSpec(memory_space=pltpu.SMEM)]
        + [pl.BlockSpec((1, 8, bq), lambda p, j: (p, 0, j))]
        + [any_space] * 3
        + [whole],
        out_specs=[blk, all_rows, all_rows]
        + [pl.BlockSpec(shape, lambda p, j: (0, 0)) for shape in sums]
        + [whole],
        out_shape=[S(do.shape, BF)] * 3
        + [S(shape, F32) for shape in sums]
        + [S(small.shape, F32)],
        scratch_shapes=[
            pltpu.VMEM((2, 2 * rows, 128), BF),
            pltpu.VMEM((2 * rows, 128), F32),
            pltpu.VMEM((2 * rows, 128), F32),
            pltpu.VMEM((2, 2, rows, 128), F32),
            pltpu.VMEM((pairs, 2, rows, 128), BF),
            pltpu.VMEM((pairs, 2, rows, 128), BF),
        ]
        + Scatter.scratch(dp, ctx, sources, small)
        + [
            pltpu.SemaphoreType.DMA((3,)),
            pltpu.SemaphoreType.DMA((remotes,)),
            pltpu.SemaphoreType.DMA((remotes,)),
            pltpu.SemaphoreType.DMA((2 * pairs,)),
            pltpu.SemaphoreType.DMA((2 * pairs,)),
        ],
        compiler_params=pltpu.CompilerParams(
            vmem_limit_bytes=VMEM_BYTES, collective_id=2, has_side_effects=True
        ),
        cost_estimate=pl.CostEstimate(
            flops=40 * rows * rows * 128 * pairs,
            bytes_accessed=26 * rows * 768,
            transcendentals=4 * rows * rows * pairs,
        ),
        name="attend_back",
    )(own, own, own, sib, sib, do, mix, lengths, lse, *sources, small)


def gelu_and_slope(x):
    t = 1.0 / (1.0 + 0.2316419 * jnp.abs(x))
    bell = 0.3989422804 * jnp.exp(-0.5 * x * x)
    poly = 1.330274429 * t - 1.821255978
    poly = poly * t + 1.781477937
    poly = poly * t - 0.356563782
    poly = poly * t + 0.319381530
    tail = bell * (poly * t)
    below = jnp.where(x < 0.0, tail, 1.0 - tail)
    return x * below, below + x * bell


def middle_kernel(dp, ctx, *refs):
    (mb, xb, rest_src, up_src, vec, bias_up, wo_src, wu_src, wd_src), refs = refs[:9], refs[9:]
    (dm, grad_sum, out_to, go_to, gu_to, gd_to, small), refs = refs[:7], refs[7:]
    (wo, wu, wd, rest, upstream, result, active, dinner, slope, fb, db, da), refs = (
        refs[:12],
        refs[12:],
    )
    (other, summed), refs = refs[:2], refs[2:]
    load_sem, local_sem, send_sem, recv_sem = refs
    groups = ctx // 2
    g = lax.axis_index("ctx") // 2
    half, width = result.shape[1:]
    tile = 2 * half
    chunks = range(wu.shape[1] // width)
    step = pl.program_id(0)
    mover = Mover(local_sem, send_sem, recv_sem)
    rest_in = Exchange(ctx, mover, rest_src, rest)
    up_in = Exchange(ctx, mover, up_src, upstream)
    give = Exchange(ctx, mover, result, out_to)
    loads = [
        pltpu.make_async_copy(source, target, load_sem.at[i])
        for i, (source, target) in enumerate(((wo_src, wo), (wu_src, wu), (wd_src, wd)))
    ]
    stores = [
        pltpu.make_async_copy(source, target, load_sem.at[i])
        for i, (source, target) in enumerate(((wo, go_to), (wu, gu_to), (summed, gd_to)))
    ]
    d, c = lax.axis_index("dp"), lax.axis_index("ctx")
    held = other.shape[2]

    def block_rows(i, k, member):
        return pl.ds(pl.multiple_of(((i * groups + k) * 2 + member) * held, 8), held)

    blocks = [(i, k) for i in range(dp) for k in range(groups)]
    to_sibling = [
        mover.remote(wd.at[block_rows(i, k, 1 - c % 2)], other.at[i, k], (d, g * 2 + 1 - c % 2))
        for i, k in blocks
    ]

    def load(index):
        @pl.when(step == 0)
        def _():
            loads[index].wait()

    @pl.when(step == 0)
    def _():
        for copy in loads:
            copy.start()
        greet([(d, (c + k) % ctx) for k in range(1, ctx)])
        for t in range(groups):
            rest_in.start(t)
            up_in.start(t)
        small[...] = jnp.zeros_like(small)

    @pl.when(step < groups)
    def _():
        block = flip(g, step, groups)
        rows = pl.ds(pl.multiple_of(block * tile, tile), tile)
        pair = pl.ds(block * 2, 2)
        load(0)
        hidden = dg(mb[rows, :], wo[...], NN) + vec[2:3, :] + xb[rows, :].astype(F32)
        for t in range(groups):

            @pl.when(step == t)
            def _(t=t):
                rest_in.arrive(t)

        hidden = hidden + rest[pair].reshape(tile, width).astype(F32)
        normed, standard_one, inverse_one = normalize(hidden, vec[6:7, :], vec[4:5, :])
        low = normed.astype(BF)
        fb[rows, :] = low
        load(1)
        parts = [slice(i * width, (i + 1) * width) for i in chunks]
        inner = dg(low, wu[:, parts[0]], NN)
        for i, part in enumerate(parts):
            ahead = dg(low, wu[:, parts[i + 1]], NN) if i + 1 < len(parts) else None
            value, slope[:, part] = gelu_and_slope(inner + bias_up[:, part])
            active[rows, part] = value.astype(BF)
            inner = ahead
        load(2)
        hidden = normed + dg(active[rows, :], wd[...], NN) + vec[3:4, :]
        out, standard, inverse = normalize(hidden, vec[7:8, :], vec[5:6, :])
        result[pair] = out.astype(BF).reshape(2, half, width)
        for t in range(groups):

            @pl.when(step == t)
            def _(t=t):
                give.start(t)
                up_in.arrive(t)

        error = upstream[pair].reshape(tile, width).astype(F32)
        grad = normalize_back(error, standard, inverse, vec[7:8, :])
        low_grad = grad.astype(BF)
        db[rows, :] = low_grad
        small[1:2, :] += columns(low_grad.astype(F32))
        small[3:4, :] += columns(error)
        small[5:6, :] += columns(error * standard)
        for i in chunks:
            part = slice(i * width, (i + 1) * width)
            change = dg(low_grad, wd[part, :], NT) * slope[:, part]
            change = change.astype(BF)
            dinner[rows, part] = change
            small[6 + i : 7 + i, :] += columns(change.astype(F32))
        grad = grad + dg(dinner[rows, :], wu[...], NT)
        small[2:3, :] += columns(grad)
        small[4:5, :] += columns(grad * standard_one)
        grad = normalize_back(grad, standard_one, inverse_one, vec[6:7, :])
        grad_sum[rows, :] = grad
        low_grad = grad.astype(BF)
        da[rows, :] = low_grad
        small[0:1, :] += columns(low_grad.astype(F32))
        dm[rows, :] = dg(low_grad, wo[...], NT).astype(BF)

    @pl.when(step == groups)
    def _():
        for i in chunks:
            part = slice(i * width, (i + 1) * width)
            wd[part, :] = dg(active[:, part], db[...], TN).astype(BF)
        for copy in to_sibling:
            copy.start()
        across = fb[...].T
        for i in chunks:
            part = slice(i * width, (i + 1) * width)
            wu[:, part] = dg(across, dinner[:, part], NN).astype(BF)
        stores[1].start()
        for copy in to_sibling:
            copy.wait()
        for i, k in blocks:
            summed[i, k] = wd[block_rows(i, k, c % 2), :] + other[i, k]
        stores[2].start()
        wo[...] = dg(mb[...], da[...], TN).astype(BF)
        stores[0].start()
        for t in range(groups):
            give.arrive(t)
        for move in (rest_in, up_in, give):
            move.sent()
        for copy in stores:
            copy.wait()


def middle(mb, xb, rest, upstream, vec, bias_up, wo, wu, wd, dp, ctx):
    rows, width = mb.shape
    hidden = wu.shape[1]
    half = rows // ctx
    S = jax.ShapeDtypeStruct
    any_space = pl.BlockSpec(memory_space=pl.ANY)
    vmem = pl.BlockSpec(memory_space=pltpu.VMEM)
    held = (dp, ctx // 2, hidden // (dp * ctx), width)
    remotes = 3 * Exchange.count(ctx) + dp * (ctx // 2)
    return pl.pallas_call(
        functools.partial(middle_kernel, dp, ctx),
        grid=(ctx // 2 + 1,),
        in_specs=[vmem, vmem, any_space, any_space, vmem, vmem] + [any_space] * 3,
        out_specs=[vmem, vmem] + [any_space] * 4 + [vmem],
        out_shape=[S(mb.shape, BF), S(mb.shape, F32), S(rest.shape, BF)]
        + [S(wo.shape, BF), S(wu.shape, BF), S(held, BF)]
        + [S((16, width), F32)],
        scratch_shapes=[pltpu.VMEM(array.shape, BF) for array in (wo, wu, wd)]
        + [pltpu.VMEM(rest.shape, BF)] * 3
        + [pltpu.VMEM((rows, hidden), BF)] * 2
        + [pltpu.VMEM((2 * half, hidden), F32)]
        + [pltpu.VMEM((rows, width), BF)] * 3
        + [pltpu.VMEM(held, BF)] * 2
        + [
            pltpu.SemaphoreType.DMA((3,)),
            pltpu.SemaphoreType.DMA((3,)),
            pltpu.SemaphoreType.DMA((remotes,)),
            pltpu.SemaphoreType.DMA((remotes,)),
        ],
        compiler_params=pltpu.CompilerParams(
            vmem_limit_bytes=VMEM_BYTES, collective_id=4, has_side_effects=True
        ),
        cost_estimate=pl.CostEstimate(
            flops=2 * 3 * rows * width * (2 * hidden + width),
            bytes_accessed=50 << 20,
            transcendentals=rows * hidden,
        ),
        name="middle",
    )(mb, xb, rest, upstream, vec, bias_up, wo, wu, wd)


def normalize(hidden, scale_row, shift_row):
    centred = hidden - jnp.mean(hidden, axis=-1, keepdims=True)
    inverse = lax.rsqrt(jnp.mean(centred * centred, axis=-1, keepdims=True) + epsilon)
    standard = centred * inverse
    return (standard * scale_row + shift_row, standard, inverse)


def normalize_back(gradient, standard, inverse, scale_row):
    scaled = gradient * scale_row
    centred = scaled - jnp.mean(scaled, axis=-1, keepdims=True)
    return (centred - standard * jnp.mean(scaled * standard, axis=-1, keepdims=True)) * inverse


def write_kernel(dp, ctx, small_ref, sums_ref, out_ref, tokens_ref, *refs):
    sources, (out_to, tokens_to), refs = refs[:6], refs[6:8], refs[8:]
    targets, (vectors_to, bias_to) = refs[:6], refs[6:]
    out_to[...] = out_ref[...].astype(F32)
    tokens_to[...] = tokens_ref[...].astype(F32)

    @pl.when(pl.program_id(0) == 0)
    def _():
        for source, target in zip(sources, targets):
            target[...] = source[...]
        device = lax.axis_index("dp") * ctx + lax.axis_index("ctx")
        width = small_ref.shape[1]
        held, held_up = vectors_to.shape[1], bias_to.shape[1]
        rows = jnp.concatenate([sums_ref[0:2, :], small_ref[0:6, :]], axis=0)
        vectors_to[...] = pltpu.roll(rows, (width - device * held) % width, 1)[:, :held]
        first = device * held_up
        row = small_ref[pl.ds(6 + first // width, 1), :]
        row = jnp.broadcast_to(row, (8, width))
        bias_to[...] = pltpu.roll(row, (width - first % width) % width, 1)[0:1, :held_up]


def write_out(small, sums, out, tokens, own, held_up, dp, ctx):
    block = pl.BlockSpec((1,) + out.shape[1:], lambda i: (i, 0, 0))
    S = jax.ShapeDtypeStruct

    def whole(shape):
        return pl.BlockSpec(shape, lambda i: (0, 0))

    shapes = [array.shape for array in own]
    vectors = (8, out.shape[2] // (dp * ctx))
    return pl.pallas_call(
        functools.partial(write_kernel, dp, ctx),
        grid=(ctx,),
        in_specs=[whole(small.shape), whole(sums.shape), block, block]
        + [whole(shape) for shape in shapes],
        out_specs=[block, block]
        + [whole(shape) for shape in shapes]
        + [whole(vectors), whole((1, held_up))],
        out_shape=[S(out.shape, F32)] * 2
        + [S(shape, F32) for shape in shapes]
        + [S(vectors, F32), S((1, held_up), F32)],
        compiler_params=pltpu.CompilerParams(vmem_limit_bytes=VMEM_BYTES),
        name="write_out",
    )(small, sums, out, tokens, *own)


def on_device(
    tokens, cotangent, lengths, w_query, w_key, w_value, w_attn_out, w_up, b_up, w_down, vectors
):
    seqs, rows_dev, width = tokens.shape
    dp = lax.axis_size("dp")
    ctx = lax.axis_size("ctx")
    half = rows_dev // 2
    rows = half * ctx
    def by_owner(grad):
        return grad.reshape(dp, ctx // 2, 2, -1, grad.shape[1])

    split = tokens.reshape(ctx, half, width)
    held = w_query.shape[0]
    extra = jnp.concatenate([vectors.T, b_up.reshape(held, -1)], axis=1)
    extra = jnp.pad(extra, ((0, 0), (0, 128 - extra.shape[1])))
    low_in, left_out, upstream, full_first, *over_dp = gather_first(
        split,
        cotangent.reshape(ctx, half, width),
        jnp.concatenate([w_query, w_key, w_value, extra], axis=1),
        w_attn_out,
        w_up,
        w_down,
        dp,
        ctx,
    )
    low_in = low_in.reshape(rows, width)
    full_first = full_first.reshape(width, -1)
    vector_rows = full_first[:, 3 * width : 3 * width + 8].T.astype(F32)
    bias_columns = b_up.shape[0] // held
    full_bias_up = full_first[:, 3 * width + 8 : 3 * width + 8 + bias_columns].reshape(-1).astype(F32)
    low_mixed, mixed, lse, own, sib, full_attn, full_up, full_down = attention_forward(
        low_in, full_first, vector_rows, lengths, over_dp, dp, ctx
    )
    full_attn = full_attn.reshape(width, width)
    full_up = full_up.reshape(width, -1)
    full_down = full_down.reshape(-1, width)

    d_mixed, grad_sum, result, d_attn, d_up, part_down, small = middle(
        low_mixed,
        low_in,
        left_out,
        upstream,
        vector_rows,
        full_bias_up.reshape(1, -1),
        full_attn,
        full_up,
        full_down,
        dp,
        ctx,
    )
    dq, dk, dv, own_attn, own_down, own_up, small = attention_backward(
        own,
        sib,
        d_mixed,
        mixed,
        lengths,
        lse,
        [by_owner(d_attn), part_down, by_owner(d_up)],
        small,
        dp,
        ctx,
    )
    own_query, own_key, own_value, sums, grad_tokens = finish_gradients(
        low_in, dq, dk, dv, full_first, grad_sum, dp, ctx
    )
    output, grad_tokens, *own, own_vectors, own_bias_up = write_out(
        small,
        sums,
        result,
        grad_tokens,
        [own_query, own_key, own_value, own_attn, own_up, own_down],
        b_up.shape[0],
        dp,
        ctx,
    )
    own_query, own_key, own_value, own_attn, own_up, own_down = own
    output = output.reshape(seqs, rows_dev, width)
    grad_tokens = grad_tokens.reshape(seqs, rows_dev, width)
    own_bias_up = own_bias_up.reshape(-1)
    return (
        output,
        grad_tokens,
        own_query,
        own_key,
        own_value,
        own_attn,
        own_up,
        own_bias_up,
        own_down,
        own_vectors,
    )


def solution(mesh):
    in_specs = (
        P("dp", "ctx", None),
        P("dp", "ctx", None),
        P(),
        P(("dp", "ctx"), None),
        P(("dp", "ctx"), None),
        P(("dp", "ctx"), None),
        P(("dp", "ctx"), None),
        P(("dp", "ctx"), None),
        P(("dp", "ctx")),
        P(("dp", "ctx"), None),
        P(None, ("dp", "ctx")),
    )
    out_specs = (
        P("dp", "ctx", None),
        P("dp", "ctx", None),
        P(("dp", "ctx"), None),
        P(("dp", "ctx"), None),
        P(("dp", "ctx"), None),
        P(("dp", "ctx"), None),
        P(("dp", "ctx"), None),
        P(("dp", "ctx")),
        P(("dp", "ctx"), None),
        P(None, ("dp", "ctx")),
    )
    return jax.shard_map(
        on_device, mesh=mesh, in_specs=in_specs, out_specs=out_specs, check_vma=False
    )
```

```python
import functools
import jax
import jax.numpy as jnp
from jax import lax
from jax.experimental import pallas as pl
from jax.experimental.pallas import tpu as pltpu
from jax.sharding import PartitionSpec as P

HEAD_DIM = 64
F32 = jnp.float32
BF = jnp.bfloat16
NN = (((1,), (0,)), ((), ()))
NT = (((1,), (1,)), ((), ()))
TN = (((0,), (0,)), ((), ()))
epsilon = 1e-12
masked_score = -1e30
VMEM_BYTES = 58 << 20


def dg(left, right, dims):
    return lax.dot_general(left, right, dims, preferred_element_type=F32)


MESH = pl.DeviceIdType.MESH


class Mover:
    def __init__(self, local_sem, send_sem, recv_sem):
        self.local_sem, self.send_sem, self.recv_sem = local_sem, send_sem, recv_sem
        self.locals = self.remotes = 0

    def local(self, source, target):
        copy = pltpu.make_async_copy(source, target, self.local_sem.at[self.locals])
        self.locals += 1
        return copy

    def remote(self, source, target, device):
        number = self.remotes
        self.remotes += 1
        return pltpu.make_async_remote_copy(
            src_ref=source,
            dst_ref=target,
            send_sem=self.send_sem.at[number],
            recv_sem=self.recv_sem.at[number],
            device_id=device,
            device_id_type=MESH,
        )


def greet(devices):
    barrier = pltpu.get_barrier_semaphore()
    for device in devices:
        pl.semaphore_signal(barrier, inc=1, device_id=device, device_id_type=MESH)
    pl.semaphore_wait(barrier, len(devices))


def place(dp, ctx):
    d, c = lax.axis_index("dp"), lax.axis_index("ctx")
    groups = ctx // 2
    g, m = c // 2, c % 2
    over_dp = [((d + k) % dp, c) for k in range(1, dp)]
    over_groups = [(d, (g + k) % groups * 2 + m) for k in range(1, groups)]
    return d, c, g, m, over_dp, over_groups, (d, g * 2 + 1 - m)


def flip(group, step, groups):
    total, bit = 0, 1
    while bit < groups:
        total = total + (group // bit + step // bit) % 2 * bit
        bit *= 2
    return total


class Spread:
    def __init__(self, dp, ctx, sources, targets, mover):
        d, c, g, m, over_dp, over_groups, sibling = place(dp, ctx)
        groups = ctx // 2
        bits = [1 << i for i in range(groups.bit_length() - 1)]
        self.levels = len(bits)
        self.devices = [(d, flip(g, bit, groups) * 2 + m) for bit in bits] + [sibling]
        self.own, self.copies, self.onward = [], [], []
        for source, target in zip(sources, targets):

            def column(mask):
                return flip(g, mask, groups) * 2 + m

            self.own.append([] if source is None else [mover.local(source, target.at[:, c])])
            source = target.at[:, c] if source is None else source
            copies = [[] for _ in range(self.levels + 1)]
            for start, order in ((0, bits), (dp // 2, bits[::-1])):
                part = pl.ds(start, dp // 2)
                for i, bit in enumerate(order):
                    for mask in range(groups):
                        if any(mask & other for other in order[i:]):
                            continue
                        place_in = target.at[part, column(mask)]
                        copies[bin(mask).count("1")].append(
                            mover.remote(
                                place_in if mask else source.at[part], place_in, (d, column(bit))
                            )
                        )
            self.copies.append(copies)
            onward = [[mover.remote(source, target.at[:, c], sibling)]]
            onward += [[] for _ in range(self.levels)]
            for mask in range(1, groups):
                block = target.at[:, column(mask)]
                onward[bin(mask).count("1")].append(mover.remote(block, block, sibling))
            self.onward.append(onward)

    @staticmethod
    def count(ctx, arrays):
        return arrays * (2 * (ctx // 2 - 1) + ctx // 2)

    def begin(self):
        for own, copies, onward in zip(self.own, self.copies, self.onward):
            for copy in copies[0] + own + onward[0]:
                copy.start()

    def forward(self, index, level):
        for copy in self.copies[index][level - 1]:
            copy.wait_recv()
        for copy in self.copies[index][level] + self.onward[index][level]:
            copy.start()

    def finish(self):
        for own, copies, onward in zip(self.own, self.copies, self.onward):
            for copy in own + sum(onward, []):
                copy.wait()
            for copy in sum(copies, []):
                copy.wait_send()


def gather_kernel(dp, ctx, *refs):
    (tokens, cotangent, w, wo, wu, wd), refs = refs[:6], refs[6:]
    (x_in, rest_to, up_to, w_full, zo, zu, zd), refs = refs[:7], refs[7:]
    wide, wide_up, x, rest, up, local_sem, send_sem, recv_sem, move_sem = refs
    d, c, g, m, over_dp, over_groups, sibling = place(dp, ctx)
    groups = ctx // 2
    moves = [
        pltpu.make_async_copy(source, target, move_sem.at[i])
        for i, (source, target) in enumerate(
            ((tokens, wide), (cotangent, wide_up), (rest, rest_to), (up, up_to))
        )
    ]
    moves[0].start()
    greet(over_dp + [(d, (c + k) % ctx) for k in range(1, ctx)])
    mover = Mover(local_sem, send_sem, recv_sem)
    own = [
        mover.local(source, target)
        for source, target in (
            (w, w_full.at[d, c]),
            (x.at[c], x_in.at[c]),
            (wo, zo.at[d]),
            (wu, zu.at[d]),
            (wd, zd.at[d]),
        )
    ]
    along = [mover.remote(w, w_full.at[d, c], device) for device in over_dp]
    rows = [
        mover.remote(x.at[(c + k) % ctx], x_in.at[c], (d, (c + k) % ctx)) for k in range(1, ctx)
    ]
    others = [
        mover.remote(source, target.at[d], device)
        for source, target in ((wo, zo), (wu, zu), (wd, zd))
        for device in over_dp
    ]
    spread = Spread(dp, ctx, [None], [w_full], mover)
    for copy in own[:1] + along:
        copy.start()
    moves[0].wait()
    moves[1].start()
    x[...] = wide[...].astype(BF)
    for copy in rows + own[1:]:
        copy.start()
    for copy in along:
        copy.wait_recv()
    own[0].wait()
    spread.begin()
    for copy in others:
        copy.start()
    rest[...] = (wide[...] - x[...].astype(F32)).astype(BF)
    moves[2].start()
    moves[1].wait()
    up[...] = wide_up[...].astype(BF)
    moves[3].start()
    for level in range(1, spread.levels + 1):
        spread.forward(0, level)
    for copy in rows + others + moves[2:] + own[1:]:
        copy.wait()
    spread.finish()
    for copy in along:
        copy.wait_send()


def gather_first(tokens, cotangent, w, wo, wu, wd, dp, ctx):
    remotes = (dp - 1) + Spread.count(ctx, 1) + (ctx - 1) + 3 * (dp - 1)
    any_space = pl.BlockSpec(memory_space=pl.ANY)
    return pl.pallas_call(
        functools.partial(gather_kernel, dp, ctx),
        in_specs=[any_space] * 6,
        out_specs=[any_space] * 7,
        out_shape=[jax.ShapeDtypeStruct(tokens.shape, BF)] * 3
        + [jax.ShapeDtypeStruct((dp, ctx) + w.shape, BF)]
        + [jax.ShapeDtypeStruct((dp,) + array.shape, BF) for array in (wo, wu, wd)],
        scratch_shapes=[pltpu.VMEM(tokens.shape, F32)] * 2
        + [pltpu.VMEM(tokens.shape, BF)] * 3
        + [
            pltpu.SemaphoreType.DMA((5,)),
            pltpu.SemaphoreType.DMA((remotes,)),
            pltpu.SemaphoreType.DMA((remotes,)),
            pltpu.SemaphoreType.DMA((4,)),
        ],
        compiler_params=pltpu.CompilerParams(
            collective_id=0, has_side_effects=True, vmem_limit_bytes=VMEM_BYTES
        ),
        name="gather_first",
    )(tokens, cotangent, w, wo, wu, wd)


class Scatter:
    def __init__(self, dp, ctx, sources, outs, buffers, small, small_out, small_buffers, mover):
        d, c, g, m, over_dp, over_groups, sibling = place(dp, ctx)
        groups = ctx // 2
        self.dp, self.groups, self.d, self.g = dp, groups, d, g
        self.devices = over_groups + over_dp + [sibling]
        self.outs = list(outs)
        self.buffers = buffers
        self.own, self.pair, self.across, self.along = [], [], [], []
        for source, (mine, other, came, sums, last) in zip(sources, buffers):
            summed = len(source.shape) == 4
            if summed:
                self.own.append(mover.local(source, mine))
                self.pair.append([])
            else:
                self.own.append(mover.local(source.at[:, :, m], mine))
                self.pair.append([mover.remote(source.at[:, :, 1 - m], other, sibling)])
            onward = source if summed else mine
            self.across.append(
                [
                    mover.remote(onward.at[:, (g + k) % groups], came.at[k - 1], over_groups[k - 1])
                    for k in range(1, groups)
                ]
            )
            self.along.append(
                [
                    mover.remote(sums.at[(d + k) % dp], last.at[k - 1], over_dp[k - 1])
                    for k in range(1, dp)
                ]
            )
        self.small, self.small_out = small, small_out
        one, came, two, groups_in, three, dp_in = small_buffers
        self.small_buffers = small_buffers
        self.pair.append([mover.remote(one, came, sibling)])
        self.across.append(
            [mover.remote(two, groups_in.at[k - 1], over_groups[k - 1]) for k in range(1, groups)]
        )
        self.along.append(
            [mover.remote(three, dp_in.at[k - 1], over_dp[k - 1]) for k in range(1, dp)]
        )

    @staticmethod
    def count(dp, ctx, arrays):
        return (arrays + 1) * (1 + ctx // 2 - 1 + dp - 1)

    @staticmethod
    def scratch(dp, ctx, sources, small):
        groups = ctx // 2
        shapes = []
        for s in sources:
            block = s.shape[-2:]
            shapes += [
                pltpu.VMEM((dp, groups) + block, BF),
                pltpu.VMEM((dp, groups) + block if len(s.shape) == 5 else (8, 128), BF),
                pltpu.VMEM((groups - 1, dp) + block, BF),
                pltpu.VMEM((dp,) + block, BF),
                pltpu.VMEM((dp - 1,) + block, BF),
            ]
        shape = small.shape
        shapes += [pltpu.VMEM(shape, F32)] * 3
        shapes += [
            pltpu.VMEM((groups - 1,) + shape, F32),
            pltpu.VMEM(shape, F32),
            pltpu.VMEM((dp - 1,) + shape, F32),
        ]
        return shapes

    def begin_small(self):
        self.small_buffers[0][...] = self.small[...]
        self.pair[-1][0].start()

    def begin(self, index):
        for copy in self.pair[index] or self.across[index]:
            copy.start()
        self.own[index].start()

    def first(self, index):
        mine, other = self.buffers[index][:2]
        groups = self.groups
        self.own[index].wait()
        if not self.pair[index]:
            return
        self.pair[index][0].wait_recv()

        def add(i, carry):
            at = (i // groups, i % groups)
            mine[at] = mine[at] + other[at]
            return carry

        lax.fori_loop(0, self.dp * groups, add, 0)
        for copy in self.across[index]:
            copy.start()

    def first_small(self):
        one, came, two = self.small_buffers[:3]
        self.pair[-1][0].wait_recv()
        two[...] = one[...] + came[...]
        for copy in self.across[-1]:
            copy.start()

    def middle(self, index):
        mine, _, came, sums, _ = self.buffers[index]
        for copy in self.across[index]:
            copy.wait_recv()

        def add(k, carry):
            total = mine[k, self.g].astype(F32)
            for j in range(self.groups - 1):
                total = total + came[j, k].astype(F32)
            sums[k] = total.astype(BF)
            return carry

        lax.fori_loop(0, self.dp, add, 0)
        for copy in self.along[index]:
            copy.start()

    def middle_small(self):
        _, _, two, groups_in, three, _ = self.small_buffers
        for copy in self.across[-1]:
            copy.wait_recv()
        total = two[...]
        for j in range(self.groups - 1):
            total = total + groups_in[j]
        three[...] = total
        for copy in self.along[-1]:
            copy.start()

    def finish(self):
        for index, out in enumerate(self.outs):
            sums, last = self.buffers[index][3:]
            for copy in self.along[index]:
                copy.wait_recv()
            total = sums[self.d].astype(F32)
            for j in range(self.dp - 1):
                total = total + last[j].astype(F32)
            out[...] = total
        three, dp_in = self.small_buffers[4:]
        for copy in self.along[-1]:
            copy.wait_recv()
        total = three[...]
        for j in range(self.dp - 1):
            total = total + dp_in[j]
        self.small_out[...] = total
        for batch in self.pair + self.across + self.along:
            for copy in batch:
                copy.wait_send()


class Exchange:
    def __init__(self, ctx, mover, source, target):
        d, c = lax.axis_index("dp"), lax.axis_index("ctx")
        groups = ctx // 2
        self.steps = []
        for t in range(groups):
            group = flip(c // 2, t, groups)
            same, other = group * 2 + c % 2, group * 2 + 1 - c % 2
            if t == 0:
                self.own = mover.local(source.at[c], target.at[c])
                batch = []
            else:
                batch = [mover.remote(source.at[same], target.at[c], (d, same))]
            batch.append(mover.remote(source.at[other], target.at[c], (d, other)))
            self.steps.append(batch)

    @staticmethod
    def count(ctx):
        return ctx - 1

    def start(self, t):
        if t == 0:
            self.own.start()
        for copy in self.steps[t]:
            copy.start()

    def arrive(self, t):
        if t == 0:
            self.own.wait()
        for copy in self.steps[t]:
            copy.wait_recv()

    def sent(self):
        for batch in self.steps:
            for copy in batch:
                copy.wait_send()


def columns(values):
    return jnp.sum(values, axis=0, keepdims=True)


def finish_kernel(dp, ctx, *refs):
    (xb, dq, dk, dv, w, grad_sum), refs = refs[:6], refs[6:]
    outs, small_out, x_out, refs = refs[:3], refs[3], refs[4], refs[5:]
    grads, result, small, refs = refs[:3], refs[3], refs[4], refs[5:]
    buffers, small_buffers, (local_sem, send_sem, recv_sem) = refs[:15], refs[15:21], refs[21:]
    d, c = lax.axis_index("dp"), lax.axis_index("ctx")
    groups = ctx // 2
    g = c // 2
    half, width = result.shape[1:]
    held = grads[0].shape[3]
    mover = Mover(local_sem, send_sem, recv_sem)
    scatter = Scatter(
        dp,
        ctx,
        grads,
        outs,
        [buffers[i * 5 : i * 5 + 5] for i in range(3)],
        small,
        small_out,
        small_buffers,
        mover,
    )
    give = Exchange(ctx, mover, result, x_out)
    greet([((d + k) % dp, c) for k in range(1, dp)] + [(d, (c + k) % ctx) for k in range(1, ctx)])
    small[...] = jnp.zeros_like(small)
    small[0:1, :] = columns(dq[...].astype(F32))
    small[1:2, :] = columns(dv[...].astype(F32))
    scatter.begin_small()

    across = xb[...].T

    def weight_gradient(index, rows_grad):
        total = dg(across, rows_grad[...], NN)
        for block in range(dp * ctx):
            at = (block // ctx, block % ctx // 2, block % 2)
            grads[index][at] = total[block * held : (block + 1) * held].astype(BF)
        scatter.begin(index)

    def row_tile(t):
        block = flip(g, t, groups)
        rows = pl.ds(pl.multiple_of(block * 2 * half, 2 * half), 2 * half)
        total = grad_sum[rows, :]
        for i, rows_grad in enumerate((dq, dk, dv)):
            total = total + dg(rows_grad[rows, :], w[:, i * width : (i + 1) * width], NT)
        result[pl.ds(block * 2, 2)] = total.astype(BF).reshape(2, half, width)
        give.start(t)

    tiles = list(range(groups - 1, -1, -1))
    for index, rows_grad in enumerate((dq, dk, dv)):
        weight_gradient(index, rows_grad)
        row_tile(tiles.pop(0))
        if index == 0:
            scatter.first_small()
        scatter.first(index)
    for t in tiles:
        row_tile(t)
    scatter.middle_small()
    for index in range(3):
        scatter.middle(index)
    scatter.finish()
    for t in range(groups):
        give.arrive(t)
    give.sent()


def finish_gradients(xb, dq, dk, dv, w, grad_sum, dp, ctx):
    rows, width = xb.shape
    remotes = Scatter.count(dp, ctx, 3) + Exchange.count(ctx)
    S = jax.ShapeDtypeStruct
    vmem = pl.BlockSpec(memory_space=pltpu.VMEM)
    source = S((dp, ctx // 2, 2, width // (dp * ctx), width), BF)
    small = S((8, width), F32)
    moved = (ctx, rows // ctx, width)
    return pl.pallas_call(
        functools.partial(finish_kernel, dp, ctx),
        in_specs=[vmem] * 6,
        out_specs=[vmem] * 4 + [pl.BlockSpec(memory_space=pl.ANY)],
        out_shape=[S(source.shape[3:], F32)] * 3 + [small, S(moved, BF)],
        scratch_shapes=[pltpu.VMEM(source.shape, BF)] * 3
        + [pltpu.VMEM(moved, BF), pltpu.VMEM(small.shape, F32)]
        + Scatter.scratch(dp, ctx, [source] * 3, small)
        + [
            pltpu.SemaphoreType.DMA((4,)),
            pltpu.SemaphoreType.DMA((remotes,)),
            pltpu.SemaphoreType.DMA((remotes,)),
        ],
        compiler_params=pltpu.CompilerParams(
            collective_id=3, has_side_effects=True, vmem_limit_bytes=VMEM_BYTES
        ),
        name="finish_gradients",
    )(xb, dq, dk, dv, w, grad_sum)


def head_lanes(shape, h):
    lane = lax.broadcasted_iota(jnp.int32, shape, len(shape) - 1)
    return (lane >= 64) == (h == 1), lane == (64 if h == 0 else 0)


def load_keys(keys, own_ref, sib_ref, lengths_ref, ctx):
    c = lax.axis_index("ctx")
    rows = own_ref.shape[0]
    half = rows // ctx
    length = lengths_ref[lax.axis_index("dp") * (ctx // 2) + c // 2]
    slot = lax.broadcasted_iota(jnp.int32, (rows, 128), 0)
    source = lax.broadcasted_iota(jnp.int32, (ctx, half, 128), 0).reshape(rows, 128)
    high = (2 * ctx - 1 - 2 * source) * half + slot
    for i, ref in enumerate((own_ref, sib_ref)):
        member = c % 2 if i == 0 else 1 - c % 2
        counted = jnp.where(member == 0, slot, high) < length
        for h in range(2):
            inside, spare = head_lanes((rows, 128), h)
            rest = jnp.where(spare & ~counted, masked_score, 0.0).astype(BF)
            keys[h, i * rows : (i + 1) * rows, :] = jnp.where(inside, ref[...], rest)


def forward_kernel(dp, ctx, bq, *refs):
    (x_ref, w_ref, vec_ref, lengths_ref), gathered, refs = refs[:4], refs[4:7], refs[7:]
    (mb_ref, mix_ref, lse_ref, own_to, sib_to), spread_to, refs = refs[:5], refs[5:8], refs[8:]
    keys, own, sib, local_sem, send_sem, recv_sem, pair_send, pair_recv, store_sem = refs
    spread = Spread(dp, ctx, gathered, spread_to, Mover(local_sem, send_sem, recv_sem))
    pairs, steps = pl.num_programs(0), pl.num_programs(1)
    pair, j = pl.program_id(0), pl.program_id(1)
    step = pair * steps + j
    last = forward_steps(pairs, steps)
    half, width = x_ref.shape

    def to_sibling(number):
        return pltpu.make_async_remote_copy(
            src_ref=own.at[number, pl.ds(1, 2)],
            dst_ref=sib.at[number],
            send_sem=pair_send.at[number],
            recv_sem=pair_recv.at[number],
            device_id=spread.devices[-1],
            device_id_type=MESH,
        )

    def stores(number):
        return [
            pltpu.make_async_copy(own.at[number], own_to.at[number], store_sem.at[number, 0]),
            pltpu.make_async_copy(sib.at[number], sib_to.at[number], store_sem.at[number, 1]),
        ]

    def project(number):
        lanes = [pl.ds(pl.multiple_of(number * 128 + i * width, 128), 128) for i in range(3)]
        weights = jnp.concatenate([w_ref[:, part] for part in lanes], axis=1)
        rows = dg(x_ref[...], weights, NN)
        own[number, 0] = (rows[:, :128] + vec_ref[0:1, lanes[0]]).astype(BF)
        own[number, 1] = rows[:, 128:256].astype(BF)
        own[number, 2] = (rows[:, 256:] + vec_ref[1:2, lanes[0]]).astype(BF)
        to_sibling(number).start()

    @pl.when(step == 0)
    def _():
        greet(spread.devices)
        spread.begin()
        project(pair)

    @pl.when(j == 0)
    def _():
        to_sibling(pair).wait_recv()
        for copy in stores(pair):
            copy.start()
        load_keys(keys, own.at[pair, 1], sib.at[pair, 0], lengths_ref, ctx)

    @pl.when((j == 1) & (pair < pairs - 1))
    def _():
        project(pair + 1)

    rows = pl.ds(pl.multiple_of(j * bq, bq), bq)
    q = own[pair, 0, rows, :] * jnp.asarray(0.125, BF)
    scores = []
    for h in range(2):
        inside, spare = head_lanes((bq, 128), h)
        rest = jnp.where(spare, jnp.ones((), BF), jnp.zeros((), BF))
        scores.append(dg(jnp.where(inside, q, rest), keys[h], NT))
    outs, lses = [], []
    for h in range(2):
        top = jnp.max(scores[h], axis=1, keepdims=True)
        weights = jnp.exp(scores[h] - top)
        total = jnp.sum(weights, axis=1, keepdims=True)
        low = weights.astype(BF)
        mixed = dg(low[:, :half], own[pair, 2], NN) + dg(low[:, half:], sib[pair, 1], NN)
        outs.append(mixed / total)
        lses.append(top + jnp.log(total))
    lane = lax.broadcasted_iota(jnp.int32, (bq, 128), 1)
    mixed = jnp.where(lane < 64, outs[0], outs[1])
    mix_ref[...] = mixed
    mb_ref[...] = mixed.astype(BF)
    lse_ref[0] = jnp.where(lane == 0, lses[0], lses[1]).T[:8]

    for index, ats in enumerate(last):
        for level in range(1, spread.levels + 1):

            @pl.when(step == ats[0] + (ats[1] - ats[0]) * (level - 1) // (spread.levels - 1))
            def _(index=index, level=level):
                spread.forward(index, level)

    @pl.when(step == pairs * steps - 1)
    def _():
        spread.finish()
        for number in range(pairs):
            to_sibling(number).wait_send()
            for copy in stores(number):
                copy.wait()


def attention_forward(x, w, vec, lengths, gathered, dp, ctx, bq=256):
    rows, width = x.shape
    pairs = width // 128
    S = jax.ShapeDtypeStruct
    blk = pl.BlockSpec((bq, 128), lambda p, j: (j, p))
    any_space = pl.BlockSpec(memory_space=pl.ANY)
    vmem = pl.BlockSpec(memory_space=pltpu.VMEM)
    remotes = Spread.count(ctx, 3)
    return pl.pallas_call(
        functools.partial(forward_kernel, dp, ctx, bq),
        grid=(pairs, rows // bq),
        in_specs=[vmem] * 3 + [pl.BlockSpec(memory_space=pltpu.SMEM)] + [any_space] * 3,
        out_specs=[blk, blk, pl.BlockSpec((1, 8, bq), lambda p, j: (p, 0, j))] + [any_space] * 5,
        out_shape=[S(x.shape, BF), S(x.shape, F32), S((pairs, 8, rows), F32)]
        + [S((pairs, count, rows, 128), BF) for count in (3, 2)]
        + [S((dp, ctx) + array.shape[1:], BF) for array in gathered],
        scratch_shapes=[
            pltpu.VMEM((2, 2 * rows, 128), BF),
            pltpu.VMEM((pairs, 3, rows, 128), BF),
            pltpu.VMEM((pairs, 2, rows, 128), BF),
            pltpu.SemaphoreType.DMA((3,)),
            pltpu.SemaphoreType.DMA((remotes,)),
            pltpu.SemaphoreType.DMA((remotes,)),
            pltpu.SemaphoreType.DMA((pairs,)),
            pltpu.SemaphoreType.DMA((pairs,)),
            pltpu.SemaphoreType.DMA((pairs, 2)),
        ],
        compiler_params=pltpu.CompilerParams(
            vmem_limit_bytes=VMEM_BYTES, collective_id=1, has_side_effects=True
        ),
        cost_estimate=pl.CostEstimate(
            flops=16 * rows * rows * 128 * pairs,
            bytes_accessed=14 * rows * 768,
            transcendentals=4 * rows * rows * pairs,
        ),
        name="attend",
    )(x, w, vec, lengths, *gathered)


def forward_steps(pairs, steps):
    count = pairs * steps
    return [(count * a // 24, count * b // 24) for a, b in ((11, 18), (12, 19), (13, 20))]


def backward_steps(pairs, steps):
    count = pairs * steps
    first = [count * at // 12 for at in (0, 0, 1)]
    middle = [count * at // 12 for at in (5, 4, 8)]
    return first, middle


def backward_kernel(dp, ctx, ck, *refs):
    (q_ref, ko_ref, vo_ref, ks_ref, vs_ref, do_ref, mix_ref, lengths_ref, lse_ref), refs = (
        refs[:9],
        refs[9:],
    )
    q_ref, ko_ref, vo_ref, ks_ref, vs_ref = (
        ref.at[0, 0] for ref in (q_ref, ko_ref, vo_ref, ks_ref, vs_ref)
    )
    sources, small, refs = refs[:3], refs[3], refs[4:]
    (dq_ref, dk_ref, dv_ref), refs = refs[:3], refs[3:]
    summed, small_out, refs = refs[:3], refs[3], refs[4:]
    (keys, dk, dv, held, going, coming), refs = refs[:6], refs[6:]
    buffers, small_buffers, refs = refs[:15], refs[15:21], refs[21:]
    local_sem, send_sem, recv_sem, pair_send, pair_recv = refs
    scatter = Scatter(
        dp,
        ctx,
        sources,
        summed,
        [buffers[i * 5 : i * 5 + 5] for i in range(3)],
        small,
        small_out,
        small_buffers,
        Mover(local_sem, send_sem, recv_sem),
    )
    steps = pl.num_programs(1)
    j = pl.program_id(1)
    step = pl.program_id(0) * steps + j

    pair = pl.program_id(0)
    sibling = scatter.devices[-1]

    def to_sibling(number):
        return [
            pltpu.make_async_remote_copy(
                src_ref=going.at[number, i],
                dst_ref=coming.at[number, i],
                send_sem=pair_send.at[number * 2 + i],
                recv_sem=pair_recv.at[number * 2 + i],
                device_id=sibling,
                device_id_type=MESH,
            )
            for i in range(2)
        ]

    def settle(number):
        lanes = pl.ds(pl.multiple_of(number * 128, 128), 128)
        for i, (copy, out) in enumerate(zip(to_sibling(number), (dk_ref, dv_ref))):
            copy.wait_recv()
            total = held[number % 2, i] + coming[number, i].astype(F32)
            out[:, lanes] = total.astype(BF)

    @pl.when(step == 0)
    def _():
        greet(scatter.devices)
        scatter.begin(1)
        scatter.begin_small()
        scatter.begin(0)
        scatter.begin(2)

    @pl.when((j == 0) & (pair > 0))
    def _():
        settle(pair - 1)

    @pl.when(j == 0)
    def _():
        load_keys(keys, ko_ref, ks_ref, lengths_ref, ctx)
        dk[...] = jnp.zeros_like(dk)
        dv[...] = jnp.zeros_like(dv)

    half, bq = ko_ref.shape[0], q_ref.shape[0]
    q = q_ref[...] * jnp.asarray(0.125, BF)
    do = do_ref[...]
    prod = (do.astype(F32) * mix_ref[...]).T
    zero, one = jnp.zeros((), BF), jnp.ones((), BF)
    heads = []
    for h in range(2):
        inside, spare = head_lanes((bq, 128), h)
        heads.append(
            (
                jnp.where(inside, q, jnp.where(spare, one, zero)),
                jnp.where(inside, q, zero),
                jnp.where(inside, do, zero),
                lse_ref[0, h : h + 1, :],
                jnp.sum(prod[h * 64 : (h + 1) * 64], axis=0, keepdims=True),
            )
        )
    dq = jnp.zeros((bq, 128), F32)
    for first in range(0, 2 * half, ck):
        rows = slice(first, first + ck)
        v = vo_ref[rows, :] if first < half else vs_ref[first - half : first - half + ck, :]
        for h in range(2):
            qm, qz, dom, lse, delta = heads[h]
            k = keys[h, rows, :]
            p = jnp.exp(dg(k, qm, NT) - lse)
            ds = (p * (dg(v, dom, NT) - delta)).astype(BF)
            dv[rows, :] += dg(p.astype(BF), dom, NN)
            dk[rows, :] += dg(ds, qz, NN)
            dq = dq + dg(ds, k, TN)
    dq_ref[...] = (dq * 0.125).astype(BF)

    @pl.when(j == steps - 1)
    def _():
        for i, total in enumerate((dk, dv)):
            held[pair % 2, i] = total[:half, :]
            going[pair, i] = total[half:, :].astype(BF)
        for copy in to_sibling(pair):
            copy.start()

    first, middle_at = backward_steps(pl.num_programs(0), steps)

    @pl.when(step == first[0])
    def _():
        scatter.first_small()

    @pl.when(step == middle_at[0])
    def _():
        scatter.middle_small()

    for index in range(3):

        @pl.when(step == first[index])
        def _(index=index):
            scatter.first(index)

        @pl.when(step == middle_at[index])
        def _(index=index):
            scatter.middle(index)

    @pl.when(step == pl.num_programs(0) * steps - 1)
    def _():
        scatter.finish()
        settle(pair)
        for number in range(pl.num_programs(0)):
            for copy in to_sibling(number):
                copy.wait_send()


def attention_backward(own, sib, do, mix, lengths, lse, sources, small, dp, ctx, bq=512, ck=512):
    rows, width = do.shape
    pairs = width // 128
    S = jax.ShapeDtypeStruct
    blk = pl.BlockSpec((bq, 128), lambda p, j: (j, p))
    whole_of = [
        pl.BlockSpec((1, 1, rows, 128), lambda p, j, i=i: (p, i, 0, 0)) for i in (1, 2, 0, 1)
    ]
    any_space = pl.BlockSpec(memory_space=pl.ANY)
    remotes = Scatter.count(dp, ctx, 3)
    whole = pl.BlockSpec(small.shape, lambda p, j: (0, 0))
    sums = [s.shape[-2:] for s in sources]
    all_rows = pl.BlockSpec((rows, width), lambda p, j: (0, 0))
    return pl.pallas_call(
        functools.partial(backward_kernel, dp, ctx, ck),
        grid=(pairs, rows // bq),
        in_specs=[pl.BlockSpec((1, 1, bq, 128), lambda p, j: (p, 0, j, 0))]
        + whole_of
        + [blk, blk]
        + [pl.BlockSpec(memory_space=pltpu.SMEM)]
        + [pl.BlockSpec((1, 8, bq), lambda p, j: (p, 0, j))]
        + [any_space] * 3
        + [whole],
        out_specs=[blk, all_rows, all_rows]
        + [pl.BlockSpec(shape, lambda p, j: (0, 0)) for shape in sums]
        + [whole],
        out_shape=[S(do.shape, BF)] * 3
        + [S(shape, F32) for shape in sums]
        + [S(small.shape, F32)],
        scratch_shapes=[
            pltpu.VMEM((2, 2 * rows, 128), BF),
            pltpu.VMEM((2 * rows, 128), F32),
            pltpu.VMEM((2 * rows, 128), F32),
            pltpu.VMEM((2, 2, rows, 128), F32),
            pltpu.VMEM((pairs, 2, rows, 128), BF),
            pltpu.VMEM((pairs, 2, rows, 128), BF),
        ]
        + Scatter.scratch(dp, ctx, sources, small)
        + [
            pltpu.SemaphoreType.DMA((3,)),
            pltpu.SemaphoreType.DMA((remotes,)),
            pltpu.SemaphoreType.DMA((remotes,)),
            pltpu.SemaphoreType.DMA((2 * pairs,)),
            pltpu.SemaphoreType.DMA((2 * pairs,)),
        ],
        compiler_params=pltpu.CompilerParams(
            vmem_limit_bytes=VMEM_BYTES, collective_id=2, has_side_effects=True
        ),
        cost_estimate=pl.CostEstimate(
            flops=40 * rows * rows * 128 * pairs,
            bytes_accessed=26 * rows * 768,
            transcendentals=4 * rows * rows * pairs,
        ),
        name="attend_back",
    )(own, own, own, sib, sib, do, mix, lengths, lse, *sources, small)


def gelu_and_slope(x):
    t = 1.0 / (1.0 + 0.2316419 * jnp.abs(x))
    bell = 0.3989422804 * jnp.exp(-0.5 * x * x)
    poly = 1.330274429 * t - 1.821255978
    poly = poly * t + 1.781477937
    poly = poly * t - 0.356563782
    poly = poly * t + 0.319381530
    tail = bell * (poly * t)
    below = jnp.where(x < 0.0, tail, 1.0 - tail)
    return x * below, below + x * bell


def middle_kernel(dp, ctx, *refs):
    (mb, xb, rest_src, up_src, vec, bias_up, wo_src, wu_src, wd_src), refs = refs[:9], refs[9:]
    (dm, grad_sum, out_to, go_to, gu_to, gd_to, small), refs = refs[:7], refs[7:]
    (wo, wu, wd, rest, upstream, result, active, dinner, slope, fb, db, da), refs = (
        refs[:12],
        refs[12:],
    )
    (other, summed), refs = refs[:2], refs[2:]
    load_sem, local_sem, send_sem, recv_sem = refs
    groups = ctx // 2
    g = lax.axis_index("ctx") // 2
    half, width = result.shape[1:]
    tile = 2 * half
    chunks = range(wu.shape[1] // width)
    step = pl.program_id(0)
    mover = Mover(local_sem, send_sem, recv_sem)
    rest_in = Exchange(ctx, mover, rest_src, rest)
    up_in = Exchange(ctx, mover, up_src, upstream)
    give = Exchange(ctx, mover, result, out_to)
    loads = [
        pltpu.make_async_copy(source, target, load_sem.at[i])
        for i, (source, target) in enumerate(((wo_src, wo), (wu_src, wu), (wd_src, wd)))
    ]
    stores = [
        pltpu.make_async_copy(source, target, load_sem.at[i])
        for i, (source, target) in enumerate(((wo, go_to), (wu, gu_to), (summed, gd_to)))
    ]
    d, c = lax.axis_index("dp"), lax.axis_index("ctx")
    held = other.shape[2]

    def block_rows(i, k, member):
        return pl.ds(pl.multiple_of(((i * groups + k) * 2 + member) * held, 8), held)

    blocks = [(i, k) for i in range(dp) for k in range(groups)]
    to_sibling = [
        mover.remote(wd.at[block_rows(i, k, 1 - c % 2)], other.at[i, k], (d, g * 2 + 1 - c % 2))
        for i, k in blocks
    ]

    def load(index):
        @pl.when(step == 0)
        def _():
            loads[index].wait()

    @pl.when(step == 0)
    def _():
        for copy in loads:
            copy.start()
        greet([(d, (c + k) % ctx) for k in range(1, ctx)])
        for t in range(groups):
            rest_in.start(t)
            up_in.start(t)
        small[...] = jnp.zeros_like(small)

    @pl.when(step < groups)
    def _():
        block = flip(g, step, groups)
        rows = pl.ds(pl.multiple_of(block * tile, tile), tile)
        pair = pl.ds(block * 2, 2)
        load(0)
        hidden = dg(mb[rows, :], wo[...], NN) + vec[2:3, :] + xb[rows, :].astype(F32)
        for t in range(groups):

            @pl.when(step == t)
            def _(t=t):
                rest_in.arrive(t)

        hidden = hidden + rest[pair].reshape(tile, width).astype(F32)
        normed, standard_one, inverse_one = normalize(hidden, vec[6:7, :], vec[4:5, :])
        low = normed.astype(BF)
        fb[rows, :] = low
        load(1)
        parts = [slice(i * width, (i + 1) * width) for i in chunks]
        inner = dg(low, wu[:, parts[0]], NN)
        for i, part in enumerate(parts):
            ahead = dg(low, wu[:, parts[i + 1]], NN) if i + 1 < len(parts) else None
            value, slope[:, part] = gelu_and_slope(inner + bias_up[:, part])
            active[rows, part] = value.astype(BF)
            inner = ahead
        load(2)
        hidden = normed + dg(active[rows, :], wd[...], NN) + vec[3:4, :]
        out, standard, inverse = normalize(hidden, vec[7:8, :], vec[5:6, :])
        result[pair] = out.astype(BF).reshape(2, half, width)
        for t in range(groups):

            @pl.when(step == t)
            def _(t=t):
                give.start(t)
                up_in.arrive(t)

        error = upstream[pair].reshape(tile, width).astype(F32)
        grad = normalize_back(error, standard, inverse, vec[7:8, :])
        low_grad = grad.astype(BF)
        db[rows, :] = low_grad
        small[1:2, :] += columns(low_grad.astype(F32))
        small[3:4, :] += columns(error)
        small[5:6, :] += columns(error * standard)
        for i in chunks:
            part = slice(i * width, (i + 1) * width)
            change = dg(low_grad, wd[part, :], NT) * slope[:, part]
            change = change.astype(BF)
            dinner[rows, part] = change
            small[6 + i : 7 + i, :] += columns(change.astype(F32))
        grad = grad + dg(dinner[rows, :], wu[...], NT)
        small[2:3, :] += columns(grad)
        small[4:5, :] += columns(grad * standard_one)
        grad = normalize_back(grad, standard_one, inverse_one, vec[6:7, :])
        grad_sum[rows, :] = grad
        low_grad = grad.astype(BF)
        da[rows, :] = low_grad
        small[0:1, :] += columns(low_grad.astype(F32))
        dm[rows, :] = dg(low_grad, wo[...], NT).astype(BF)

    @pl.when(step == groups)
    def _():
        for i in chunks:
            part = slice(i * width, (i + 1) * width)
            wd[part, :] = dg(active[:, part], db[...], TN).astype(BF)
        for copy in to_sibling:
            copy.start()
        across = fb[...].T
        for i in chunks:
            part = slice(i * width, (i + 1) * width)
            wu[:, part] = dg(across, dinner[:, part], NN).astype(BF)
        stores[1].start()
        for copy in to_sibling:
            copy.wait()
        for i, k in blocks:
            summed[i, k] = wd[block_rows(i, k, c % 2), :] + other[i, k]
        stores[2].start()
        wo[...] = dg(mb[...], da[...], TN).astype(BF)
        stores[0].start()
        for t in range(groups):
            give.arrive(t)
        for move in (rest_in, up_in, give):
            move.sent()
        for copy in stores:
            copy.wait()


def middle(mb, xb, rest, upstream, vec, bias_up, wo, wu, wd, dp, ctx):
    rows, width = mb.shape
    hidden = wu.shape[1]
    half = rows // ctx
    S = jax.ShapeDtypeStruct
    any_space = pl.BlockSpec(memory_space=pl.ANY)
    vmem = pl.BlockSpec(memory_space=pltpu.VMEM)
    held = (dp, ctx // 2, hidden // (dp * ctx), width)
    remotes = 3 * Exchange.count(ctx) + dp * (ctx // 2)
    return pl.pallas_call(
        functools.partial(middle_kernel, dp, ctx),
        grid=(ctx // 2 + 1,),
        in_specs=[vmem, vmem, any_space, any_space, vmem, vmem] + [any_space] * 3,
        out_specs=[vmem, vmem] + [any_space] * 4 + [vmem],
        out_shape=[S(mb.shape, BF), S(mb.shape, F32), S(rest.shape, BF)]
        + [S(wo.shape, BF), S(wu.shape, BF), S(held, BF)]
        + [S((16, width), F32)],
        scratch_shapes=[pltpu.VMEM(array.shape, BF) for array in (wo, wu, wd)]
        + [pltpu.VMEM(rest.shape, BF)] * 3
        + [pltpu.VMEM((rows, hidden), BF)] * 2
        + [pltpu.VMEM((2 * half, hidden), F32)]
        + [pltpu.VMEM((rows, width), BF)] * 3
        + [pltpu.VMEM(held, BF)] * 2
        + [
            pltpu.SemaphoreType.DMA((3,)),
            pltpu.SemaphoreType.DMA((3,)),
            pltpu.SemaphoreType.DMA((remotes,)),
            pltpu.SemaphoreType.DMA((remotes,)),
        ],
        compiler_params=pltpu.CompilerParams(
            vmem_limit_bytes=VMEM_BYTES, collective_id=4, has_side_effects=True
        ),
        cost_estimate=pl.CostEstimate(
            flops=2 * 3 * rows * width * (2 * hidden + width),
            bytes_accessed=50 << 20,
            transcendentals=rows * hidden,
        ),
        name="middle",
    )(mb, xb, rest, upstream, vec, bias_up, wo, wu, wd)


def normalize(hidden, scale_row, shift_row):
    centred = hidden - jnp.mean(hidden, axis=-1, keepdims=True)
    inverse = lax.rsqrt(jnp.mean(centred * centred, axis=-1, keepdims=True) + epsilon)
    standard = centred * inverse
    return (standard * scale_row + shift_row, standard, inverse)


def normalize_back(gradient, standard, inverse, scale_row):
    scaled = gradient * scale_row
    centred = scaled - jnp.mean(scaled, axis=-1, keepdims=True)
    return (centred - standard * jnp.mean(scaled * standard, axis=-1, keepdims=True)) * inverse


def write_kernel(dp, ctx, small_ref, sums_ref, out_ref, tokens_ref, *refs):
    sources, (out_to, tokens_to), refs = refs[:6], refs[6:8], refs[8:]
    targets, (vectors_to, bias_to) = refs[:6], refs[6:]
    out_to[...] = out_ref[...].astype(F32)
    tokens_to[...] = tokens_ref[...].astype(F32)

    @pl.when(pl.program_id(0) == 0)
    def _():
        for source, target in zip(sources, targets):
            target[...] = source[...]
        device = lax.axis_index("dp") * ctx + lax.axis_index("ctx")
        width = small_ref.shape[1]
        held, held_up = vectors_to.shape[1], bias_to.shape[1]
        rows = jnp.concatenate([sums_ref[0:2, :], small_ref[0:6, :]], axis=0)
        vectors_to[...] = pltpu.roll(rows, (width - device * held) % width, 1)[:, :held]
        first = device * held_up
        row = small_ref[pl.ds(6 + first // width, 1), :]
        row = jnp.broadcast_to(row, (8, width))
        bias_to[...] = pltpu.roll(row, (width - first % width) % width, 1)[0:1, :held_up]


def write_out(small, sums, out, tokens, own, held_up, dp, ctx):
    block = pl.BlockSpec((2,) + out.shape[1:], lambda i: (i, 0, 0))
    S = jax.ShapeDtypeStruct

    def whole(shape):
        return pl.BlockSpec(shape, lambda i: (0, 0))

    shapes = [array.shape for array in own]
    vectors = (8, out.shape[2] // (dp * ctx))
    return pl.pallas_call(
        functools.partial(write_kernel, dp, ctx),
        grid=(ctx // 2,),
        in_specs=[whole(small.shape), whole(sums.shape), block, block]
        + [whole(shape) for shape in shapes],
        out_specs=[block, block]
        + [whole(shape) for shape in shapes]
        + [whole(vectors), whole((1, held_up))],
        out_shape=[S(out.shape, F32)] * 2
        + [S(shape, F32) for shape in shapes]
        + [S(vectors, F32), S((1, held_up), F32)],
        compiler_params=pltpu.CompilerParams(vmem_limit_bytes=VMEM_BYTES),
        name="write_out",
    )(small, sums, out, tokens, *own)


def on_device(
    tokens, cotangent, lengths, w_query, w_key, w_value, w_attn_out, w_up, b_up, w_down, vectors
):
    seqs, rows_dev, width = tokens.shape
    dp = lax.axis_size("dp")
    ctx = lax.axis_size("ctx")
    half = rows_dev // 2
    rows = half * ctx
    def by_owner(grad):
        return grad.reshape(dp, ctx // 2, 2, -1, grad.shape[1])

    split = tokens.reshape(ctx, half, width)
    held = w_query.shape[0]
    extra = jnp.concatenate([vectors.T, b_up.reshape(held, -1)], axis=1)
    extra = jnp.pad(extra, ((0, 0), (0, 128 - extra.shape[1])))
    low_in, left_out, upstream, full_first, *over_dp = gather_first(
        split,
        cotangent.reshape(ctx, half, width),
        jnp.concatenate([w_query, w_key, w_value, extra], axis=1),
        w_attn_out,
        w_up,
        w_down,
        dp,
        ctx,
    )
    low_in = low_in.reshape(rows, width)
    full_first = full_first.reshape(width, -1)
    vector_rows = full_first[:, 3 * width : 3 * width + 8].T.astype(F32)
    bias_columns = b_up.shape[0] // held
    full_bias_up = full_first[:, 3 * width + 8 : 3 * width + 8 + bias_columns].reshape(-1).astype(F32)
    low_mixed, mixed, lse, own, sib, full_attn, full_up, full_down = attention_forward(
        low_in, full_first, vector_rows, lengths, over_dp, dp, ctx
    )
    full_attn = full_attn.reshape(width, width)
    full_up = full_up.reshape(width, -1)
    full_down = full_down.reshape(-1, width)

    d_mixed, grad_sum, result, d_attn, d_up, part_down, small = middle(
        low_mixed,
        low_in,
        left_out,
        upstream,
        vector_rows,
        full_bias_up.reshape(1, -1),
        full_attn,
        full_up,
        full_down,
        dp,
        ctx,
    )
    dq, dk, dv, own_attn, own_down, own_up, small = attention_backward(
        own,
        sib,
        d_mixed,
        mixed,
        lengths,
        lse,
        [by_owner(d_attn), part_down, by_owner(d_up)],
        small,
        dp,
        ctx,
    )
    own_query, own_key, own_value, sums, grad_tokens = finish_gradients(
        low_in, dq, dk, dv, full_first, grad_sum, dp, ctx
    )
    output, grad_tokens, *own, own_vectors, own_bias_up = write_out(
        small,
        sums,
        result,
        grad_tokens,
        [own_query, own_key, own_value, own_attn, own_up, own_down],
        b_up.shape[0],
        dp,
        ctx,
    )
    own_query, own_key, own_value, own_attn, own_up, own_down = own
    output = output.reshape(seqs, rows_dev, width)
    grad_tokens = grad_tokens.reshape(seqs, rows_dev, width)
    own_bias_up = own_bias_up.reshape(-1)
    return (
        output,
        grad_tokens,
        own_query,
        own_key,
        own_value,
        own_attn,
        own_up,
        own_bias_up,
        own_down,
        own_vectors,
    )


def solution(mesh):
    in_specs = (
        P("dp", "ctx", None),
        P("dp", "ctx", None),
        P(),
        P(("dp", "ctx"), None),
        P(("dp", "ctx"), None),
        P(("dp", "ctx"), None),
        P(("dp", "ctx"), None),
        P(("dp", "ctx"), None),
        P(("dp", "ctx")),
        P(("dp", "ctx"), None),
        P(None, ("dp", "ctx")),
    )
    out_specs = (
        P("dp", "ctx", None),
        P("dp", "ctx", None),
        P(("dp", "ctx"), None),
        P(("dp", "ctx"), None),
        P(("dp", "ctx"), None),
        P(("dp", "ctx"), None),
        P(("dp", "ctx"), None),
        P(("dp", "ctx")),
        P(("dp", "ctx"), None),
        P(None, ("dp", "ctx")),
    )
    return jax.shard_map(
        on_device, mesh=mesh, in_specs=in_specs, out_specs=out_specs, check_vma=False
    )
```

```python
import functools
import jax
import jax.numpy as jnp
from jax import lax
from jax.experimental import pallas as pl
from jax.experimental.pallas import tpu as pltpu
from jax.sharding import PartitionSpec as P

HEAD_DIM = 64
F32 = jnp.float32
BF = jnp.bfloat16
NN = (((1,), (0,)), ((), ()))
NT = (((1,), (1,)), ((), ()))
TN = (((0,), (0,)), ((), ()))
epsilon = 1e-12
masked_score = -1e30
VMEM_BYTES = 58 << 20


def dg(left, right, dims):
    return lax.dot_general(left, right, dims, preferred_element_type=F32)


MESH = pl.DeviceIdType.MESH


class Mover:
    def __init__(self, local_sem, send_sem, recv_sem):
        self.local_sem, self.send_sem, self.recv_sem = local_sem, send_sem, recv_sem
        self.locals = self.remotes = 0

    def local(self, source, target):
        copy = pltpu.make_async_copy(source, target, self.local_sem.at[self.locals])
        self.locals += 1
        return copy

    def remote(self, source, target, device):
        number = self.remotes
        self.remotes += 1
        return pltpu.make_async_remote_copy(
            src_ref=source,
            dst_ref=target,
            send_sem=self.send_sem.at[number],
            recv_sem=self.recv_sem.at[number],
            device_id=device,
            device_id_type=MESH,
        )


def greet(devices):
    barrier = pltpu.get_barrier_semaphore()
    for device in devices:
        pl.semaphore_signal(barrier, inc=1, device_id=device, device_id_type=MESH)
    pl.semaphore_wait(barrier, len(devices))


def place(dp, ctx):
    d, c = lax.axis_index("dp"), lax.axis_index("ctx")
    groups = ctx // 2
    g, m = c // 2, c % 2
    over_dp = [((d + k) % dp, c) for k in range(1, dp)]
    over_groups = [(d, (g + k) % groups * 2 + m) for k in range(1, groups)]
    return d, c, g, m, over_dp, over_groups, (d, g * 2 + 1 - m)


def flip(group, step, groups):
    total, bit = 0, 1
    while bit < groups:
        total = total + (group // bit + step // bit) % 2 * bit
        bit *= 2
    return total


class Spread:
    def __init__(self, dp, ctx, sources, targets, mover):
        d, c, g, m, over_dp, over_groups, sibling = place(dp, ctx)
        groups = ctx // 2
        bits = [1 << i for i in range(groups.bit_length() - 1)]
        self.levels = len(bits)
        self.devices = [(d, flip(g, bit, groups) * 2 + m) for bit in bits] + [sibling]
        self.own, self.copies, self.onward = [], [], []
        for source, target in zip(sources, targets):

            def column(mask):
                return flip(g, mask, groups) * 2 + m

            self.own.append([] if source is None else [mover.local(source, target.at[:, c])])
            source = target.at[:, c] if source is None else source
            copies = [[] for _ in range(self.levels + 1)]
            for start, order in ((0, bits), (dp // 2, bits[::-1])):
                part = pl.ds(start, dp // 2)
                for i, bit in enumerate(order):
                    for mask in range(groups):
                        if any(mask & other for other in order[i:]):
                            continue
                        place_in = target.at[part, column(mask)]
                        copies[bin(mask).count("1")].append(
                            mover.remote(
                                place_in if mask else source.at[part], place_in, (d, column(bit))
                            )
                        )
            self.copies.append(copies)
            onward = [[mover.remote(source, target.at[:, c], sibling)]]
            onward += [[] for _ in range(self.levels)]
            for mask in range(1, groups):
                block = target.at[:, column(mask)]
                onward[bin(mask).count("1")].append(mover.remote(block, block, sibling))
            self.onward.append(onward)

    @staticmethod
    def count(ctx, arrays):
        return arrays * (2 * (ctx // 2 - 1) + ctx // 2)

    def begin(self):
        for own, copies, onward in zip(self.own, self.copies, self.onward):
            for copy in copies[0] + own + onward[0]:
                copy.start()

    def forward(self, index, level):
        for copy in self.copies[index][level - 1]:
            copy.wait_recv()
        for copy in self.copies[index][level] + self.onward[index][level]:
            copy.start()

    def finish(self):
        for own, copies, onward in zip(self.own, self.copies, self.onward):
            for copy in own + sum(onward, []):
                copy.wait()
            for copy in sum(copies, []):
                copy.wait_send()


def gather_kernel(dp, ctx, *refs):
    (tokens, cotangent, w, wo, wu, wd), refs = refs[:6], refs[6:]
    (x_in, rest_to, up_to, w_full, zo, zu, zd), refs = refs[:7], refs[7:]
    wide, wide_up, x, rest, up, local_sem, send_sem, recv_sem, move_sem = refs
    d, c, g, m, over_dp, over_groups, sibling = place(dp, ctx)
    groups = ctx // 2
    moves = [
        pltpu.make_async_copy(source, target, move_sem.at[i])
        for i, (source, target) in enumerate(
            ((tokens, wide), (cotangent, wide_up), (rest, rest_to), (up, up_to))
        )
    ]
    moves[0].start()
    greet(over_dp + [(d, (c + k) % ctx) for k in range(1, ctx)])
    mover = Mover(local_sem, send_sem, recv_sem)
    own = [
        mover.local(source, target)
        for source, target in (
            (w, w_full.at[d, c]),
            (x.at[c], x_in.at[c]),
            (wo, zo.at[d]),
            (wu, zu.at[d]),
            (wd, zd.at[d]),
        )
    ]
    along = [mover.remote(w, w_full.at[d, c], device) for device in over_dp]
    rows = [
        mover.remote(x.at[(c + k) % ctx], x_in.at[c], (d, (c + k) % ctx)) for k in range(1, ctx)
    ]
    others = [
        mover.remote(source, target.at[d], device)
        for source, target in ((wo, zo), (wu, zu), (wd, zd))
        for device in over_dp
    ]
    spread = Spread(dp, ctx, [None], [w_full], mover)
    for copy in own[:1] + along:
        copy.start()
    moves[0].wait()
    moves[1].start()
    x[...] = wide[...].astype(BF)
    for copy in rows + own[1:]:
        copy.start()
    for copy in along:
        copy.wait_recv()
    own[0].wait()
    spread.begin()
    for copy in others:
        copy.start()
    rest[...] = (wide[...] - x[...].astype(F32)).astype(BF)
    moves[2].start()
    moves[1].wait()
    up[...] = wide_up[...].astype(BF)
    moves[3].start()
    for level in range(1, spread.levels + 1):
        spread.forward(0, level)
    for copy in rows + others + moves[2:] + own[1:]:
        copy.wait()
    spread.finish()
    for copy in along:
        copy.wait_send()


def gather_first(tokens, cotangent, w, wo, wu, wd, dp, ctx):
    remotes = (dp - 1) + Spread.count(ctx, 1) + (ctx - 1) + 3 * (dp - 1)
    any_space = pl.BlockSpec(memory_space=pl.ANY)
    return pl.pallas_call(
        functools.partial(gather_kernel, dp, ctx),
        in_specs=[any_space] * 6,
        out_specs=[any_space] * 7,
        out_shape=[jax.ShapeDtypeStruct(tokens.shape, BF)] * 3
        + [jax.ShapeDtypeStruct((dp, ctx) + w.shape, BF)]
        + [jax.ShapeDtypeStruct((dp,) + array.shape, BF) for array in (wo, wu, wd)],
        scratch_shapes=[pltpu.VMEM(tokens.shape, F32)] * 2
        + [pltpu.VMEM(tokens.shape, BF)] * 3
        + [
            pltpu.SemaphoreType.DMA((5,)),
            pltpu.SemaphoreType.DMA((remotes,)),
            pltpu.SemaphoreType.DMA((remotes,)),
            pltpu.SemaphoreType.DMA((4,)),
        ],
        compiler_params=pltpu.CompilerParams(
            collective_id=0, has_side_effects=True, vmem_limit_bytes=VMEM_BYTES
        ),
        name="gather_first",
    )(tokens, cotangent, w, wo, wu, wd)


class Scatter:
    def __init__(self, dp, ctx, sources, outs, buffers, small, small_out, small_buffers, mover):
        d, c, g, m, over_dp, over_groups, sibling = place(dp, ctx)
        groups = ctx // 2
        self.dp, self.groups, self.d, self.g = dp, groups, d, g
        self.devices = over_groups + over_dp + [sibling]
        self.outs = list(outs)
        self.buffers = buffers
        self.own, self.pair, self.across, self.along = [], [], [], []
        for source, (mine, other, came, sums, last) in zip(sources, buffers):
            summed = len(source.shape) == 4
            if summed:
                self.own.append(mover.local(source, mine))
                self.pair.append([])
            else:
                self.own.append(mover.local(source.at[:, :, m], mine))
                self.pair.append([mover.remote(source.at[:, :, 1 - m], other, sibling)])
            onward = source if summed else mine
            self.across.append(
                [
                    mover.remote(onward.at[:, (g + k) % groups], came.at[k - 1], over_groups[k - 1])
                    for k in range(1, groups)
                ]
            )
            self.along.append(
                [
                    mover.remote(sums.at[(d + k) % dp], last.at[k - 1], over_dp[k - 1])
                    for k in range(1, dp)
                ]
            )
        self.small, self.small_out = small, small_out
        one, came, two, groups_in, three, dp_in = small_buffers
        self.small_buffers = small_buffers
        self.pair.append([mover.remote(one, came, sibling)])
        self.across.append(
            [mover.remote(two, groups_in.at[k - 1], over_groups[k - 1]) for k in range(1, groups)]
        )
        self.along.append(
            [mover.remote(three, dp_in.at[k - 1], over_dp[k - 1]) for k in range(1, dp)]
        )

    @staticmethod
    def count(dp, ctx, arrays):
        return (arrays + 1) * (1 + ctx // 2 - 1 + dp - 1)

    @staticmethod
    def scratch(dp, ctx, sources, small):
        groups = ctx // 2
        shapes = []
        for s in sources:
            block = s.shape[-2:]
            shapes += [
                pltpu.VMEM((dp, groups) + block, BF),
                pltpu.VMEM((dp, groups) + block if len(s.shape) == 5 else (8, 128), BF),
                pltpu.VMEM((groups - 1, dp) + block, BF),
                pltpu.VMEM((dp,) + block, BF),
                pltpu.VMEM((dp - 1,) + block, BF),
            ]
        shape = small.shape
        shapes += [pltpu.VMEM(shape, F32)] * 3
        shapes += [
            pltpu.VMEM((groups - 1,) + shape, F32),
            pltpu.VMEM(shape, F32),
            pltpu.VMEM((dp - 1,) + shape, F32),
        ]
        return shapes

    def begin_small(self):
        self.small_buffers[0][...] = self.small[...]
        self.pair[-1][0].start()

    def begin(self, index):
        for copy in self.pair[index] or self.across[index]:
            copy.start()
        self.own[index].start()

    def first(self, index):
        mine, other = self.buffers[index][:2]
        groups = self.groups
        self.own[index].wait()
        if not self.pair[index]:
            return
        self.pair[index][0].wait_recv()

        def add(i, carry):
            at = (i // groups, i % groups)
            mine[at] = mine[at] + other[at]
            return carry

        lax.fori_loop(0, self.dp * groups, add, 0)
        for copy in self.across[index]:
            copy.start()

    def first_small(self):
        one, came, two = self.small_buffers[:3]
        self.pair[-1][0].wait_recv()
        two[...] = one[...] + came[...]
        for copy in self.across[-1]:
            copy.start()

    def middle(self, index):
        mine, _, came, sums, _ = self.buffers[index]
        for copy in self.across[index]:
            copy.wait_recv()

        def add(k, carry):
            total = mine[k, self.g].astype(F32)
            for j in range(self.groups - 1):
                total = total + came[j, k].astype(F32)
            sums[k] = total.astype(BF)
            return carry

        lax.fori_loop(0, self.dp, add, 0)
        for copy in self.along[index]:
            copy.start()

    def middle_small(self):
        _, _, two, groups_in, three, _ = self.small_buffers
        for copy in self.across[-1]:
            copy.wait_recv()
        total = two[...]
        for j in range(self.groups - 1):
            total = total + groups_in[j]
        three[...] = total
        for copy in self.along[-1]:
            copy.start()

    def finish(self):
        for index, out in enumerate(self.outs):
            sums, last = self.buffers[index][3:]
            for copy in self.along[index]:
                copy.wait_recv()
            total = sums[self.d].astype(F32)
            for j in range(self.dp - 1):
                total = total + last[j].astype(F32)
            out[...] = total
        three, dp_in = self.small_buffers[4:]
        for copy in self.along[-1]:
            copy.wait_recv()
        total = three[...]
        for j in range(self.dp - 1):
            total = total + dp_in[j]
        self.small_out[...] = total
        for batch in self.pair + self.across + self.along:
            for copy in batch:
                copy.wait_send()


class Exchange:
    def __init__(self, ctx, mover, source, target):
        d, c = lax.axis_index("dp"), lax.axis_index("ctx")
        groups = ctx // 2
        self.steps = []
        for t in range(groups):
            group = flip(c // 2, t, groups)
            same, other = group * 2 + c % 2, group * 2 + 1 - c % 2
            if t == 0:
                self.own = mover.local(source.at[c], target.at[c])
                batch = []
            else:
                batch = [mover.remote(source.at[same], target.at[c], (d, same))]
            batch.append(mover.remote(source.at[other], target.at[c], (d, other)))
            self.steps.append(batch)

    @staticmethod
    def count(ctx):
        return ctx - 1

    def start(self, t):
        if t == 0:
            self.own.start()
        for copy in self.steps[t]:
            copy.start()

    def arrive(self, t):
        if t == 0:
            self.own.wait()
        for copy in self.steps[t]:
            copy.wait_recv()

    def sent(self):
        for batch in self.steps:
            for copy in batch:
                copy.wait_send()


def columns(values):
    return jnp.sum(values, axis=0, keepdims=True)


def finish_kernel(dp, ctx, *refs):
    loaded, refs = refs[:6], refs[6:]
    outs, small_out, x_out, refs = refs[:3], refs[3], refs[4], refs[5:]
    grads, result, small, refs = refs[:3], refs[3], refs[4], refs[5:]
    (xb, dq, dk, dv, w, grad_sum), refs = refs[:6], refs[6:]
    buffers, small_buffers, refs = refs[:15], refs[15:21], refs[21:]
    local_sem, send_sem, recv_sem, load_sem = refs
    loads = [
        pltpu.make_async_copy(source, target, load_sem.at[i])
        for i, (source, target) in enumerate(zip(loaded, (xb, dq, dk, dv, w, grad_sum)))
    ]
    for copy in loads:
        copy.start()
    d, c = lax.axis_index("dp"), lax.axis_index("ctx")
    groups = ctx // 2
    g = c // 2
    half, width = result.shape[1:]
    held, late = grads[0].shape[3:]
    mover = Mover(local_sem, send_sem, recv_sem)
    scatter = Scatter(
        dp,
        ctx,
        grads,
        outs,
        [buffers[i * 5 : i * 5 + 5] for i in range(3)],
        small,
        small_out,
        small_buffers,
        mover,
    )
    give = Exchange(ctx, mover, result, x_out)
    greet([((d + k) % dp, c) for k in range(1, dp)] + [(d, (c + k) % ctx) for k in range(1, ctx)])
    small[...] = jnp.zeros_like(small)
    loads[0].wait()
    across = xb[...].T

    def weight_gradient(index, rows_grad):
        loads[1 + index].wait()
        total = dg(across, rows_grad[:, width - late :], NN)
        for block in range(dp * ctx):
            at = (block // ctx, block % ctx // 2, block % 2)
            grads[index][at] = total[block * held : (block + 1) * held].astype(BF)
        scatter.begin(index)

    def row_tile(t):
        block = flip(g, t, groups)
        rows = pl.ds(pl.multiple_of(block * 2 * half, 2 * half), 2 * half)
        total = grad_sum[rows, :]
        for i, rows_grad in enumerate((dq, dk, dv)):
            total = total + dg(rows_grad[rows, :], w[:, i * width : (i + 1) * width], NT)
        result[pl.ds(block * 2, 2)] = total.astype(BF).reshape(2, half, width)
        give.start(t)

    tiles = list(range(groups - 1, -1, -1))
    weight_gradient(0, dq)
    weight_gradient(1, dk)
    scatter.first(0)
    weight_gradient(2, dv)
    scatter.first(1)
    for copy in loads[4:]:
        copy.wait()
    row_tile(tiles.pop(0))
    scatter.first(2)
    small[0:1, :] = columns(dq[...].astype(F32))
    small[1:2, :] = columns(dv[...].astype(F32))
    scatter.begin_small()
    row_tile(tiles.pop(0))
    scatter.first_small()
    for t in tiles:
        row_tile(t)
    scatter.middle_small()
    for index in range(3):
        scatter.middle(index)
    scatter.finish()
    for t in range(groups):
        give.arrive(t)
    give.sent()


def finish_gradients(xb, dq, dk, dv, w, grad_sum, dp, ctx):
    rows, width = xb.shape
    remotes = Scatter.count(dp, ctx, 3) + Exchange.count(ctx)
    S = jax.ShapeDtypeStruct
    vmem = pl.BlockSpec(memory_space=pltpu.VMEM)
    late = width - width // 256 * 128
    source = S((dp, ctx // 2, 2, width // (dp * ctx), late), BF)
    small = S((8, width), F32)
    moved = (ctx, rows // ctx, width)
    return pl.pallas_call(
        functools.partial(finish_kernel, dp, ctx),
        in_specs=[pl.BlockSpec(memory_space=pl.ANY)] * 6,
        out_specs=[vmem] * 4 + [pl.BlockSpec(memory_space=pl.ANY)],
        out_shape=[S(source.shape[3:], F32)] * 3 + [small, S(moved, BF)],
        scratch_shapes=[pltpu.VMEM(source.shape, BF)] * 3
        + [pltpu.VMEM(moved, BF), pltpu.VMEM(small.shape, F32)]
        + [pltpu.VMEM(array.shape, array.dtype) for array in (xb, dq, dk, dv, w, grad_sum)]
        + Scatter.scratch(dp, ctx, [source] * 3, small)
        + [
            pltpu.SemaphoreType.DMA((4,)),
            pltpu.SemaphoreType.DMA((remotes,)),
            pltpu.SemaphoreType.DMA((remotes,)),
            pltpu.SemaphoreType.DMA((6,)),
        ],
        compiler_params=pltpu.CompilerParams(
            collective_id=3, has_side_effects=True, vmem_limit_bytes=VMEM_BYTES
        ),
        name="finish_gradients",
    )(xb, dq, dk, dv, w, grad_sum)


def head_lanes(shape, h):
    lane = lax.broadcasted_iota(jnp.int32, shape, len(shape) - 1)
    return (lane >= 64) == (h == 1), lane == (64 if h == 0 else 0)


def load_keys(keys, own_ref, sib_ref, lengths_ref, ctx):
    c = lax.axis_index("ctx")
    rows = own_ref.shape[0]
    half = rows // ctx
    length = lengths_ref[lax.axis_index("dp") * (ctx // 2) + c // 2]
    slot = lax.broadcasted_iota(jnp.int32, (rows, 128), 0)
    source = lax.broadcasted_iota(jnp.int32, (ctx, half, 128), 0).reshape(rows, 128)
    high = (2 * ctx - 1 - 2 * source) * half + slot
    for i, ref in enumerate((own_ref, sib_ref)):
        member = c % 2 if i == 0 else 1 - c % 2
        counted = jnp.where(member == 0, slot, high) < length
        for h in range(2):
            inside, spare = head_lanes((rows, 128), h)
            rest = jnp.where(spare & ~counted, masked_score, 0.0).astype(BF)
            keys[h, i * rows : (i + 1) * rows, :] = jnp.where(inside, ref[...], rest)


def forward_kernel(dp, ctx, bq, *refs):
    (x_ref, w_ref, vec_ref, lengths_ref), gathered, refs = refs[:4], refs[4:7], refs[7:]
    (mb_ref, mix_ref, lse_ref, own_to, sib_to), spread_to, refs = refs[:5], refs[5:8], refs[8:]
    keys, own, sib, local_sem, send_sem, recv_sem, pair_send, pair_recv, store_sem = refs
    spread = Spread(dp, ctx, gathered, spread_to, Mover(local_sem, send_sem, recv_sem))
    pairs, steps = pl.num_programs(0), pl.num_programs(1)
    pair, j = pl.program_id(0), pl.program_id(1)
    step = pair * steps + j
    last = forward_steps(pairs, steps)
    half, width = x_ref.shape

    def to_sibling(number):
        return pltpu.make_async_remote_copy(
            src_ref=own.at[number, pl.ds(1, 2)],
            dst_ref=sib.at[number],
            send_sem=pair_send.at[number],
            recv_sem=pair_recv.at[number],
            device_id=spread.devices[-1],
            device_id_type=MESH,
        )

    def stores(number):
        return [
            pltpu.make_async_copy(own.at[number], own_to.at[number], store_sem.at[number, 0]),
            pltpu.make_async_copy(sib.at[number], sib_to.at[number], store_sem.at[number, 1]),
        ]

    def project(number):
        lanes = [pl.ds(pl.multiple_of(number * 128 + i * width, 128), 128) for i in range(3)]
        weights = jnp.concatenate([w_ref[:, part] for part in lanes], axis=1)
        rows = dg(x_ref[...], weights, NN)
        own[number, 0] = (rows[:, :128] + vec_ref[0:1, lanes[0]]).astype(BF)
        own[number, 1] = rows[:, 128:256].astype(BF)
        own[number, 2] = (rows[:, 256:] + vec_ref[1:2, lanes[0]]).astype(BF)
        to_sibling(number).start()

    @pl.when(step == 0)
    def _():
        greet(spread.devices)
        spread.begin()
        project(pair)

    @pl.when(j == 0)
    def _():
        to_sibling(pair).wait_recv()
        for copy in stores(pair):
            copy.start()
        load_keys(keys, own.at[pair, 1], sib.at[pair, 0], lengths_ref, ctx)

    @pl.when((j == 1) & (pair < pairs - 1))
    def _():
        project(pair + 1)

    rows = pl.ds(pl.multiple_of(j * bq, bq), bq)
    q = own[pair, 0, rows, :] * jnp.asarray(0.125, BF)
    scores = []
    for h in range(2):
        inside, spare = head_lanes((bq, 128), h)
        rest = jnp.where(spare, jnp.ones((), BF), jnp.zeros((), BF))
        scores.append(dg(jnp.where(inside, q, rest), keys[h], NT))
    outs, lses = [], []
    for h in range(2):
        top = jnp.max(scores[h], axis=1, keepdims=True)
        weights = jnp.exp(scores[h] - top)
        total = jnp.sum(weights, axis=1, keepdims=True)
        low = weights.astype(BF)
        mixed = dg(low[:, :half], own[pair, 2], NN) + dg(low[:, half:], sib[pair, 1], NN)
        outs.append(mixed / total)
        lses.append(top + jnp.log(total))
    lane = lax.broadcasted_iota(jnp.int32, (bq, 128), 1)
    mixed = jnp.where(lane < 64, outs[0], outs[1])
    mix_ref[...] = mixed
    mb_ref[...] = mixed.astype(BF)
    lse_ref[0] = jnp.where(lane == 0, lses[0], lses[1]).T[:8]

    for index, ats in enumerate(last):
        for level in range(1, spread.levels + 1):

            @pl.when(step == ats[0] + (ats[1] - ats[0]) * (level - 1) // (spread.levels - 1))
            def _(index=index, level=level):
                spread.forward(index, level)

    @pl.when(step == pairs * steps - 1)
    def _():
        spread.finish()
        for number in range(pairs):
            to_sibling(number).wait_send()
            for copy in stores(number):
                copy.wait()


def attention_forward(x, w, vec, lengths, gathered, dp, ctx, bq=256):
    rows, width = x.shape
    pairs = width // 128
    S = jax.ShapeDtypeStruct
    blk = pl.BlockSpec((bq, 128), lambda p, j: (j, p))
    any_space = pl.BlockSpec(memory_space=pl.ANY)
    vmem = pl.BlockSpec(memory_space=pltpu.VMEM)
    remotes = Spread.count(ctx, 3)
    return pl.pallas_call(
        functools.partial(forward_kernel, dp, ctx, bq),
        grid=(pairs, rows // bq),
        in_specs=[vmem] * 3 + [pl.BlockSpec(memory_space=pltpu.SMEM)] + [any_space] * 3,
        out_specs=[blk, blk, pl.BlockSpec((1, 8, bq), lambda p, j: (p, 0, j))] + [any_space] * 5,
        out_shape=[S(x.shape, BF), S(x.shape, F32), S((pairs, 8, rows), F32)]
        + [S((pairs, count, rows, 128), BF) for count in (3, 2)]
        + [S((dp, ctx) + array.shape[1:], BF) for array in gathered],
        scratch_shapes=[
            pltpu.VMEM((2, 2 * rows, 128), BF),
            pltpu.VMEM((pairs, 3, rows, 128), BF),
            pltpu.VMEM((pairs, 2, rows, 128), BF),
            pltpu.SemaphoreType.DMA((3,)),
            pltpu.SemaphoreType.DMA((remotes,)),
            pltpu.SemaphoreType.DMA((remotes,)),
            pltpu.SemaphoreType.DMA((pairs,)),
            pltpu.SemaphoreType.DMA((pairs,)),
            pltpu.SemaphoreType.DMA((pairs, 2)),
        ],
        compiler_params=pltpu.CompilerParams(
            vmem_limit_bytes=VMEM_BYTES, collective_id=1, has_side_effects=True
        ),
        cost_estimate=pl.CostEstimate(
            flops=16 * rows * rows * 128 * pairs,
            bytes_accessed=14 * rows * 768,
            transcendentals=4 * rows * rows * pairs,
        ),
        name="attend",
    )(x, w, vec, lengths, *gathered)


def forward_steps(pairs, steps):
    count = pairs * steps
    return [(count * a // 24, count * b // 24) for a, b in ((11, 18), (12, 19), (13, 20))]


def backward_steps(pairs, steps):
    count = pairs * steps
    first = [count * at // 12 for at in (0, 0, 1, 7)]
    middle = [count * at // 12 for at in (5, 4, 8, 10)]
    return first, middle


def backward_kernel(dp, ctx, ck, *refs):
    (q_ref, ko_ref, vo_ref, ks_ref, vs_ref, do_ref, mix_ref, lengths_ref, lse_ref), refs = (
        refs[:9],
        refs[9:],
    )
    q_ref, ko_ref, vo_ref, ks_ref, vs_ref = (
        ref.at[0, 0] for ref in (q_ref, ko_ref, vo_ref, ks_ref, vs_ref)
    )
    sources, small, x_ref, refs = refs[:3], refs[3], refs[4], refs[5:]
    (dq_ref, dk_ref, dv_ref), refs = refs[:3], refs[3:]
    summed, small_out, refs = refs[:4], refs[4], refs[5:]
    (keys, dk, dv, held, going, coming, across, dq_held, early), refs = refs[:9], refs[9:]
    buffers, small_buffers, refs = refs[:20], refs[20:26], refs[26:]
    local_sem, send_sem, recv_sem, pair_send, pair_recv = refs
    scatter = Scatter(
        dp,
        ctx,
        [*sources, early],
        summed,
        [buffers[i * 5 : i * 5 + 5] for i in range(4)],
        small,
        small_out,
        small_buffers,
        Mover(local_sem, send_sem, recv_sem),
    )
    steps = pl.num_programs(1)
    j = pl.program_id(1)
    step = pl.program_id(0) * steps + j

    pair = pl.program_id(0)
    sibling = scatter.devices[-1]

    def to_sibling(number):
        return [
            pltpu.make_async_remote_copy(
                src_ref=going.at[number, i],
                dst_ref=coming.at[number, i],
                send_sem=pair_send.at[number * 2 + i],
                recv_sem=pair_recv.at[number * 2 + i],
                device_id=sibling,
                device_id_type=MESH,
            )
            for i in range(2)
        ]

    def settle(number):
        lanes = pl.ds(pl.multiple_of(number * 128, 128), 128)
        totals = []
        for i, (copy, out) in enumerate(zip(to_sibling(number), (dk_ref, dv_ref))):
            copy.wait_recv()
            total = held[number % 2, i] + coming[number, i].astype(F32)
            totals.append(total.astype(BF))
            out[:, lanes] = totals[-1]
        return totals

    @pl.when(step == 0)
    def _():
        greet(scatter.devices)
        scatter.begin(1)
        scatter.begin_small()
        scatter.begin(0)
        scatter.begin(2)
        across[...] = x_ref[...].T

    early_pairs = early.shape[4] // 384

    @pl.when((j == 0) & (pair > 0) & (pair <= early_pairs))
    def _():
        rows_grad = jnp.concatenate([dq_held[...], *settle(pair - 1)], axis=1)
        total = dg(across[...], rows_grad, NN)
        lanes = pl.ds(pl.multiple_of((pair - 1) * 384, 128), 384)
        owned = early.shape[3]
        for block in range(dp * ctx):
            at = (block // ctx, block % ctx // 2, block % 2)
            part = total[block * owned : (block + 1) * owned]
            early[(*at, slice(None), lanes)] = part.astype(BF)

    @pl.when((j == 0) & (pair == early_pairs))
    def _():
        scatter.begin(3)

    @pl.when((j == 0) & (pair > early_pairs))
    def _():
        settle(pair - 1)

    @pl.when(j == 0)
    def _():
        load_keys(keys, ko_ref, ks_ref, lengths_ref, ctx)
        dk[...] = jnp.zeros_like(dk)
        dv[...] = jnp.zeros_like(dv)

    half, bq = ko_ref.shape[0], q_ref.shape[0]
    q = q_ref[...] * jnp.asarray(0.125, BF)
    do = do_ref[...]
    prod = (do.astype(F32) * mix_ref[...]).T
    zero, one = jnp.zeros((), BF), jnp.ones((), BF)
    heads = []
    for h in range(2):
        inside, spare = head_lanes((bq, 128), h)
        heads.append(
            (
                jnp.where(inside, q, jnp.where(spare, one, zero)),
                jnp.where(inside, q, zero),
                jnp.where(inside, do, zero),
                lse_ref[0, h : h + 1, :],
                jnp.sum(prod[h * 64 : (h + 1) * 64], axis=0, keepdims=True),
            )
        )
    dq = jnp.zeros((bq, 128), F32)
    for first in range(0, 2 * half, ck):
        rows = slice(first, first + ck)
        v = vo_ref[rows, :] if first < half else vs_ref[first - half : first - half + ck, :]
        for h in range(2):
            qm, qz, dom, lse, delta = heads[h]
            k = keys[h, rows, :]
            p = jnp.exp(dg(k, qm, NT) - lse)
            ds = (p * (dg(v, dom, NT) - delta)).astype(BF)
            dv[rows, :] += dg(p.astype(BF), dom, NN)
            dk[rows, :] += dg(ds, qz, NN)
            dq = dq + dg(ds, k, TN)
    low_dq = (dq * 0.125).astype(BF)
    dq_ref[...] = low_dq
    dq_held[pl.ds(pl.multiple_of(j * bq, bq), bq), :] = low_dq

    @pl.when(j == steps - 1)
    def _():
        for i, total in enumerate((dk, dv)):
            held[pair % 2, i] = total[:half, :]
            going[pair, i] = total[half:, :].astype(BF)
        for copy in to_sibling(pair):
            copy.start()

    first, middle_at = backward_steps(pl.num_programs(0), steps)

    @pl.when(step == first[0])
    def _():
        scatter.first_small()

    @pl.when(step == middle_at[0])
    def _():
        scatter.middle_small()

    for index in range(4):

        @pl.when(step == first[index])
        def _(index=index):
            scatter.first(index)

        @pl.when(step == middle_at[index])
        def _(index=index):
            scatter.middle(index)

    @pl.when(step == pl.num_programs(0) * steps - 1)
    def _():
        scatter.finish()
        settle(pair)
        for number in range(pl.num_programs(0)):
            for copy in to_sibling(number):
                copy.wait_send()


def attention_backward(
    own, sib, do, mix, lengths, lse, sources, small, x, dp, ctx, bq=512, ck=512
):
    rows, width = do.shape
    pairs = width // 128
    S = jax.ShapeDtypeStruct
    blk = pl.BlockSpec((bq, 128), lambda p, j: (j, p))
    whole_of = [
        pl.BlockSpec((1, 1, rows, 128), lambda p, j, i=i: (p, i, 0, 0)) for i in (1, 2, 0, 1)
    ]
    any_space = pl.BlockSpec(memory_space=pl.ANY)
    early = jax.ShapeDtypeStruct(
        (dp, ctx // 2, 2, width // (dp * ctx), pairs // 2 * 384), BF
    )
    every = [*sources, early]
    remotes = Scatter.count(dp, ctx, 4)
    whole = pl.BlockSpec(small.shape, lambda p, j: (0, 0))
    sums = [s.shape[-2:] for s in every]
    all_rows = pl.BlockSpec((rows, width), lambda p, j: (0, 0))
    return pl.pallas_call(
        functools.partial(backward_kernel, dp, ctx, ck),
        grid=(pairs, rows // bq),
        in_specs=[pl.BlockSpec((1, 1, bq, 128), lambda p, j: (p, 0, j, 0))]
        + whole_of
        + [blk, blk]
        + [pl.BlockSpec(memory_space=pltpu.SMEM)]
        + [pl.BlockSpec((1, 8, bq), lambda p, j: (p, 0, j))]
        + [any_space] * 3
        + [whole, pl.BlockSpec(memory_space=pltpu.VMEM)],
        out_specs=[blk, all_rows, all_rows]
        + [pl.BlockSpec(shape, lambda p, j: (0, 0)) for shape in sums]
        + [whole],
        out_shape=[S(do.shape, BF)] * 3
        + [S(shape, F32) for shape in sums]
        + [S(small.shape, F32)],
        scratch_shapes=[
            pltpu.VMEM((2, 2 * rows, 128), BF),
            pltpu.VMEM((2 * rows, 128), F32),
            pltpu.VMEM((2 * rows, 128), F32),
            pltpu.VMEM((2, 2, rows, 128), F32),
            pltpu.VMEM((pairs, 2, rows, 128), BF),
            pltpu.VMEM((pairs, 2, rows, 128), BF),
            pltpu.VMEM((width, rows), BF),
            pltpu.VMEM((rows, 128), BF),
            pltpu.VMEM(early.shape, BF),
        ]
        + Scatter.scratch(dp, ctx, every, small)
        + [
            pltpu.SemaphoreType.DMA((4,)),
            pltpu.SemaphoreType.DMA((remotes,)),
            pltpu.SemaphoreType.DMA((remotes,)),
            pltpu.SemaphoreType.DMA((2 * pairs,)),
            pltpu.SemaphoreType.DMA((2 * pairs,)),
        ],
        compiler_params=pltpu.CompilerParams(
            vmem_limit_bytes=VMEM_BYTES, collective_id=2, has_side_effects=True
        ),
        cost_estimate=pl.CostEstimate(
            flops=40 * rows * rows * 128 * pairs,
            bytes_accessed=26 * rows * 768,
            transcendentals=4 * rows * rows * pairs,
        ),
        name="attend_back",
    )(own, own, own, sib, sib, do, mix, lengths, lse, *sources, small, x)


def gelu_and_slope(x):
    t = 1.0 / (1.0 + 0.2316419 * jnp.abs(x))
    bell = 0.3989422804 * jnp.exp(-0.5 * x * x)
    poly = 1.330274429 * t - 1.821255978
    poly = poly * t + 1.781477937
    poly = poly * t - 0.356563782
    poly = poly * t + 0.319381530
    tail = bell * (poly * t)
    below = jnp.where(x < 0.0, tail, 1.0 - tail)
    return x * below, below + x * bell


def middle_kernel(dp, ctx, *refs):
    (mb, xb, rest_src, up_src, vec, bias_up, wo_src, wu_src, wd_src), refs = refs[:9], refs[9:]
    (dm, grad_sum, out_to, go_to, gu_to, gd_to, small), refs = refs[:7], refs[7:]
    (wo, wu, wd, rest, upstream, result, active, dinner, slope, fb, db, da), refs = (
        refs[:12],
        refs[12:],
    )
    (other, summed), refs = refs[:2], refs[2:]
    load_sem, local_sem, send_sem, recv_sem = refs
    groups = ctx // 2
    g = lax.axis_index("ctx") // 2
    half, width = result.shape[1:]
    tile = 2 * half
    chunks = range(wu.shape[1] // width)
    step = pl.program_id(0)
    mover = Mover(local_sem, send_sem, recv_sem)
    rest_in = Exchange(ctx, mover, rest_src, rest)
    up_in = Exchange(ctx, mover, up_src, upstream)
    give = Exchange(ctx, mover, result, out_to)
    loads = [
        pltpu.make_async_copy(source, target, load_sem.at[i])
        for i, (source, target) in enumerate(((wo_src, wo), (wu_src, wu), (wd_src, wd)))
    ]
    stores = [
        pltpu.make_async_copy(source, target, load_sem.at[i])
        for i, (source, target) in enumerate(((wo, go_to), (wu, gu_to), (summed, gd_to)))
    ]
    d, c = lax.axis_index("dp"), lax.axis_index("ctx")
    held = other.shape[2]

    def block_rows(i, k, member):
        return pl.ds(pl.multiple_of(((i * groups + k) * 2 + member) * held, 8), held)

    blocks = [(i, k) for i in range(dp) for k in range(groups)]
    to_sibling = [
        mover.remote(wd.at[block_rows(i, k, 1 - c % 2)], other.at[i, k], (d, g * 2 + 1 - c % 2))
        for i, k in blocks
    ]

    def load(index):
        @pl.when(step == 0)
        def _():
            loads[index].wait()

    @pl.when(step == 0)
    def _():
        for copy in loads:
            copy.start()
        greet([(d, (c + k) % ctx) for k in range(1, ctx)])
        for t in range(groups):
            rest_in.start(t)
            up_in.start(t)
        small[...] = jnp.zeros_like(small)

    @pl.when(step < groups)
    def _():
        block = flip(g, step, groups)
        rows = pl.ds(pl.multiple_of(block * tile, tile), tile)
        pair = pl.ds(block * 2, 2)
        load(0)
        hidden = dg(mb[rows, :], wo[...], NN) + vec[2:3, :] + xb[rows, :].astype(F32)
        for t in range(groups):

            @pl.when(step == t)
            def _(t=t):
                rest_in.arrive(t)

        hidden = hidden + rest[pair].reshape(tile, width).astype(F32)
        normed, standard_one, inverse_one = normalize(hidden, vec[6:7, :], vec[4:5, :])
        low = normed.astype(BF)
        fb[rows, :] = low
        load(1)
        parts = [slice(i * width, (i + 1) * width) for i in chunks]
        inner = dg(low, wu[:, parts[0]], NN)
        for i, part in enumerate(parts):
            ahead = dg(low, wu[:, parts[i + 1]], NN) if i + 1 < len(parts) else None
            value, slope[:, part] = gelu_and_slope(inner + bias_up[:, part])
            active[rows, part] = value.astype(BF)
            inner = ahead
        load(2)
        hidden = normed + dg(active[rows, :], wd[...], NN) + vec[3:4, :]
        out, standard, inverse = normalize(hidden, vec[7:8, :], vec[5:6, :])
        result[pair] = out.astype(BF).reshape(2, half, width)
        for t in range(groups):

            @pl.when(step == t)
            def _(t=t):
                give.start(t)
                up_in.arrive(t)

        error = upstream[pair].reshape(tile, width).astype(F32)
        grad = normalize_back(error, standard, inverse, vec[7:8, :])
        low_grad = grad.astype(BF)
        db[rows, :] = low_grad
        small[1:2, :] += columns(low_grad.astype(F32))
        small[3:4, :] += columns(error)
        small[5:6, :] += columns(error * standard)
        for i in chunks:
            part = slice(i * width, (i + 1) * width)
            change = dg(low_grad, wd[part, :], NT) * slope[:, part]
            change = change.astype(BF)
            dinner[rows, part] = change
            small[6 + i : 7 + i, :] += columns(change.astype(F32))
        grad = grad + dg(dinner[rows, :], wu[...], NT)
        small[2:3, :] += columns(grad)
        small[4:5, :] += columns(grad * standard_one)
        grad = normalize_back(grad, standard_one, inverse_one, vec[6:7, :])
        grad_sum[rows, :] = grad
        low_grad = grad.astype(BF)
        da[rows, :] = low_grad
        small[0:1, :] += columns(low_grad.astype(F32))
        dm[rows, :] = dg(low_grad, wo[...], NT).astype(BF)

    @pl.when(step == groups)
    def _():
        for i in chunks:
            part = slice(i * width, (i + 1) * width)
            wd[part, :] = dg(active[:, part], db[...], TN).astype(BF)
        for copy in to_sibling:
            copy.start()
        across = fb[...].T
        for i in chunks:
            part = slice(i * width, (i + 1) * width)
            wu[:, part] = dg(across, dinner[:, part], NN).astype(BF)
        stores[1].start()
        for copy in to_sibling:
            copy.wait()
        for i, k in blocks:
            summed[i, k] = wd[block_rows(i, k, c % 2), :] + other[i, k]
        stores[2].start()
        wo[...] = dg(mb[...], da[...], TN).astype(BF)
        stores[0].start()
        for t in range(groups):
            give.arrive(t)
        for move in (rest_in, up_in, give):
            move.sent()
        for copy in stores:
            copy.wait()


def middle(mb, xb, rest, upstream, vec, bias_up, wo, wu, wd, dp, ctx):
    rows, width = mb.shape
    hidden = wu.shape[1]
    half = rows // ctx
    S = jax.ShapeDtypeStruct
    any_space = pl.BlockSpec(memory_space=pl.ANY)
    vmem = pl.BlockSpec(memory_space=pltpu.VMEM)
    held = (dp, ctx // 2, hidden // (dp * ctx), width)
    remotes = 3 * Exchange.count(ctx) + dp * (ctx // 2)
    return pl.pallas_call(
        functools.partial(middle_kernel, dp, ctx),
        grid=(ctx // 2 + 1,),
        in_specs=[vmem, vmem, any_space, any_space, vmem, vmem] + [any_space] * 3,
        out_specs=[vmem, vmem] + [any_space] * 4 + [vmem],
        out_shape=[S(mb.shape, BF), S(mb.shape, F32), S(rest.shape, BF)]
        + [S(wo.shape, BF), S(wu.shape, BF), S(held, BF)]
        + [S((16, width), F32)],
        scratch_shapes=[pltpu.VMEM(array.shape, BF) for array in (wo, wu, wd)]
        + [pltpu.VMEM(rest.shape, BF)] * 3
        + [pltpu.VMEM((rows, hidden), BF)] * 2
        + [pltpu.VMEM((2 * half, hidden), F32)]
        + [pltpu.VMEM((rows, width), BF)] * 3
        + [pltpu.VMEM(held, BF)] * 2
        + [
            pltpu.SemaphoreType.DMA((3,)),
            pltpu.SemaphoreType.DMA((3,)),
            pltpu.SemaphoreType.DMA((remotes,)),
            pltpu.SemaphoreType.DMA((remotes,)),
        ],
        compiler_params=pltpu.CompilerParams(
            vmem_limit_bytes=VMEM_BYTES, collective_id=4, has_side_effects=True
        ),
        cost_estimate=pl.CostEstimate(
            flops=2 * 3 * rows * width * (2 * hidden + width),
            bytes_accessed=50 << 20,
            transcendentals=rows * hidden,
        ),
        name="middle",
    )(mb, xb, rest, upstream, vec, bias_up, wo, wu, wd)


def normalize(hidden, scale_row, shift_row):
    centred = hidden - jnp.mean(hidden, axis=-1, keepdims=True)
    inverse = lax.rsqrt(jnp.mean(centred * centred, axis=-1, keepdims=True) + epsilon)
    standard = centred * inverse
    return (standard * scale_row + shift_row, standard, inverse)


def normalize_back(gradient, standard, inverse, scale_row):
    scaled = gradient * scale_row
    centred = scaled - jnp.mean(scaled, axis=-1, keepdims=True)
    return (centred - standard * jnp.mean(scaled * standard, axis=-1, keepdims=True)) * inverse


def write_kernel(dp, ctx, small_ref, sums_ref, out_ref, tokens_ref, *refs):
    sources, early, (out_to, tokens_to), refs = refs[:6], refs[6], refs[7:9], refs[9:]
    targets, (vectors_to, bias_to) = refs[:6], refs[6:]
    out_to[...] = out_ref[...].astype(F32)
    tokens_to[...] = tokens_ref[...].astype(F32)

    @pl.when(pl.program_id(0) == 0)
    def _():
        for i in range(3):
            late = sources[i].shape[1]
            first = targets[i].shape[1] - late
            targets[i][:, first:] = sources[i][...]
            for lane in range(0, first, 128):
                at = lane * 3 + i * 128
                targets[i][:, lane : lane + 128] = early[:, at : at + 128]
        for source, target in zip(sources[3:], targets[3:]):
            target[...] = source[...]
        device = lax.axis_index("dp") * ctx + lax.axis_index("ctx")
        width = small_ref.shape[1]
        held, held_up = vectors_to.shape[1], bias_to.shape[1]
        rows = jnp.concatenate([sums_ref[0:2, :], small_ref[0:6, :]], axis=0)
        vectors_to[...] = pltpu.roll(rows, (width - device * held) % width, 1)[:, :held]
        first = device * held_up
        row = small_ref[pl.ds(6 + first // width, 1), :]
        row = jnp.broadcast_to(row, (8, width))
        bias_to[...] = pltpu.roll(row, (width - first % width) % width, 1)[0:1, :held_up]


def write_out(small, sums, out, tokens, own, early, held_up, dp, ctx):
    block = pl.BlockSpec((2,) + out.shape[1:], lambda i: (i, 0, 0))
    S = jax.ShapeDtypeStruct

    def whole(shape):
        return pl.BlockSpec(shape, lambda i: (0, 0))

    given = [array.shape for array in (*own, early)]
    shapes = [(own[0].shape[0], out.shape[2])] * 3 + [array.shape for array in own[3:]]
    vectors = (8, out.shape[2] // (dp * ctx))
    return pl.pallas_call(
        functools.partial(write_kernel, dp, ctx),
        grid=(ctx // 2,),
        in_specs=[whole(small.shape), whole(sums.shape), block, block]
        + [whole(shape) for shape in given],
        out_specs=[block, block]
        + [whole(shape) for shape in shapes]
        + [whole(vectors), whole((1, held_up))],
        out_shape=[S(out.shape, F32)] * 2
        + [S(shape, F32) for shape in shapes]
        + [S(vectors, F32), S((1, held_up), F32)],
        compiler_params=pltpu.CompilerParams(vmem_limit_bytes=VMEM_BYTES),
        name="write_out",
    )(small, sums, out, tokens, *own, early)


def on_device(
    tokens, cotangent, lengths, w_query, w_key, w_value, w_attn_out, w_up, b_up, w_down, vectors
):
    seqs, rows_dev, width = tokens.shape
    dp = lax.axis_size("dp")
    ctx = lax.axis_size("ctx")
    half = rows_dev // 2
    rows = half * ctx
    def by_owner(grad):
        return grad.reshape(dp, ctx // 2, 2, -1, grad.shape[1])

    split = tokens.reshape(ctx, half, width)
    held = w_query.shape[0]
    extra = jnp.concatenate([vectors.T, b_up.reshape(held, -1)], axis=1)
    extra = jnp.pad(extra, ((0, 0), (0, 128 - extra.shape[1])))
    low_in, left_out, upstream, full_first, *over_dp = gather_first(
        split,
        cotangent.reshape(ctx, half, width),
        jnp.concatenate([w_query, w_key, w_value, extra], axis=1),
        w_attn_out,
        w_up,
        w_down,
        dp,
        ctx,
    )
    low_in = low_in.reshape(rows, width)
    full_first = full_first.reshape(width, -1)
    vector_rows = full_first[:, 3 * width : 3 * width + 8].T.astype(F32)
    bias_columns = b_up.shape[0] // held
    full_bias_up = full_first[:, 3 * width + 8 : 3 * width + 8 + bias_columns].reshape(-1).astype(F32)
    low_mixed, mixed, lse, own, sib, full_attn, full_up, full_down = attention_forward(
        low_in, full_first, vector_rows, lengths, over_dp, dp, ctx
    )
    full_attn = full_attn.reshape(width, width)
    full_up = full_up.reshape(width, -1)
    full_down = full_down.reshape(-1, width)

    d_mixed, grad_sum, result, d_attn, d_up, part_down, small = middle(
        low_mixed,
        low_in,
        left_out,
        upstream,
        vector_rows,
        full_bias_up.reshape(1, -1),
        full_attn,
        full_up,
        full_down,
        dp,
        ctx,
    )
    dq, dk, dv, own_attn, own_down, own_up, own_early, small = attention_backward(
        own,
        sib,
        d_mixed,
        mixed,
        lengths,
        lse,
        [by_owner(d_attn), part_down, by_owner(d_up)],
        small,
        low_in,
        dp,
        ctx,
    )
    own_query, own_key, own_value, sums, grad_tokens = finish_gradients(
        low_in, dq, dk, dv, full_first, grad_sum, dp, ctx
    )
    output, grad_tokens, *own, own_vectors, own_bias_up = write_out(
        small,
        sums,
        result,
        grad_tokens,
        [own_query, own_key, own_value, own_attn, own_up, own_down],
        own_early,
        b_up.shape[0],
        dp,
        ctx,
    )
    own_query, own_key, own_value, own_attn, own_up, own_down = own
    output = output.reshape(seqs, rows_dev, width)
    grad_tokens = grad_tokens.reshape(seqs, rows_dev, width)
    own_bias_up = own_bias_up.reshape(-1)
    return (
        output,
        grad_tokens,
        own_query,
        own_key,
        own_value,
        own_attn,
        own_up,
        own_bias_up,
        own_down,
        own_vectors,
    )


def solution(mesh):
    in_specs = (
        P("dp", "ctx", None),
        P("dp", "ctx", None),
        P(),
        P(("dp", "ctx"), None),
        P(("dp", "ctx"), None),
        P(("dp", "ctx"), None),
        P(("dp", "ctx"), None),
        P(("dp", "ctx"), None),
        P(("dp", "ctx")),
        P(("dp", "ctx"), None),
        P(None, ("dp", "ctx")),
    )
    out_specs = (
        P("dp", "ctx", None),
        P("dp", "ctx", None),
        P(("dp", "ctx"), None),
        P(("dp", "ctx"), None),
        P(("dp", "ctx"), None),
        P(("dp", "ctx"), None),
        P(("dp", "ctx"), None),
        P(("dp", "ctx")),
        P(("dp", "ctx"), None),
        P(None, ("dp", "ctx")),
    )
    return jax.shard_map(
        on_device, mesh=mesh, in_specs=in_specs, out_specs=out_specs, check_vma=False
    )
```

```python
import functools
import jax
import jax.numpy as jnp
from jax import lax
from jax.experimental import pallas as pl
from jax.experimental.pallas import tpu as pltpu
from jax.sharding import PartitionSpec as P

HEAD_DIM = 64
F32 = jnp.float32
BF = jnp.bfloat16
NN = (((1,), (0,)), ((), ()))
NT = (((1,), (1,)), ((), ()))
TN = (((0,), (0,)), ((), ()))
epsilon = 1e-12
masked_score = -1e30
VMEM_BYTES = 58 << 20


def dg(left, right, dims):
    return lax.dot_general(left, right, dims, preferred_element_type=F32)


MESH = pl.DeviceIdType.MESH


class Mover:
    def __init__(self, local_sem, send_sem, recv_sem):
        self.local_sem, self.send_sem, self.recv_sem = local_sem, send_sem, recv_sem
        self.locals = self.remotes = 0

    def local(self, source, target):
        copy = pltpu.make_async_copy(source, target, self.local_sem.at[self.locals])
        self.locals += 1
        return copy

    def remote(self, source, target, device):
        number = self.remotes
        self.remotes += 1
        return pltpu.make_async_remote_copy(
            src_ref=source,
            dst_ref=target,
            send_sem=self.send_sem.at[number],
            recv_sem=self.recv_sem.at[number],
            device_id=device,
            device_id_type=MESH,
        )


def greet(devices):
    barrier = pltpu.get_barrier_semaphore()
    for device in devices:
        pl.semaphore_signal(barrier, inc=1, device_id=device, device_id_type=MESH)
    pl.semaphore_wait(barrier, len(devices))


def place(dp, ctx):
    d, c = lax.axis_index("dp"), lax.axis_index("ctx")
    groups = ctx // 2
    g, m = c // 2, c % 2
    over_dp = [((d + k) % dp, c) for k in range(1, dp)]
    over_groups = [(d, (g + k) % groups * 2 + m) for k in range(1, groups)]
    return d, c, g, m, over_dp, over_groups, (d, g * 2 + 1 - m)


def flip(group, step, groups):
    total, bit = 0, 1
    while bit < groups:
        total = total + (group // bit + step // bit) % 2 * bit
        bit *= 2
    return total


class Spread:
    def __init__(self, dp, ctx, sources, targets, mover):
        d, c, g, m, over_dp, over_groups, sibling = place(dp, ctx)
        groups = ctx // 2
        bits = [1 << i for i in range(groups.bit_length() - 1)]
        self.levels = len(bits)
        self.devices = [(d, flip(g, bit, groups) * 2 + m) for bit in bits] + [sibling]
        self.own, self.copies, self.onward = [], [], []
        for source, target in zip(sources, targets):

            def column(mask):
                return flip(g, mask, groups) * 2 + m

            self.own.append([] if source is None else [mover.local(source, target.at[:, c])])
            source = target.at[:, c] if source is None else source
            copies = [[] for _ in range(self.levels + 1)]
            for start, order in ((0, bits), (dp // 2, bits[::-1])):
                part = pl.ds(start, dp // 2)
                for i, bit in enumerate(order):
                    for mask in range(groups):
                        if any(mask & other for other in order[i:]):
                            continue
                        place_in = target.at[part, column(mask)]
                        copies[bin(mask).count("1")].append(
                            mover.remote(
                                place_in if mask else source.at[part], place_in, (d, column(bit))
                            )
                        )
            self.copies.append(copies)
            onward = [[mover.remote(source, target.at[:, c], sibling)]]
            onward += [[] for _ in range(self.levels)]
            for mask in range(1, groups):
                block = target.at[:, column(mask)]
                onward[bin(mask).count("1")].append(mover.remote(block, block, sibling))
            self.onward.append(onward)

    @staticmethod
    def count(ctx, arrays):
        return arrays * (2 * (ctx // 2 - 1) + ctx // 2)

    def begin(self):
        for own, copies, onward in zip(self.own, self.copies, self.onward):
            for copy in copies[0] + own + onward[0]:
                copy.start()

    def forward(self, index, level):
        for copy in self.copies[index][level - 1]:
            copy.wait_recv()
        for copy in self.copies[index][level] + self.onward[index][level]:
            copy.start()

    def finish(self):
        for own, copies, onward in zip(self.own, self.copies, self.onward):
            for copy in own + sum(onward, []):
                copy.wait()
            for copy in sum(copies, []):
                copy.wait_send()


def gather_kernel(dp, ctx, *refs):
    (tokens, cotangent, w, wo, wu, wd), refs = refs[:6], refs[6:]
    (x_in, rest_to, up_to, w_full, zo, zu, zd), refs = refs[:7], refs[7:]
    wide, wide_up, x, rest, up, local_sem, send_sem, recv_sem, move_sem = refs
    d, c, g, m, over_dp, over_groups, sibling = place(dp, ctx)
    groups = ctx // 2
    moves = [
        pltpu.make_async_copy(source, target, move_sem.at[i])
        for i, (source, target) in enumerate(
            ((tokens, wide), (cotangent, wide_up), (rest, rest_to), (up, up_to))
        )
    ]
    moves[0].start()
    greet(over_dp + [(d, (c + k) % ctx) for k in range(1, ctx)])
    mover = Mover(local_sem, send_sem, recv_sem)
    own = [
        mover.local(source, target)
        for source, target in (
            (w, w_full.at[d, c]),
            (x.at[c], x_in.at[c]),
            (wo, zo.at[d]),
            (wu, zu.at[d]),
            (wd, zd.at[d]),
        )
    ]
    along = [mover.remote(w, w_full.at[d, c], device) for device in over_dp]
    rows = [
        mover.remote(x.at[(c + k) % ctx], x_in.at[c], (d, (c + k) % ctx)) for k in range(1, ctx)
    ]
    others = [
        mover.remote(source, target.at[d], device)
        for source, target in ((wo, zo), (wu, zu), (wd, zd))
        for device in over_dp
    ]
    spread = Spread(dp, ctx, [None], [w_full], mover)
    for copy in own[:1] + along:
        copy.start()
    moves[0].wait()
    moves[1].start()
    x[...] = wide[...].astype(BF)
    for copy in rows + own[1:]:
        copy.start()
    for copy in along:
        copy.wait_recv()
    own[0].wait()
    spread.begin()
    for copy in others:
        copy.start()
    rest[...] = (wide[...] - x[...].astype(F32)).astype(BF)
    moves[2].start()
    moves[1].wait()
    up[...] = wide_up[...].astype(BF)
    moves[3].start()
    for level in range(1, spread.levels + 1):
        spread.forward(0, level)
    for copy in rows + others + moves[2:] + own[1:]:
        copy.wait()
    spread.finish()
    for copy in along:
        copy.wait_send()


def gather_first(tokens, cotangent, w, wo, wu, wd, dp, ctx):
    remotes = (dp - 1) + Spread.count(ctx, 1) + (ctx - 1) + 3 * (dp - 1)
    any_space = pl.BlockSpec(memory_space=pl.ANY)
    return pl.pallas_call(
        functools.partial(gather_kernel, dp, ctx),
        in_specs=[any_space] * 6,
        out_specs=[any_space] * 7,
        out_shape=[jax.ShapeDtypeStruct(tokens.shape, BF)] * 3
        + [jax.ShapeDtypeStruct((dp, ctx) + w.shape, BF)]
        + [jax.ShapeDtypeStruct((dp,) + array.shape, BF) for array in (wo, wu, wd)],
        scratch_shapes=[pltpu.VMEM(tokens.shape, F32)] * 2
        + [pltpu.VMEM(tokens.shape, BF)] * 3
        + [
            pltpu.SemaphoreType.DMA((5,)),
            pltpu.SemaphoreType.DMA((remotes,)),
            pltpu.SemaphoreType.DMA((remotes,)),
            pltpu.SemaphoreType.DMA((4,)),
        ],
        compiler_params=pltpu.CompilerParams(
            collective_id=0, has_side_effects=True, vmem_limit_bytes=VMEM_BYTES
        ),
        name="gather_first",
    )(tokens, cotangent, w, wo, wu, wd)


class Scatter:
    def __init__(self, dp, ctx, sources, outs, buffers, small, small_out, small_buffers, mover):
        d, c, g, m, over_dp, over_groups, sibling = place(dp, ctx)
        groups = ctx // 2
        self.dp, self.groups, self.d, self.g = dp, groups, d, g
        self.devices = over_groups + over_dp + [sibling]
        self.outs = list(outs)
        self.buffers = buffers
        self.own, self.pair, self.across, self.along = [], [], [], []
        for source, (mine, other, came, sums, last) in zip(sources, buffers):
            summed = len(source.shape) == 4
            if summed:
                self.own.append(mover.local(source, mine))
                self.pair.append([])
            else:
                self.own.append(mover.local(source.at[:, :, m], mine))
                self.pair.append([mover.remote(source.at[:, :, 1 - m], other, sibling)])
            onward = source if summed else mine
            self.across.append(
                [
                    mover.remote(onward.at[:, (g + k) % groups], came.at[k - 1], over_groups[k - 1])
                    for k in range(1, groups)
                ]
            )
            self.along.append(
                [
                    mover.remote(sums.at[(d + k) % dp], last.at[k - 1], over_dp[k - 1])
                    for k in range(1, dp)
                ]
            )
        self.small, self.small_out = small, small_out
        one, came, two, groups_in, three, dp_in = small_buffers
        self.small_buffers = small_buffers
        self.pair.append([mover.remote(one, came, sibling)])
        self.across.append(
            [mover.remote(two, groups_in.at[k - 1], over_groups[k - 1]) for k in range(1, groups)]
        )
        self.along.append(
            [mover.remote(three, dp_in.at[k - 1], over_dp[k - 1]) for k in range(1, dp)]
        )

    @staticmethod
    def count(dp, ctx, arrays):
        return (arrays + 1) * (1 + ctx // 2 - 1 + dp - 1)

    @staticmethod
    def scratch(dp, ctx, sources, small):
        groups = ctx // 2
        shapes = []
        for s in sources:
            block = s.shape[-2:]
            shapes += [
                pltpu.VMEM((dp, groups) + block, BF),
                pltpu.VMEM((dp, groups) + block if len(s.shape) == 5 else (8, 128), BF),
                pltpu.VMEM((groups - 1, dp) + block, BF),
                pltpu.VMEM((dp,) + block, BF),
                pltpu.VMEM((dp - 1,) + block, BF),
            ]
        shape = small.shape
        shapes += [pltpu.VMEM(shape, F32)] * 3
        shapes += [
            pltpu.VMEM((groups - 1,) + shape, F32),
            pltpu.VMEM(shape, F32),
            pltpu.VMEM((dp - 1,) + shape, F32),
        ]
        return shapes

    def begin_small(self):
        self.small_buffers[0][...] = self.small[...]
        self.pair[-1][0].start()

    def begin(self, index):
        for copy in self.pair[index] or self.across[index]:
            copy.start()
        self.own[index].start()

    def first(self, index):
        mine, other = self.buffers[index][:2]
        groups = self.groups
        self.own[index].wait()
        if not self.pair[index]:
            return
        self.pair[index][0].wait_recv()

        def add(i, carry):
            at = (i // groups, i % groups)
            mine[at] = mine[at] + other[at]
            return carry

        lax.fori_loop(0, self.dp * groups, add, 0)
        for copy in self.across[index]:
            copy.start()

    def first_small(self):
        one, came, two = self.small_buffers[:3]
        self.pair[-1][0].wait_recv()
        two[...] = one[...] + came[...]
        for copy in self.across[-1]:
            copy.start()

    def middle(self, index):
        mine, _, came, sums, _ = self.buffers[index]
        for copy in self.across[index]:
            copy.wait_recv()

        def add(k, carry):
            total = mine[k, self.g].astype(F32)
            for j in range(self.groups - 1):
                total = total + came[j, k].astype(F32)
            sums[k] = total.astype(BF)
            return carry

        lax.fori_loop(0, self.dp, add, 0)
        for copy in self.along[index]:
            copy.start()

    def middle_small(self):
        _, _, two, groups_in, three, _ = self.small_buffers
        for copy in self.across[-1]:
            copy.wait_recv()
        total = two[...]
        for j in range(self.groups - 1):
            total = total + groups_in[j]
        three[...] = total
        for copy in self.along[-1]:
            copy.start()

    def finish(self):
        for index, out in enumerate(self.outs):
            sums, last = self.buffers[index][3:]
            for copy in self.along[index]:
                copy.wait_recv()
            total = sums[self.d].astype(F32)
            for j in range(self.dp - 1):
                total = total + last[j].astype(F32)
            out[...] = total
        three, dp_in = self.small_buffers[4:]
        for copy in self.along[-1]:
            copy.wait_recv()
        total = three[...]
        for j in range(self.dp - 1):
            total = total + dp_in[j]
        self.small_out[...] = total
        for batch in self.pair + self.across + self.along:
            for copy in batch:
                copy.wait_send()


class Exchange:
    def __init__(self, ctx, mover, source, target):
        d, c = lax.axis_index("dp"), lax.axis_index("ctx")
        groups = ctx // 2
        self.steps = []
        for t in range(groups):
            group = flip(c // 2, t, groups)
            same, other = group * 2 + c % 2, group * 2 + 1 - c % 2
            if t == 0:
                self.own = mover.local(source.at[c], target.at[c])
                batch = []
            else:
                batch = [mover.remote(source.at[same], target.at[c], (d, same))]
            batch.append(mover.remote(source.at[other], target.at[c], (d, other)))
            self.steps.append(batch)

    @staticmethod
    def count(ctx):
        return ctx - 1

    def start(self, t):
        if t == 0:
            self.own.start()
        for copy in self.steps[t]:
            copy.start()

    def arrive(self, t):
        if t == 0:
            self.own.wait()
        for copy in self.steps[t]:
            copy.wait_recv()

    def sent(self):
        for batch in self.steps:
            for copy in batch:
                copy.wait_send()


def columns(values):
    return jnp.sum(values, axis=0, keepdims=True)


def finish_kernel(dp, ctx, *refs):
    loaded, refs = refs[:6], refs[6:]
    outs, small_out, x_out, refs = refs[:3], refs[3], refs[4], refs[5:]
    grads, result, small, refs = refs[:3], refs[3], refs[4], refs[5:]
    (xb, dq, dk, dv, w, grad_sum), refs = refs[:6], refs[6:]
    buffers, small_buffers, refs = refs[:15], refs[15:21], refs[21:]
    local_sem, send_sem, recv_sem, load_sem = refs
    loads = [
        pltpu.make_async_copy(source, target, load_sem.at[i])
        for i, (source, target) in enumerate(zip(loaded, (xb, dq, dk, dv, w, grad_sum)))
    ]
    for copy in loads:
        copy.start()
    d, c = lax.axis_index("dp"), lax.axis_index("ctx")
    groups = ctx // 2
    g = c // 2
    half, width = result.shape[1:]
    held, late = grads[0].shape[3:]
    mover = Mover(local_sem, send_sem, recv_sem)
    scatter = Scatter(
        dp,
        ctx,
        grads,
        outs,
        [buffers[i * 5 : i * 5 + 5] for i in range(3)],
        small,
        small_out,
        small_buffers,
        mover,
    )
    give = Exchange(ctx, mover, result, x_out)
    greet([((d + k) % dp, c) for k in range(1, dp)] + [(d, (c + k) % ctx) for k in range(1, ctx)])
    small[...] = jnp.zeros_like(small)
    loads[0].wait()
    across = xb[...].T

    def weight_gradient(index, rows_grad):
        loads[1 + index].wait()
        total = dg(across, rows_grad[:, width - late :], NN)
        for block in range(dp * ctx):
            at = (block // ctx, block % ctx // 2, block % 2)
            grads[index][at] = total[block * held : (block + 1) * held].astype(BF)
        scatter.begin(index)

    def row_tile(t):
        block = flip(g, t, groups)
        rows = pl.ds(pl.multiple_of(block * 2 * half, 2 * half), 2 * half)
        total = grad_sum[rows, :]
        for i, rows_grad in enumerate((dq, dk, dv)):
            total = total + dg(rows_grad[rows, :], w[:, i * width : (i + 1) * width], NT)
        result[pl.ds(block * 2, 2)] = total.astype(BF).reshape(2, half, width)
        give.start(t)

    tiles = list(range(groups - 1, -1, -1))
    weight_gradient(0, dq)
    weight_gradient(1, dk)
    scatter.first(0)
    weight_gradient(2, dv)
    scatter.first(1)
    for copy in loads[4:]:
        copy.wait()
    row_tile(tiles.pop(0))
    scatter.first(2)
    small[0:1, :] = columns(dq[...].astype(F32))
    small[1:2, :] = columns(dv[...].astype(F32))
    scatter.begin_small()
    row_tile(tiles.pop(0))
    scatter.first_small()
    for t in tiles:
        row_tile(t)
    scatter.middle_small()
    for index in range(3):
        scatter.middle(index)
    scatter.finish()
    for t in range(groups):
        give.arrive(t)
    give.sent()


def finish_gradients(xb, dq, dk, dv, w, grad_sum, dp, ctx):
    rows, width = xb.shape
    remotes = Scatter.count(dp, ctx, 3) + Exchange.count(ctx)
    S = jax.ShapeDtypeStruct
    vmem = pl.BlockSpec(memory_space=pltpu.VMEM)
    late = width - width // 256 * 128
    source = S((dp, ctx // 2, 2, width // (dp * ctx), late), BF)
    small = S((8, width), F32)
    moved = (ctx, rows // ctx, width)
    return pl.pallas_call(
        functools.partial(finish_kernel, dp, ctx),
        in_specs=[pl.BlockSpec(memory_space=pl.ANY)] * 6,
        out_specs=[vmem] * 4 + [pl.BlockSpec(memory_space=pl.ANY)],
        out_shape=[S(source.shape[3:], F32)] * 3 + [small, S(moved, BF)],
        scratch_shapes=[pltpu.VMEM(source.shape, BF)] * 3
        + [pltpu.VMEM(moved, BF), pltpu.VMEM(small.shape, F32)]
        + [pltpu.VMEM(array.shape, array.dtype) for array in (xb, dq, dk, dv, w, grad_sum)]
        + Scatter.scratch(dp, ctx, [source] * 3, small)
        + [
            pltpu.SemaphoreType.DMA((4,)),
            pltpu.SemaphoreType.DMA((remotes,)),
            pltpu.SemaphoreType.DMA((remotes,)),
            pltpu.SemaphoreType.DMA((6,)),
        ],
        compiler_params=pltpu.CompilerParams(
            collective_id=3, has_side_effects=True, vmem_limit_bytes=VMEM_BYTES
        ),
        name="finish_gradients",
    )(xb, dq, dk, dv, w, grad_sum)


def head_lanes(shape, h):
    lane = lax.broadcasted_iota(jnp.int32, shape, len(shape) - 1)
    return (lane >= 64) == (h == 1), lane == (64 if h == 0 else 0)


def load_keys(keys, own_ref, sib_ref, lengths_ref, ctx):
    c = lax.axis_index("ctx")
    rows = own_ref.shape[0]
    half = rows // ctx
    length = lengths_ref[lax.axis_index("dp") * (ctx // 2) + c // 2]
    slot = lax.broadcasted_iota(jnp.int32, (rows, 128), 0)
    source = lax.broadcasted_iota(jnp.int32, (ctx, half, 128), 0).reshape(rows, 128)
    high = (2 * ctx - 1 - 2 * source) * half + slot
    for i, ref in enumerate((own_ref, sib_ref)):
        member = c % 2 if i == 0 else 1 - c % 2
        counted = jnp.where(member == 0, slot, high) < length
        for h in range(2):
            inside, spare = head_lanes((rows, 128), h)
            rest = jnp.where(spare & ~counted, masked_score, 0.0).astype(BF)
            keys[h, i * rows : (i + 1) * rows, :] = jnp.where(inside, ref[...], rest)


def forward_kernel(dp, ctx, bq, *refs):
    (x_ref, w_ref, vec_ref, lengths_ref), gathered, refs = refs[:4], refs[4:7], refs[7:]
    (mb_ref, mix_ref, lse_ref, own_to, sib_to), spread_to, refs = refs[:5], refs[5:8], refs[8:]
    keys, own, sib, local_sem, send_sem, recv_sem, pair_send, pair_recv, store_sem = refs
    spread = Spread(dp, ctx, gathered, spread_to, Mover(local_sem, send_sem, recv_sem))
    pairs, steps = pl.num_programs(0), pl.num_programs(1)
    pair, j = pl.program_id(0), pl.program_id(1)
    step = pair * steps + j
    last = forward_steps(pairs, steps)
    half, width = x_ref.shape

    def to_sibling(number):
        return pltpu.make_async_remote_copy(
            src_ref=own.at[number, pl.ds(1, 2)],
            dst_ref=sib.at[number],
            send_sem=pair_send.at[number],
            recv_sem=pair_recv.at[number],
            device_id=spread.devices[-1],
            device_id_type=MESH,
        )

    def stores(number):
        return [
            pltpu.make_async_copy(own.at[number], own_to.at[number], store_sem.at[number, 0]),
            pltpu.make_async_copy(sib.at[number], sib_to.at[number], store_sem.at[number, 1]),
        ]

    def project(number):
        lanes = [pl.ds(pl.multiple_of(number * 128 + i * width, 128), 128) for i in range(3)]
        weights = jnp.concatenate([w_ref[:, part] for part in lanes], axis=1)
        rows = dg(x_ref[...], weights, NN)
        own[number, 0] = (rows[:, :128] + vec_ref[0:1, lanes[0]]).astype(BF)
        own[number, 1] = rows[:, 128:256].astype(BF)
        own[number, 2] = (rows[:, 256:] + vec_ref[1:2, lanes[0]]).astype(BF)
        to_sibling(number).start()

    @pl.when(step == 0)
    def _():
        greet(spread.devices)
        spread.begin()
        project(pair)

    @pl.when(j == 0)
    def _():
        to_sibling(pair).wait_recv()
        for copy in stores(pair):
            copy.start()
        load_keys(keys, own.at[pair, 1], sib.at[pair, 0], lengths_ref, ctx)

    @pl.when((j == 1) & (pair < pairs - 1))
    def _():
        project(pair + 1)

    rows = pl.ds(pl.multiple_of(j * bq, bq), bq)
    q = own[pair, 0, rows, :] * jnp.asarray(0.125, BF)
    scores = []
    for h in range(2):
        inside, spare = head_lanes((bq, 128), h)
        rest = jnp.where(spare, jnp.ones((), BF), jnp.zeros((), BF))
        scores.append(dg(jnp.where(inside, q, rest), keys[h], NT))
    outs, lses = [], []
    for h in range(2):
        top = jnp.max(scores[h], axis=1, keepdims=True)
        weights = jnp.exp(scores[h] - top)
        total = jnp.sum(weights, axis=1, keepdims=True)
        low = weights.astype(BF)
        mixed = dg(low[:, :half], own[pair, 2], NN) + dg(low[:, half:], sib[pair, 1], NN)
        outs.append(mixed / total)
        lses.append(top + jnp.log(total))
    lane = lax.broadcasted_iota(jnp.int32, (bq, 128), 1)
    mixed = jnp.where(lane < 64, outs[0], outs[1])
    mix_ref[...] = mixed
    mb_ref[...] = mixed.astype(BF)
    lse_ref[0] = jnp.where(lane == 0, lses[0], lses[1]).T[:8]

    for index, ats in enumerate(last):
        for level in range(1, spread.levels + 1):

            @pl.when(step == ats[0] + (ats[1] - ats[0]) * (level - 1) // (spread.levels - 1))
            def _(index=index, level=level):
                spread.forward(index, level)

    @pl.when(step == pairs * steps - 1)
    def _():
        spread.finish()
        for number in range(pairs):
            to_sibling(number).wait_send()
            for copy in stores(number):
                copy.wait()


def attention_forward(x, w, vec, lengths, gathered, dp, ctx, bq=256):
    rows, width = x.shape
    pairs = width // 128
    S = jax.ShapeDtypeStruct
    blk = pl.BlockSpec((bq, 128), lambda p, j: (j, p))
    any_space = pl.BlockSpec(memory_space=pl.ANY)
    vmem = pl.BlockSpec(memory_space=pltpu.VMEM)
    remotes = Spread.count(ctx, 3)
    return pl.pallas_call(
        functools.partial(forward_kernel, dp, ctx, bq),
        grid=(pairs, rows // bq),
        in_specs=[vmem] * 3 + [pl.BlockSpec(memory_space=pltpu.SMEM)] + [any_space] * 3,
        out_specs=[blk, blk, pl.BlockSpec((1, 8, bq), lambda p, j: (p, 0, j))] + [any_space] * 5,
        out_shape=[S(x.shape, BF), S(x.shape, F32), S((pairs, 8, rows), F32)]
        + [S((pairs, count, rows, 128), BF) for count in (3, 2)]
        + [S((dp, ctx) + array.shape[1:], BF) for array in gathered],
        scratch_shapes=[
            pltpu.VMEM((2, 2 * rows, 128), BF),
            pltpu.VMEM((pairs, 3, rows, 128), BF),
            pltpu.VMEM((pairs, 2, rows, 128), BF),
            pltpu.SemaphoreType.DMA((3,)),
            pltpu.SemaphoreType.DMA((remotes,)),
            pltpu.SemaphoreType.DMA((remotes,)),
            pltpu.SemaphoreType.DMA((pairs,)),
            pltpu.SemaphoreType.DMA((pairs,)),
            pltpu.SemaphoreType.DMA((pairs, 2)),
        ],
        compiler_params=pltpu.CompilerParams(
            vmem_limit_bytes=VMEM_BYTES, collective_id=1, has_side_effects=True
        ),
        cost_estimate=pl.CostEstimate(
            flops=16 * rows * rows * 128 * pairs,
            bytes_accessed=14 * rows * 768,
            transcendentals=4 * rows * rows * pairs,
        ),
        name="attend",
    )(x, w, vec, lengths, *gathered)


def forward_steps(pairs, steps):
    count = pairs * steps
    return [(count * a // 24, count * b // 24) for a, b in ((11, 18), (12, 19), (13, 20))]


def backward_steps(pairs, steps):
    count = pairs * steps
    first = [count * at // 12 for at in (0, 0, 1, 7)]
    middle = [count * at // 12 for at in (5, 4, 8, 10)]
    return first, middle


def backward_kernel(dp, ctx, ck, *refs):
    (q_ref, ko_ref, vo_ref, ks_ref, vs_ref, do_ref, mix_ref, lengths_ref, lse_ref), refs = (
        refs[:9],
        refs[9:],
    )
    q_ref, ko_ref, vo_ref, ks_ref, vs_ref = (
        ref.at[0, 0] for ref in (q_ref, ko_ref, vo_ref, ks_ref, vs_ref)
    )
    sources, small, x_ref, refs = refs[:3], refs[3], refs[4], refs[5:]
    (dq_ref, dk_ref, dv_ref), refs = refs[:3], refs[3:]
    summed, small_out, refs = refs[:4], refs[4], refs[5:]
    (keys, dk, dv, held, going, coming, across, dq_held, early), refs = refs[:9], refs[9:]
    buffers, small_buffers, refs = refs[:20], refs[20:26], refs[26:]
    local_sem, send_sem, recv_sem, pair_send, pair_recv = refs
    scatter = Scatter(
        dp,
        ctx,
        [*sources, early],
        summed,
        [buffers[i * 5 : i * 5 + 5] for i in range(4)],
        small,
        small_out,
        small_buffers,
        Mover(local_sem, send_sem, recv_sem),
    )
    steps = pl.num_programs(1)
    j = pl.program_id(1)
    step = pl.program_id(0) * steps + j

    pair = pl.program_id(0)
    sibling = scatter.devices[-1]

    def to_sibling(number):
        return [
            pltpu.make_async_remote_copy(
                src_ref=going.at[number, i],
                dst_ref=coming.at[number, i],
                send_sem=pair_send.at[number * 2 + i],
                recv_sem=pair_recv.at[number * 2 + i],
                device_id=sibling,
                device_id_type=MESH,
            )
            for i in range(2)
        ]

    def settle(number):
        lanes = pl.ds(pl.multiple_of(number * 128, 128), 128)
        totals = []
        for i, (copy, out) in enumerate(zip(to_sibling(number), (dk_ref, dv_ref))):
            copy.wait_recv()
            total = held[number % 2, i] + coming[number, i].astype(F32)
            totals.append(total.astype(BF))
            out[:, lanes] = totals[-1]
        return totals

    @pl.when(step == 0)
    def _():
        greet(scatter.devices)
        scatter.begin(1)
        scatter.begin_small()
        scatter.begin(0)
        scatter.begin(2)
        across[...] = x_ref[...].T

    early_pairs = early.shape[4] // 384

    @pl.when((j == 0) & (pair > 0) & (pair <= early_pairs))
    def _():
        rows_grad = jnp.concatenate([dq_held[...], *settle(pair - 1)], axis=1)
        total = dg(across[...], rows_grad, NN)
        lanes = pl.ds(pl.multiple_of((pair - 1) * 384, 128), 384)
        owned = early.shape[3]
        for block in range(dp * ctx):
            at = (block // ctx, block % ctx // 2, block % 2)
            part = total[block * owned : (block + 1) * owned]
            early[(*at, slice(None), lanes)] = part.astype(BF)

    @pl.when((j == 0) & (pair == early_pairs))
    def _():
        scatter.begin(3)

    @pl.when((j == 0) & (pair > early_pairs))
    def _():
        settle(pair - 1)

    @pl.when(j == 0)
    def _():
        load_keys(keys, ko_ref, ks_ref, lengths_ref, ctx)
        dk[...] = jnp.zeros_like(dk)
        dv[...] = jnp.zeros_like(dv)

    half, bq = ko_ref.shape[0], q_ref.shape[0]
    q = q_ref[...] * jnp.asarray(0.125, BF)
    do = do_ref[...]
    prod = (do.astype(F32) * mix_ref[...]).T
    zero, one = jnp.zeros((), BF), jnp.ones((), BF)
    heads = []
    for h in range(2):
        inside, spare = head_lanes((bq, 128), h)
        heads.append(
            (
                jnp.where(inside, q, jnp.where(spare, one, zero)),
                jnp.where(inside, q, zero),
                jnp.where(inside, do, zero),
                lse_ref[0, h : h + 1, :],
                jnp.sum(prod[h * 64 : (h + 1) * 64], axis=0, keepdims=True),
            )
        )
    dq = jnp.zeros((bq, 128), F32)
    for first in range(0, 2 * half, ck):
        rows = slice(first, first + ck)
        v = vo_ref[rows, :] if first < half else vs_ref[first - half : first - half + ck, :]
        for h in range(2):
            qm, qz, dom, lse, delta = heads[h]
            k = keys[h, rows, :]
            p = jnp.exp(dg(k, qm, NT) - lse)
            ds = (p * (dg(v, dom, NT) - delta)).astype(BF)
            dv[rows, :] += dg(p.astype(BF), dom, NN)
            dk[rows, :] += dg(ds, qz, NN)
            dq = dq + dg(ds, k, TN)
    low_dq = (dq * 0.125).astype(BF)
    dq_ref[...] = low_dq
    dq_held[pl.ds(pl.multiple_of(j * bq, bq), bq), :] = low_dq

    @pl.when(j == steps - 1)
    def _():
        for i, total in enumerate((dk, dv)):
            held[pair % 2, i] = total[:half, :]
            going[pair, i] = total[half:, :].astype(BF)
        for copy in to_sibling(pair):
            copy.start()

    first, middle_at = backward_steps(pl.num_programs(0), steps)

    @pl.when(step == first[0])
    def _():
        scatter.first_small()

    @pl.when(step == middle_at[0])
    def _():
        scatter.middle_small()

    for index in range(4):

        @pl.when(step == first[index])
        def _(index=index):
            scatter.first(index)

        @pl.when(step == middle_at[index])
        def _(index=index):
            scatter.middle(index)

    @pl.when(step == pl.num_programs(0) * steps - 1)
    def _():
        scatter.finish()
        settle(pair)
        for number in range(pl.num_programs(0)):
            for copy in to_sibling(number):
                copy.wait_send()


def attention_backward(
    own, sib, do, mix, lengths, lse, sources, small, x, dp, ctx, bq=1024, ck=256
):
    rows, width = do.shape
    pairs = width // 128
    S = jax.ShapeDtypeStruct
    blk = pl.BlockSpec((bq, 128), lambda p, j: (j, p))
    whole_of = [
        pl.BlockSpec((1, 1, rows, 128), lambda p, j, i=i: (p, i, 0, 0)) for i in (1, 2, 0, 1)
    ]
    any_space = pl.BlockSpec(memory_space=pl.ANY)
    early = jax.ShapeDtypeStruct(
        (dp, ctx // 2, 2, width // (dp * ctx), pairs // 2 * 384), BF
    )
    every = [*sources, early]
    remotes = Scatter.count(dp, ctx, 4)
    whole = pl.BlockSpec(small.shape, lambda p, j: (0, 0))
    sums = [s.shape[-2:] for s in every]
    all_rows = pl.BlockSpec((rows, width), lambda p, j: (0, 0))
    return pl.pallas_call(
        functools.partial(backward_kernel, dp, ctx, ck),
        grid=(pairs, rows // bq),
        in_specs=[pl.BlockSpec((1, 1, bq, 128), lambda p, j: (p, 0, j, 0))]
        + whole_of
        + [blk, blk]
        + [pl.BlockSpec(memory_space=pltpu.SMEM)]
        + [pl.BlockSpec((1, 8, bq), lambda p, j: (p, 0, j))]
        + [any_space] * 3
        + [whole, pl.BlockSpec(memory_space=pltpu.VMEM)],
        out_specs=[blk, all_rows, all_rows]
        + [pl.BlockSpec(shape, lambda p, j: (0, 0)) for shape in sums]
        + [whole],
        out_shape=[S(do.shape, BF)] * 3
        + [S(shape, F32) for shape in sums]
        + [S(small.shape, F32)],
        scratch_shapes=[
            pltpu.VMEM((2, 2 * rows, 128), BF),
            pltpu.VMEM((2 * rows, 128), F32),
            pltpu.VMEM((2 * rows, 128), F32),
            pltpu.VMEM((2, 2, rows, 128), F32),
            pltpu.VMEM((pairs, 2, rows, 128), BF),
            pltpu.VMEM((pairs, 2, rows, 128), BF),
            pltpu.VMEM((width, rows), BF),
            pltpu.VMEM((rows, 128), BF),
            pltpu.VMEM(early.shape, BF),
        ]
        + Scatter.scratch(dp, ctx, every, small)
        + [
            pltpu.SemaphoreType.DMA((4,)),
            pltpu.SemaphoreType.DMA((remotes,)),
            pltpu.SemaphoreType.DMA((remotes,)),
            pltpu.SemaphoreType.DMA((2 * pairs,)),
            pltpu.SemaphoreType.DMA((2 * pairs,)),
        ],
        compiler_params=pltpu.CompilerParams(
            vmem_limit_bytes=VMEM_BYTES, collective_id=2, has_side_effects=True
        ),
        cost_estimate=pl.CostEstimate(
            flops=40 * rows * rows * 128 * pairs,
            bytes_accessed=26 * rows * 768,
            transcendentals=4 * rows * rows * pairs,
        ),
        name="attend_back",
    )(own, own, own, sib, sib, do, mix, lengths, lse, *sources, small, x)


def gelu_and_slope(x):
    t = pl.reciprocal(1.0 + 0.2316419 * jnp.abs(x))
    bell = 0.3989422804 * jnp.exp(-0.5 * x * x)
    poly = 1.330274429 * t - 1.821255978
    poly = poly * t + 1.781477937
    poly = poly * t - 0.356563782
    poly = poly * t + 0.319381530
    tail = bell * (poly * t)
    below = jnp.where(x < 0.0, tail, 1.0 - tail)
    return x * below, below + x * bell


def middle_kernel(dp, ctx, *refs):
    (mb, xb, rest_src, up_src, vec, bias_up, wo_src, wu_src, wd_src), refs = refs[:9], refs[9:]
    (dm, grad_sum, out_to, go_to, gu_to, gd_to, small), refs = refs[:7], refs[7:]
    (wo, wu, wd, rest, upstream, result, active, dinner, slope, fb, db, da), refs = (
        refs[:12],
        refs[12:],
    )
    (other, summed), refs = refs[:2], refs[2:]
    load_sem, local_sem, send_sem, recv_sem = refs
    groups = ctx // 2
    g = lax.axis_index("ctx") // 2
    half, width = result.shape[1:]
    tile = 2 * half
    chunks = range(wu.shape[1] // width)
    step = pl.program_id(0)
    mover = Mover(local_sem, send_sem, recv_sem)
    rest_in = Exchange(ctx, mover, rest_src, rest)
    up_in = Exchange(ctx, mover, up_src, upstream)
    give = Exchange(ctx, mover, result, out_to)
    loads = [
        pltpu.make_async_copy(source, target, load_sem.at[i])
        for i, (source, target) in enumerate(((wo_src, wo), (wu_src, wu), (wd_src, wd)))
    ]
    stores = [
        pltpu.make_async_copy(source, target, load_sem.at[i])
        for i, (source, target) in enumerate(((wo, go_to), (wu, gu_to), (summed, gd_to)))
    ]
    d, c = lax.axis_index("dp"), lax.axis_index("ctx")
    held = other.shape[2]

    def block_rows(i, k, member):
        return pl.ds(pl.multiple_of(((i * groups + k) * 2 + member) * held, 8), held)

    blocks = [(i, k) for i in range(dp) for k in range(groups)]
    to_sibling = [
        mover.remote(wd.at[block_rows(i, k, 1 - c % 2)], other.at[i, k], (d, g * 2 + 1 - c % 2))
        for i, k in blocks
    ]

    def load(index):
        @pl.when(step == 0)
        def _():
            loads[index].wait()

    @pl.when(step == 0)
    def _():
        for copy in loads:
            copy.start()
        greet([(d, (c + k) % ctx) for k in range(1, ctx)])
        for t in range(groups):
            rest_in.start(t)
            up_in.start(t)
        small[...] = jnp.zeros_like(small)

    @pl.when(step < groups)
    def _():
        block = flip(g, step, groups)
        rows = pl.ds(pl.multiple_of(block * tile, tile), tile)
        pair = pl.ds(block * 2, 2)
        load(0)
        hidden = dg(mb[rows, :], wo[...], NN) + vec[2:3, :] + xb[rows, :].astype(F32)
        for t in range(groups):

            @pl.when(step == t)
            def _(t=t):
                rest_in.arrive(t)

        hidden = hidden + rest[pair].reshape(tile, width).astype(F32)
        normed, standard_one, inverse_one = normalize(hidden, vec[6:7, :], vec[4:5, :])
        low = normed.astype(BF)
        fb[rows, :] = low
        load(1)
        parts = [slice(i * width, (i + 1) * width) for i in chunks]
        inner = dg(low, wu[:, parts[0]], NN)
        for i, part in enumerate(parts):
            ahead = dg(low, wu[:, parts[i + 1]], NN) if i + 1 < len(parts) else None
            value, slope[:, part] = gelu_and_slope(inner + bias_up[:, part])
            active[rows, part] = value.astype(BF)
            inner = ahead
        load(2)
        hidden = normed + dg(active[rows, :], wd[...], NN) + vec[3:4, :]
        out, standard, inverse = normalize(hidden, vec[7:8, :], vec[5:6, :])
        result[pair] = out.astype(BF).reshape(2, half, width)
        for t in range(groups):

            @pl.when(step == t)
            def _(t=t):
                give.start(t)
                up_in.arrive(t)

        error = upstream[pair].reshape(tile, width).astype(F32)
        grad = normalize_back(error, standard, inverse, vec[7:8, :])
        low_grad = grad.astype(BF)
        db[rows, :] = low_grad
        small[1:2, :] += columns(low_grad.astype(F32))
        small[3:4, :] += columns(error)
        small[5:6, :] += columns(error * standard)
        for i in chunks:
            part = slice(i * width, (i + 1) * width)
            change = dg(low_grad, wd[part, :], NT) * slope[:, part]
            change = change.astype(BF)
            dinner[rows, part] = change
            small[6 + i : 7 + i, :] += columns(change.astype(F32))
        grad = grad + dg(dinner[rows, :], wu[...], NT)
        small[2:3, :] += columns(grad)
        small[4:5, :] += columns(grad * standard_one)
        grad = normalize_back(grad, standard_one, inverse_one, vec[6:7, :])
        grad_sum[rows, :] = grad
        low_grad = grad.astype(BF)
        da[rows, :] = low_grad
        small[0:1, :] += columns(low_grad.astype(F32))
        dm[rows, :] = dg(low_grad, wo[...], NT).astype(BF)

    @pl.when(step == groups)
    def _():
        for i in chunks:
            part = slice(i * width, (i + 1) * width)
            wd[part, :] = dg(active[:, part], db[...], TN).astype(BF)
        for copy in to_sibling:
            copy.start()
        across = fb[...].T
        for i in chunks:
            part = slice(i * width, (i + 1) * width)
            wu[:, part] = dg(across, dinner[:, part], NN).astype(BF)
        stores[1].start()
        for copy in to_sibling:
            copy.wait()
        for i, k in blocks:
            summed[i, k] = wd[block_rows(i, k, c % 2), :] + other[i, k]
        stores[2].start()
        wo[...] = dg(mb[...], da[...], TN).astype(BF)
        stores[0].start()
        for t in range(groups):
            give.arrive(t)
        for move in (rest_in, up_in, give):
            move.sent()
        for copy in stores:
            copy.wait()


def middle(mb, xb, rest, upstream, vec, bias_up, wo, wu, wd, dp, ctx):
    rows, width = mb.shape
    hidden = wu.shape[1]
    half = rows // ctx
    S = jax.ShapeDtypeStruct
    any_space = pl.BlockSpec(memory_space=pl.ANY)
    vmem = pl.BlockSpec(memory_space=pltpu.VMEM)
    held = (dp, ctx // 2, hidden // (dp * ctx), width)
    remotes = 3 * Exchange.count(ctx) + dp * (ctx // 2)
    return pl.pallas_call(
        functools.partial(middle_kernel, dp, ctx),
        grid=(ctx // 2 + 1,),
        in_specs=[vmem, vmem, any_space, any_space, vmem, vmem] + [any_space] * 3,
        out_specs=[vmem, vmem] + [any_space] * 4 + [vmem],
        out_shape=[S(mb.shape, BF), S(mb.shape, F32), S(rest.shape, BF)]
        + [S(wo.shape, BF), S(wu.shape, BF), S(held, BF)]
        + [S((16, width), F32)],
        scratch_shapes=[pltpu.VMEM(array.shape, BF) for array in (wo, wu, wd)]
        + [pltpu.VMEM(rest.shape, BF)] * 3
        + [pltpu.VMEM((rows, hidden), BF)] * 2
        + [pltpu.VMEM((2 * half, hidden), F32)]
        + [pltpu.VMEM((rows, width), BF)] * 3
        + [pltpu.VMEM(held, BF)] * 2
        + [
            pltpu.SemaphoreType.DMA((3,)),
            pltpu.SemaphoreType.DMA((3,)),
            pltpu.SemaphoreType.DMA((remotes,)),
            pltpu.SemaphoreType.DMA((remotes,)),
        ],
        compiler_params=pltpu.CompilerParams(
            vmem_limit_bytes=VMEM_BYTES, collective_id=4, has_side_effects=True
        ),
        cost_estimate=pl.CostEstimate(
            flops=2 * 3 * rows * width * (2 * hidden + width),
            bytes_accessed=50 << 20,
            transcendentals=rows * hidden,
        ),
        name="middle",
    )(mb, xb, rest, upstream, vec, bias_up, wo, wu, wd)


def normalize(hidden, scale_row, shift_row):
    centred = hidden - jnp.mean(hidden, axis=-1, keepdims=True)
    inverse = lax.rsqrt(jnp.mean(centred * centred, axis=-1, keepdims=True) + epsilon)
    standard = centred * inverse
    return (standard * scale_row + shift_row, standard, inverse)


def normalize_back(gradient, standard, inverse, scale_row):
    scaled = gradient * scale_row
    centred = scaled - jnp.mean(scaled, axis=-1, keepdims=True)
    return (centred - standard * jnp.mean(scaled * standard, axis=-1, keepdims=True)) * inverse


def write_kernel(dp, ctx, small_ref, sums_ref, out_ref, tokens_ref, *refs):
    sources, early, (out_to, tokens_to), refs = refs[:6], refs[6], refs[7:9], refs[9:]
    targets, (vectors_to, bias_to) = refs[:6], refs[6:]
    out_to[...] = out_ref[...].astype(F32)
    tokens_to[...] = tokens_ref[...].astype(F32)

    @pl.when(pl.program_id(0) == 0)
    def _():
        for i in range(3):
            late = sources[i].shape[1]
            first = targets[i].shape[1] - late
            targets[i][:, first:] = sources[i][...]
            for lane in range(0, first, 128):
                at = lane * 3 + i * 128
                targets[i][:, lane : lane + 128] = early[:, at : at + 128]
        for source, target in zip(sources[3:], targets[3:]):
            target[...] = source[...]
        device = lax.axis_index("dp") * ctx + lax.axis_index("ctx")
        width = small_ref.shape[1]
        held, held_up = vectors_to.shape[1], bias_to.shape[1]
        rows = jnp.concatenate([sums_ref[0:2, :], small_ref[0:6, :]], axis=0)
        vectors_to[...] = pltpu.roll(rows, (width - device * held) % width, 1)[:, :held]
        first = device * held_up
        row = small_ref[pl.ds(6 + first // width, 1), :]
        row = jnp.broadcast_to(row, (8, width))
        bias_to[...] = pltpu.roll(row, (width - first % width) % width, 1)[0:1, :held_up]


def write_out(small, sums, out, tokens, own, early, held_up, dp, ctx):
    block = pl.BlockSpec((ctx // 2,) + out.shape[1:], lambda i: (i, 0, 0))
    S = jax.ShapeDtypeStruct

    def whole(shape):
        return pl.BlockSpec(shape, lambda i: (0, 0))

    given = [array.shape for array in (*own, early)]
    shapes = [(own[0].shape[0], out.shape[2])] * 3 + [array.shape for array in own[3:]]
    vectors = (8, out.shape[2] // (dp * ctx))
    return pl.pallas_call(
        functools.partial(write_kernel, dp, ctx),
        grid=(2,),
        in_specs=[whole(small.shape), whole(sums.shape), block, block]
        + [whole(shape) for shape in given],
        out_specs=[block, block]
        + [whole(shape) for shape in shapes]
        + [whole(vectors), whole((1, held_up))],
        out_shape=[S(out.shape, F32)] * 2
        + [S(shape, F32) for shape in shapes]
        + [S(vectors, F32), S((1, held_up), F32)],
        compiler_params=pltpu.CompilerParams(vmem_limit_bytes=VMEM_BYTES),
        name="write_out",
    )(small, sums, out, tokens, *own, early)


def on_device(
    tokens, cotangent, lengths, w_query, w_key, w_value, w_attn_out, w_up, b_up, w_down, vectors
):
    seqs, rows_dev, width = tokens.shape
    dp = lax.axis_size("dp")
    ctx = lax.axis_size("ctx")
    half = rows_dev // 2
    rows = half * ctx
    def by_owner(grad):
        return grad.reshape(dp, ctx // 2, 2, -1, grad.shape[1])

    split = tokens.reshape(ctx, half, width)
    held = w_query.shape[0]
    extra = jnp.concatenate([vectors.T, b_up.reshape(held, -1)], axis=1)
    extra = jnp.pad(extra, ((0, 0), (0, 128 - extra.shape[1])))
    low_in, left_out, upstream, full_first, *over_dp = gather_first(
        split,
        cotangent.reshape(ctx, half, width),
        jnp.concatenate([w_query, w_key, w_value, extra], axis=1),
        w_attn_out,
        w_up,
        w_down,
        dp,
        ctx,
    )
    low_in = low_in.reshape(rows, width)
    full_first = full_first.reshape(width, -1)
    vector_rows = full_first[:, 3 * width : 3 * width + 8].T.astype(F32)
    bias_columns = b_up.shape[0] // held
    full_bias_up = full_first[:, 3 * width + 8 : 3 * width + 8 + bias_columns].reshape(-1).astype(F32)
    low_mixed, mixed, lse, own, sib, full_attn, full_up, full_down = attention_forward(
        low_in, full_first, vector_rows, lengths, over_dp, dp, ctx
    )
    full_attn = full_attn.reshape(width, width)
    full_up = full_up.reshape(width, -1)
    full_down = full_down.reshape(-1, width)

    d_mixed, grad_sum, result, d_attn, d_up, part_down, small = middle(
        low_mixed,
        low_in,
        left_out,
        upstream,
        vector_rows,
        full_bias_up.reshape(1, -1),
        full_attn,
        full_up,
        full_down,
        dp,
        ctx,
    )
    dq, dk, dv, own_attn, own_down, own_up, own_early, small = attention_backward(
        own,
        sib,
        d_mixed,
        mixed,
        lengths,
        lse,
        [by_owner(d_attn), part_down, by_owner(d_up)],
        small,
        low_in,
        dp,
        ctx,
    )
    own_query, own_key, own_value, sums, grad_tokens = finish_gradients(
        low_in, dq, dk, dv, full_first, grad_sum, dp, ctx
    )
    output, grad_tokens, *own, own_vectors, own_bias_up = write_out(
        small,
        sums,
        result,
        grad_tokens,
        [own_query, own_key, own_value, own_attn, own_up, own_down],
        own_early,
        b_up.shape[0],
        dp,
        ctx,
    )
    own_query, own_key, own_value, own_attn, own_up, own_down = own
    output = output.reshape(seqs, rows_dev, width)
    grad_tokens = grad_tokens.reshape(seqs, rows_dev, width)
    own_bias_up = own_bias_up.reshape(-1)
    return (
        output,
        grad_tokens,
        own_query,
        own_key,
        own_value,
        own_attn,
        own_up,
        own_bias_up,
        own_down,
        own_vectors,
    )


def solution(mesh):
    in_specs = (
        P("dp", "ctx", None),
        P("dp", "ctx", None),
        P(),
        P(("dp", "ctx"), None),
        P(("dp", "ctx"), None),
        P(("dp", "ctx"), None),
        P(("dp", "ctx"), None),
        P(("dp", "ctx"), None),
        P(("dp", "ctx")),
        P(("dp", "ctx"), None),
        P(None, ("dp", "ctx")),
    )
    out_specs = (
        P("dp", "ctx", None),
        P("dp", "ctx", None),
        P(("dp", "ctx"), None),
        P(("dp", "ctx"), None),
        P(("dp", "ctx"), None),
        P(("dp", "ctx"), None),
        P(("dp", "ctx"), None),
        P(("dp", "ctx")),
        P(("dp", "ctx"), None),
        P(None, ("dp", "ctx")),
    )
    return jax.shard_map(
        on_device, mesh=mesh, in_specs=in_specs, out_specs=out_specs, check_vma=False
    )
```
